32 devices in a mesh: wide: 8 (over z, y), narrow: 4 (over x, core).
Axes of the slice: x: 2, y: 2, z: 4, core: 2. Of those that a mesh axis runs over, the one named last changes fastest.
Arguments:
- tokens: bfloat16 [16384, 1024], P(('wide', 'narrow')), may hold values from -6 to 6
- cotangent: bfloat16 [16384, 1024], P(('wide', 'narrow')), may hold values from -6 to 6
- segment_ids: int32 [16384], P(('wide', 'narrow')), may hold values from 0 to 2, as said below
- key_keep: int32 [16384], P(('wide', 'narrow')), may hold values from 0 to 1, as said below
- patch_coords: int32 [3, 16384], P(None, ('wide', 'narrow')), may hold values from 0 to 13, as said below
- step_count: int32 [1], replicated, may hold values from 2 to 20
- weight_qkv: float32 [1024, 3072], P('wide'), may hold values from -0.25 to 0.25
- weight_out: float32 [1024, 1024], P('wide'), may hold values from -0.75 to 0.75
- weight_up: float32 [1024, 4096], P('wide'), may hold values from -0.1875 to 0.1875
- weight_down: float32 [1024, 4096], P('wide'), may hold values from -0.09375 to 0.09375
- vectors: float32 [13, 1024], P(None, 'wide'), may hold values from -0.6 to 1.45, as said below
- first_qkv: float32 [1024, 3072], P('wide'), may hold values from -0.00018310547 to 0.00018310547
- first_out: float32 [1024, 1024], P('wide'), may hold values from -0.00018310547 to 0.00018310547
- first_up: float32 [1024, 4096], P('wide'), may hold values from -6.1035156e-05 to 6.1035156e-05
- first_down: float32 [1024, 4096], P('wide'), may hold values from -0.00018310547 to 0.00018310547
- first_vectors: float32 [13, 1024], P(None, 'wide'), may hold values from -0.00018310547 to 0.00018310547
- second_qkv: float32 [1024, 3072], P('wide'), may hold values from 7.938887e-11 to 3.1755548e-10
- second_out: float32 [1024, 1024], P('wide'), may hold values from 7.938887e-11 to 3.1755548e-10
- second_up: float32 [1024, 4096], P('wide'), may hold values from 1.03205534e-11 to 3.9694435e-11
- second_down: float32 [1024, 4096], P('wide'), may hold values from 7.938887e-11 to 3.1755548e-10
- second_vectors: float32 [13, 1024], P(None, 'wide'), may hold values from 7.938887e-11 to 3.1755548e-10
Outputs:
- layer_out: bfloat16 [16384, 1024], P(('wide', 'narrow'))
- grad_tokens: bfloat16 [16384, 1024], P(('wide', 'narrow'))
- updated_qkv: float32 [1024, 3072], P('wide')
- updated_out: float32 [1024, 1024], P('wide')
- updated_up: float32 [1024, 4096], P('wide')
- updated_down: float32 [1024, 4096], P('wide')
- updated_vectors: float32 [13, 1024], P(None, 'wide')
- moment_qkv: float32 [1024, 3072], P('wide')
- moment_out: float32 [1024, 1024], P('wide')
- moment_up: float32 [1024, 4096], P('wide')
- moment_down: float32 [1024, 4096], P('wide')
- moment_vectors: float32 [13, 1024], P(None, 'wide')
- square_qkv: float32 [1024, 3072], P('wide')
- square_out: float32 [1024, 1024], P('wide')
- square_up: float32 [1024, 4096], P('wide')
- square_down: float32 [1024, 4096], P('wide')
- square_vectors: float32 [13, 1024], P(None, 'wide')
- grad_norm: float32 [], replicated
- grad_down_bias: float32 [1024], P('wide')
The draws below stay inside these ranges and needn't reach their ends.
Inputs may be any that keep to these rules, and one draw needn't show every extreme that they name: `segment_ids`: within each aligned block of 2048 tokens, segment numbers start at 0 and never fall; each segment is a clip of 784 or 1568 tokens, the last one cut at the block's end. `key_keep`: within each clip the tokens with 0 are its last 0 to 195 tokens; a clip's first token is always 1. `patch_coords`: position of a token in its clip as time = index // 196, row = (index // 14) mod 14, column = index mod 14. `vectors`: rows 0 and 6 lie in 0.55 to 1.45, the other rows in -0.6 to 0.6.
All inputs are finite; a program needn't handle non-finite values.
Results may differ from the reference program's by a relative error of at most 0.014.
The reference program's roundings to bfloat16 on the way count: a program that leaves them out, or rounds other values in their place, can miss the bound.
Values may be sent and summed in bfloat16 or wider, within the bound.
A program may use at most 256 MiB of HBM per device.

```python
import math
from functools import partial
import jax
import jax.numpy as jnp
from jax import lax

D = 1024
HEADS = 16
FF = 4096
GRID = 14
SHORT_T = 4
GROUP = 2048
TOKENS = 16384
NVEC = 13
NPARAM = 12596224


def pack_layout(key):
    base = jax.random.fold_in(key, 11)
    first_key, second_key = jax.random.split(base)
    blocks = TOKENS // GROUP
    frame = GRID * GRID
    short = SHORT_T * frame
    nominal = jax.random.randint(first_key, (blocks, 3), 1, 3) * short
    nominal = nominal.at[0, 0].set(short).at[0, 1].set(short).at[1, 0].set(2 * short)
    padded = jax.random.randint(second_key, (blocks, 3), 0, frame)
    place = jnp.arange(GROUP, dtype=jnp.int32)[None, :]
    first_end = nominal[:, 0:1]
    second_end = first_end + nominal[:, 1:2]
    segment = (place >= first_end).astype(jnp.int32) + (place >= second_end).astype(jnp.int32)
    start = jnp.where(segment == 0, 0, jnp.where(segment == 1, first_end, second_end))
    local = place - start
    live = nominal - padded
    length = jnp.where(segment == 0, live[:, 0:1], jnp.where(segment == 1, live[:, 1:2], live[:, 2:3]))
    keep = (local < length).astype(jnp.int32)
    return (segment.reshape(TOKENS), keep.reshape(TOKENS), local.reshape(TOKENS))


def draw_segment_ids(key, part):
    return pack_layout(key)[0]


def draw_key_keep(key, part):
    return pack_layout(key)[1]


def draw_patch_coords(key, part):
    local = pack_layout(key)[2]
    frame = GRID * GRID
    return jnp.stack([local // frame, local // GRID % GRID, local % GRID]).astype(jnp.int32)


def draw_vectors(key, part):
    base = jnp.clip(jax.random.normal(key, (NVEC, D), jnp.float32), -3.0, 3.0)
    rows_index = jnp.arange(NVEC)[:, None]
    gains = (rows_index == 0) | (rows_index == 6)
    return jnp.where(gains, 1.0 + 0.15 * base, 0.2 * base)


def block_scale(own_key, shape, cuts, low, largest):
    level = 1.0
    for axis_at, blocks in cuts:
        draws = jax.random.uniform(jax.random.fold_in(jax.random.fold_in(own_key, 6), axis_at), (blocks,), jnp.float32, low / len(cuts), largest / len(cuts))
        level = level * jnp.repeat(jnp.exp(draws), shape[axis_at] // blocks).reshape((-1,) + (1,) * (len(shape) - 1 - axis_at))
    return level


def noise(own_key, shape, deviation, reach, shards=(), held_as=jnp.bfloat16):
    drawn = deviation * jax.random.normal(own_key, shape, jnp.float32)
    if shards:
        drawn = drawn * block_scale(own_key, shape, shards, -0.22, 0.18)
    return jnp.clip(drawn, -reach, reach).astype(held_as)


def setup_inputs(seed: int = 0) -> dict:
    key_of = jax.random.split(jax.random.key(seed), 22)
    return {
        "tokens": noise(key_of[0], (TOKENS, D), 1.0, 6.0, ((0, 32),)),
        "cotangent": noise(key_of[1], (TOKENS, D), 1.0, 6.0, ((0, 32),)),
        "segment_ids": draw_segment_ids(jax.random.fold_in(key_of[21], 71), 0),
        "key_keep": draw_key_keep(jax.random.fold_in(key_of[21], 71), 0),
        "patch_coords": draw_patch_coords(jax.random.fold_in(key_of[21], 71), 0),
        "step_count": jax.random.randint(key_of[5], (1,), 2, 21).astype(jnp.int32),
        "weight_qkv": noise(key_of[6], (D, 3 * D), (D // 2) ** -0.5, 0.25, ((0, 8),), jnp.float32),
        "weight_out": noise(key_of[7], (D, D), (D // 16) ** -0.5, 0.75, ((0, 8),), jnp.float32),
        "weight_up": noise(key_of[8], (D, FF), D ** -0.5, 0.1875, ((0, 8),), jnp.float32),
        "weight_down": noise(key_of[9], (D, FF), FF ** -0.5, 0.09375, ((0, 8),), jnp.float32),
        "vectors": draw_vectors(jax.random.fold_in(key_of[21], 71), 0),
        "first_qkv": noise(key_of[11], (D, 3 * D), (0.11 / NPARAM ** 0.5), 0.00018310547, ((0, 8),), jnp.float32),
        "first_out": noise(key_of[12], (D, D), (0.11 / NPARAM ** 0.5), 0.00018310547, ((0, 8),), jnp.float32),
        "first_up": noise(key_of[13], (D, FF), (0.04 / NPARAM ** 0.5), 6.103515625e-05, ((0, 8),), jnp.float32),
        "first_down": noise(key_of[14], (D, FF), (0.11 / NPARAM ** 0.5), 0.00018310547, ((0, 8),), jnp.float32),
        "first_vectors": noise(key_of[15], (NVEC, D), (0.11 / NPARAM ** 0.5), 0.00018310547, ((1, 8),), jnp.float32),
        "second_qkv": jnp.clip(jnp.exp(math.log(3.175554819101478e-10) - 1.3862944 * jax.random.uniform(key_of[16], (D, 3 * D), jnp.float32) ** block_scale(key_of[16], (D, 3 * D), ((0, 8),), -0.2, 0.2)), 7.938887047753695e-11, 3.175554819101478e-10),
        "second_out": jnp.clip(jnp.exp(math.log(3.175554819101478e-10) - 1.3862944 * jax.random.uniform(key_of[17], (D, D), jnp.float32) ** block_scale(key_of[17], (D, D), ((0, 8),), -0.2, 0.2)), 7.938887047753695e-11, 3.175554819101478e-10),
        "second_up": jnp.clip(jnp.exp(math.log(3.969443523876848e-11) - 1.34707362 * jax.random.uniform(key_of[18], (D, FF), jnp.float32) ** block_scale(key_of[18], (D, FF), ((0, 8),), -0.2, 0.2)), 1.032055343963556e-11, 3.969443523876848e-11),
        "second_down": jnp.clip(jnp.exp(math.log(3.175554819101478e-10) - 1.3862944 * jax.random.uniform(key_of[19], (D, FF), jnp.float32) ** block_scale(key_of[19], (D, FF), ((0, 8),), -0.2, 0.2)), 7.938887047753695e-11, 3.175554819101478e-10),
        "second_vectors": jnp.clip(jnp.exp(math.log(3.175554819101478e-10) - 1.3862944 * jax.random.uniform(key_of[20], (NVEC, D), jnp.float32) ** block_scale(key_of[20], (NVEC, D), ((1, 8),), -0.2, 0.2)), 7.938887047753695e-11, 3.175554819101478e-10),
    }


@jax.custom_vjp
def low(v):
    return lax.optimization_barrier(v.astype(jnp.bfloat16)).astype(jnp.float32)

@jax.custom_vjp
def low_back(v):
    return v

def low_keep(v):
    return (low(v), None)

def low_pass(kept, grad):
    return (grad,)

def back_keep(v):
    return (v, None)

def back_low(kept, grad):
    return (low(grad),)
low.defvjp(low_keep, low_pass)
low_back.defvjp(back_keep, back_low)

def layer_norm(values, gain, shift):
    center = values - lax.optimization_barrier(jnp.mean(values, axis=-1, keepdims=True))
    spread = lax.optimization_barrier(jnp.mean(center * center, axis=-1, keepdims=True))
    return center * lax.rsqrt(spread + 1e-06) * gain + shift

def exact_gelu(values):
    return jax.nn.gelu(values, approximate=False)

def rotary(patch, head_dim):
    pairs = head_dim // 2
    index = jnp.arange(pairs)
    which = index % 3
    rates = jnp.power(10000.0, -(index // 3).astype(jnp.float32) / ((pairs + 2) // 3))
    place = patch.astype(jnp.float32)
    chosen = jnp.where(which[None, :] == 0, place[0][:, None], jnp.where(which[None, :] == 1, place[1][:, None], place[2][:, None]))
    angle = chosen * rates[None, :]
    return (jnp.cos(angle), jnp.sin(angle))

def rotate(values, cosine, sine):
    half = values.shape[-1] // 2
    first = values[..., :half]
    second = values[..., half:]
    cosine = cosine[:, None, :]
    sine = sine[:, None, :]
    return jnp.concatenate([first * cosine - second * sine, first * sine + second * cosine], axis=-1)

def highest(left, right):
    return jnp.dot(left, right, precision=lax.Precision.HIGHEST)

def group_forward(weights, block):
    qkv_w, out_w, up_w, down_w, vec = weights
    xin, segment, keep, patch = block
    count = xin.shape[0]
    width = xin.shape[1]
    head_dim = width // HEADS
    normed1 = low(layer_norm(xin, vec[0], vec[1]))
    projected = low_back(highest(normed1, qkv_w) + vec[2:5].reshape(-1))
    cosine, sine = rotary(patch, head_dim)
    query = low(rotate(projected[:, :width].reshape(count, HEADS, head_dim), cosine, sine))
    keys = low(rotate(projected[:, width:2 * width].reshape(count, HEADS, head_dim), cosine, sine))
    values = low(projected[:, 2 * width:].reshape(count, HEADS, head_dim))
    allowed = (segment[:, None] == segment[None, :]) & (keep[None, :] == 1)

    def one_head(parts):
        query_head, key_head, value_head = parts
        scores = low_back(highest(query_head, key_head.T) * head_dim ** (-0.5))
        masked = jnp.where(allowed, scores, -1e+30)
        peak = lax.optimization_barrier(jnp.max(masked, axis=-1, keepdims=True))
        expo = jnp.exp(masked - peak)
        probs = expo / lax.optimization_barrier(jnp.sum(expo, axis=-1, keepdims=True))
        return highest(low(probs), value_head)
    mixed = lax.map(jax.checkpoint(one_head), (jnp.moveaxis(query, 1, 0), jnp.moveaxis(keys, 1, 0), jnp.moveaxis(values, 1, 0)))
    mixed = low(low_back(jnp.moveaxis(mixed, 0, 1).reshape(count, width)))
    branch = low_back(highest(mixed, out_w) + vec[5])
    resid = xin + branch
    normed2 = low(layer_norm(resid, vec[6], vec[7]))
    up_pre = low_back(highest(normed2, up_w) + vec[9:].reshape(-1))
    act = low(exact_gelu(up_pre))
    down = low_back(lax.dot_general(act, down_w, (((1,), (1,)), ((), ())), precision=lax.Precision.HIGHEST) + vec[8])
    return resid + down

def forward(xin, qkv_w, out_w, up_w, down_w, vec, segment_ids, key_keep, patch_coords):
    weights = (low(qkv_w), low(out_w), low(up_w), low(down_w), low(vec))
    blocks_count = xin.shape[0] // GROUP
    blocks = (xin.reshape(blocks_count, GROUP, xin.shape[1]), segment_ids.reshape(blocks_count, GROUP), key_keep.reshape(blocks_count, GROUP), jnp.moveaxis(patch_coords.reshape(3, blocks_count, GROUP), 1, 0))
    outs = lax.map(jax.checkpoint(partial(group_forward, weights)), blocks)
    return outs.reshape(xin.shape)

def adamw(param, grad, first, second, clip, rate, decay, fix_first, fix_second):
    clipped = grad * clip
    moment = 0.9 * first + 0.1 * clipped
    square = 0.999 * second + 0.001 * clipped * clipped
    direction = moment / fix_first / (jnp.sqrt(square / fix_second) + 1e-08)
    return (param - rate * (direction + decay * param), moment, square)

def reference(tokens, cotangent, segment_ids, key_keep, patch_coords, step_count, weight_qkv, weight_out, weight_up, weight_down, vectors, first_qkv, first_out, first_up, first_down, first_vectors, second_qkv, second_out, second_up, second_down, second_vectors):
    params = (weight_qkv, weight_out, weight_up, weight_down, vectors)
    firsts = (first_qkv, first_out, first_up, first_down, first_vectors)
    seconds = (second_qkv, second_out, second_up, second_down, second_vectors)

    def run(xin, qkv_w, out_w, up_w, down_w, vec):
        return forward(xin, qkv_w, out_w, up_w, down_w, vec, segment_ids, key_keep, patch_coords)
    layer, pullback = jax.vjp(run, tokens.astype(jnp.float32), *params)
    grads = pullback(cotangent.astype(jnp.float32))
    total = jnp.float32(0.0)
    for grad in grads[1:]:
        total = total + jnp.sum(grad * grad)
    grad_norm = jnp.sqrt(total)
    clip = 1.0 / jnp.maximum(grad_norm, 1.0)
    count = step_count[0].astype(jnp.float32)
    rate = 0.4 * count / (count + 4.0)
    decay = 0.04 + 0.018 * count
    fix_first = 1.0 - jnp.power(0.9, count)
    fix_second = 1.0 - jnp.power(0.999, count)
    updated = []
    moments = []
    squares = []
    for index in range(5):
        decay_here = decay if index < 4 else 0.0
        result = adamw(params[index], grads[index + 1], firsts[index], seconds[index], clip, rate, decay_here, fix_first, fix_second)
        updated.append(result[0])
        moments.append(result[1])
        squares.append(result[2])
    return (layer.astype(jnp.bfloat16), grads[0].astype(jnp.bfloat16), updated[0], updated[1], updated[2], updated[3], updated[4], moments[0], moments[1], moments[2], moments[3], moments[4], squares[0], squares[1], squares[2], squares[3], squares[4], grad_norm, grads[5][8])
```

```python
import functools

import jax
import jax.numpy as jnp
from jax import lax
from jax.experimental import pallas as pl
from jax.experimental.pallas import tpu as pltpu
from jax.sharding import PartitionSpec as P

HEADS = 16
BLOCK = 256
BF = jnp.bfloat16
F32 = jnp.float32


def dot(a, b, ca, cb):
    return lax.dot_general(a, b, (((ca,), (cb,)), ((), ())), preferred_element_type=F32)


def swap_halves(x, half):
    lane = lax.broadcasted_iota(jnp.int32, x.shape, 1)
    width = x.shape[1]
    return jnp.where(
        lane % (2 * half) < half, pltpu.roll(x, width - half, 1), pltpu.roll(x, half, 1)
    )


def turn(x, cosine, sine, half, sign):
    parts = []
    for start in range(0, x.shape[1], 128):
        part = x[:, start : start + 128]
        other = swap_halves(part, half) * sine
        parts.append(part * cosine + other if sign > 0 else part * cosine - other)
    return jnp.concatenate(parts, axis=1)


def rotary_table(head_dim):
    half = head_dim // 2
    lane = jnp.arange(128)
    pair = lane % half
    rates = jnp.power(10000.0, -(pair // 3).astype(F32) / ((half + 2) // 3))
    row = jnp.arange(128)
    axis = row // 14
    value = (row % 14).astype(F32)
    live = (axis[:, None] == (pair % 3)[None, :]) & (row[:, None] < 42)
    angle = value[:, None] * rates[None, :]
    signs = jnp.where(lane % head_dim < half, -1.0, 1.0)
    return jnp.concatenate(
        [
            jnp.where(live, jnp.cos(angle), 0.0),
            jnp.where(live, jnp.sin(angle) * signs[None, :], 0.0),
        ],
        axis=1,
    )


def qkv_kernel(half, x_ref, w_ref, bias_ref, onehot_ref, table_ref, q_ref, k_ref, v_ref, turn_ref):
    width = q_ref.shape[1]
    angles = lax.dot_general(
        onehot_ref[...],
        table_ref[...],
        (((1,), (0,)), ((), ())),
        precision=lax.Precision.HIGHEST,
        preferred_element_type=F32,
    )
    turn_ref[...] = angles
    cosine, sine = angles[:, :128], angles[:, 128:]
    proj = dot(x_ref[...], w_ref[...], 1, 0) + bias_ref[...]
    q_ref[...] = turn(proj[:, :width], cosine, sine, half, 1).astype(BF)
    k_ref[...] = turn(proj[:, width : 2 * width], cosine, sine, half, 1).astype(BF)
    v_ref[...] = proj[:, 2 * width :].astype(BF)


def qkv_call(x, w, bias, onehot, table, half):
    rows, depth = x.shape
    width = w.shape[1] // 3
    out = jax.ShapeDtypeStruct((rows, width), BF)
    row_block = lambda cols: pl.BlockSpec((BLOCK, cols), lambda i: (i, 0))
    whole = lambda a: pl.BlockSpec(a.shape, lambda i: (0, 0))
    return pl.pallas_call(
        functools.partial(qkv_kernel, half),
        grid=(rows // BLOCK,),
        in_specs=[row_block(depth), whole(w), whole(bias), row_block(128), whole(table)],
        out_specs=[row_block(width)] * 3 + [row_block(256)],
        out_shape=[out, out, out, jax.ShapeDtypeStruct((rows, 256), F32)],
        cost_estimate=pl.CostEstimate(
            flops=2 * rows * depth * 3 * width, bytes_accessed=rows * depth * 4, transcendentals=0
        ),
        name="qkv",
    )(x, w, bias, onehot, table)


def head_lanes(shape, head, head_dim):
    lane = lax.broadcasted_iota(jnp.int32, shape, 1)
    return lane // head_dim == head


def forward_kernel(
    heads, head_dim, low_ref, high_ref, q_ref, k_ref, v_ref, seg_ref, tag_ref, o_ref, lse_ref, acc, peak, total
):
    step = pl.program_id(0)
    query = q_ref[...] * jnp.asarray(head_dim**-0.5, BF)
    seg = seg_ref[...]
    masked_query = [
        jnp.where(head_lanes(query.shape, h, head_dim), query, jnp.zeros_like(query)) for h in range(heads)
    ]
    acc[...] = jnp.zeros_like(acc)
    peak[...] = jnp.full_like(peak, -1e30)
    total[...] = jnp.zeros_like(total)

    def body(j, carry):
        start = pl.multiple_of(j * BLOCK, BLOCK)
        key = k_ref[pl.ds(start, BLOCK), :]
        value = v_ref[pl.ds(start, BLOCK), :]
        allowed = seg == tag_ref[pl.ds(j, 1), :]
        for h in range(heads):
            scores = jnp.where(allowed, dot(masked_query[h], key, 1, 1), -1e30)
            old = peak[h]
            new = jnp.maximum(old, jnp.max(scores, axis=1, keepdims=True))
            probs = jnp.exp(scores - new[:, :1])
            keep = jnp.exp(old - new)
            peak[h] = new
            total[h] = total[h] * keep + jnp.sum(probs, axis=1, keepdims=True)
            acc[h] = acc[h] * keep[:, :1] + dot(probs.astype(BF), value, 1, 0)
        return carry

    lax.fori_loop(low_ref[step], high_ref[step], body, 0)
    out = jnp.zeros(o_ref.shape, F32)
    stats = jnp.zeros((BLOCK, 128), F32)
    for h in range(heads):
        out = jnp.where(head_lanes(out.shape, h, head_dim), acc[h] / total[h][:, :1], out)
        lane = lax.broadcasted_iota(jnp.int32, stats.shape, 1)
        stats = jnp.where(lane == h, peak[h] + jnp.log(total[h]), stats)
    o_ref[...] = out.astype(BF)
    lse_ref[...] = stats.T[:8, :]


def forward_call(low, high, q, k, v, seg_col, tag_rows, head_dim):
    rows, width = q.shape
    heads = width // head_dim
    whole = lambda a: pl.BlockSpec(a.shape, lambda i, *_: (0, 0))
    grid_spec = pltpu.PrefetchScalarGridSpec(
        num_scalar_prefetch=2,
        grid=(rows // BLOCK,),
        in_specs=[
            pl.BlockSpec((BLOCK, width), lambda i, *_: (i, 0)),
            whole(k),
            whole(v),
            pl.BlockSpec((BLOCK, 1), lambda i, *_: (i, 0)),
            whole(tag_rows),
        ],
        out_specs=[
            pl.BlockSpec((BLOCK, width), lambda i, *_: (i, 0)),
            pl.BlockSpec((8, BLOCK), lambda i, *_: (0, i)),
        ],
        scratch_shapes=[
            pltpu.VMEM((heads, BLOCK, width), F32),
            pltpu.VMEM((heads, BLOCK, 128), F32),
            pltpu.VMEM((heads, BLOCK, 128), F32),
        ],
    )
    return pl.pallas_call(
        functools.partial(forward_kernel, heads, head_dim),
        grid_spec=grid_spec,
        out_shape=[jax.ShapeDtypeStruct((rows, width), BF), jax.ShapeDtypeStruct((8, rows), F32)],
        cost_estimate=pl.CostEstimate(
            flops=heads * rows * rows * width * 3, bytes_accessed=rows * width * 8, transcendentals=heads * rows * rows
        ),
        name="attention_forward",
    )(low, high, q, k, v, seg_col, tag_rows)


def backward_kernel(
    heads, head_dim, low_ref, high_ref, q_ref, k_ref, v_ref, o_ref, g_ref, lse_ref, seg_ref, tag_ref, turn_ref,
    out_ref, q_heads, g_heads, delta, grad_query,
):
    step = pl.program_id(0)
    rows, width = q_ref.shape
    scale = head_dim**-0.5
    half = head_dim // 2

    @pl.when(step == 0)
    def _():
        grad_query[...] = jnp.zeros_like(grad_query)
        row = lax.broadcasted_iota(jnp.int32, (8, width), 0)
        lane = lax.broadcasted_iota(jnp.int32, (8, width), 1)
        pick = jnp.where(lane // head_dim == row, 1.0, 0.0)

        def prepare(i, carry):
            at = pl.ds(pl.multiple_of(i * BLOCK, BLOCK), BLOCK)
            query = q_ref[at, :] * jnp.asarray(scale, BF)
            grad = g_ref[at, :]
            for h in range(heads):
                lanes = head_lanes(query.shape, h, head_dim)
                q_heads[h, at, :] = jnp.where(lanes, query, jnp.zeros_like(query))
                g_heads[h, at, :] = jnp.where(lanes, grad, jnp.zeros_like(grad))
            product = grad.astype(F32) * o_ref[at, :].astype(F32)
            delta[pl.ds(i, 1)] = lax.dot_general(
                pick,
                product,
                (((1,), (1,)), ((), ())),
                precision=lax.Precision.HIGHEST,
                preferred_element_type=F32,
            )[None]
            return carry

        lax.fori_loop(0, rows // BLOCK, prepare, 0)

    key = k_ref[...]
    value = v_ref[...]
    tag = tag_ref[...]
    masked_key = [jnp.where(head_lanes(key.shape, h, head_dim), key, jnp.zeros_like(key)) for h in range(heads)]

    def body(i, carry):
        grad_key, grad_value = carry
        at = pl.ds(pl.multiple_of(i * BLOCK, BLOCK), BLOCK)
        allowed = tag == seg_ref[pl.ds(i, 1), :]
        lse = lse_ref[pl.ds(i, 1)][0]
        dlt = delta[pl.ds(i, 1)][0]
        total = None
        for h in range(heads):
            query = q_heads[h, at, :]
            grad = g_heads[h, at, :]
            scores = dot(key, query, 1, 1)
            probs = jnp.where(allowed, jnp.exp(scores - lse[h : h + 1, :]), 0.0)
            grad_probs = dot(value, grad, 1, 1)
            grad_scores = (probs * (grad_probs - dlt[h : h + 1, :])).astype(BF)
            grad_value = grad_value + dot(probs.astype(BF), grad, 1, 0)
            grad_key = grad_key + dot(grad_scores, query, 1, 0)
            term = dot(grad_scores, masked_key[h], 0, 0)
            total = term if total is None else total + term
        grad_query[at, :] += total
        return grad_key, grad_value

    zero = jnp.zeros((BLOCK, width), F32)
    grad_key, grad_value = lax.fori_loop(low_ref[step], high_ref[step], body, (zero, zero))
    here = pl.ds(pl.multiple_of(step * BLOCK, BLOCK), BLOCK)
    cosine, sine = turn_ref[here, :128], turn_ref[here, 128:]
    out_ref[here, width : 2 * width] = turn(grad_key, cosine, sine, half, -1).astype(BF)
    out_ref[here, 2 * width :] = grad_value.astype(BF)

    @pl.when(step == pl.num_programs(0) - 1)
    def _():
        def finish(i, carry):
            at = pl.ds(pl.multiple_of(i * BLOCK, BLOCK), BLOCK)
            grads = grad_query[at, :] * scale
            out_ref[at, :width] = turn(grads, turn_ref[at, :128], turn_ref[at, 128:], half, -1).astype(BF)
            return carry

        lax.fori_loop(0, rows // BLOCK, finish, 0)


def backward_call(low, high, q, k, v, o, g, lse, seg_rows, tag_col, turns, head_dim):
    rows, width = q.shape
    heads = width // head_dim
    blocks = rows // BLOCK
    lse = jnp.moveaxis(lse.reshape(8, blocks, BLOCK), 1, 0)
    whole = lambda a: pl.BlockSpec(a.shape, lambda i, *_: (0,) * a.ndim)
    block = pl.BlockSpec((BLOCK, width), lambda i, *_: (i, 0))
    grid_spec = pltpu.PrefetchScalarGridSpec(
        num_scalar_prefetch=2,
        grid=(blocks,),
        in_specs=[
            whole(q), block, block, whole(o), whole(g), whole(lse), whole(seg_rows),
            pl.BlockSpec((BLOCK, 1), lambda i, *_: (i, 0)),
            whole(turns),
        ],
        out_specs=pl.BlockSpec((rows, 3 * width), lambda i, *_: (0, 0)),
        scratch_shapes=[
            pltpu.VMEM((heads, rows, width), BF),
            pltpu.VMEM((heads, rows, width), BF),
            pltpu.VMEM((blocks, 8, BLOCK), F32),
            pltpu.VMEM((rows, width), F32),
        ],
    )
    return pl.pallas_call(
        functools.partial(backward_kernel, heads, head_dim),
        grid_spec=grid_spec,
        out_shape=jax.ShapeDtypeStruct((rows, 3 * width), BF),
        cost_estimate=pl.CostEstimate(
            flops=heads * rows * rows * width * 7, bytes_accessed=rows * width * 20, transcendentals=heads * rows * rows
        ),
        name="attention_backward",
    )(low, high, q, k, v, o, g, lse, seg_rows, tag_col, turns)


def norm_parts(values):
    center = values - jnp.mean(values, axis=-1, keepdims=True)
    inverse = lax.rsqrt(jnp.mean(center * center, axis=-1, keepdims=True) + 1e-06)
    return center * inverse, inverse


def norm_back(grads, gain, unit, inverse):
    scaled = grads * gain
    return inverse * (
        scaled - jnp.mean(scaled, axis=-1, keepdims=True) - unit * jnp.mean(scaled * unit, axis=-1, keepdims=True)
    )


def adamw(param, grad, first, second, clip, rate, decay, fix_first, fix_second):
    clipped = grad * clip
    moment = 0.9 * first + 0.1 * clipped
    square = 0.999 * second + 0.001 * clipped * clipped
    direction = moment / fix_first / (jnp.sqrt(square / fix_second) + 1e-08)
    return (param - rate * (direction + decay * param), moment, square)


def on_device(
    tokens, cotangent, segment_ids, key_keep, patch_coords, step_count,
    weight_qkv, weight_out, weight_up, weight_down, vectors,
    first_qkv, first_out, first_up, first_down, first_vectors,
    second_qkv, second_out, second_up, second_down, second_vectors,
):
    rows, width = tokens.shape
    hidden = weight_up.shape[1]
    head_dim = width // HEADS
    narrow = lax.axis_size("narrow")
    wide = lax.axis_size("wide")
    shard_rows = width // wide
    me = lax.axis_index("narrow")
    side = me % 2
    mine = width // narrow
    half_hidden = hidden // 2
    group = rows * narrow

    def mate(value):
        return lax.ppermute(value, "narrow", [(i, i ^ 1) for i in range(narrow)])

    def across(value):
        return lax.ppermute(value, "narrow", [(i, i ^ 2) for i in range(narrow)])

    def take(value, start, size, axis=1):
        return lax.dynamic_slice_in_dim(value, start, size, axis)

    qkv_low = jnp.concatenate([take(weight_qkv, i * width + me * mine, mine) for i in range(3)], axis=1).astype(BF)
    out_low = weight_out.astype(BF)
    up_low = take(weight_up, side * half_hidden, half_hidden).astype(BF)
    down_low = take(weight_down, side * half_hidden, half_hidden).astype(BF)

    vec = lax.all_gather(vectors.astype(BF), "wide", axis=1, tiled=True).astype(F32)
    qkv_w = lax.all_gather(qkv_low, "wide", axis=0, tiled=True)
    out_w = lax.all_gather(out_low, "wide", axis=0, tiled=True)
    up_w = lax.all_gather(up_low, "wide", axis=0, tiled=True)
    down_w = lax.all_gather(down_low, "wide", axis=0, tiled=True)

    xin = tokens.astype(F32)
    unit1, inverse1 = norm_parts(xin)
    normed1 = (unit1 * vec[0] + vec[1]).astype(BF)
    normed1_all = lax.all_gather(normed1, "narrow", axis=0, tiled=True)
    tag = jnp.concatenate([segment_ids[None], key_keep[None], patch_coords], axis=0)
    tag_all = lax.all_gather(tag, "narrow", axis=1, tiled=True)
    cot_pair = jnp.concatenate([cotangent, mate(cotangent)], axis=0)

    seg = tag_all[0]
    seg_float = seg.astype(F32)
    key_tag = jnp.where(tag_all[1] == 1, seg, -1).astype(F32)
    slot = jnp.arange(128)[None, :]
    place = tag_all[2:5]
    onehot = (
        (slot == place[0][:, None]) | (slot == 14 + place[1][:, None]) | (slot == 28 + place[2][:, None])
    ).astype(F32)
    blocks = group // BLOCK
    seg_rows = seg.reshape(blocks, BLOCK)
    low = jnp.sum(seg[None, :] < seg_rows[:, :1], axis=1, dtype=jnp.int32) // BLOCK
    high = (jnp.sum(seg[None, :] <= seg_rows[:, -1:], axis=1, dtype=jnp.int32) + BLOCK - 1) // BLOCK

    bias = jnp.concatenate([take(vec[2 + i : 3 + i], me * mine, mine) for i in range(3)], axis=1)
    query, keys, values, turns = qkv_call(normed1_all, qkv_w, bias, onehot, rotary_table(head_dim), head_dim // 2)
    mixed_mine, lse = forward_call(
        low, high, query, keys, values, seg_float[:, None], key_tag.reshape(blocks, BLOCK), head_dim
    )
    mixed = lax.all_to_all(mixed_mine, "narrow", 0, 1, tiled=True)

    resid = xin + (dot(mixed, out_w, 1, 0) + vec[5])
    unit2, inverse2 = norm_parts(resid)
    normed2 = (unit2 * vec[6] + vec[7]).astype(BF)
    normed2_pair = jnp.concatenate([normed2, mate(normed2)], axis=0)
    up_bias = take(vec[9:].reshape(1, -1), side * half_hidden, half_hidden)
    up_pre = dot(normed2_pair, up_w, 1, 0) + up_bias
    erf_part = 0.5 * (1.0 + lax.erf(up_pre * (0.5**0.5)))
    act = (up_pre * erf_part).astype(BF)
    slope = erf_part + up_pre * (jnp.exp(-0.5 * up_pre * up_pre) * ((2.0 * jnp.pi) ** -0.5))
    down_part = dot(act, down_w, 1, 1)
    down = down_part[:rows] + mate(down_part[rows:])
    layer_out = (resid + (down + vec[8])).astype(BF)

    part_down = dot(cot_pair, act, 0, 0).astype(BF)
    grad_down = lax.psum_scatter(part_down, "wide", scatter_dimension=0, tiled=True)
    grad_up_act = (dot(cot_pair, down_w, 1, 0) * slope).astype(BF)
    part_up = dot(normed2_pair, grad_up_act, 0, 0).astype(BF)
    grad_up = lax.psum_scatter(part_up, "wide", scatter_dimension=0, tiled=True)
    grad_normed2_part = dot(grad_up_act, up_w, 1, 1)
    grad_normed2 = grad_normed2_part[:rows] + mate(grad_normed2_part[rows:])
    cot = cotangent.astype(F32)
    grad_resid = cot + norm_back(grad_normed2, vec[6], unit2, inverse2)
    grad_branch = grad_resid.astype(BF)
    grad_mixed = dot(grad_branch, out_w, 1, 1).astype(BF)
    part_out = dot(mixed, grad_branch, 0, 0)
    own_out = take(part_out, side * (width // 2), width // 2)
    other_out = take(part_out, (1 - side) * (width // 2), width // 2)
    part_out = (own_out + mate(other_out.astype(BF)).astype(F32)).astype(BF)
    grad_out = lax.psum_scatter(part_out, "wide", scatter_dimension=0, tiled=True)

    grad_mixed_mine = lax.all_to_all(grad_mixed, "narrow", 1, 0, tiled=True)
    grad_proj = backward_call(
        low, high, query, keys, values, mixed_mine, grad_mixed_mine, lse, seg_float.reshape(blocks, BLOCK),
        key_tag[:, None], turns, head_dim,
    )
    part_qkv = dot(normed1_all, grad_proj, 0, 0).astype(BF)
    grad_qkv = lax.psum_scatter(part_qkv, "wide", scatter_dimension=0, tiled=True)
    grad_normed1_part = dot(grad_proj, qkv_w, 1, 1)
    grad_normed1 = lax.psum_scatter(grad_normed1_part.astype(BF), "narrow", scatter_dimension=0, tiled=True).astype(F32)
    grad_tokens = (grad_resid + norm_back(grad_normed1, vec[0], unit1, inverse1)).astype(BF)

    proj_sums = jnp.sum(grad_proj.astype(F32), axis=0).reshape(3, mine)
    proj_rows = lax.dynamic_update_slice(jnp.zeros((3, width), F32), proj_sums, (0, me * mine))
    up_sums = jnp.sum(grad_up_act.astype(F32), axis=0)
    up_rows = lax.dynamic_update_slice(jnp.zeros((hidden,), F32), up_sums, (side * half_hidden,))
    vector_part = jnp.concatenate(
        [
            jnp.sum(grad_normed1 * unit1, axis=0)[None],
            jnp.sum(grad_normed1, axis=0)[None],
            proj_rows,
            jnp.sum(grad_branch.astype(F32), axis=0)[None],
            jnp.sum(grad_normed2 * unit2, axis=0)[None],
            jnp.sum(grad_normed2, axis=0)[None],
            jnp.sum(cot, axis=0)[None],
            up_rows.reshape(hidden // width, width),
        ],
        axis=0,
    )

    def join(value):
        value = value.astype(F32)
        value = value + across(value)
        other = mate(value)
        first = jnp.where(side == 0, value, other)
        second = jnp.where(side == 0, other, value)
        return jnp.concatenate([first, second], axis=1)

    total_up = join(grad_up)
    total_down = join(grad_down)
    total_out = join(grad_out)
    quarters = lax.all_gather(grad_qkv, "narrow", axis=0)
    total_qkv = jnp.moveaxis(quarters.reshape(narrow, shard_rows, 3, mine), 0, 2).reshape(shard_rows, 3 * width)
    total_qkv = total_qkv.astype(F32)

    squares = sum(jnp.sum(g * g) for g in (total_qkv, total_out, total_up, total_down))
    vector_total = lax.psum(vector_part, ("wide", "narrow"))
    squares_total = lax.psum(squares, "wide")
    grad_norm = jnp.sqrt(squares_total + jnp.sum(vector_total * vector_total))
    clip = 1.0 / jnp.maximum(grad_norm, 1.0)
    count = step_count[0].astype(F32)
    rate = 0.4 * count / (count + 4.0)
    decay = 0.04 + 0.018 * count
    fix_first = 1.0 - jnp.power(0.9, count)
    fix_second = 1.0 - jnp.power(0.999, count)
    grad_vectors = take(vector_total, lax.axis_index("wide") * shard_rows, shard_rows)

    def update(param, grad, first, second, decay_here):
        return adamw(param, grad, first, second, clip, rate, decay_here, fix_first, fix_second)

    new_qkv = update(weight_qkv, total_qkv, first_qkv, second_qkv, decay)
    new_out = update(weight_out, total_out, first_out, second_out, decay)
    new_up = update(weight_up, total_up, first_up, second_up, decay)
    new_down = update(weight_down, total_down, first_down, second_down, decay)
    new_vectors = update(vectors, grad_vectors, first_vectors, second_vectors, 0.0)
    news = (new_qkv, new_out, new_up, new_down, new_vectors)
    return (layer_out, grad_tokens) + tuple(n[i] for i in range(3) for n in news) + (grad_norm, grad_vectors[8])


def solution(mesh):
    by_token = P(("wide", "narrow"), None)
    ids = P(("wide", "narrow"))
    by_row = P("wide", None)
    by_column = P(None, "wide")
    params = (by_row,) * 4 + (by_column,)
    return jax.shard_map(
        on_device,
        mesh=mesh,
        in_specs=(by_token, by_token, ids, ids, P(None, ("wide", "narrow")), P()) + params * 3,
        out_specs=(by_token, by_token) + params * 3 + (P(), P("wide")),
        check_vma=False,
    )
```

```python
import functools

import jax
import jax.numpy as jnp
from jax import lax
from jax.experimental import pallas as pl
from jax.experimental.pallas import tpu as pltpu
from jax.sharding import PartitionSpec as P

HEADS = 16
BLOCK = 256
BF = jnp.bfloat16
F32 = jnp.float32
MESH = pl.DeviceIdType.MESH


def dot(a, b, ca, cb):
    return lax.dot_general(a, b, (((ca,), (cb,)), ((), ())), preferred_element_type=F32)


def swap_halves(x, half):
    lane = lax.broadcasted_iota(jnp.int32, x.shape, 1)
    width = x.shape[1]
    return jnp.where(
        lane % (2 * half) < half, pltpu.roll(x, width - half, 1), pltpu.roll(x, half, 1)
    )


def turn(x, cosine, sine, half, sign):
    parts = []
    for start in range(0, x.shape[1], 128):
        part = x[:, start : start + 128]
        other = swap_halves(part, half) * sine
        parts.append(part * cosine + other if sign > 0 else part * cosine - other)
    return jnp.concatenate(parts, axis=1)


def rotary_table(head_dim):
    half = head_dim // 2
    lane = jnp.arange(128)
    pair = lane % half
    rates = jnp.power(10000.0, -(pair // 3).astype(F32) / ((half + 2) // 3))
    row = jnp.arange(128)
    axis = row // 14
    value = (row % 14).astype(F32)
    live = (axis[:, None] == (pair % 3)[None, :]) & (row[:, None] < 42)
    angle = value[:, None] * rates[None, :]
    signs = jnp.where(lane % head_dim < half, -1.0, 1.0)
    return jnp.concatenate(
        [
            jnp.where(live, jnp.cos(angle), 0.0),
            jnp.where(live, jnp.sin(angle) * signs[None, :], 0.0),
        ],
        axis=1,
    )


def qkv_kernel(half, x_ref, vec_ref, w_ref, bias_ref, onehot_ref, table_ref, q_ref, k_ref, v_ref, turn_ref, norm_ref):
    width = q_ref.shape[1]
    angles = lax.dot_general(
        onehot_ref[...],
        table_ref[...],
        (((1,), (0,)), ((), ())),
        precision=lax.Precision.HIGHEST,
        preferred_element_type=F32,
    )
    turn_ref[...] = angles
    cosine, sine = angles[:, :128], angles[:, 128:]
    unit, _ = norm_parts(x_ref[...].astype(F32))
    normed = (unit * vec_ref[0:1, :] + vec_ref[1:2, :]).astype(BF)
    norm_ref[...] = normed
    proj = dot(normed, w_ref[...], 1, 0) + bias_ref[...]
    q_ref[...] = turn(proj[:, :width], cosine, sine, half, 1).astype(BF)
    k_ref[...] = turn(proj[:, width : 2 * width], cosine, sine, half, 1).astype(BF)
    v_ref[...] = proj[:, 2 * width :].astype(BF)


def qkv_call(x, vec, w, bias, onehot, table, half):
    rows, depth = x.shape
    width = w.shape[1] // 3
    out = jax.ShapeDtypeStruct((rows, width), BF)
    row_block = lambda cols: pl.BlockSpec((BLOCK, cols), lambda i: (i, 0))
    whole = lambda a: pl.BlockSpec(a.shape, lambda i: (0, 0))
    return pl.pallas_call(
        functools.partial(qkv_kernel, half),
        grid=(rows // BLOCK,),
        in_specs=[row_block(depth), whole(vec), whole(w), whole(bias), row_block(128), whole(table)],
        out_specs=[row_block(width)] * 3 + [row_block(256), row_block(depth)],
        out_shape=[
            out, out, out, jax.ShapeDtypeStruct((rows, 256), F32), jax.ShapeDtypeStruct((rows, depth), BF)
        ],
        cost_estimate=pl.CostEstimate(
            flops=2 * rows * depth * 3 * width, bytes_accessed=rows * depth * 6, transcendentals=0
        ),
        name="qkv",
    )(x, vec, w, bias, onehot, table)


def greet(targets):
    barrier = pltpu.get_barrier_semaphore()
    for target in targets:
        pl.semaphore_signal(barrier, inc=1, device_id=target, device_id_type=MESH)
    pl.semaphore_wait(barrier, len(targets))


def others(name, index, size):
    return [{name: lax.rem(index + d, size)} for d in range(1, size)]


class Copies:
    def __init__(self, send, recv):
        self.send, self.recv, self.all = send, recv, []

    def start(self, src, dst, **target):
        i = len(self.all)
        copy = pltpu.make_async_remote_copy(
            src_ref=src, dst_ref=dst, send_sem=self.send.at[i], recv_sem=self.recv.at[i],
            device_id=target, device_id_type=MESH,
        )
        copy.start()
        self.all.append([copy, False])
        return i

    def arrived(self, i):
        if not self.all[i][1]:
            self.all[i][0].wait_recv()
            self.all[i][1] = True

    def finish(self):
        for i in range(len(self.all)):
            self.arrived(i)
        for copy, _ in self.all:
            copy.wait_send()


def rows_at(index, size):
    return pl.ds(pl.multiple_of(index * size, size), size)


def gather_kernel(
    wide, narrow, tok, qkv, vec, tag, tok_all, qkv_all, vec_all, tag_all, send, recv, local
):
    w, n = lax.axis_index("wide"), lax.axis_index("narrow")
    column = wide // 2
    z, y = w // 2, lax.rem(w, 2)
    near, mate, cross = w + 1 - 2 * y, n + 1 - 2 * lax.rem(n, 2), lax.rem(n + 2, narrow)
    wide_rows, group_rows = qkv.shape[0], tok.shape[0]
    pieces = 4
    piece = group_rows // pieces
    greet(others("wide", w, wide) + others("narrow", n, narrow))
    go = Copies(send, recv)
    for d in range(1, wide):
        go.start(vec, vec_all.at[w], wide=lax.rem(w + d, wide))
    for d in range(1, narrow):
        go.start(tag, tag_all.at[n], narrow=lax.rem(n + d, narrow))
    own_rows = rows_at(w, wide_rows)
    token_rows = lambda i, p: rows_at(i * pieces + p, piece)
    far = [go.start(qkv, qkv_all.at[own_rows], wide=lax.rem(z + d, column) * 2 + y) for d in range(1, column)]
    over = [
        go.start(tok.at[pl.ds(p * piece, piece)], tok_all.at[token_rows(n, p)], narrow=cross) for p in range(pieces)
    ]
    go.start(qkv, qkv_all.at[own_rows], wide=near)
    for p in range(pieces):
        go.start(tok.at[pl.ds(p * piece, piece)], tok_all.at[token_rows(n, p)], narrow=mate)
    own = [
        pltpu.make_async_copy(tok, tok_all.at[rows_at(n, group_rows)], local.at[0]),
        pltpu.make_async_copy(qkv, qkv_all.at[own_rows], local.at[1]),
        pltpu.make_async_copy(vec, vec_all.at[w], local.at[2]),
        pltpu.make_async_copy(tag, tag_all.at[n], local.at[3]),
    ]
    for copy in own:
        copy.start()
    for i in range(max(pieces, column - 1)):
        if i < column - 1:
            go.arrived(far[i])
            block = qkv_all.at[rows_at(lax.rem(z - (i + 1) + column, column) * 2 + y, wide_rows)]
            go.start(block, block, wide=near)
        if i < pieces:
            go.arrived(over[i])
            block = tok_all.at[token_rows(cross, i)]
            go.start(block, block, narrow=mate)
    for copy in own:
        copy.wait()
    go.finish()


def gather_call(tok, qkv, vec, tag, wide, narrow):
    copies = (wide - 1) + (narrow - 1) + 2 * (wide // 2 - 1) + 1 + 12
    vmem = pl.BlockSpec(memory_space=pltpu.VMEM)
    anywhere = pl.BlockSpec(memory_space=pl.ANY)
    return pl.pallas_call(
        functools.partial(gather_kernel, wide, narrow),
        in_specs=[vmem] * 4,
        out_specs=[anywhere] * 4,
        out_shape=[
            jax.ShapeDtypeStruct((narrow * tok.shape[0], tok.shape[1]), BF),
            jax.ShapeDtypeStruct((wide * qkv.shape[0], qkv.shape[1]), BF),
            jax.ShapeDtypeStruct((wide,) + vec.shape, BF),
            jax.ShapeDtypeStruct((narrow,) + tag.shape, jnp.int32),
        ],
        scratch_shapes=[
            pltpu.SemaphoreType.DMA((copies,)),
            pltpu.SemaphoreType.DMA((copies,)),
            pltpu.SemaphoreType.DMA((4,)),
        ],
        compiler_params=pltpu.CompilerParams(collective_id=0, has_side_effects=True),
        name="gather",
    )(tok, qkv, vec, tag)


def tail_kernel(
    wide, narrow, part, grad_proj, weight, tok, vec_in, normed_out, quarters_out, vec_out,
    partial, mate_in, cross_out, cross_in, near_in, far_out, far_in, shards, vec_box, sums, send, recv,
):
    w, n = lax.axis_index("wide"), lax.axis_index("narrow")
    column = wide // 2
    z, y = w // 2, lax.rem(w, 2)
    x, c = n // 2, lax.rem(n, 2)
    near, mate, cross = w + 1 - 2 * y, n + 1 - 2 * c, lax.rem(n + 2, narrow)
    wide_rows, group_rows = part.shape[0] // wide, normed_out.shape[0]
    towards = [lax.rem(z + d, column) for d in range(1, column + 1)]
    greet([{"wide": near}] + [{"wide": to * 2 + y} for to in towards[:-1]] + others("narrow", n, narrow))
    go = Copies(send, recv)
    first = [
        go.start(part.at[rows_at(towards[k] * 2 + 1 - y, wide_rows)], near_in.at[k], wide=near) for k in range(column)
    ]

    sums[...] = jnp.zeros_like(sums)
    owners = [(1 - x) * 2 + 1 - c, x * 2 + 1 - c, (1 - x) * 2 + c, n]
    mates = []
    for slot, owner in enumerate(owners):

        def body(i, carry):
            at = pl.ds(pl.multiple_of(owner * group_rows + i * BLOCK, BLOCK), BLOCK)
            here = pl.ds(pl.multiple_of(i * BLOCK, BLOCK), BLOCK)
            grads = dot(grad_proj[at, :], weight[...], 1, 1)
            unit, _ = norm_parts(tok[at, :].astype(F32))
            sums[0:1, :] += jnp.sum(grads * unit, axis=0, keepdims=True)
            sums[1:2, :] += jnp.sum(grads, axis=0, keepdims=True)
            if slot < 3:
                partial[slot, here, :] = grads.astype(BF)
            else:
                normed_out[here, :] = grads
            return carry

        lax.fori_loop(0, group_rows // BLOCK, body, 0)
        if slot < 2:
            mates.append(go.start(partial.at[slot], mate_in.at[slot], narrow=mate))

    vec_box[pl.ds(n, 1)] = vec_in[...][None]
    vec_box[pl.ds(n, 1), 0:2, :] = sums[0:2, :][None]
    vecs = [go.start(vec_box.at[n], vec_box.at[n], narrow=lax.rem(n + d, narrow)) for d in range(1, narrow)]

    go.arrived(mates[0])
    half = group_rows // 2
    overs = []
    for p in range(2):
        at = pl.ds(p * half, half)
        cross_out[at, :] = (partial[2, at, :].astype(F32) + mate_in[0, at, :].astype(F32)).astype(BF)
        overs.append(go.start(cross_out.at[at], cross_in.at[at], narrow=cross))

    seconds = []
    total = None
    for k in range(column):
        go.arrived(first[k])
        mine = part[rows_at(towards[k] * 2 + y, wide_rows), :].astype(F32) + near_in[k].astype(F32)
        if k < column - 1:
            far_out[k] = mine.astype(BF)
            seconds.append(go.start(far_out.at[k], far_in.at[k], wide=towards[k] * 2 + y))
        else:
            total = mine
    for k in range(column - 1):
        go.arrived(seconds[k])
        total = total + far_in[k].astype(F32)
    shards[pl.ds(n, 1)] = total.astype(BF)[None]
    over = go.start(shards.at[n], shards.at[n], narrow=cross)
    go.start(shards.at[n], shards.at[n], narrow=mate)

    go.arrived(mates[1])
    for p in range(2):
        go.arrived(overs[p])
        at = pl.ds(p * half, half)
        normed_out[at, :] += mate_in[1, at, :].astype(F32) + cross_in[at, :].astype(F32)
    for i in vecs:
        go.arrived(i)
    group = vec_box[0]
    for i in range(1, narrow):
        group = group + vec_box[i]
    vec_out[...] = group

    go.arrived(over)
    go.start(shards.at[cross], shards.at[cross], narrow=mate)
    go.finish()
    quarters_out[...] = shards[...]


def tail_call(part, grad_proj, weight, tok, vec_in, wide, narrow):
    depth, cols = part.shape
    rows = tok.shape[0] // narrow
    wide_rows = depth // wide
    column = wide // 2
    copies = 2 * column - 1 + 2 + (narrow - 1) + 2 + 3
    vmem = pl.BlockSpec(memory_space=pltpu.VMEM)
    return pl.pallas_call(
        functools.partial(tail_kernel, wide, narrow),
        in_specs=[vmem] * 5,
        out_specs=[vmem] * 3,
        out_shape=[
            jax.ShapeDtypeStruct((rows, depth), F32),
            jax.ShapeDtypeStruct((narrow, wide_rows, cols), BF),
            jax.ShapeDtypeStruct(vec_in.shape, F32),
        ],
        scratch_shapes=[
            pltpu.VMEM((3, rows, depth), BF),
            pltpu.VMEM((2, rows, depth), BF),
            pltpu.VMEM((rows, depth), BF),
            pltpu.VMEM((rows, depth), BF),
            pltpu.VMEM((column, wide_rows, cols), BF),
            pltpu.VMEM((column - 1, wide_rows, cols), BF),
            pltpu.VMEM((column - 1, wide_rows, cols), BF),
            pltpu.VMEM((narrow, wide_rows, cols), BF),
            pltpu.VMEM((narrow,) + vec_in.shape, F32),
            pltpu.VMEM((8, depth), F32),
            pltpu.SemaphoreType.DMA((copies,)),
            pltpu.SemaphoreType.DMA((copies,)),
        ],
        compiler_params=pltpu.CompilerParams(
            collective_id=1, has_side_effects=True, vmem_limit_bytes=56 * 1024 * 1024
        ),
        name="tail",
    )(part, grad_proj, weight, tok, vec_in)


def norm_kernel(wide, slices, total_out, square_out, box, squares, send, recv):
    w = lax.axis_index("wide")
    greet(others("wide", w, wide))
    go = Copies(send, recv)
    peers = [lax.rem(w + d, wide) for d in range(1, wide)]
    for peer in peers:
        go.start(slices.at[peer], box.at[w], wide=peer)
    box[pl.ds(w, 1)] = slices[pl.ds(w, 1)]
    for i in range(wide - 1):
        go.arrived(i)
    total = box[0]
    for i in range(1, wide):
        total = total + box[i]
    total_out[...] = total
    row = lax.broadcasted_iota(jnp.int32, total.shape, 0)
    entries = jnp.where(row == 15, 0.0, total)
    entries = entries * entries
    squares[pl.ds(w, 1)] = (entries[:8] + entries[8:])[None]
    for peer in peers:
        go.start(squares.at[w], squares.at[w], wide=peer)
    go.finish()
    all_squares = squares[0]
    for i in range(1, wide):
        all_squares = all_squares + squares[i]
    square_out[...] = all_squares


def norm_call(slices, wide):
    vmem = pl.BlockSpec(memory_space=pltpu.VMEM)
    copies = 2 * (wide - 1)
    return pl.pallas_call(
        functools.partial(norm_kernel, wide),
        in_specs=[vmem],
        out_specs=[vmem] * 2,
        out_shape=[jax.ShapeDtypeStruct((16, 128), F32), jax.ShapeDtypeStruct((8, 128), F32)],
        scratch_shapes=[
            pltpu.VMEM((wide, 16, 128), F32),
            pltpu.VMEM((wide, 8, 128), F32),
            pltpu.SemaphoreType.DMA((copies,)),
            pltpu.SemaphoreType.DMA((copies,)),
        ],
        compiler_params=pltpu.CompilerParams(collective_id=2, has_side_effects=True),
        name="norm",
    )(slices)


def head_lanes(shape, head, head_dim):
    lane = lax.broadcasted_iota(jnp.int32, shape, 1)
    return lane // head_dim == head


def forward_kernel(
    heads, head_dim, low_ref, high_ref, q_ref, k_ref, v_ref, seg_ref, tag_ref, o_ref, lse_ref,
    values_turned, acc, peak, total,
):
    step = pl.program_id(0)
    width = q_ref.shape[1]

    @pl.when(step == 0)
    def _():
        values_turned[...] = v_ref[...].T

    query = q_ref[...] * jnp.asarray(head_dim**-0.5, BF)
    seg = seg_ref[0]
    masked_query = [
        jnp.where(head_lanes(query.shape, h, head_dim), query, jnp.zeros_like(query)) for h in range(heads)
    ]
    acc[...] = jnp.zeros_like(acc)
    peak[...] = jnp.full_like(peak, -1e30)
    total[...] = jnp.zeros_like(total)

    def body(j, carry):
        start = pl.multiple_of(j * BLOCK, BLOCK)
        key = k_ref[pl.ds(start, BLOCK), :]
        allowed = tag_ref[pl.ds(start, BLOCK), :] == seg
        scores = [jnp.where(allowed, dot(key, masked_query[h], 1, 1), -1e30) for h in range(heads)]
        for h in range(heads):
            rows = slice(h * head_dim, (h + 1) * head_dim)
            old = peak[h : h + 1, :]
            new = jnp.maximum(old, jnp.max(scores[h], axis=0, keepdims=True))
            probs = jnp.exp(scores[h] - new)
            keep = jnp.exp(old - new)
            peak[h : h + 1, :] = new
            total[h : h + 1, :] = total[h : h + 1, :] * keep + jnp.sum(probs, axis=0, keepdims=True)
            value = values_turned[rows, pl.ds(start, BLOCK)]
            acc[rows, :] = acc[rows, :] * keep + dot(value, probs.astype(BF), 1, 0)
        return carry

    lax.fori_loop(low_ref[step], high_ref[step], body, 0)
    parts = [acc[h * head_dim : (h + 1) * head_dim, :] / total[h : h + 1, :] for h in range(heads)]
    o_ref[...] = jnp.concatenate(parts, axis=0).T.astype(BF)
    lse_ref[0] = peak[...] + jnp.log(jnp.maximum(total[...], 1e-30))


def forward_call(low, high, q, k, v, seg_rows, tag_col, head_dim):
    rows, width = q.shape
    heads = width // head_dim
    blocks = rows // BLOCK
    whole = lambda a: pl.BlockSpec(a.shape, lambda i, *_: (0,) * a.ndim)
    grid_spec = pltpu.PrefetchScalarGridSpec(
        num_scalar_prefetch=2,
        grid=(blocks,),
        in_specs=[
            pl.BlockSpec((BLOCK, width), lambda i, *_: (i, 0)),
            whole(k),
            whole(v),
            pl.BlockSpec((1, 1, BLOCK), lambda i, *_: (i, 0, 0)),
            whole(tag_col),
        ],
        out_specs=[
            pl.BlockSpec((BLOCK, width), lambda i, *_: (i, 0)),
            pl.BlockSpec((1, 8, BLOCK), lambda i, *_: (i, 0, 0)),
        ],
        scratch_shapes=[
            pltpu.VMEM((width, rows), BF),
            pltpu.VMEM((width, BLOCK), F32),
            pltpu.VMEM((8, BLOCK), F32),
            pltpu.VMEM((8, BLOCK), F32),
        ],
    )
    return pl.pallas_call(
        functools.partial(forward_kernel, heads, head_dim),
        grid_spec=grid_spec,
        out_shape=[jax.ShapeDtypeStruct((rows, width), BF), jax.ShapeDtypeStruct((blocks, 8, BLOCK), F32)],
        cost_estimate=pl.CostEstimate(
            flops=heads * rows * rows * width * 3, bytes_accessed=rows * width * 8, transcendentals=heads * rows * rows
        ),
        name="attention_forward",
    )(low, high, q, k, v, seg_rows[:, None, :], tag_col)


def backward_kernel(
    heads, head_dim, low_ref, high_ref, q_ref, k_ref, v_ref, o_ref, g_ref, lse_ref, seg_ref, tag_ref, turn_ref,
    out_ref, q_heads, g_heads, delta, grad_query,
):
    step = pl.program_id(0)
    rows, width = q_ref.shape
    scale = head_dim**-0.5
    half = head_dim // 2

    @pl.when(step == 0)
    def _():
        grad_query[...] = jnp.zeros_like(grad_query)
        row = lax.broadcasted_iota(jnp.int32, (8, width), 0)
        lane = lax.broadcasted_iota(jnp.int32, (8, width), 1)
        pick = jnp.where(lane // head_dim == row, 1.0, 0.0)

        def prepare(i, carry):
            at = pl.ds(pl.multiple_of(i * BLOCK, BLOCK), BLOCK)
            query = q_ref[at, :] * jnp.asarray(scale, BF)
            grad = g_ref[at, :]
            for h in range(heads):
                lanes = head_lanes(query.shape, h, head_dim)
                q_heads[h, at, :] = jnp.where(lanes, query, jnp.zeros_like(query))
                g_heads[h, at, :] = jnp.where(lanes, grad, jnp.zeros_like(grad))
            product = grad.astype(F32) * o_ref[at, :].astype(F32)
            delta[pl.ds(i, 1)] = lax.dot_general(
                pick,
                product,
                (((1,), (1,)), ((), ())),
                precision=lax.Precision.HIGHEST,
                preferred_element_type=F32,
            )[None]
            return carry

        lax.fori_loop(0, rows // BLOCK, prepare, 0)

    key = k_ref[...]
    value = v_ref[...]
    tag = tag_ref[...]
    masked_key = [jnp.where(head_lanes(key.shape, h, head_dim), key, jnp.zeros_like(key)) for h in range(heads)]

    def body(i, carry):
        grad_key, grad_value = carry
        at = pl.ds(pl.multiple_of(i * BLOCK, BLOCK), BLOCK)
        allowed = tag == seg_ref[pl.ds(i, 1), :]
        lse = lse_ref[pl.ds(i, 1)][0]
        dlt = delta[pl.ds(i, 1)][0]
        total = None
        for h in range(heads):
            query = q_heads[h, at, :]
            grad = g_heads[h, at, :]
            scores = dot(key, query, 1, 1)
            probs = jnp.where(allowed, jnp.exp(scores - lse[h : h + 1, :]), 0.0)
            grad_probs = dot(value, grad, 1, 1)
            grad_scores = (probs * (grad_probs - dlt[h : h + 1, :])).astype(BF)
            grad_value = grad_value + dot(probs.astype(BF), grad, 1, 0)
            grad_key = grad_key + dot(grad_scores, query, 1, 0)
            term = dot(grad_scores, masked_key[h], 0, 0)
            total = term if total is None else total + term
        grad_query[at, :] += total
        return grad_key, grad_value

    zero = jnp.zeros((BLOCK, width), F32)
    grad_key, grad_value = lax.fori_loop(low_ref[step], high_ref[step], body, (zero, zero))
    here = pl.ds(pl.multiple_of(step * BLOCK, BLOCK), BLOCK)
    cosine, sine = turn_ref[here, :128], turn_ref[here, 128:]
    out_ref[here, width : 2 * width] = turn(grad_key, cosine, sine, half, -1).astype(BF)
    out_ref[here, 2 * width :] = grad_value.astype(BF)

    @pl.when(step == pl.num_programs(0) - 1)
    def _():
        def finish(i, carry):
            at = pl.ds(pl.multiple_of(i * BLOCK, BLOCK), BLOCK)
            grads = grad_query[at, :] * scale
            out_ref[at, :width] = turn(grads, turn_ref[at, :128], turn_ref[at, 128:], half, -1).astype(BF)
            return carry

        lax.fori_loop(0, rows // BLOCK, finish, 0)


def backward_call(low, high, q, k, v, o, g, lse, seg_rows, tag_col, turns, head_dim):
    rows, width = q.shape
    heads = width // head_dim
    blocks = rows // BLOCK
    whole = lambda a: pl.BlockSpec(a.shape, lambda i, *_: (0,) * a.ndim)
    block = pl.BlockSpec((BLOCK, width), lambda i, *_: (i, 0))
    grid_spec = pltpu.PrefetchScalarGridSpec(
        num_scalar_prefetch=2,
        grid=(blocks,),
        in_specs=[
            whole(q), block, block, whole(o), whole(g), whole(lse), whole(seg_rows),
            pl.BlockSpec((BLOCK, 1), lambda i, *_: (i, 0)),
            whole(turns),
        ],
        out_specs=pl.BlockSpec((rows, 3 * width), lambda i, *_: (0, 0)),
        scratch_shapes=[
            pltpu.VMEM((heads, rows, width), BF),
            pltpu.VMEM((heads, rows, width), BF),
            pltpu.VMEM((blocks, 8, BLOCK), F32),
            pltpu.VMEM((rows, width), F32),
        ],
    )
    return pl.pallas_call(
        functools.partial(backward_kernel, heads, head_dim),
        grid_spec=grid_spec,
        out_shape=jax.ShapeDtypeStruct((rows, 3 * width), BF),
        cost_estimate=pl.CostEstimate(
            flops=heads * rows * rows * width * 7, bytes_accessed=rows * width * 20, transcendentals=heads * rows * rows
        ),
        name="attention_backward",
    )(low, high, q, k, v, o, g, lse, seg_rows, tag_col, turns)


def norm_parts(values):
    center = values - jnp.mean(values, axis=-1, keepdims=True)
    inverse = lax.rsqrt(jnp.mean(center * center, axis=-1, keepdims=True) + 1e-06)
    return center * inverse, inverse


def norm_back(grads, gain, unit, inverse):
    scaled = grads * gain
    return inverse * (
        scaled - jnp.mean(scaled, axis=-1, keepdims=True) - unit * jnp.mean(scaled * unit, axis=-1, keepdims=True)
    )


def adamw(param, grad, first, second, clip, rate, decay, fix_first, fix_second):
    clipped = grad * clip
    moment = 0.9 * first + 0.1 * clipped
    square = 0.999 * second + 0.001 * clipped * clipped
    direction = moment / fix_first / (jnp.sqrt(square / fix_second) + 1e-08)
    return (param - rate * (direction + decay * param), moment, square)


def on_device(
    tokens, cotangent, segment_ids, key_keep, patch_coords, step_count,
    weight_qkv, weight_out, weight_up, weight_down, vectors,
    first_qkv, first_out, first_up, first_down, first_vectors,
    second_qkv, second_out, second_up, second_down, second_vectors,
):
    rows, width = tokens.shape
    hidden = weight_up.shape[1]
    head_dim = width // HEADS
    narrow = lax.axis_size("narrow")
    wide = lax.axis_size("wide")
    shard_rows = width // wide
    me = lax.axis_index("narrow")
    side = me % 2
    mine = width // narrow
    half_hidden = hidden // 2
    group = rows * narrow

    def mate(value):
        return lax.ppermute(value, "narrow", [(i, i ^ 1) for i in range(narrow)])

    def across(value):
        return lax.ppermute(value, "narrow", [(i, i ^ 2) for i in range(narrow)])

    def scatter(part):
        w = lax.axis_index("wide")
        z, y = w // 2, w % 2
        column = wide // 2
        blocks = part.reshape(column, 2, shard_rows, part.shape[1])
        pick = lambda value, at, axis: lax.dynamic_index_in_dim(value, at, axis, keepdims=False)
        came = lax.ppermute(pick(blocks, 1 - y, 1), "wide", [(i, i ^ 1) for i in range(wide)])
        both = (pick(blocks, y, 1).astype(F32) + came.astype(F32)).astype(BF)
        total = pick(both, z, 0).astype(F32)
        for d in range(1, column):
            pairs = [(i, (i // 2 + d) % column * 2 + i % 2) for i in range(wide)]
            total = total + lax.ppermute(pick(both, (z + d) % column, 0), "wide", pairs).astype(F32)
        return total.astype(BF)

    def take(value, start, size, axis=1):
        return lax.dynamic_slice_in_dim(value, start, size, axis)

    qkv_low = jnp.concatenate([take(weight_qkv, i * width + me * mine, mine) for i in range(3)], axis=1).astype(BF)
    out_low = weight_out.astype(BF)
    up_low = take(weight_up, side * half_hidden, half_hidden).astype(BF)
    down_low = take(weight_down, side * half_hidden, half_hidden).astype(BF)

    shard_cols = vectors.shape[1]
    vec_shard = jnp.pad(vectors.astype(BF), ((0, 16 - vectors.shape[0]), (0, -shard_cols % 128)))
    tag = jnp.concatenate([segment_ids[None], key_keep[None], patch_coords, patch_coords], axis=0)
    tokens_all, qkv_w, vec_all, tag_all = gather_call(tokens, qkv_low, vec_shard, tag, wide, narrow)
    vec_all = vec_all[:, :, :shard_cols]
    vec = jnp.moveaxis(vec_all, 0, 1).reshape(16, width).astype(F32)[: vectors.shape[0]]
    tag_all = jnp.moveaxis(tag_all, 0, 1).reshape(8, group)
    out_w = lax.all_gather(out_low, "wide", axis=0, tiled=True)
    up_w = lax.all_gather(up_low, "wide", axis=0, tiled=True)
    down_w = lax.all_gather(down_low, "wide", axis=0, tiled=True)

    xin = tokens.astype(F32)
    unit1, inverse1 = norm_parts(xin)
    cot_pair = jnp.concatenate([cotangent, mate(cotangent)], axis=0)

    seg = tag_all[0]
    seg_float = seg.astype(F32)
    key_tag = jnp.where(tag_all[1] == 1, seg, -1).astype(F32)
    slot = jnp.arange(128)[None, :]
    place = tag_all[2:5]
    onehot = (
        (slot == place[0][:, None]) | (slot == 14 + place[1][:, None]) | (slot == 28 + place[2][:, None])
    ).astype(F32)
    blocks = group // BLOCK
    seg_rows = seg.reshape(blocks, BLOCK)
    low = jnp.sum(seg[None, :] < seg_rows[:, :1], axis=1, dtype=jnp.int32) // BLOCK
    high = (jnp.sum(seg[None, :] <= seg_rows[:, -1:], axis=1, dtype=jnp.int32) + BLOCK - 1) // BLOCK

    bias = jnp.concatenate([take(vec[2 + i : 3 + i], me * mine, mine) for i in range(3)], axis=1)
    query, keys, values, turns, normed1_all = qkv_call(tokens_all, vec[:2], qkv_w, bias, onehot, rotary_table(head_dim), head_dim // 2)
    mixed_mine, lse = forward_call(
        low, high, query, keys, values, seg_float.reshape(blocks, BLOCK), key_tag[:, None], head_dim
    )
    mixed = lax.all_to_all(mixed_mine, "narrow", 0, 1, tiled=True)

    resid = xin + (dot(mixed, out_w, 1, 0) + vec[5])
    unit2, inverse2 = norm_parts(resid)
    normed2 = (unit2 * vec[6] + vec[7]).astype(BF)
    normed2_pair = jnp.concatenate([normed2, mate(normed2)], axis=0)
    up_bias = take(vec[9:].reshape(1, -1), side * half_hidden, half_hidden)
    up_pre = dot(normed2_pair, up_w, 1, 0) + up_bias
    erf_part = 0.5 * (1.0 + lax.erf(up_pre * (0.5**0.5)))
    act = (up_pre * erf_part).astype(BF)
    slope = erf_part + up_pre * (jnp.exp(-0.5 * up_pre * up_pre) * ((2.0 * jnp.pi) ** -0.5))
    down_part = dot(act, down_w, 1, 1)
    down = down_part[:rows] + mate(down_part[rows:])
    layer_out = (resid + (down + vec[8])).astype(BF)

    part_down = dot(cot_pair, act, 0, 0).astype(BF)
    grad_down = lax.psum_scatter(part_down, "wide", scatter_dimension=0, tiled=True)
    grad_up_act = (dot(cot_pair, down_w, 1, 0) * slope).astype(BF)
    part_up = dot(normed2_pair, grad_up_act, 0, 0).astype(BF)
    grad_up = lax.psum_scatter(part_up, "wide", scatter_dimension=0, tiled=True)
    grad_normed2_part = dot(grad_up_act, up_w, 1, 1)
    grad_normed2 = grad_normed2_part[:rows] + mate(grad_normed2_part[rows:])
    cot = cotangent.astype(F32)
    grad_resid = cot + norm_back(grad_normed2, vec[6], unit2, inverse2)
    grad_branch = grad_resid.astype(BF)
    grad_mixed = dot(grad_branch, out_w, 1, 1).astype(BF)
    part_out = dot(mixed, grad_branch, 0, 0)
    own_out = take(part_out, side * (width // 2), width // 2)
    other_out = take(part_out, (1 - side) * (width // 2), width // 2)
    part_out = (own_out + mate(other_out.astype(BF)).astype(F32)).astype(BF)
    grad_out = scatter(part_out)

    grad_mixed_mine = lax.all_to_all(grad_mixed, "narrow", 1, 0, tiled=True)
    grad_proj = backward_call(
        low, high, query, keys, values, mixed_mine, grad_mixed_mine, lse, seg_float.reshape(blocks, BLOCK),
        key_tag[:, None], turns, head_dim,
    )
    part_qkv = dot(normed1_all, grad_proj, 0, 0).astype(BF)

    proj_sums = jnp.sum(grad_proj.astype(F32), axis=0).reshape(3, mine)
    proj_rows = lax.dynamic_update_slice(jnp.zeros((3, width), F32), proj_sums, (0, me * mine))
    up_sums = jnp.sum(grad_up_act.astype(F32), axis=0)
    up_rows = lax.dynamic_update_slice(jnp.zeros((hidden,), F32), up_sums, (side * half_hidden,))
    vector_part = jnp.concatenate(
        [
            jnp.zeros((2, width), F32),
            proj_rows,
            jnp.sum(grad_branch.astype(F32), axis=0)[None],
            jnp.sum(grad_normed2 * unit2, axis=0)[None],
            jnp.sum(grad_normed2, axis=0)[None],
            jnp.sum(cot, axis=0)[None],
            up_rows.reshape(hidden // width, width),
            jnp.zeros((16 - vectors.shape[0], width), F32),
        ],
        axis=0,
    )
    grad_normed1, quarters, vector_group = tail_call(
        part_qkv, grad_proj, qkv_w, tokens_all, vector_part, wide, narrow
    )
    grad_tokens = (grad_resid + norm_back(grad_normed1, vec[0], unit1, inverse1)).astype(BF)

    def join(value):
        other = across(value)
        mine = value.astype(F32) + other.astype(F32)
        theirs = mate(value).astype(F32) + mate(other).astype(F32)
        first = jnp.where(side == 0, mine, theirs)
        second = jnp.where(side == 0, theirs, mine)
        return jnp.concatenate([first, second], axis=1)

    total_up = join(grad_up)
    total_down = join(grad_down)
    total_out = join(grad_out)
    total_qkv = jnp.concatenate(
        [quarters[i, :, j * mine : (j + 1) * mine] for j in range(3) for i in range(narrow)], axis=1
    ).astype(F32)

    squares = sum(jnp.sum(g * g) for g in (total_qkv, total_out, total_up, total_down))
    slices = jnp.moveaxis(vector_group.reshape(16, wide, shard_rows), 1, 0)
    slices = jnp.pad(slices, ((0, 0), (0, 0), (0, -shard_rows % 128)))
    place = (jnp.arange(16)[:, None] == 15) & (jnp.arange(slices.shape[2])[None, :] == 0)
    slices = jnp.where(place[None], squares, slices)
    vector_total, vector_squares = norm_call(slices, wide)
    grad_norm = jnp.sqrt(vector_total[15, 0] + jnp.sum(vector_squares))
    clip = 1.0 / jnp.maximum(grad_norm, 1.0)
    count = step_count[0].astype(F32)
    rate = 0.4 * count / (count + 4.0)
    decay = 0.04 + 0.018 * count
    fix_first = 1.0 - jnp.power(0.9, count)
    fix_second = 1.0 - jnp.power(0.999, count)
    grad_vectors = vector_total[: vectors.shape[0], :shard_rows]

    def update(param, grad, first, second, decay_here):
        return adamw(param, grad, first, second, clip, rate, decay_here, fix_first, fix_second)

    new_qkv = update(weight_qkv, total_qkv, first_qkv, second_qkv, decay)
    new_out = update(weight_out, total_out, first_out, second_out, decay)
    new_up = update(weight_up, total_up, first_up, second_up, decay)
    new_down = update(weight_down, total_down, first_down, second_down, decay)
    new_vectors = update(vectors, grad_vectors, first_vectors, second_vectors, 0.0)
    news = (new_qkv, new_out, new_up, new_down, new_vectors)
    return (layer_out, grad_tokens) + tuple(n[i] for i in range(3) for n in news) + (grad_norm, grad_vectors[8])


def solution(mesh):
    by_token = P(("wide", "narrow"), None)
    ids = P(("wide", "narrow"))
    by_row = P("wide", None)
    by_column = P(None, "wide")
    params = (by_row,) * 4 + (by_column,)
    return jax.shard_map(
        on_device,
        mesh=mesh,
        in_specs=(by_token, by_token, ids, ids, P(None, ("wide", "narrow")), P()) + params * 3,
        out_specs=(by_token, by_token) + params * 3 + (P(), P("wide")),
        check_vma=False,
    )
```

```python
import functools

import jax
import jax.numpy as jnp
from jax import lax
from jax.experimental import pallas as pl
from jax.experimental.pallas import tpu as pltpu
from jax.sharding import PartitionSpec as P

HEADS = 16
BLOCK = 256
BF = jnp.bfloat16
F32 = jnp.float32
MESH = pl.DeviceIdType.MESH


def dot(a, b, ca, cb):
    return lax.dot_general(a, b, (((ca,), (cb,)), ((), ())), preferred_element_type=F32)


def swap_halves(x, half):
    lane = lax.broadcasted_iota(jnp.int32, x.shape, 1)
    width = x.shape[1]
    return jnp.where(
        lane % (2 * half) < half, pltpu.roll(x, width - half, 1), pltpu.roll(x, half, 1)
    )


def turn(x, cosine, sine, half, sign):
    parts = []
    for start in range(0, x.shape[1], 128):
        part = x[:, start : start + 128]
        other = swap_halves(part, half) * sine
        parts.append(part * cosine + other if sign > 0 else part * cosine - other)
    return jnp.concatenate(parts, axis=1)


def rotary_table(head_dim):
    half = head_dim // 2
    lane = jnp.arange(128)
    pair = lane % half
    rates = jnp.power(10000.0, -(pair // 3).astype(F32) / ((half + 2) // 3))
    row = jnp.arange(128)
    axis = row // 14
    value = (row % 14).astype(F32)
    live = (axis[:, None] == (pair % 3)[None, :]) & (row[:, None] < 42)
    angle = value[:, None] * rates[None, :]
    signs = jnp.where(lane % head_dim < half, -1.0, 1.0)
    return jnp.concatenate(
        [
            jnp.where(live, jnp.cos(angle), 0.0),
            jnp.where(live, jnp.sin(angle) * signs[None, :], 0.0),
        ],
        axis=1,
    )


def qkv_kernel(half, x_ref, vec_ref, w_ref, bias_ref, onehot_ref, table_ref, q_ref, k_ref, v_ref, turn_ref, norm_ref):
    width = q_ref.shape[1]
    angles = lax.dot_general(
        onehot_ref[...],
        table_ref[...],
        (((1,), (0,)), ((), ())),
        precision=lax.Precision.HIGHEST,
        preferred_element_type=F32,
    )
    turn_ref[...] = angles
    cosine, sine = angles[:, :128], angles[:, 128:]
    unit, _ = norm_parts(x_ref[...].astype(F32))
    normed = (unit * vec_ref[0:1, :] + vec_ref[1:2, :]).astype(BF)
    norm_ref[...] = normed
    proj = dot(normed, w_ref[...], 1, 0) + bias_ref[...]
    q_ref[...] = turn(proj[:, :width], cosine, sine, half, 1).astype(BF)
    k_ref[...] = turn(proj[:, width : 2 * width], cosine, sine, half, 1).astype(BF)
    v_ref[...] = proj[:, 2 * width :].astype(BF)


def qkv_call(x, vec, w, bias, onehot, table, half):
    rows, depth = x.shape
    width = w.shape[1] // 3
    out = jax.ShapeDtypeStruct((rows, width), BF)
    row_block = lambda cols: pl.BlockSpec((BLOCK, cols), lambda i: (i, 0))
    whole = lambda a: pl.BlockSpec(a.shape, lambda i: (0, 0))
    return pl.pallas_call(
        functools.partial(qkv_kernel, half),
        grid=(rows // BLOCK,),
        in_specs=[row_block(depth), whole(vec), whole(w), whole(bias), row_block(128), whole(table)],
        out_specs=[row_block(width)] * 3 + [row_block(256), row_block(depth)],
        out_shape=[
            out, out, out, jax.ShapeDtypeStruct((rows, 256), F32), jax.ShapeDtypeStruct((rows, depth), BF)
        ],
        cost_estimate=pl.CostEstimate(
            flops=2 * rows * depth * 3 * width, bytes_accessed=rows * depth * 6, transcendentals=0
        ),
        name="qkv",
    )(x, vec, w, bias, onehot, table)


def greet(targets):
    barrier = pltpu.get_barrier_semaphore()
    for target in targets:
        pl.semaphore_signal(barrier, inc=1, device_id=target, device_id_type=MESH)
    pl.semaphore_wait(barrier, len(targets))


def others(name, index, size):
    return [{name: lax.rem(index + d, size)} for d in range(1, size)]


class Copies:
    def __init__(self, send, recv):
        self.send, self.recv, self.all = send, recv, []

    def make(self, src, dst, **target):
        i = len(self.all)
        copy = pltpu.make_async_remote_copy(
            src_ref=src, dst_ref=dst, send_sem=self.send.at[i], recv_sem=self.recv.at[i],
            device_id=target, device_id_type=MESH,
        )
        self.all.append([copy, False])
        return i

    def launch(self, *indices):
        for i in indices:
            self.all[i][0].start()

    def start(self, src, dst, **target):
        i = self.make(src, dst, **target)
        self.launch(i)
        return i

    def arrived(self, i):
        if not self.all[i][1]:
            self.all[i][0].wait_recv()
            self.all[i][1] = True

    def finish(self):
        for i in range(len(self.all)):
            self.arrived(i)
        for copy, _ in self.all:
            copy.wait_send()


def rows_at(index, size):
    return pl.ds(pl.multiple_of(index * size, size), size)


def gather_kernel(
    wide, narrow, tok, qkv, vec, tag, tok_all, qkv_all, vec_all, tag_all, send, recv, local
):
    w, n = lax.axis_index("wide"), lax.axis_index("narrow")
    column = wide // 2
    z, y = w // 2, lax.rem(w, 2)
    near, mate, cross = w + 1 - 2 * y, n + 1 - 2 * lax.rem(n, 2), lax.rem(n + 2, narrow)
    wide_rows, group_rows = qkv.shape[0], tok.shape[0]
    pieces = 4
    piece = group_rows // pieces
    greet(others("wide", w, wide) + others("narrow", n, narrow))
    go = Copies(send, recv)
    for d in range(1, wide):
        go.start(vec, vec_all.at[w], wide=lax.rem(w + d, wide))
    for d in range(1, narrow):
        go.start(tag, tag_all.at[n], narrow=lax.rem(n + d, narrow))
    own_rows = rows_at(w, wide_rows)
    token_rows = lambda i, p: rows_at(i * pieces + p, piece)
    far = [go.start(qkv, qkv_all.at[own_rows], wide=lax.rem(z + d, column) * 2 + y) for d in range(1, column)]
    over = [
        go.start(tok.at[pl.ds(p * piece, piece)], tok_all.at[token_rows(n, p)], narrow=cross) for p in range(pieces)
    ]
    go.start(qkv, qkv_all.at[own_rows], wide=near)
    for p in range(pieces):
        go.start(tok.at[pl.ds(p * piece, piece)], tok_all.at[token_rows(n, p)], narrow=mate)
    own = [
        pltpu.make_async_copy(tok, tok_all.at[rows_at(n, group_rows)], local.at[0]),
        pltpu.make_async_copy(qkv, qkv_all.at[own_rows], local.at[1]),
        pltpu.make_async_copy(vec, vec_all.at[w], local.at[2]),
        pltpu.make_async_copy(tag, tag_all.at[n], local.at[3]),
    ]
    for copy in own:
        copy.start()
    for i in range(max(pieces, column - 1)):
        if i < column - 1:
            go.arrived(far[i])
            block = qkv_all.at[rows_at(lax.rem(z - (i + 1) + column, column) * 2 + y, wide_rows)]
            go.start(block, block, wide=near)
        if i < pieces:
            go.arrived(over[i])
            block = tok_all.at[token_rows(cross, i)]
            go.start(block, block, narrow=mate)
    for copy in own:
        copy.wait()
    go.finish()


def gather_call(tok, qkv, vec, tag, wide, narrow):
    copies = (wide - 1) + (narrow - 1) + 2 * (wide // 2 - 1) + 1 + 12
    vmem = pl.BlockSpec(memory_space=pltpu.VMEM)
    anywhere = pl.BlockSpec(memory_space=pl.ANY)
    return pl.pallas_call(
        functools.partial(gather_kernel, wide, narrow),
        in_specs=[vmem] * 4,
        out_specs=[anywhere] * 4,
        out_shape=[
            jax.ShapeDtypeStruct((narrow * tok.shape[0], tok.shape[1]), BF),
            jax.ShapeDtypeStruct((wide * qkv.shape[0], qkv.shape[1]), BF),
            jax.ShapeDtypeStruct((wide,) + vec.shape, BF),
            jax.ShapeDtypeStruct((narrow,) + tag.shape, jnp.int32),
        ],
        scratch_shapes=[
            pltpu.SemaphoreType.DMA((copies,)),
            pltpu.SemaphoreType.DMA((copies,)),
            pltpu.SemaphoreType.DMA((4,)),
        ],
        compiler_params=pltpu.CompilerParams(collective_id=0, has_side_effects=True),
        name="gather",
    )(tok, qkv, vec, tag)


def tail_kernel(
    wide, narrow, part, grad_proj, weight, tok, vec_in, normed_out, quarters_out, vec_out,
    partial, mate_in, cross_out, cross_in, near_in, far_out, far_in, shards, vec_box, sums, send, recv,
):
    w, n = lax.axis_index("wide"), lax.axis_index("narrow")
    column = wide // 2
    z, y = w // 2, lax.rem(w, 2)
    x, c = n // 2, lax.rem(n, 2)
    near, mate, cross = w + 1 - 2 * y, n + 1 - 2 * c, lax.rem(n + 2, narrow)
    wide_rows, group_rows = part.shape[0] // wide, normed_out.shape[0]
    towards = [lax.rem(z + d, column) for d in range(1, column + 1)]
    greet([{"wide": near}] + [{"wide": to * 2 + y} for to in towards[:-1]] + others("narrow", n, narrow))
    go = Copies(send, recv)
    first = [
        go.start(part.at[rows_at(towards[k] * 2 + 1 - y, wide_rows)], near_in.at[k], wide=near) for k in range(column)
    ]

    sums[...] = jnp.zeros_like(sums)
    owners = [(1 - x) * 2 + 1 - c, x * 2 + 1 - c, (1 - x) * 2 + c, n]
    mates = []
    for slot, owner in enumerate(owners):

        def body(i, carry):
            at = pl.ds(pl.multiple_of(owner * group_rows + i * BLOCK, BLOCK), BLOCK)
            here = pl.ds(pl.multiple_of(i * BLOCK, BLOCK), BLOCK)
            grads = dot(grad_proj[at, :], weight[...], 1, 1)
            unit, _ = norm_parts(tok[at, :].astype(F32))
            sums[0:1, :] += jnp.sum(grads * unit, axis=0, keepdims=True)
            sums[1:2, :] += jnp.sum(grads, axis=0, keepdims=True)
            if slot < 3:
                partial[slot, here, :] = grads.astype(BF)
            else:
                normed_out[here, :] = grads
            return carry

        lax.fori_loop(0, group_rows // BLOCK, body, 0)
        if slot < 2:
            mates.append(go.start(partial.at[slot], mate_in.at[slot], narrow=mate))

    vec_box[pl.ds(n, 1)] = vec_in[...][None]
    vec_box[pl.ds(n, 1), 0:2, :] = sums[0:2, :][None]
    vecs = [go.start(vec_box.at[n], vec_box.at[n], narrow=lax.rem(n + d, narrow)) for d in range(1, narrow)]

    go.arrived(mates[0])
    half = group_rows // 2
    overs = []
    for p in range(2):
        at = pl.ds(p * half, half)
        cross_out[at, :] = (partial[2, at, :].astype(F32) + mate_in[0, at, :].astype(F32)).astype(BF)
        overs.append(go.start(cross_out.at[at], cross_in.at[at], narrow=cross))

    seconds = []
    total = None
    for k in range(column):
        go.arrived(first[k])
        mine = part[rows_at(towards[k] * 2 + y, wide_rows), :].astype(F32) + near_in[k].astype(F32)
        if k < column - 1:
            far_out[k] = mine.astype(BF)
            seconds.append(go.start(far_out.at[k], far_in.at[k], wide=towards[k] * 2 + y))
        else:
            total = mine
    for k in range(column - 1):
        go.arrived(seconds[k])
        total = total + far_in[k].astype(F32)
    shards[pl.ds(n, 1)] = total.astype(BF)[None]
    over = go.start(shards.at[n], shards.at[n], narrow=cross)
    go.start(shards.at[n], shards.at[n], narrow=mate)

    go.arrived(mates[1])
    for p in range(2):
        go.arrived(overs[p])
        at = pl.ds(p * half, half)
        normed_out[at, :] += mate_in[1, at, :].astype(F32) + cross_in[at, :].astype(F32)
    for i in vecs:
        go.arrived(i)
    group = vec_box[0]
    for i in range(1, narrow):
        group = group + vec_box[i]
    vec_out[...] = group

    go.arrived(over)
    go.start(shards.at[cross], shards.at[cross], narrow=mate)
    go.finish()
    quarters_out[...] = shards[...]


def tail_call(part, grad_proj, weight, tok, vec_in, wide, narrow):
    depth, cols = part.shape
    rows = tok.shape[0] // narrow
    wide_rows = depth // wide
    column = wide // 2
    copies = 2 * column - 1 + 2 + (narrow - 1) + 2 + 3
    vmem = pl.BlockSpec(memory_space=pltpu.VMEM)
    return pl.pallas_call(
        functools.partial(tail_kernel, wide, narrow),
        in_specs=[vmem] * 5,
        out_specs=[vmem] * 3,
        out_shape=[
            jax.ShapeDtypeStruct((rows, depth), F32),
            jax.ShapeDtypeStruct((narrow, wide_rows, cols), BF),
            jax.ShapeDtypeStruct(vec_in.shape, F32),
        ],
        scratch_shapes=[
            pltpu.VMEM((3, rows, depth), BF),
            pltpu.VMEM((2, rows, depth), BF),
            pltpu.VMEM((rows, depth), BF),
            pltpu.VMEM((rows, depth), BF),
            pltpu.VMEM((column, wide_rows, cols), BF),
            pltpu.VMEM((column - 1, wide_rows, cols), BF),
            pltpu.VMEM((column - 1, wide_rows, cols), BF),
            pltpu.VMEM((narrow, wide_rows, cols), BF),
            pltpu.VMEM((narrow,) + vec_in.shape, F32),
            pltpu.VMEM((8, depth), F32),
            pltpu.SemaphoreType.DMA((copies,)),
            pltpu.SemaphoreType.DMA((copies,)),
        ],
        compiler_params=pltpu.CompilerParams(
            collective_id=1, has_side_effects=True, vmem_limit_bytes=56 * 1024 * 1024
        ),
        name="tail",
    )(part, grad_proj, weight, tok, vec_in)


def norm_kernel(wide, slices, total_out, square_out, box, squares, send, recv):
    w = lax.axis_index("wide")
    greet(others("wide", w, wide))
    go = Copies(send, recv)
    peers = [lax.rem(w + d, wide) for d in range(1, wide)]
    for peer in peers:
        go.start(slices.at[peer], box.at[w], wide=peer)
    box[pl.ds(w, 1)] = slices[pl.ds(w, 1)]
    for i in range(wide - 1):
        go.arrived(i)
    total = box[0]
    for i in range(1, wide):
        total = total + box[i]
    total_out[...] = total
    row = lax.broadcasted_iota(jnp.int32, total.shape, 0)
    entries = jnp.where(row == 15, 0.0, total)
    entries = entries * entries
    squares[pl.ds(w, 1)] = (entries[:8] + entries[8:])[None]
    for peer in peers:
        go.start(squares.at[w], squares.at[w], wide=peer)
    go.finish()
    all_squares = squares[0]
    for i in range(1, wide):
        all_squares = all_squares + squares[i]
    square_out[...] = all_squares


def norm_call(slices, wide):
    vmem = pl.BlockSpec(memory_space=pltpu.VMEM)
    copies = 2 * (wide - 1)
    return pl.pallas_call(
        functools.partial(norm_kernel, wide),
        in_specs=[vmem],
        out_specs=[vmem] * 2,
        out_shape=[jax.ShapeDtypeStruct((16, 128), F32), jax.ShapeDtypeStruct((8, 128), F32)],
        scratch_shapes=[
            pltpu.VMEM((wide, 16, 128), F32),
            pltpu.VMEM((wide, 8, 128), F32),
            pltpu.SemaphoreType.DMA((copies,)),
            pltpu.SemaphoreType.DMA((copies,)),
        ],
        compiler_params=pltpu.CompilerParams(collective_id=2, has_side_effects=True),
        name="norm",
    )(slices)


CLIP = 784


def head_lanes(shape, head, head_dim):
    lane = lax.broadcasted_iota(jnp.int32, shape, 1)
    return lane // head_dim == head


def meeting(block, blocks):
    before, after = CLIP // BLOCK, -(-2 * CLIP // BLOCK)
    low = before * (block // after)
    high = blocks - (blocks - after) * (1 - jnp.minimum(block // before, 1))
    return low, high


def forward_kernel(
    heads, head_dim, wide, narrow,
    q_ref, k_ref, v_ref, seg_ref, tag_ref, up_ref, out_ref,
    o_ref, lse_ref, mixed_ref, up_all, out_all,
    values_turned, acc, peak, total, o_box, send, recv, mix_send, mix_recv, local,
):
    step = pl.program_id(0)
    rows, width = q_ref.shape
    blocks = rows // BLOCK
    per = blocks // narrow
    last = blocks - 1
    w, n = lax.axis_index("wide"), lax.axis_index("narrow")
    column = wide // 2
    z, y, side = w // 2, lax.rem(w, 2), lax.rem(n, 2)
    near, mate = w + 1 - 2 * y, n + 1 - 2 * side
    block = lax.rem((n + 1) * per + step, blocks)

    go = Copies(send, recv)
    wide_rows, half = out_ref.shape
    out_cols = pl.ds(pl.multiple_of(side * half, half), half)
    pieces = 2
    piece = up_ref.shape[1] // pieces
    up_at = lambda i, p: up_all.at[rows_at(i, wide_rows), pl.ds(p * piece, piece)]
    out_at = lambda i: out_all.at[rows_at(i, wide_rows), out_cols]
    source = lambda d: lax.rem(z - d + column, column) * 2 + y
    target = lambda d: lax.rem(z + d, column) * 2 + y
    starts, early, late = [], [], []
    out_near = [go.make(out_ref, out_at(w), wide=near)]
    out_mate = [go.make(out_ref, out_at(w), narrow=mate)]
    starts += out_near + out_mate
    for d in range(1, column):
        far = go.make(out_ref, out_at(w), wide=target(d))
        block_ref = out_at(source(d))
        out_near.append(go.make(block_ref, block_ref, wide=near))
        starts.append(far)
        early.append((far, [out_near[-1], go.make(block_ref, block_ref, narrow=mate)]))
    for d in range(column):
        block_ref = out_at(lax.rem(z - d + column, column) * 2 + 1 - y)
        late.append((out_near[d], [go.make(block_ref, block_ref, narrow=mate)]))
    for p in range(pieces):
        cols = pl.ds(p * piece, piece)
        starts.append(go.make(up_ref.at[:, cols], up_at(w, p), wide=near))
        for d in range(1, column):
            far = go.make(up_ref.at[:, cols], up_at(w, p), wide=target(d))
            block_ref = up_at(source(d), p)
            starts.append(far)
            early.append((far, [go.make(block_ref, block_ref, wide=near)]))
    actions = early + late
    own = [
        pltpu.make_async_copy(up_ref, up_all.at[rows_at(w, wide_rows)], local.at[0]),
        pltpu.make_async_copy(out_ref, out_at(w), local.at[1]),
    ]

    mine = pl.ds(pl.multiple_of(n * width, width), width)

    def result(s):
        at = lax.rem((n + 1) * per + s, blocks)
        return pltpu.make_async_remote_copy(
            src_ref=o_box.at[rows_at(at, BLOCK)],
            dst_ref=mixed_ref.at[rows_at(lax.rem(s, per), BLOCK), mine],
            send_sem=mix_send.at[s],
            recv_sem=mix_recv.at[s],
            device_id={"narrow": lax.rem(n + 1 + s // per, narrow)},
            device_id_type=MESH,
        )

    def result_here(s):
        return pltpu.make_async_copy(
            o_box.at[rows_at(n * per + s, BLOCK)], mixed_ref.at[rows_at(s, BLOCK), mine], local.at[2 + s]
        )

    @pl.when(step == 0)
    def _():
        greet(
            [{"wide": near}] + [{"wide": target(d)} for d in range(1, column)] + others("narrow", n, narrow)
        )
        go.launch(*starts)
        for copy in own:
            copy.start()
        values_turned[...] = v_ref[...].T

    share = -(-len(actions) // last)
    for i in range(last):
        some = actions[i * share : (i + 1) * share]

        @pl.when(step == i + 1)
        def _():
            for arrival, follow in some:
                go.arrived(arrival)
                go.launch(*follow)

    at = rows_at(block, BLOCK)
    query = q_ref[at, :] * jnp.asarray(head_dim**-0.5, BF)
    seg = seg_ref[pl.ds(block, 1)][0]
    masked_query = [
        jnp.where(head_lanes(query.shape, h, head_dim), query, jnp.zeros_like(query)) for h in range(heads)
    ]
    acc[...] = jnp.zeros_like(acc)
    peak[...] = jnp.full_like(peak, -1e30)
    total[...] = jnp.zeros_like(total)

    def body(j, carry):
        start = pl.multiple_of(j * BLOCK, BLOCK)
        key = k_ref[pl.ds(start, BLOCK), :]
        allowed = tag_ref[pl.ds(start, BLOCK), :] == seg
        scores = [jnp.where(allowed, dot(key, masked_query[h], 1, 1), -1e30) for h in range(heads)]
        for h in range(heads):
            lines = slice(h * head_dim, (h + 1) * head_dim)
            old = peak[h : h + 1, :]
            new = jnp.maximum(old, jnp.max(scores[h], axis=0, keepdims=True))
            probs = jnp.exp(scores[h] - new)
            keep = jnp.exp(old - new)
            peak[h : h + 1, :] = new
            total[h : h + 1, :] = total[h : h + 1, :] * keep + jnp.sum(probs, axis=0, keepdims=True)
            value = values_turned[lines, pl.ds(start, BLOCK)]
            acc[lines, :] = acc[lines, :] * keep + dot(value, probs.astype(BF), 1, 0)
        return carry

    low, high = meeting(block, blocks)
    lax.fori_loop(low, high, body, 0)
    parts = [acc[h * head_dim : (h + 1) * head_dim, :] / total[h : h + 1, :] for h in range(heads)]
    out = jnp.concatenate(parts, axis=0).T.astype(BF)
    o_ref[at, :] = out
    o_box[at, :] = out
    lse_ref[pl.ds(block, 1)] = (peak[...] + jnp.log(jnp.maximum(total[...], 1e-30)))[None]

    @pl.when(step < blocks - per)
    def _():
        result(step).start()

    @pl.when(step == last)
    def _():
        for s in range(per):
            result_here(s).start()
        for copy in own:
            copy.wait()
        for s in range(blocks - per):
            result(s).wait()
        for s in range(per):
            result_here(s).wait()
        go.finish()


def forward_call(q, k, v, seg_rows, tag_col, up_low, out_half, head_dim, wide, narrow):
    rows, width = q.shape
    heads = width // head_dim
    blocks = rows // BLOCK
    column = wide // 2
    copies = 2 + 3 * (column - 1) + column + 2 * (2 * column - 1)
    whole = lambda a: pl.BlockSpec(a.shape, lambda i: (0,) * a.ndim)
    anywhere = pl.BlockSpec(memory_space=pl.ANY)
    lse = jax.ShapeDtypeStruct((blocks, 8, BLOCK), F32)
    seg_rows = seg_rows[:, None, :]
    return pl.pallas_call(
        functools.partial(forward_kernel, heads, head_dim, wide, narrow),
        grid=(blocks,),
        in_specs=[whole(a) for a in (q, k, v, seg_rows, tag_col, up_low, out_half)],
        out_specs=[whole(q), whole(lse), anywhere, anywhere, anywhere],
        out_shape=[
            jax.ShapeDtypeStruct((rows, width), BF),
            lse,
            jax.ShapeDtypeStruct((rows // narrow, width * narrow), BF),
            jax.ShapeDtypeStruct((up_low.shape[0] * wide, up_low.shape[1]), BF),
            jax.ShapeDtypeStruct((out_half.shape[0] * wide, 2 * out_half.shape[1]), BF),
        ],
        scratch_shapes=[
            pltpu.VMEM((width, rows), BF),
            pltpu.VMEM((width, BLOCK), F32),
            pltpu.VMEM((8, BLOCK), F32),
            pltpu.VMEM((8, BLOCK), F32),
            pltpu.VMEM((rows, width), BF),
            pltpu.SemaphoreType.DMA((copies,)),
            pltpu.SemaphoreType.DMA((copies,)),
            pltpu.SemaphoreType.DMA((blocks,)),
            pltpu.SemaphoreType.DMA((blocks,)),
            pltpu.SemaphoreType.DMA((2 + blocks // narrow,)),
        ],
        compiler_params=pltpu.CompilerParams(collective_id=3, has_side_effects=True),
        cost_estimate=pl.CostEstimate(
            flops=heads * rows * rows * width * 4, bytes_accessed=rows * width * 8, transcendentals=heads * rows * rows
        ),
        name="attention_forward",
    )(q, k, v, seg_rows, tag_col, up_low, out_half)


def backward_kernel(
    heads, head_dim, low_ref, high_ref, q_ref, k_ref, v_ref, o_ref, g_ref, lse_ref, seg_ref, tag_ref, turn_ref,
    out_ref, q_heads, g_heads, delta, grad_query,
):
    step = pl.program_id(0)
    rows, width = q_ref.shape
    scale = head_dim**-0.5
    half = head_dim // 2

    @pl.when(step == 0)
    def _():
        grad_query[...] = jnp.zeros_like(grad_query)
        row = lax.broadcasted_iota(jnp.int32, (8, width), 0)
        lane = lax.broadcasted_iota(jnp.int32, (8, width), 1)
        pick = jnp.where(lane // head_dim == row, 1.0, 0.0)

        def prepare(i, carry):
            at = pl.ds(pl.multiple_of(i * BLOCK, BLOCK), BLOCK)
            query = q_ref[at, :] * jnp.asarray(scale, BF)
            grad = g_ref[at, :]
            for h in range(heads):
                lanes = head_lanes(query.shape, h, head_dim)
                q_heads[h, at, :] = jnp.where(lanes, query, jnp.zeros_like(query))
                g_heads[h, at, :] = jnp.where(lanes, grad, jnp.zeros_like(grad))
            product = grad.astype(F32) * o_ref[at, :].astype(F32)
            delta[pl.ds(i, 1)] = lax.dot_general(
                pick,
                product,
                (((1,), (1,)), ((), ())),
                precision=lax.Precision.HIGHEST,
                preferred_element_type=F32,
            )[None]
            return carry

        lax.fori_loop(0, rows // BLOCK, prepare, 0)

    key = k_ref[...]
    value = v_ref[...]
    tag = tag_ref[...]
    masked_key = [jnp.where(head_lanes(key.shape, h, head_dim), key, jnp.zeros_like(key)) for h in range(heads)]

    def body(i, carry):
        grad_key, grad_value = carry
        at = pl.ds(pl.multiple_of(i * BLOCK, BLOCK), BLOCK)
        allowed = tag == seg_ref[pl.ds(i, 1), :]
        lse = lse_ref[pl.ds(i, 1)][0]
        dlt = delta[pl.ds(i, 1)][0]
        total = None
        for h in range(heads):
            query = q_heads[h, at, :]
            grad = g_heads[h, at, :]
            scores = dot(key, query, 1, 1)
            probs = jnp.where(allowed, jnp.exp(scores - lse[h : h + 1, :]), 0.0)
            grad_probs = dot(value, grad, 1, 1)
            grad_scores = (probs * (grad_probs - dlt[h : h + 1, :])).astype(BF)
            grad_value = grad_value + dot(probs.astype(BF), grad, 1, 0)
            grad_key = grad_key + dot(grad_scores, query, 1, 0)
            term = dot(grad_scores, masked_key[h], 0, 0)
            total = term if total is None else total + term
        grad_query[at, :] += total
        return grad_key, grad_value

    zero = jnp.zeros((BLOCK, width), F32)
    grad_key, grad_value = lax.fori_loop(low_ref[step], high_ref[step], body, (zero, zero))
    here = pl.ds(pl.multiple_of(step * BLOCK, BLOCK), BLOCK)
    cosine, sine = turn_ref[here, :128], turn_ref[here, 128:]
    out_ref[here, width : 2 * width] = turn(grad_key, cosine, sine, half, -1).astype(BF)
    out_ref[here, 2 * width :] = grad_value.astype(BF)

    @pl.when(step == pl.num_programs(0) - 1)
    def _():
        def finish(i, carry):
            at = pl.ds(pl.multiple_of(i * BLOCK, BLOCK), BLOCK)
            grads = grad_query[at, :] * scale
            out_ref[at, :width] = turn(grads, turn_ref[at, :128], turn_ref[at, 128:], half, -1).astype(BF)
            return carry

        lax.fori_loop(0, rows // BLOCK, finish, 0)


def backward_call(low, high, q, k, v, o, g, lse, seg_rows, tag_col, turns, head_dim):
    rows, width = q.shape
    heads = width // head_dim
    blocks = rows // BLOCK
    whole = lambda a: pl.BlockSpec(a.shape, lambda i, *_: (0,) * a.ndim)
    block = pl.BlockSpec((BLOCK, width), lambda i, *_: (i, 0))
    grid_spec = pltpu.PrefetchScalarGridSpec(
        num_scalar_prefetch=2,
        grid=(blocks,),
        in_specs=[
            whole(q), block, block, whole(o), whole(g), whole(lse), whole(seg_rows),
            pl.BlockSpec((BLOCK, 1), lambda i, *_: (i, 0)),
            whole(turns),
        ],
        out_specs=pl.BlockSpec((rows, 3 * width), lambda i, *_: (0, 0)),
        scratch_shapes=[
            pltpu.VMEM((heads, rows, width), BF),
            pltpu.VMEM((heads, rows, width), BF),
            pltpu.VMEM((blocks, 8, BLOCK), F32),
            pltpu.VMEM((rows, width), F32),
        ],
    )
    return pl.pallas_call(
        functools.partial(backward_kernel, heads, head_dim),
        grid_spec=grid_spec,
        out_shape=jax.ShapeDtypeStruct((rows, 3 * width), BF),
        cost_estimate=pl.CostEstimate(
            flops=heads * rows * rows * width * 7, bytes_accessed=rows * width * 20, transcendentals=heads * rows * rows
        ),
        name="attention_backward",
    )(low, high, q, k, v, o, g, lse, seg_rows, tag_col, turns)


def norm_parts(values):
    center = values - jnp.mean(values, axis=-1, keepdims=True)
    inverse = lax.rsqrt(jnp.mean(center * center, axis=-1, keepdims=True) + 1e-06)
    return center * inverse, inverse


def norm_back(grads, gain, unit, inverse):
    scaled = grads * gain
    return inverse * (
        scaled - jnp.mean(scaled, axis=-1, keepdims=True) - unit * jnp.mean(scaled * unit, axis=-1, keepdims=True)
    )


def adamw(param, grad, first, second, clip, rate, decay, fix_first, fix_second):
    clipped = grad * clip
    moment = 0.9 * first + 0.1 * clipped
    square = 0.999 * second + 0.001 * clipped * clipped
    direction = moment / fix_first / (jnp.sqrt(square / fix_second) + 1e-08)
    return (param - rate * (direction + decay * param), moment, square)


def on_device(
    tokens, cotangent, segment_ids, key_keep, patch_coords, step_count,
    weight_qkv, weight_out, weight_up, weight_down, vectors,
    first_qkv, first_out, first_up, first_down, first_vectors,
    second_qkv, second_out, second_up, second_down, second_vectors,
):
    rows, width = tokens.shape
    hidden = weight_up.shape[1]
    head_dim = width // HEADS
    narrow = lax.axis_size("narrow")
    wide = lax.axis_size("wide")
    shard_rows = width // wide
    me = lax.axis_index("narrow")
    side = me % 2
    mine = width // narrow
    half_hidden = hidden // 2
    group = rows * narrow

    def mate(value):
        return lax.ppermute(value, "narrow", [(i, i ^ 1) for i in range(narrow)])

    def across(value):
        return lax.ppermute(value, "narrow", [(i, i ^ 2) for i in range(narrow)])

    def scatter(part):
        w = lax.axis_index("wide")
        z, y = w // 2, w % 2
        column = wide // 2
        blocks = part.reshape(column, 2, shard_rows, part.shape[1])
        pick = lambda value, at, axis: lax.dynamic_index_in_dim(value, at, axis, keepdims=False)
        came = lax.ppermute(pick(blocks, 1 - y, 1), "wide", [(i, i ^ 1) for i in range(wide)])
        both = (pick(blocks, y, 1).astype(F32) + came.astype(F32)).astype(BF)
        total = pick(both, z, 0).astype(F32)
        for d in range(1, column):
            pairs = [(i, (i // 2 + d) % column * 2 + i % 2) for i in range(wide)]
            total = total + lax.ppermute(pick(both, (z + d) % column, 0), "wide", pairs).astype(F32)
        return total.astype(BF)

    def take(value, start, size, axis=1):
        return lax.dynamic_slice_in_dim(value, start, size, axis)

    qkv_low = jnp.concatenate([take(weight_qkv, i * width + me * mine, mine) for i in range(3)], axis=1).astype(BF)
    out_low = take(weight_out, side * (width // 2), width // 2).astype(BF)
    up_low = take(weight_up, side * half_hidden, half_hidden).astype(BF)
    down_low = take(weight_down, side * half_hidden, half_hidden).astype(BF)

    shard_cols = vectors.shape[1]
    vec_shard = jnp.pad(vectors.astype(BF), ((0, 16 - vectors.shape[0]), (0, -shard_cols % 128)))
    tag = jnp.concatenate([segment_ids[None], key_keep[None], patch_coords, patch_coords], axis=0)
    tokens_all, qkv_w, vec_all, tag_all = gather_call(tokens, qkv_low, vec_shard, tag, wide, narrow)
    vec_all = vec_all[:, :, :shard_cols]
    vec = jnp.moveaxis(vec_all, 0, 1).reshape(16, width).astype(F32)[: vectors.shape[0]]
    tag_all = jnp.moveaxis(tag_all, 0, 1).reshape(8, group)
    down_w = lax.all_gather(down_low, "wide", axis=0, tiled=True)

    xin = tokens.astype(F32)
    unit1, inverse1 = norm_parts(xin)
    cot_pair = jnp.concatenate([cotangent, mate(cotangent)], axis=0)

    seg = tag_all[0]
    seg_float = seg.astype(F32)
    key_tag = jnp.where(tag_all[1] == 1, seg, -1).astype(F32)
    slot = jnp.arange(128)[None, :]
    place = tag_all[2:5]
    onehot = (
        (slot == place[0][:, None]) | (slot == 14 + place[1][:, None]) | (slot == 28 + place[2][:, None])
    ).astype(F32)
    blocks = group // BLOCK
    seg_rows = seg.reshape(blocks, BLOCK)
    low = jnp.sum(seg[None, :] < seg_rows[:, :1], axis=1, dtype=jnp.int32) // BLOCK
    high = (jnp.sum(seg[None, :] <= seg_rows[:, -1:], axis=1, dtype=jnp.int32) + BLOCK - 1) // BLOCK

    bias = jnp.concatenate([take(vec[2 + i : 3 + i], me * mine, mine) for i in range(3)], axis=1)
    query, keys, values, turns, normed1_all = qkv_call(tokens_all, vec[:2], qkv_w, bias, onehot, rotary_table(head_dim), head_dim // 2)
    mixed_mine, lse, mixed, up_w, out_w = forward_call(
        query, keys, values, seg_float.reshape(blocks, BLOCK), key_tag[:, None], up_low, out_low, head_dim, wide, narrow
    )

    resid = xin + (dot(mixed, out_w, 1, 0) + vec[5])
    unit2, inverse2 = norm_parts(resid)
    normed2 = (unit2 * vec[6] + vec[7]).astype(BF)
    normed2_pair = jnp.concatenate([normed2, mate(normed2)], axis=0)
    up_bias = take(vec[9:].reshape(1, -1), side * half_hidden, half_hidden)
    up_pre = dot(normed2_pair, up_w, 1, 0) + up_bias
    erf_part = 0.5 * (1.0 + lax.erf(up_pre * (0.5**0.5)))
    act = (up_pre * erf_part).astype(BF)
    slope = erf_part + up_pre * (jnp.exp(-0.5 * up_pre * up_pre) * ((2.0 * jnp.pi) ** -0.5))
    down_part = dot(act, down_w, 1, 1)
    down = down_part[:rows] + mate(down_part[rows:])
    layer_out = (resid + (down + vec[8])).astype(BF)

    part_down = dot(cot_pair, act, 0, 0).astype(BF)
    grad_down = lax.psum_scatter(part_down, "wide", scatter_dimension=0, tiled=True)
    grad_up_act = (dot(cot_pair, down_w, 1, 0) * slope).astype(BF)
    part_up = dot(normed2_pair, grad_up_act, 0, 0).astype(BF)
    grad_up = lax.psum_scatter(part_up, "wide", scatter_dimension=0, tiled=True)
    grad_normed2_part = dot(grad_up_act, up_w, 1, 1)
    grad_normed2 = grad_normed2_part[:rows] + mate(grad_normed2_part[rows:])
    cot = cotangent.astype(F32)
    grad_resid = cot + norm_back(grad_normed2, vec[6], unit2, inverse2)
    grad_branch = grad_resid.astype(BF)
    grad_mixed = dot(grad_branch, out_w, 1, 1).astype(BF)
    part_out = dot(mixed, grad_branch, 0, 0)
    own_out = take(part_out, side * (width // 2), width // 2)
    other_out = take(part_out, (1 - side) * (width // 2), width // 2)
    part_out = (own_out + mate(other_out.astype(BF)).astype(F32)).astype(BF)
    grad_out = scatter(part_out)

    grad_mixed_mine = lax.all_to_all(grad_mixed, "narrow", 1, 0, tiled=True)
    grad_proj = backward_call(
        low, high, query, keys, values, mixed_mine, grad_mixed_mine, lse, seg_float.reshape(blocks, BLOCK),
        key_tag[:, None], turns, head_dim,
    )
    part_qkv = dot(normed1_all, grad_proj, 0, 0).astype(BF)

    proj_sums = jnp.sum(grad_proj.astype(F32), axis=0).reshape(3, mine)
    proj_rows = lax.dynamic_update_slice(jnp.zeros((3, width), F32), proj_sums, (0, me * mine))
    up_sums = jnp.sum(grad_up_act.astype(F32), axis=0)
    up_rows = lax.dynamic_update_slice(jnp.zeros((hidden,), F32), up_sums, (side * half_hidden,))
    vector_part = jnp.concatenate(
        [
            jnp.zeros((2, width), F32),
            proj_rows,
            jnp.sum(grad_branch.astype(F32), axis=0)[None],
            jnp.sum(grad_normed2 * unit2, axis=0)[None],
            jnp.sum(grad_normed2, axis=0)[None],
            jnp.sum(cot, axis=0)[None],
            up_rows.reshape(hidden // width, width),
            jnp.zeros((16 - vectors.shape[0], width), F32),
        ],
        axis=0,
    )
    grad_normed1, quarters, vector_group = tail_call(
        part_qkv, grad_proj, qkv_w, tokens_all, vector_part, wide, narrow
    )
    grad_tokens = (grad_resid + norm_back(grad_normed1, vec[0], unit1, inverse1)).astype(BF)

    def join(value):
        other = across(value)
        mine = value.astype(F32) + other.astype(F32)
        theirs = mate(value).astype(F32) + mate(other).astype(F32)
        first = jnp.where(side == 0, mine, theirs)
        second = jnp.where(side == 0, theirs, mine)
        return jnp.concatenate([first, second], axis=1)

    total_up = join(grad_up)
    total_down = join(grad_down)
    total_out = join(grad_out)
    total_qkv = jnp.concatenate(
        [quarters[i, :, j * mine : (j + 1) * mine] for j in range(3) for i in range(narrow)], axis=1
    ).astype(F32)

    squares = sum(jnp.sum(g * g) for g in (total_qkv, total_out, total_up, total_down))
    slices = jnp.moveaxis(vector_group.reshape(16, wide, shard_rows), 1, 0)
    slices = jnp.pad(slices, ((0, 0), (0, 0), (0, -shard_rows % 128)))
    place = (jnp.arange(16)[:, None] == 15) & (jnp.arange(slices.shape[2])[None, :] == 0)
    slices = jnp.where(place[None], squares, slices)
    vector_total, vector_squares = norm_call(slices, wide)
    grad_norm = jnp.sqrt(vector_total[15, 0] + jnp.sum(vector_squares))
    clip = 1.0 / jnp.maximum(grad_norm, 1.0)
    count = step_count[0].astype(F32)
    rate = 0.4 * count / (count + 4.0)
    decay = 0.04 + 0.018 * count
    fix_first = 1.0 - jnp.power(0.9, count)
    fix_second = 1.0 - jnp.power(0.999, count)
    grad_vectors = vector_total[: vectors.shape[0], :shard_rows]

    def update(param, grad, first, second, decay_here):
        return adamw(param, grad, first, second, clip, rate, decay_here, fix_first, fix_second)

    new_qkv = update(weight_qkv, total_qkv, first_qkv, second_qkv, decay)
    new_out = update(weight_out, total_out, first_out, second_out, decay)
    new_up = update(weight_up, total_up, first_up, second_up, decay)
    new_down = update(weight_down, total_down, first_down, second_down, decay)
    new_vectors = update(vectors, grad_vectors, first_vectors, second_vectors, 0.0)
    news = (new_qkv, new_out, new_up, new_down, new_vectors)
    return (layer_out, grad_tokens) + tuple(n[i] for i in range(3) for n in news) + (grad_norm, grad_vectors[8])


def solution(mesh):
    by_token = P(("wide", "narrow"), None)
    ids = P(("wide", "narrow"))
    by_row = P("wide", None)
    by_column = P(None, "wide")
    params = (by_row,) * 4 + (by_column,)
    return jax.shard_map(
        on_device,
        mesh=mesh,
        in_specs=(by_token, by_token, ids, ids, P(None, ("wide", "narrow")), P()) + params * 3,
        out_specs=(by_token, by_token) + params * 3 + (P(), P("wide")),
        check_vma=False,
    )
```

```python
import functools

import jax
import jax.numpy as jnp
from jax import lax
from jax.experimental import pallas as pl
from jax.experimental.pallas import tpu as pltpu
from jax.sharding import PartitionSpec as P

HEADS = 16
BLOCK = 256
BF = jnp.bfloat16
F32 = jnp.float32
MESH = pl.DeviceIdType.MESH


def dot(a, b, ca, cb):
    return lax.dot_general(a, b, (((ca,), (cb,)), ((), ())), preferred_element_type=F32)


def swap_halves(x, half):
    lane = lax.broadcasted_iota(jnp.int32, x.shape, 1)
    width = x.shape[1]
    return jnp.where(
        lane % (2 * half) < half, pltpu.roll(x, width - half, 1), pltpu.roll(x, half, 1)
    )


def turn(x, cosine, sine, half, sign):
    parts = []
    for start in range(0, x.shape[1], 128):
        part = x[:, start : start + 128]
        other = swap_halves(part, half) * sine
        parts.append(part * cosine + other if sign > 0 else part * cosine - other)
    return jnp.concatenate(parts, axis=1)


def rotary_table(head_dim):
    half = head_dim // 2
    lane = jnp.arange(128)
    pair = lane % half
    rates = jnp.power(10000.0, -(pair // 3).astype(F32) / ((half + 2) // 3))
    row = jnp.arange(128)
    axis = row // 14
    value = (row % 14).astype(F32)
    live = (axis[:, None] == (pair % 3)[None, :]) & (row[:, None] < 42)
    angle = value[:, None] * rates[None, :]
    signs = jnp.where(lane % head_dim < half, -1.0, 1.0)
    return jnp.concatenate(
        [
            jnp.where(live, jnp.cos(angle), 0.0),
            jnp.where(live, jnp.sin(angle) * signs[None, :], 0.0),
        ],
        axis=1,
    )


def qkv_kernel(half, x_ref, vec_ref, w_ref, bias_ref, onehot_ref, table_ref, q_ref, k_ref, v_ref, turn_ref, norm_ref):
    width = q_ref.shape[1]
    angles = lax.dot_general(
        onehot_ref[...],
        table_ref[...],
        (((1,), (0,)), ((), ())),
        precision=lax.Precision.HIGHEST,
        preferred_element_type=F32,
    )
    turn_ref[...] = angles
    cosine, sine = angles[:, :128], angles[:, 128:]
    unit, _ = norm_parts(x_ref[...].astype(F32))
    normed = (unit * vec_ref[0:1, :] + vec_ref[1:2, :]).astype(BF)
    norm_ref[...] = normed
    proj = dot(normed, w_ref[...], 1, 0) + bias_ref[...]
    q_ref[...] = turn(proj[:, :width], cosine, sine, half, 1).astype(BF)
    k_ref[...] = turn(proj[:, width : 2 * width], cosine, sine, half, 1).astype(BF)
    v_ref[...] = proj[:, 2 * width :].astype(BF)


def qkv_call(x, vec, w, bias, onehot, table, half):
    rows, depth = x.shape
    width = w.shape[1] // 3
    out = jax.ShapeDtypeStruct((rows, width), BF)
    row_block = lambda cols: pl.BlockSpec((BLOCK, cols), lambda i: (i, 0))
    whole = lambda a: pl.BlockSpec(a.shape, lambda i: (0, 0))
    return pl.pallas_call(
        functools.partial(qkv_kernel, half),
        grid=(rows // BLOCK,),
        in_specs=[row_block(depth), whole(vec), whole(w), whole(bias), row_block(128), whole(table)],
        out_specs=[row_block(width)] * 3 + [row_block(256), row_block(depth)],
        out_shape=[
            out, out, out, jax.ShapeDtypeStruct((rows, 256), F32), jax.ShapeDtypeStruct((rows, depth), BF)
        ],
        cost_estimate=pl.CostEstimate(
            flops=2 * rows * depth * 3 * width, bytes_accessed=rows * depth * 6, transcendentals=0
        ),
        name="qkv",
    )(x, vec, w, bias, onehot, table)


def greet(targets):
    barrier = pltpu.get_barrier_semaphore()
    for target in targets:
        pl.semaphore_signal(barrier, inc=1, device_id=target, device_id_type=MESH)
    pl.semaphore_wait(barrier, len(targets))


def others(name, index, size):
    return [{name: lax.rem(index + d, size)} for d in range(1, size)]


class Copies:
    def __init__(self, send, recv):
        self.send, self.recv, self.all = send, recv, []

    def make(self, src, dst, **target):
        i = len(self.all)
        copy = pltpu.make_async_remote_copy(
            src_ref=src, dst_ref=dst, send_sem=self.send.at[i], recv_sem=self.recv.at[i],
            device_id=target, device_id_type=MESH,
        )
        self.all.append([copy, False])
        return i

    def launch(self, *indices):
        for i in indices:
            self.all[i][0].start()

    def start(self, src, dst, **target):
        i = self.make(src, dst, **target)
        self.launch(i)
        return i

    def arrived(self, i):
        if not self.all[i][1]:
            self.all[i][0].wait_recv()
            self.all[i][1] = True

    def finish(self):
        for i in range(len(self.all)):
            self.arrived(i)
        for copy, _ in self.all:
            copy.wait_send()


def rows_at(index, size):
    return pl.ds(pl.multiple_of(index * size, size), size)


def gather_kernel(
    wide, narrow, tok, qkv, vec, tag, tok_all, qkv_all, vec_all, tag_all, send, recv, local
):
    w, n = lax.axis_index("wide"), lax.axis_index("narrow")
    column = wide // 2
    z, y = w // 2, lax.rem(w, 2)
    near, mate, cross = w + 1 - 2 * y, n + 1 - 2 * lax.rem(n, 2), lax.rem(n + 2, narrow)
    wide_rows, group_rows = qkv.shape[0], tok.shape[0]
    pieces = 4
    piece = group_rows // pieces
    greet(others("wide", w, wide) + others("narrow", n, narrow))
    go = Copies(send, recv)
    for d in range(1, wide):
        go.start(vec, vec_all.at[w], wide=lax.rem(w + d, wide))
    for d in range(1, narrow):
        go.start(tag, tag_all.at[n], narrow=lax.rem(n + d, narrow))
    own_rows = rows_at(w, wide_rows)
    token_rows = lambda i, p: rows_at(i * pieces + p, piece)
    far = [go.start(qkv, qkv_all.at[own_rows], wide=lax.rem(z + d, column) * 2 + y) for d in range(1, column)]
    over = [
        go.start(tok.at[pl.ds(p * piece, piece)], tok_all.at[token_rows(n, p)], narrow=cross) for p in range(pieces)
    ]
    go.start(qkv, qkv_all.at[own_rows], wide=near)
    for p in range(pieces):
        go.start(tok.at[pl.ds(p * piece, piece)], tok_all.at[token_rows(n, p)], narrow=mate)
    own = [
        pltpu.make_async_copy(tok, tok_all.at[rows_at(n, group_rows)], local.at[0]),
        pltpu.make_async_copy(qkv, qkv_all.at[own_rows], local.at[1]),
        pltpu.make_async_copy(vec, vec_all.at[w], local.at[2]),
        pltpu.make_async_copy(tag, tag_all.at[n], local.at[3]),
    ]
    for copy in own:
        copy.start()
    for i in range(max(pieces, column - 1)):
        if i < column - 1:
            go.arrived(far[i])
            block = qkv_all.at[rows_at(lax.rem(z - (i + 1) + column, column) * 2 + y, wide_rows)]
            go.start(block, block, wide=near)
        if i < pieces:
            go.arrived(over[i])
            block = tok_all.at[token_rows(cross, i)]
            go.start(block, block, narrow=mate)
    for copy in own:
        copy.wait()
    go.finish()


def gather_call(tok, qkv, vec, tag, wide, narrow):
    copies = (wide - 1) + (narrow - 1) + 2 * (wide // 2 - 1) + 1 + 12
    vmem = pl.BlockSpec(memory_space=pltpu.VMEM)
    anywhere = pl.BlockSpec(memory_space=pl.ANY)
    return pl.pallas_call(
        functools.partial(gather_kernel, wide, narrow),
        in_specs=[vmem] * 4,
        out_specs=[anywhere] * 4,
        out_shape=[
            jax.ShapeDtypeStruct((narrow * tok.shape[0], tok.shape[1]), BF),
            jax.ShapeDtypeStruct((wide * qkv.shape[0], qkv.shape[1]), BF),
            jax.ShapeDtypeStruct((wide,) + vec.shape, BF),
            jax.ShapeDtypeStruct((narrow,) + tag.shape, jnp.int32),
        ],
        scratch_shapes=[
            pltpu.SemaphoreType.DMA((copies,)),
            pltpu.SemaphoreType.DMA((copies,)),
            pltpu.SemaphoreType.DMA((4,)),
        ],
        compiler_params=pltpu.CompilerParams(collective_id=0, has_side_effects=True),
        name="gather",
    )(tok, qkv, vec, tag)


def tail_kernel(
    wide, narrow, part, grad_proj, weight, tok, vec_in, down, normed_out, quarters_out, vec_out, down_out,
    partial, mate_in, cross_out, cross_in, near_in, far_out, far_in, shards, vec_box, sums, down_box, send, recv,
):
    w, n = lax.axis_index("wide"), lax.axis_index("narrow")
    column = wide // 2
    z, y = w // 2, lax.rem(w, 2)
    x, c = n // 2, lax.rem(n, 2)
    near, mate, cross = w + 1 - 2 * y, n + 1 - 2 * c, lax.rem(n + 2, narrow)
    wide_rows, group_rows = part.shape[0] // wide, normed_out.shape[0]
    towards = [lax.rem(z + d, column) for d in range(1, column + 1)]
    greet([{"wide": near}] + [{"wide": to * 2 + y} for to in towards[:-1]] + others("narrow", n, narrow))
    go = Copies(send, recv)
    first = [
        go.start(part.at[rows_at(towards[k] * 2 + 1 - y, wide_rows)], near_in.at[k], wide=near) for k in range(column)
    ]

    down_over = go.start(down, down_box.at[n], narrow=cross)
    go.start(down, down_box.at[n], narrow=mate)
    down_box[pl.ds(n, 1)] = down[...][None]

    sums[...] = jnp.zeros_like(sums)
    owners = [(1 - x) * 2 + 1 - c, x * 2 + 1 - c, (1 - x) * 2 + c, n]
    mates = []
    for slot, owner in enumerate(owners):

        def body(i, carry):
            at = pl.ds(pl.multiple_of(owner * group_rows + i * BLOCK, BLOCK), BLOCK)
            here = pl.ds(pl.multiple_of(i * BLOCK, BLOCK), BLOCK)
            grads = dot(grad_proj[at, :], weight[...], 1, 1)
            unit, _ = norm_parts(tok[at, :].astype(F32))
            sums[0:1, :] += jnp.sum(grads * unit, axis=0, keepdims=True)
            sums[1:2, :] += jnp.sum(grads, axis=0, keepdims=True)
            if slot < 3:
                partial[slot, here, :] = grads.astype(BF)
            else:
                normed_out[here, :] = grads
            return carry

        lax.fori_loop(0, group_rows // BLOCK, body, 0)
        if slot < 2:
            mates.append(go.start(partial.at[slot], mate_in.at[slot], narrow=mate))

    vec_box[pl.ds(n, 1)] = vec_in[...][None]
    vec_box[pl.ds(n, 1), 0:2, :] = sums[0:2, :][None]
    vecs = [go.start(vec_box.at[n], vec_box.at[n], narrow=lax.rem(n + d, narrow)) for d in range(1, narrow)]

    go.arrived(down_over)
    go.start(down_box.at[cross], down_box.at[cross], narrow=mate)
    go.arrived(mates[0])
    half = group_rows // 2
    overs = []
    for p in range(2):
        at = pl.ds(p * half, half)
        cross_out[at, :] = (partial[2, at, :].astype(F32) + mate_in[0, at, :].astype(F32)).astype(BF)
        overs.append(go.start(cross_out.at[at], cross_in.at[at], narrow=cross))

    seconds = []
    total = None
    for k in range(column):
        go.arrived(first[k])
        mine = part[rows_at(towards[k] * 2 + y, wide_rows), :].astype(F32) + near_in[k].astype(F32)
        if k < column - 1:
            far_out[k] = mine.astype(BF)
            seconds.append(go.start(far_out.at[k], far_in.at[k], wide=towards[k] * 2 + y))
        else:
            total = mine
    for k in range(column - 1):
        go.arrived(seconds[k])
        total = total + far_in[k].astype(F32)
    shards[pl.ds(n, 1)] = total.astype(BF)[None]
    over = go.start(shards.at[n], shards.at[n], narrow=cross)
    go.start(shards.at[n], shards.at[n], narrow=mate)

    go.arrived(mates[1])
    for p in range(2):
        go.arrived(overs[p])
        at = pl.ds(p * half, half)
        normed_out[at, :] += mate_in[1, at, :].astype(F32) + cross_in[at, :].astype(F32)
    for i in vecs:
        go.arrived(i)
    group = vec_box[0]
    for i in range(1, narrow):
        group = group + vec_box[i]
    vec_out[...] = group

    go.arrived(over)
    go.start(shards.at[cross], shards.at[cross], narrow=mate)
    go.finish()
    quarters_out[...] = shards[...]
    down_out[...] = down_box[...]


def tail_call(part, grad_proj, weight, tok, vec_in, down, wide, narrow):
    depth, cols = part.shape
    rows = tok.shape[0] // narrow
    wide_rows = depth // wide
    column = wide // 2
    copies = 2 * column - 1 + 2 + (narrow - 1) + 2 + 3 + 3
    vmem = pl.BlockSpec(memory_space=pltpu.VMEM)
    return pl.pallas_call(
        functools.partial(tail_kernel, wide, narrow),
        in_specs=[vmem] * 6,
        out_specs=[vmem] * 4,
        out_shape=[
            jax.ShapeDtypeStruct((rows, depth), F32),
            jax.ShapeDtypeStruct((narrow, wide_rows, cols), BF),
            jax.ShapeDtypeStruct(vec_in.shape, F32),
            jax.ShapeDtypeStruct((narrow,) + down.shape, BF),
        ],
        scratch_shapes=[
            pltpu.VMEM((3, rows, depth), BF),
            pltpu.VMEM((2, rows, depth), BF),
            pltpu.VMEM((rows, depth), BF),
            pltpu.VMEM((rows, depth), BF),
            pltpu.VMEM((column, wide_rows, cols), BF),
            pltpu.VMEM((column - 1, wide_rows, cols), BF),
            pltpu.VMEM((column - 1, wide_rows, cols), BF),
            pltpu.VMEM((narrow, wide_rows, cols), BF),
            pltpu.VMEM((narrow,) + vec_in.shape, F32),
            pltpu.VMEM((8, depth), F32),
            pltpu.VMEM((narrow,) + down.shape, BF),
            pltpu.SemaphoreType.DMA((copies,)),
            pltpu.SemaphoreType.DMA((copies,)),
        ],
        compiler_params=pltpu.CompilerParams(
            collective_id=1, has_side_effects=True, vmem_limit_bytes=56 * 1024 * 1024
        ),
        name="tail",
    )(part, grad_proj, weight, tok, vec_in, down)


def norm_kernel(wide, slices, total_out, square_out, box, squares, send, recv):
    w = lax.axis_index("wide")
    greet(others("wide", w, wide))
    go = Copies(send, recv)
    peers = [lax.rem(w + d, wide) for d in range(1, wide)]
    for peer in peers:
        go.start(slices.at[peer], box.at[w], wide=peer)
    box[pl.ds(w, 1)] = slices[pl.ds(w, 1)]
    for i in range(wide - 1):
        go.arrived(i)
    total = box[0]
    for i in range(1, wide):
        total = total + box[i]
    total_out[...] = total
    row = lax.broadcasted_iota(jnp.int32, total.shape, 0)
    entries = jnp.where(row == 15, 0.0, total)
    entries = entries * entries
    squares[pl.ds(w, 1)] = (entries[:8] + entries[8:])[None]
    for peer in peers:
        go.start(squares.at[w], squares.at[w], wide=peer)
    go.finish()
    all_squares = squares[0]
    for i in range(1, wide):
        all_squares = all_squares + squares[i]
    square_out[...] = all_squares


def norm_call(slices, wide):
    vmem = pl.BlockSpec(memory_space=pltpu.VMEM)
    copies = 2 * (wide - 1)
    return pl.pallas_call(
        functools.partial(norm_kernel, wide),
        in_specs=[vmem],
        out_specs=[vmem] * 2,
        out_shape=[jax.ShapeDtypeStruct((16, 128), F32), jax.ShapeDtypeStruct((8, 128), F32)],
        scratch_shapes=[
            pltpu.VMEM((wide, 16, 128), F32),
            pltpu.VMEM((wide, 8, 128), F32),
            pltpu.SemaphoreType.DMA((copies,)),
            pltpu.SemaphoreType.DMA((copies,)),
        ],
        compiler_params=pltpu.CompilerParams(collective_id=2, has_side_effects=True),
        name="norm",
    )(slices)


CLIP = 784


def head_lanes(shape, head, head_dim):
    lane = lax.broadcasted_iota(jnp.int32, shape, 1)
    return lane // head_dim == head


def meeting(block, blocks):
    before, after = CLIP // BLOCK, -(-2 * CLIP // BLOCK)
    low = before * (block // after)
    high = blocks - (blocks - after) * (1 - jnp.minimum(block // before, 1))
    return low, high


def forward_kernel(
    heads, head_dim, wide, narrow,
    q_ref, k_ref, v_ref, seg_ref, tag_ref, up_ref, out_ref,
    o_ref, lse_ref, mixed_ref, up_all, out_all,
    values_turned, acc, peak, total, o_box, send, recv, mix_send, mix_recv, local,
):
    step = pl.program_id(0)
    rows, width = q_ref.shape
    blocks = rows // BLOCK
    per = blocks // narrow
    last = blocks - 1
    w, n = lax.axis_index("wide"), lax.axis_index("narrow")
    column = wide // 2
    z, y, side = w // 2, lax.rem(w, 2), lax.rem(n, 2)
    near, mate = w + 1 - 2 * y, n + 1 - 2 * side
    block = lax.rem((n + 1) * per + step, blocks)

    go = Copies(send, recv)
    wide_rows, half = out_ref.shape
    out_cols = pl.ds(pl.multiple_of(side * half, half), half)
    quarter = up_ref.shape[1] // 4
    cross = lax.rem(n + 2, narrow)
    shared = pl.ds(pl.multiple_of(n // 2 * quarter, quarter), quarter)
    both = pl.ds(2 * quarter, 2 * quarter)
    up_at = lambda i, cols: up_all.at[rows_at(i, wide_rows), cols]
    out_at = lambda i: out_all.at[rows_at(i, wide_rows), out_cols]
    source = lambda d: lax.rem(z - d + column, column) * 2 + y
    target = lambda d: lax.rem(z + d, column) * 2 + y
    starts, early, late = [], [], []
    out_near = [go.make(out_ref, out_at(w), wide=near)]
    out_mate = [go.make(out_ref, out_at(w), narrow=mate)]
    starts += out_near + out_mate
    for d in range(1, column):
        far = go.make(out_ref, out_at(w), wide=target(d))
        block_ref = out_at(source(d))
        out_near.append(go.make(block_ref, block_ref, wide=near))
        starts.append(far)
        early.append((far, [out_near[-1], go.make(block_ref, block_ref, narrow=mate)]))
    for d in range(column):
        block_ref = out_at(lax.rem(z - d + column, column) * 2 + 1 - y)
        late.append((out_near[d], [go.make(block_ref, block_ref, narrow=mate)]))
    for cols in (shared, both):
        passes = lambda i: [] if cols is both else [go.make(up_at(i, cols), up_at(i, cols), narrow=cross)]
        up_near = [go.make(up_ref.at[:, cols], up_at(w, cols), wide=near)]
        starts += up_near
        if cols is shared:
            starts.append(go.make(up_ref.at[:, cols], up_at(w, cols), narrow=cross))
        for d in range(1, column):
            far = go.make(up_ref.at[:, cols], up_at(w, cols), wide=target(d))
            block_ref = up_at(source(d), cols)
            starts.append(far)
            up_near.append(go.make(block_ref, block_ref, wide=near))
            early.append((far, [up_near[-1]] + passes(source(d))))
        if cols is shared:
            for d in range(column):
                early.append((up_near[d], passes(lax.rem(z - d + column, column) * 2 + 1 - y)))
    actions = early + late
    own = [
        pltpu.make_async_copy(up_ref.at[:, shared], up_at(w, shared), local.at[0]),
        pltpu.make_async_copy(out_ref, out_at(w), local.at[1]),
        pltpu.make_async_copy(up_ref.at[:, both], up_at(w, both), local.at[2 + per]),
    ]

    mine = pl.ds(pl.multiple_of(n * width, width), width)

    def result(s):
        at = lax.rem((n + 1) * per + s, blocks)
        return pltpu.make_async_remote_copy(
            src_ref=o_box.at[rows_at(at, BLOCK)],
            dst_ref=mixed_ref.at[rows_at(lax.rem(s, per), BLOCK), mine],
            send_sem=mix_send.at[s],
            recv_sem=mix_recv.at[s],
            device_id={"narrow": lax.rem(n + 1 + s // per, narrow)},
            device_id_type=MESH,
        )

    def result_here(s):
        return pltpu.make_async_copy(
            o_box.at[rows_at(n * per + s, BLOCK)], mixed_ref.at[rows_at(s, BLOCK), mine], local.at[2 + s]
        )

    @pl.when(step == 0)
    def _():
        greet(
            [{"wide": near}] + [{"wide": target(d)} for d in range(1, column)] + others("narrow", n, narrow)
        )
        go.launch(*starts)
        for copy in own:
            copy.start()
        values_turned[...] = v_ref[...].T

    share = -(-len(actions) // last)
    for i in range(last):
        some = actions[i * share : (i + 1) * share]

        @pl.when(step == i + 1)
        def _():
            for arrival, follow in some:
                go.arrived(arrival)
                go.launch(*follow)

    at = rows_at(block, BLOCK)
    query = q_ref[at, :] * jnp.asarray(head_dim**-0.5, BF)
    seg = seg_ref[pl.ds(block, 1)][0]
    masked_query = [
        jnp.where(head_lanes(query.shape, h, head_dim), query, jnp.zeros_like(query)) for h in range(heads)
    ]
    acc[...] = jnp.zeros_like(acc)
    peak[...] = jnp.full_like(peak, -1e30)
    total[...] = jnp.zeros_like(total)

    def body(j, carry):
        start = pl.multiple_of(j * BLOCK, BLOCK)
        key = k_ref[pl.ds(start, BLOCK), :]
        allowed = tag_ref[pl.ds(start, BLOCK), :] == seg
        scores = [jnp.where(allowed, dot(key, masked_query[h], 1, 1), -1e30) for h in range(heads)]
        for h in range(heads):
            lines = slice(h * head_dim, (h + 1) * head_dim)
            old = peak[h : h + 1, :]
            new = jnp.maximum(old, jnp.max(scores[h], axis=0, keepdims=True))
            probs = jnp.exp(scores[h] - new)
            keep = jnp.exp(old - new)
            peak[h : h + 1, :] = new
            total[h : h + 1, :] = total[h : h + 1, :] * keep + jnp.sum(probs, axis=0, keepdims=True)
            value = values_turned[lines, pl.ds(start, BLOCK)]
            acc[lines, :] = acc[lines, :] * keep + dot(value, probs.astype(BF), 1, 0)
        return carry

    low, high = meeting(block, blocks)
    lax.fori_loop(low, high, body, 0)
    parts = [acc[h * head_dim : (h + 1) * head_dim, :] / total[h : h + 1, :] for h in range(heads)]
    out = jnp.concatenate(parts, axis=0).T.astype(BF)
    o_ref[at, :] = out
    o_box[at, :] = out
    lse_ref[pl.ds(block, 1)] = (peak[...] + jnp.log(jnp.maximum(total[...], 1e-30)))[None]

    @pl.when(step < blocks - per)
    def _():
        result(step).start()

    @pl.when(step == last)
    def _():
        for s in range(per):
            result_here(s).start()
        for copy in own:
            copy.wait()
        for s in range(blocks - per):
            result(s).wait()
        for s in range(per):
            result_here(s).wait()
        go.finish()


def forward_call(q, k, v, seg_rows, tag_col, up_low, out_half, head_dim, wide, narrow):
    rows, width = q.shape
    heads = width // head_dim
    blocks = rows // BLOCK
    column = wide // 2
    copies = 2 + 3 * (column - 1) + column + 2 * (2 * column - 1) + 2 * column
    whole = lambda a: pl.BlockSpec(a.shape, lambda i: (0,) * a.ndim)
    anywhere = pl.BlockSpec(memory_space=pl.ANY)
    lse = jax.ShapeDtypeStruct((blocks, 8, BLOCK), F32)
    seg_rows = seg_rows[:, None, :]
    return pl.pallas_call(
        functools.partial(forward_kernel, heads, head_dim, wide, narrow),
        grid=(blocks,),
        in_specs=[whole(a) for a in (q, k, v, seg_rows, tag_col, up_low, out_half)],
        out_specs=[whole(q), whole(lse), anywhere, anywhere, anywhere],
        out_shape=[
            jax.ShapeDtypeStruct((rows, width), BF),
            lse,
            jax.ShapeDtypeStruct((rows // narrow, width * narrow), BF),
            jax.ShapeDtypeStruct((up_low.shape[0] * wide, up_low.shape[1]), BF),
            jax.ShapeDtypeStruct((out_half.shape[0] * wide, 2 * out_half.shape[1]), BF),
        ],
        scratch_shapes=[
            pltpu.VMEM((width, rows), BF),
            pltpu.VMEM((width, BLOCK), F32),
            pltpu.VMEM((8, BLOCK), F32),
            pltpu.VMEM((8, BLOCK), F32),
            pltpu.VMEM((rows, width), BF),
            pltpu.SemaphoreType.DMA((copies,)),
            pltpu.SemaphoreType.DMA((copies,)),
            pltpu.SemaphoreType.DMA((blocks,)),
            pltpu.SemaphoreType.DMA((blocks,)),
            pltpu.SemaphoreType.DMA((3 + blocks // narrow,)),
        ],
        compiler_params=pltpu.CompilerParams(collective_id=3, has_side_effects=True),
        cost_estimate=pl.CostEstimate(
            flops=heads * rows * rows * width * 4, bytes_accessed=rows * width * 8, transcendentals=heads * rows * rows
        ),
        name="attention_forward",
    )(q, k, v, seg_rows, tag_col, up_low, out_half)


class Scatter:
    def __init__(self, go, wide, narrow, part, near_in, own, far_out, far_in, box, local):
        w, self.n = lax.axis_index("wide"), lax.axis_index("narrow")
        self.go, self.column = go, wide // 2
        self.near_in, self.own, self.far_out, self.far_in, self.box = near_in, own, far_out, far_in, box
        z, y = w // 2, lax.rem(w, 2)
        near, mate, cross = w + 1 - 2 * y, self.n + 1 - 2 * lax.rem(self.n, 2), lax.rem(self.n + 2, narrow)
        size = part.shape[0] // wide
        towards = [lax.rem(z + d, self.column) for d in range(1, self.column + 1)]
        self.first = [
            go.make(part.at[rows_at(to * 2 + 1 - y, size)], near_in.at[k], wide=near) for k, to in enumerate(towards)
        ]
        self.loads = [
            pltpu.make_async_copy(part.at[rows_at(to * 2 + y, size)], own.at[k], local.at[k])
            for k, to in enumerate(towards)
        ]
        self.second = [
            go.make(far_out.at[k], far_in.at[k], wide=to * 2 + y) for k, to in enumerate(towards[:-1])
        ]
        self.over = go.make(box.at[self.n], box.at[self.n], narrow=cross)
        self.beside = go.make(box.at[self.n], box.at[self.n], narrow=mate)
        self.passed = go.make(box.at[cross], box.at[cross], narrow=mate)

    def begin(self):
        self.go.launch(*self.first)
        for copy in self.loads:
            copy.start()

    def relay(self, k):
        self.go.arrived(self.first[k])
        self.loads[k].wait()
        if k < self.column - 1:
            self.far_out[k] = (self.own[k].astype(F32) + self.near_in[k].astype(F32)).astype(BF)
            self.go.launch(self.second[k])

    def total(self):
        value = self.own[self.column - 1].astype(F32) + self.near_in[self.column - 1].astype(F32)
        for k in range(self.column - 1):
            self.go.arrived(self.second[k])
            value = value + self.far_in[k].astype(F32)
        self.box[pl.ds(self.n, 1)] = value.astype(BF)[None]
        self.go.launch(self.over, self.beside)

    def share(self):
        self.go.arrived(self.over)
        self.go.launch(self.passed)

    @staticmethod
    def copies(wide):
        return 2 * (wide // 2) - 1 + 3

    @staticmethod
    def scratch(wide, narrow, rows, cols):
        column, size = wide // 2, rows // wide
        sizes = [column, column, column - 1, column - 1, narrow]
        return [pltpu.VMEM((count, size, cols), BF) for count in sizes] + [pltpu.SemaphoreType.DMA((column,))]


def backward_kernel(
    heads, head_dim, wide, narrow,
    q_ref, k_ref, v_ref, o_ref, g_ref, lse_ref, seg_ref, tag_ref, turn_ref, part_out, part_up,
    grads_out, shards_out, shards_up,
    q_heads, g_heads, delta, grad_query, send, recv, *boxes,
):
    step = pl.program_id(0)
    rows, width = q_ref.shape
    blocks = rows // BLOCK
    last = blocks - 1
    scale = head_dim**-0.5
    half = head_dim // 2
    go = Copies(send, recv)
    column = wide // 2
    outs = Scatter(go, wide, narrow, part_out, *boxes[:6])
    ups = Scatter(go, wide, narrow, part_up, *boxes[6:])

    @pl.when(step == 0)
    def _():
        w, n = lax.axis_index("wide"), lax.axis_index("narrow")
        z, y = w // 2, lax.rem(w, 2)
        greet(
            [{"wide": w + 1 - 2 * y}]
            + [{"wide": lax.rem(z + d, column) * 2 + y} for d in range(1, column)]
            + [{"narrow": n + 1 - 2 * lax.rem(n, 2)}, {"narrow": lax.rem(n + 2, narrow)}]
        )
        outs.begin()
        ups.begin()

    actions = [[] for _ in range(last)]
    for k in range(column):
        actions[1 + 2 * k // column].append(functools.partial(outs.relay, k))
        actions[2 + 4 * k // column].append(functools.partial(ups.relay, k))
    actions[last - 3].append(outs.total)
    actions[last - 2].append(outs.share)
    for i in range(last):
        if actions[i]:

            @pl.when(step == i + 1)
            def _():
                for action in actions[i]:
                    action()

    @pl.when(step == 0)
    def _():
        grad_query[...] = jnp.zeros_like(grad_query)
        row = lax.broadcasted_iota(jnp.int32, (8, width), 0)
        lane = lax.broadcasted_iota(jnp.int32, (8, width), 1)
        pick = jnp.where(lane // head_dim == row, 1.0, 0.0)

        def prepare(i, carry):
            at = pl.ds(pl.multiple_of(i * BLOCK, BLOCK), BLOCK)
            query = q_ref[at, :] * jnp.asarray(scale, BF)
            grad = g_ref[at, :]
            for h in range(heads):
                lanes = head_lanes(query.shape, h, head_dim)
                q_heads[h, at, :] = jnp.where(lanes, query, jnp.zeros_like(query))
                g_heads[h, at, :] = jnp.where(lanes, grad, jnp.zeros_like(grad))
            product = grad.astype(F32) * o_ref[at, :].astype(F32)
            delta[pl.ds(i, 1)] = lax.dot_general(
                pick,
                product,
                (((1,), (1,)), ((), ())),
                precision=lax.Precision.HIGHEST,
                preferred_element_type=F32,
            )[None]
            return carry

        lax.fori_loop(0, blocks, prepare, 0)

    key = k_ref[...]
    value = v_ref[...]
    tag = tag_ref[...]
    masked_key = [jnp.where(head_lanes(key.shape, h, head_dim), key, jnp.zeros_like(key)) for h in range(heads)]

    def body(i, carry):
        grad_key, grad_value = carry
        at = pl.ds(pl.multiple_of(i * BLOCK, BLOCK), BLOCK)
        allowed = tag == seg_ref[pl.ds(i, 1), :]
        lse = lse_ref[pl.ds(i, 1)][0]
        dlt = delta[pl.ds(i, 1)][0]
        total = None
        for h in range(heads):
            query = q_heads[h, at, :]
            grad = g_heads[h, at, :]
            scores = dot(key, query, 1, 1)
            probs = jnp.where(allowed, jnp.exp(scores - lse[h : h + 1, :]), 0.0)
            grad_probs = dot(value, grad, 1, 1)
            grad_scores = (probs * (grad_probs - dlt[h : h + 1, :])).astype(BF)
            grad_value = grad_value + dot(probs.astype(BF), grad, 1, 0)
            grad_key = grad_key + dot(grad_scores, query, 1, 0)
            term = dot(grad_scores, masked_key[h], 0, 0)
            total = term if total is None else total + term
        grad_query[at, :] += total
        return grad_key, grad_value

    zero = jnp.zeros((BLOCK, width), F32)
    low, high = meeting(step, blocks)
    grad_key, grad_value = lax.fori_loop(low, high, body, (zero, zero))
    here = pl.ds(pl.multiple_of(step * BLOCK, BLOCK), BLOCK)
    cosine, sine = turn_ref[here, :128], turn_ref[here, 128:]
    grads_out[here, width : 2 * width] = turn(grad_key, cosine, sine, half, -1).astype(BF)
    grads_out[here, 2 * width :] = grad_value.astype(BF)

    @pl.when(step == last)
    def _():
        ups.total()

        def finish(i, carry):
            at = pl.ds(pl.multiple_of(i * BLOCK, BLOCK), BLOCK)
            grads = grad_query[at, :] * scale
            grads_out[at, :width] = turn(grads, turn_ref[at, :128], turn_ref[at, 128:], half, -1).astype(BF)
            return carry

        lax.fori_loop(0, blocks, finish, 0)
        ups.share()
        go.finish()
        shards_out[...] = outs.box[...]
        shards_up[...] = ups.box[...]


def backward_call(q, k, v, o, g, lse, seg_rows, tag_col, turns, part_out, part_up, head_dim, wide, narrow):
    rows, width = q.shape
    heads = width // head_dim
    blocks = rows // BLOCK
    whole = lambda a: pl.BlockSpec(a.shape, lambda i: (0,) * len(a.shape), pipeline_mode=pl.Buffered(1))
    block = pl.BlockSpec((BLOCK, width), lambda i: (i, 0))
    anywhere = pl.BlockSpec(memory_space=pl.ANY)
    depth = part_up.shape[0]
    results = [
        jax.ShapeDtypeStruct((rows, 3 * width), BF),
        jax.ShapeDtypeStruct((narrow, depth // wide, part_out.shape[1]), BF),
        jax.ShapeDtypeStruct((narrow, depth // wide, part_up.shape[1]), BF),
    ]
    copies = 2 * Scatter.copies(wide)
    return pl.pallas_call(
        functools.partial(backward_kernel, heads, head_dim, wide, narrow),
        grid=(blocks,),
        in_specs=[
            whole(q), block, block, whole(o), whole(g), whole(lse), whole(seg_rows),
            pl.BlockSpec((BLOCK, 1), lambda i: (i, 0)),
            whole(turns), anywhere, anywhere,
        ],
        out_specs=[whole(a) for a in results],
        out_shape=results,
        scratch_shapes=[
            pltpu.VMEM((heads, rows, width), BF),
            pltpu.VMEM((heads, rows, width), BF),
            pltpu.VMEM((blocks, 8, BLOCK), F32),
            pltpu.VMEM((rows, width), F32),
            pltpu.SemaphoreType.DMA((copies,)),
            pltpu.SemaphoreType.DMA((copies,)),
        ]
        + Scatter.scratch(wide, narrow, depth, part_out.shape[1])
        + Scatter.scratch(wide, narrow, depth, part_up.shape[1]),
        compiler_params=pltpu.CompilerParams(
            collective_id=4, has_side_effects=True, vmem_limit_bytes=60 * 1024 * 1024
        ),
        cost_estimate=pl.CostEstimate(
            flops=heads * rows * rows * width * 7, bytes_accessed=rows * width * 20, transcendentals=heads * rows * rows
        ),
        name="attention_backward",
    )(q, k, v, o, g, lse, seg_rows, tag_col, turns, part_out, part_up)


def norm_parts(values):
    center = values - jnp.mean(values, axis=-1, keepdims=True)
    inverse = lax.rsqrt(jnp.mean(center * center, axis=-1, keepdims=True) + 1e-06)
    return center * inverse, inverse


def norm_back(grads, gain, unit, inverse):
    scaled = grads * gain
    return inverse * (
        scaled - jnp.mean(scaled, axis=-1, keepdims=True) - unit * jnp.mean(scaled * unit, axis=-1, keepdims=True)
    )


def adamw(param, grad, first, second, clip, rate, decay, fix_first, fix_second):
    clipped = grad * clip
    moment = 0.9 * first + 0.1 * clipped
    square = 0.999 * second + 0.001 * clipped * clipped
    direction = moment / fix_first / (jnp.sqrt(square / fix_second) + 1e-08)
    return (param - rate * (direction + decay * param), moment, square)


def on_device(
    tokens, cotangent, segment_ids, key_keep, patch_coords, step_count,
    weight_qkv, weight_out, weight_up, weight_down, vectors,
    first_qkv, first_out, first_up, first_down, first_vectors,
    second_qkv, second_out, second_up, second_down, second_vectors,
):
    rows, width = tokens.shape
    hidden = weight_up.shape[1]
    head_dim = width // HEADS
    narrow = lax.axis_size("narrow")
    wide = lax.axis_size("wide")
    shard_rows = width // wide
    me = lax.axis_index("narrow")
    side = me % 2
    mine = width // narrow
    half_hidden = hidden // 2
    group = rows * narrow

    def mate(value):
        return lax.ppermute(value, "narrow", [(i, i ^ 1) for i in range(narrow)])

    def across(value):
        return lax.ppermute(value, "narrow", [(i, i ^ 2) for i in range(narrow)])

    def take(value, start, size, axis=1):
        return lax.dynamic_slice_in_dim(value, start, size, axis)

    qkv_low = jnp.concatenate([take(weight_qkv, i * width + me * mine, mine) for i in range(3)], axis=1).astype(BF)
    out_low = take(weight_out, side * (width // 2), width // 2).astype(BF)
    up_low = take(weight_up, side * half_hidden, half_hidden).astype(BF)
    down_low = take(weight_down, side * half_hidden, half_hidden).astype(BF)

    shard_cols = vectors.shape[1]
    vec_shard = jnp.pad(vectors.astype(BF), ((0, 16 - vectors.shape[0]), (0, -shard_cols % 128)))
    tag = jnp.concatenate([segment_ids[None], key_keep[None], patch_coords, patch_coords], axis=0)
    tokens_all, qkv_w, vec_all, tag_all = gather_call(tokens, qkv_low, vec_shard, tag, wide, narrow)
    vec_all = vec_all[:, :, :shard_cols]
    vec = jnp.moveaxis(vec_all, 0, 1).reshape(16, width).astype(F32)[: vectors.shape[0]]
    tag_all = jnp.moveaxis(tag_all, 0, 1).reshape(8, group)
    down_w = lax.all_gather(down_low, "wide", axis=0, tiled=True)

    xin = tokens.astype(F32)
    unit1, inverse1 = norm_parts(xin)
    cot_pair = jnp.concatenate([cotangent, mate(cotangent)], axis=0)

    seg = tag_all[0]
    seg_float = seg.astype(F32)
    key_tag = jnp.where(tag_all[1] == 1, seg, -1).astype(F32)
    slot = jnp.arange(128)[None, :]
    place = tag_all[2:5]
    onehot = (
        (slot == place[0][:, None]) | (slot == 14 + place[1][:, None]) | (slot == 28 + place[2][:, None])
    ).astype(F32)
    blocks = group // BLOCK
    bias = jnp.concatenate([take(vec[2 + i : 3 + i], me * mine, mine) for i in range(3)], axis=1)
    query, keys, values, turns, normed1_all = qkv_call(tokens_all, vec[:2], qkv_w, bias, onehot, rotary_table(head_dim), head_dim // 2)
    mixed_mine, lse, mixed, up_w, out_w = forward_call(
        query, keys, values, seg_float.reshape(blocks, BLOCK), key_tag[:, None], up_low, out_low, head_dim, wide, narrow
    )

    resid = xin + (dot(mixed, out_w, 1, 0) + vec[5])
    unit2, inverse2 = norm_parts(resid)
    normed2 = (unit2 * vec[6] + vec[7]).astype(BF)
    normed2_pair = jnp.concatenate([normed2, mate(normed2)], axis=0)
    up_bias = take(vec[9:].reshape(1, -1), side * half_hidden, half_hidden)
    up_pre = dot(normed2_pair, up_w, 1, 0) + up_bias
    erf_part = 0.5 * (1.0 + lax.erf(up_pre * (0.5**0.5)))
    act = (up_pre * erf_part).astype(BF)
    slope = erf_part + up_pre * (jnp.exp(-0.5 * up_pre * up_pre) * ((2.0 * jnp.pi) ** -0.5))
    down_part = dot(act, down_w, 1, 1)
    down = down_part[:rows] + mate(down_part[rows:])
    layer_out = (resid + (down + vec[8])).astype(BF)

    part_down = dot(cot_pair, act, 0, 0).astype(BF)
    grad_down = lax.psum_scatter(part_down, "wide", scatter_dimension=0, tiled=True)
    grad_up_act = (dot(cot_pair, down_w, 1, 0) * slope).astype(BF)
    part_up = dot(normed2_pair, grad_up_act, 0, 0).astype(BF)
    grad_normed2_part = dot(grad_up_act, up_w, 1, 1)
    grad_normed2 = grad_normed2_part[:rows] + mate(grad_normed2_part[rows:])
    cot = cotangent.astype(F32)
    grad_resid = cot + norm_back(grad_normed2, vec[6], unit2, inverse2)
    grad_branch = grad_resid.astype(BF)
    grad_mixed = dot(grad_branch, out_w, 1, 1).astype(BF)
    part_out = dot(mixed, grad_branch, 0, 0)
    own_out = take(part_out, side * (width // 2), width // 2)
    other_out = take(part_out, (1 - side) * (width // 2), width // 2)
    part_out = (own_out + mate(other_out.astype(BF)).astype(F32)).astype(BF)

    grad_mixed_mine = lax.all_to_all(grad_mixed, "narrow", 1, 0, tiled=True)
    grad_proj, shards_out, shards_up = backward_call(
        query, keys, values, mixed_mine, grad_mixed_mine, lse, seg_float.reshape(blocks, BLOCK),
        key_tag[:, None], turns, part_out, part_up, head_dim, wide, narrow,
    )
    part_qkv = dot(normed1_all, grad_proj, 0, 0).astype(BF)

    proj_sums = jnp.sum(grad_proj.astype(F32), axis=0).reshape(3, mine)
    proj_rows = lax.dynamic_update_slice(jnp.zeros((3, width), F32), proj_sums, (0, me * mine))
    up_sums = jnp.sum(grad_up_act.astype(F32), axis=0)
    up_rows = lax.dynamic_update_slice(jnp.zeros((hidden,), F32), up_sums, (side * half_hidden,))
    vector_part = jnp.concatenate(
        [
            jnp.zeros((2, width), F32),
            proj_rows,
            jnp.sum(grad_branch.astype(F32), axis=0)[None],
            jnp.sum(grad_normed2 * unit2, axis=0)[None],
            jnp.sum(grad_normed2, axis=0)[None],
            jnp.sum(cot, axis=0)[None],
            up_rows.reshape(hidden // width, width),
            jnp.zeros((16 - vectors.shape[0], width), F32),
        ],
        axis=0,
    )
    grad_normed1, quarters, vector_group, shards_down = tail_call(
        part_qkv, grad_proj, qkv_w, tokens_all, vector_part, grad_down, wide, narrow
    )
    grad_tokens = (grad_resid + norm_back(grad_normed1, vec[0], unit1, inverse1)).astype(BF)

    def join(shards):
        shards = shards.astype(F32)
        return jnp.concatenate([shards[0] + shards[2], shards[1] + shards[3]], axis=1)

    total_up = join(shards_up)
    total_down = join(shards_down)
    total_out = join(shards_out)
    total_qkv = jnp.concatenate(
        [quarters[i, :, j * mine : (j + 1) * mine] for j in range(3) for i in range(narrow)], axis=1
    ).astype(F32)

    squares = sum(jnp.sum(g * g) for g in (total_qkv, total_out, total_up, total_down))
    slices = jnp.moveaxis(vector_group.reshape(16, wide, shard_rows), 1, 0)
    slices = jnp.pad(slices, ((0, 0), (0, 0), (0, -shard_rows % 128)))
    place = (jnp.arange(16)[:, None] == 15) & (jnp.arange(slices.shape[2])[None, :] == 0)
    slices = jnp.where(place[None], squares, slices)
    vector_total, vector_squares = norm_call(slices, wide)
    grad_norm = jnp.sqrt(vector_total[15, 0] + jnp.sum(vector_squares))
    clip = 1.0 / jnp.maximum(grad_norm, 1.0)
    count = step_count[0].astype(F32)
    rate = 0.4 * count / (count + 4.0)
    decay = 0.04 + 0.018 * count
    fix_first = 1.0 - jnp.power(0.9, count)
    fix_second = 1.0 - jnp.power(0.999, count)
    grad_vectors = vector_total[: vectors.shape[0], :shard_rows]

    def update(param, grad, first, second, decay_here):
        return adamw(param, grad, first, second, clip, rate, decay_here, fix_first, fix_second)

    new_qkv = update(weight_qkv, total_qkv, first_qkv, second_qkv, decay)
    new_out = update(weight_out, total_out, first_out, second_out, decay)
    new_up = update(weight_up, total_up, first_up, second_up, decay)
    new_down = update(weight_down, total_down, first_down, second_down, decay)
    new_vectors = update(vectors, grad_vectors, first_vectors, second_vectors, 0.0)
    news = (new_qkv, new_out, new_up, new_down, new_vectors)
    return (layer_out, grad_tokens) + tuple(n[i] for i in range(3) for n in news) + (grad_norm, grad_vectors[8])


def solution(mesh):
    by_token = P(("wide", "narrow"), None)
    ids = P(("wide", "narrow"))
    by_row = P("wide", None)
    by_column = P(None, "wide")
    params = (by_row,) * 4 + (by_column,)
    return jax.shard_map(
        on_device,
        mesh=mesh,
        in_specs=(by_token, by_token, ids, ids, P(None, ("wide", "narrow")), P()) + params * 3,
        out_specs=(by_token, by_token) + params * 3 + (P(), P("wide")),
        check_vma=False,
    )
```

```python
import functools

import jax
import jax.numpy as jnp
from jax import lax
from jax.experimental import pallas as pl
from jax.experimental.pallas import tpu as pltpu
from jax.sharding import PartitionSpec as P

HEADS = 16
BLOCK = 256
BF = jnp.bfloat16
F32 = jnp.float32
MESH = pl.DeviceIdType.MESH


def dot(a, b, ca, cb):
    return lax.dot_general(a, b, (((ca,), (cb,)), ((), ())), preferred_element_type=F32)


def swap_halves(x, half):
    lane = lax.broadcasted_iota(jnp.int32, x.shape, 1)
    width = x.shape[1]
    return jnp.where(
        lane % (2 * half) < half, pltpu.roll(x, width - half, 1), pltpu.roll(x, half, 1)
    )


def turn(x, cosine, sine, half, sign):
    parts = []
    for start in range(0, x.shape[1], 128):
        part = x[:, start : start + 128]
        other = swap_halves(part, half) * sine
        parts.append(part * cosine + other if sign > 0 else part * cosine - other)
    return jnp.concatenate(parts, axis=1)


def rotary_table(head_dim):
    half = head_dim // 2
    lane = jnp.arange(128)
    pair = lane % half
    rates = jnp.power(10000.0, -(pair // 3).astype(F32) / ((half + 2) // 3))
    row = jnp.arange(128)
    axis = row // 14
    value = (row % 14).astype(F32)
    live = (axis[:, None] == (pair % 3)[None, :]) & (row[:, None] < 42)
    angle = value[:, None] * rates[None, :]
    signs = jnp.where(lane % head_dim < half, -1.0, 1.0)
    return jnp.concatenate(
        [
            jnp.where(live, jnp.cos(angle), 0.0),
            jnp.where(live, jnp.sin(angle) * signs[None, :], 0.0),
        ],
        axis=1,
    )


def greet(targets):
    barrier = pltpu.get_barrier_semaphore()
    for target in targets:
        pl.semaphore_signal(barrier, inc=1, device_id=target, device_id_type=MESH)
    pl.semaphore_wait(barrier, len(targets))


def others(name, index, size):
    return [{name: lax.rem(index + d, size)} for d in range(1, size)]


class Copies:
    def __init__(self, send, recv):
        self.send, self.recv, self.all = send, recv, []

    def make(self, src, dst, **target):
        i = len(self.all)
        copy = pltpu.make_async_remote_copy(
            src_ref=src, dst_ref=dst, send_sem=self.send.at[i], recv_sem=self.recv.at[i],
            device_id=target, device_id_type=MESH,
        )
        self.all.append([copy, False])
        return i

    def launch(self, *indices):
        for i in indices:
            self.all[i][0].start()

    def start(self, src, dst, **target):
        i = self.make(src, dst, **target)
        self.launch(i)
        return i

    def arrived(self, i):
        if not self.all[i][1]:
            self.all[i][0].wait_recv()
            self.all[i][1] = True

    def finish(self):
        for i in range(len(self.all)):
            self.arrived(i)
        for copy, _ in self.all:
            copy.wait_send()


def rows_at(index, size):
    return pl.ds(pl.multiple_of(index * size, size), size)


def tail_kernel(
    wide, narrow, part, grad_proj, weight, tok, vec_in, normed_out, quarters_out, vec_out,
    partial, mate_in, cross_out, cross_in, near_in, far_out, far_in, shards, vec_box, sums, send, recv,
):
    w, n = lax.axis_index("wide"), lax.axis_index("narrow")
    column = wide // 2
    z, y = w // 2, lax.rem(w, 2)
    x, c = n // 2, lax.rem(n, 2)
    near, mate, cross = w + 1 - 2 * y, n + 1 - 2 * c, lax.rem(n + 2, narrow)
    wide_rows, group_rows = part.shape[0] // wide, normed_out.shape[0]
    towards = [lax.rem(z + d, column) for d in range(1, column + 1)]
    greet([{"wide": near}] + [{"wide": to * 2 + y} for to in towards[:-1]] + others("narrow", n, narrow))
    go = Copies(send, recv)
    first = [
        go.start(part.at[rows_at(towards[k] * 2 + 1 - y, wide_rows)], near_in.at[k], wide=near) for k in range(column)
    ]

    seconds, kept = [], []

    def relay(k):
        go.arrived(first[k])
        value = part[rows_at(towards[k] * 2 + y, wide_rows), :].astype(F32) + near_in[k].astype(F32)
        if k < column - 1:
            far_out[k] = value.astype(BF)
            seconds.append(go.start(far_out.at[k], far_in.at[k], wide=towards[k] * 2 + y))
        else:
            kept.append(value)

    sums[...] = jnp.zeros_like(sums)
    owners = [(1 - x) * 2 + 1 - c, (1 - x) * 2 + c, x * 2 + 1 - c, n]
    half = group_rows // 2
    mates, overs = [], []
    for slot, owner in enumerate(owners):

        def body(i, carry):
            at = pl.ds(pl.multiple_of(owner * group_rows + i * BLOCK, BLOCK), BLOCK)
            here = pl.ds(pl.multiple_of(i * BLOCK, BLOCK), BLOCK)
            grads = dot(grad_proj[at, :], weight[...], 1, 1)
            unit, _ = norm_parts(tok[at, :].astype(F32))
            sums[0:1, :] += jnp.sum(grads * unit, axis=0, keepdims=True)
            sums[1:2, :] += jnp.sum(grads, axis=0, keepdims=True)
            if slot < 3:
                partial[slot, here, :] = grads.astype(BF)
            else:
                normed_out[here, :] = grads
            return carry

        lax.fori_loop(0, group_rows // BLOCK, body, 0)
        if slot == 0:
            mates.append(go.start(partial.at[0], mate_in.at[0], narrow=mate))
        if slot == 2:
            mates.append(go.start(partial.at[2], mate_in.at[1], narrow=mate))
        if slot == 1:
            go.arrived(mates[0])
            for p in range(2):
                at = pl.ds(p * half, half)
                cross_out[at, :] = (partial[1, at, :].astype(F32) + mate_in[0, at, :].astype(F32)).astype(BF)
                overs.append(go.start(cross_out.at[at], cross_in.at[at], narrow=cross))
        for k in range(column * slot // 4, column * (slot + 1) // 4):
            if k < column - 1:
                relay(k)

    vec_box[pl.ds(n, 1)] = vec_in[...][None]
    vec_box[pl.ds(n, 1), 0:2, :] = sums[0:2, :][None]
    vecs = [go.start(vec_box.at[n], vec_box.at[n], narrow=lax.rem(n + d, narrow)) for d in range(1, narrow)]
    relay(column - 1)
    total = kept[0]
    for k in range(column - 1):
        go.arrived(seconds[k])
        total = total + far_in[k].astype(F32)
    shards[pl.ds(n, 1)] = total.astype(BF)[None]
    over = go.start(shards.at[n], shards.at[n], narrow=cross)
    go.start(shards.at[n], shards.at[n], narrow=mate)

    go.arrived(mates[1])
    for p in range(2):
        go.arrived(overs[p])
        at = pl.ds(p * half, half)
        normed_out[at, :] += mate_in[1, at, :].astype(F32) + cross_in[at, :].astype(F32)
    for i in vecs:
        go.arrived(i)
    group = vec_box[0]
    for i in range(1, narrow):
        group = group + vec_box[i]
    vec_out[...] = group

    go.arrived(over)
    go.start(shards.at[cross], shards.at[cross], narrow=mate)
    go.finish()
    quarters_out[...] = shards[...]


def tail_call(part, grad_proj, weight, tok, vec_in, wide, narrow):
    depth, cols = part.shape
    rows = tok.shape[0] // narrow
    wide_rows = depth // wide
    column = wide // 2
    copies = 2 * column - 1 + 2 + (narrow - 1) + 2 + 3
    vmem = pl.BlockSpec(memory_space=pltpu.VMEM)
    return pl.pallas_call(
        functools.partial(tail_kernel, wide, narrow),
        in_specs=[vmem] * 5,
        out_specs=[vmem] * 3,
        out_shape=[
            jax.ShapeDtypeStruct((rows, depth), F32),
            jax.ShapeDtypeStruct((narrow, wide_rows, cols), BF),
            jax.ShapeDtypeStruct(vec_in.shape, F32),
        ],
        scratch_shapes=[
            pltpu.VMEM((3, rows, depth), BF),
            pltpu.VMEM((2, rows, depth), BF),
            pltpu.VMEM((rows, depth), BF),
            pltpu.VMEM((rows, depth), BF),
            pltpu.VMEM((column, wide_rows, cols), BF),
            pltpu.VMEM((column - 1, wide_rows, cols), BF),
            pltpu.VMEM((column - 1, wide_rows, cols), BF),
            pltpu.VMEM((narrow, wide_rows, cols), BF),
            pltpu.VMEM((narrow,) + vec_in.shape, F32),
            pltpu.VMEM((8, depth), F32),
            pltpu.SemaphoreType.DMA((copies,)),
            pltpu.SemaphoreType.DMA((copies,)),
        ],
        compiler_params=pltpu.CompilerParams(
            collective_id=1, has_side_effects=True, vmem_limit_bytes=56 * 1024 * 1024
        ),
        name="tail",
    )(part, grad_proj, weight, tok, vec_in)


def norm_kernel(wide, slices, total_out, square_out, box, squares, send, recv):
    w = lax.axis_index("wide")
    greet(others("wide", w, wide))
    go = Copies(send, recv)
    peers = [lax.rem(w + d, wide) for d in range(1, wide)]
    for peer in peers:
        go.start(slices.at[peer], box.at[w], wide=peer)
    box[pl.ds(w, 1)] = slices[pl.ds(w, 1)]
    for i in range(wide - 1):
        go.arrived(i)
    total = box[0]
    for i in range(1, wide):
        total = total + box[i]
    total_out[...] = total
    row = lax.broadcasted_iota(jnp.int32, total.shape, 0)
    entries = jnp.where(row == 15, 0.0, total)
    entries = entries * entries
    squares[pl.ds(w, 1)] = (entries[:8] + entries[8:])[None]
    for peer in peers:
        go.start(squares.at[w], squares.at[w], wide=peer)
    go.finish()
    all_squares = squares[0]
    for i in range(1, wide):
        all_squares = all_squares + squares[i]
    square_out[...] = all_squares


def norm_call(slices, wide):
    vmem = pl.BlockSpec(memory_space=pltpu.VMEM)
    copies = 2 * (wide - 1)
    return pl.pallas_call(
        functools.partial(norm_kernel, wide),
        in_specs=[vmem],
        out_specs=[vmem] * 2,
        out_shape=[jax.ShapeDtypeStruct((16, 128), F32), jax.ShapeDtypeStruct((8, 128), F32)],
        scratch_shapes=[
            pltpu.VMEM((wide, 16, 128), F32),
            pltpu.VMEM((wide, 8, 128), F32),
            pltpu.SemaphoreType.DMA((copies,)),
            pltpu.SemaphoreType.DMA((copies,)),
        ],
        compiler_params=pltpu.CompilerParams(collective_id=2, has_side_effects=True),
        name="norm",
    )(slices)


CLIP = 784


def head_lanes(shape, head, head_dim):
    lane = lax.broadcasted_iota(jnp.int32, shape, 1)
    return lane // head_dim == head


def meeting(block, blocks):
    before, after = CLIP // BLOCK, -(-2 * CLIP // BLOCK)
    low = before * (block // after)
    high = blocks - (blocks - after) * (1 - jnp.minimum(block // before, 1))
    return low, high


def forward_kernel(
    heads, head_dim, wide, narrow,
    tok, vec, tag, table, qkv_f32, out_f32, up_f32, down_f32,
    q_ref, k_ref, v_ref, turn_ref, norm_ref, vec_ref, seg_ref, tag_ref, o_ref, lse_ref,
    tok_all, qkv_all, mixed_ref, out_all, up_all, down_all,
    vec_box, tag_box, tok_box, qkv_box, qkv_own, out_own, up_own, down_own, stage_qkv, stage_out, stage_up, stage_down,
    values_turned, acc, peak, total, o_box, send, recv, mix_send, mix_recv, local, leave,
):
    step = pl.program_id(0)
    rows, width = q_ref.shape
    depth = tok.shape[1]
    blocks = rows // BLOCK
    per = blocks // narrow
    final = 2 * blocks
    w, n = lax.axis_index("wide"), lax.axis_index("narrow")
    column = wide // 2
    z, y, side = w // 2, lax.rem(w, 2), lax.rem(n, 2)
    near, mate, cross = w + 1 - 2 * y, n + 1 - 2 * side, lax.rem(n + 2, narrow)
    source = lambda d: lax.rem(z - d + column, column) * 2 + y
    target = lambda d: lax.rem(z + d, column) * 2 + y
    beside = lambda d: lax.rem(z - d + column, column) * 2 + 1 - y
    wide_rows, out_half = out_own.shape
    half = up_own.shape[1]
    group_rows = tok.shape[0]

    loads = [
        pltpu.make_async_copy(
            qkv_f32.at[:, pl.ds(pl.multiple_of(i * depth + n * width, width), width)],
            stage_qkv.at[:, pl.ds(i * width, width)],
            local.at[i],
        )
        for i in range(3)
    ] + [
        pltpu.make_async_copy(
            whole.at[:, pl.ds(pl.multiple_of(side * size, size), size)], stage, local.at[3 + i]
        )
        for i, (whole, stage, size) in enumerate(
            [(out_f32, stage_out, out_half), (up_f32, stage_up, half), (down_f32, stage_down, half)]
        )
    ]

    go = Copies(send, recv)
    small = [go.make(vec, vec_box.at[w], wide=lax.rem(w + d, wide)) for d in range(1, wide)]
    small += [go.make(tag, tag_box.at[n], narrow=lax.rem(n + d, narrow)) for d in range(1, narrow)]
    pieces = 4
    piece = group_rows // pieces
    token_rows = lambda i, p: tok_box.at[rows_at(i * pieces + p, piece)]
    own_piece = lambda p: tok.at[pl.ds(p * piece, piece)]
    over = [go.make(own_piece(p), token_rows(n, p), narrow=cross) for p in range(pieces)]
    to_mate = [go.make(own_piece(p), token_rows(n, p), narrow=mate) for p in range(pieces)]
    passed = [go.make(token_rows(cross, p), token_rows(cross, p), narrow=mate) for p in range(pieces)]
    qkv_at = lambda i: qkv_box.at[rows_at(i, wide_rows)]
    qkv_far = [go.make(qkv_own, qkv_at(w), wide=target(d)) for d in range(1, column)]
    qkv_near = [go.make(qkv_own, qkv_at(w), wide=near)]
    qkv_near += [go.make(qkv_at(source(d)), qkv_at(source(d)), wide=near) for d in range(1, column)]

    at_step = [[] for _ in range(final + 2)]
    out_cols = pl.ds(pl.multiple_of(side * out_half, out_half), out_half)
    out_at = lambda i: out_all.at[rows_at(i, wide_rows), out_cols]
    out_near = [go.make(out_own, out_at(w), wide=near)]
    out_starts = [out_near[0], go.make(out_own, out_at(w), narrow=mate)]
    for d in range(1, column):
        out_starts.append(go.make(out_own, out_at(w), wide=target(d)))
        ref = out_at(source(d))
        out_near.append(go.make(ref, ref, wide=near))
        at_step[5].append((out_starts[-1], [out_near[-1], go.make(ref, ref, narrow=mate)]))
    for d in range(column):
        ref = out_at(beside(d))
        at_step[blocks + 2].append((out_near[d], [go.make(ref, ref, narrow=mate)]))

    quarter = half // 4
    shared = pl.ds(pl.multiple_of(n // 2 * quarter, quarter), quarter)
    both = pl.ds(2 * quarter, 2 * quarter)
    own_out = [pltpu.make_async_copy(out_own, out_at(w), leave.at[0])]

    def spread(own, result, steps, slot):
        starts = []
        for cols in (shared, both):
            piece_at = lambda i: result.at[rows_at(i, wide_rows), cols]
            passes = lambda i: [go.make(piece_at(i), piece_at(i), narrow=cross)] if cols is shared else []
            nears = [go.make(own.at[:, cols], piece_at(w), wide=near)]
            starts += nears
            if cols is shared:
                starts.append(go.make(own.at[:, cols], piece_at(w), narrow=cross))
            for d in range(1, column):
                starts.append(go.make(own.at[:, cols], piece_at(w), wide=target(d)))
                ref = piece_at(source(d))
                nears.append(go.make(ref, ref, wide=near))
                turn_at = steps[0] if cols is shared else steps[2] + (d - 1) * 2 // column
                at_step[min(turn_at, final + 1)].append((starts[-1], [nears[-1]] + passes(source(d))))
            if cols is shared:
                for d in range(column):
                    at_step[steps[1]].append((nears[d], passes(beside(d))))
            own_out.append(pltpu.make_async_copy(own.at[:, cols], piece_at(w), leave.at[slot + (cols is both)]))
        return starts

    up_starts = spread(up_own, up_all, (blocks + 1, blocks + 3, blocks + 4), 1)
    down_starts = spread(down_own, down_all, (final - 1, final + 1, final + 1), 3)

    mine = pl.ds(pl.multiple_of(n * width, width), width)

    def result(s):
        at = lax.rem((n + 1) * per + s, blocks)
        return pltpu.make_async_remote_copy(
            src_ref=o_box.at[rows_at(at, BLOCK)],
            dst_ref=mixed_ref.at[rows_at(lax.rem(s, per), BLOCK), mine],
            send_sem=mix_send.at[s],
            recv_sem=mix_recv.at[s],
            device_id={"narrow": lax.rem(n + 1 + s // per, narrow)},
            device_id_type=MESH,
        )

    def result_here(s):
        return pltpu.make_async_copy(
            o_box.at[rows_at(n * per + s, BLOCK)], mixed_ref.at[rows_at(s, BLOCK), mine], leave.at[7 + s]
        )

    kept = [
        pltpu.make_async_copy(tok_box, tok_all, leave.at[5]),
        pltpu.make_async_copy(qkv_box, qkv_all, leave.at[6]),
    ]

    @pl.when(step == 0)
    def _():
        for copy in loads:
            copy.start()
        greet(others("wide", w, wide) + others("narrow", n, narrow))
        go.launch(*small, *over)
        for copy in loads[:3]:
            copy.wait()
        qkv_own[...] = stage_qkv[...].astype(BF)
        go.launch(*qkv_far, qkv_near[0], *to_mate)
        for copy, stage, own, starts in zip(
            loads[3:],
            (stage_out, stage_up, stage_down),
            (out_own, up_own, down_own),
            (out_starts, up_starts, down_starts),
        ):
            copy.wait()
            own[...] = stage[...].astype(BF)
            go.launch(*starts)
        tok_box[rows_at(n, group_rows), :] = tok[...]
        qkv_box[rows_at(w, wide_rows), :] = qkv_own[...]
        vec_box[pl.ds(w, 1)] = vec[...][None]
        tag_box[pl.ds(n, 1)] = tag[...][None]
        for copy in own_out:
            copy.start()
        for i in small:
            go.arrived(i)
        cols = depth // wide
        for i in range(wide):
            vec_ref[:, i * cols : (i + 1) * cols] = vec_box[i].astype(F32)[:, :cols]
        for i in range(max(pieces, column - 1)):
            if i < column - 1:
                go.arrived(qkv_far[i])
                go.launch(qkv_near[i + 1])
            if i < pieces:
                go.arrived(over[i])
                go.launch(passed[i])
        for i in qkv_near + to_mate + passed:
            go.arrived(i)
        for copy in kept:
            copy.start()

    for i in range(1, final + 1):
        if at_step[i]:

            @pl.when(step == i)
            def _():
                for arrival, follow in at_step[i]:
                    go.arrived(arrival)
                    go.launch(*follow)

    @pl.when((step > 0) & (step <= blocks))
    def _():
        block = step - 1
        at = rows_at(block, BLOCK)
        marks = tag_box[pl.ds(block // per, 1), :, pl.ds(pl.multiple_of(lax.rem(block, per) * BLOCK, BLOCK), BLOCK)]
        marks = marks[0].astype(F32)
        seg_ref[pl.ds(block, 1)] = marks[0:1][None]
        marks = marks.T
        tag_ref[at, :] = jnp.where(marks[:, 1:2] == 1.0, marks[:, 0:1], -1.0)
        slot = lax.broadcasted_iota(jnp.int32, (BLOCK, 128), 1).astype(F32)
        spot = (slot == marks[:, 2:3]) | (slot == 14 + marks[:, 3:4]) | (slot == 28 + marks[:, 4:5])
        angles = lax.dot_general(
            jnp.where(spot, 1.0, 0.0),
            table[...],
            (((1,), (0,)), ((), ())),
            precision=lax.Precision.HIGHEST,
            preferred_element_type=F32,
        )
        turn_ref[at, :] = angles
        cosine, sine = angles[:, :128], angles[:, 128:]
        unit, _ = norm_parts(tok_box[at, :].astype(F32))
        normed = (unit * vec_ref[0:1, :] + vec_ref[1:2, :]).astype(BF)
        norm_ref[...] = normed
        proj = dot(normed, qkv_box[...], 1, 0)
        parts = [proj[:, i * width : (i + 1) * width] + vec_ref[2 + i : 3 + i, mine] for i in range(3)]
        q_ref[at, :] = turn(parts[0], cosine, sine, head_dim // 2, 1).astype(BF)
        k_ref[at, :] = turn(parts[1], cosine, sine, head_dim // 2, 1).astype(BF)
        v_ref[at, :] = parts[2].astype(BF)
        values_turned[:, at] = parts[2].T.astype(BF)

    @pl.when(step > blocks)
    def _():
        place = step - blocks - 1
        block = lax.rem((n + 1) * per + place, blocks)
        at = rows_at(block, BLOCK)
        query = q_ref[at, :] * jnp.asarray(head_dim**-0.5, BF)
        seg = seg_ref[pl.ds(block, 1)][0]
        masked_query = [
            jnp.where(head_lanes(query.shape, h, head_dim), query, jnp.zeros_like(query)) for h in range(heads)
        ]
        acc[...] = jnp.zeros_like(acc)
        peak[...] = jnp.full_like(peak, -1e30)
        total[...] = jnp.zeros_like(total)

        def body(j, carry):
            start = pl.multiple_of(j * BLOCK, BLOCK)
            key = k_ref[pl.ds(start, BLOCK), :]
            allowed = tag_ref[pl.ds(start, BLOCK), :] == seg
            scores = [jnp.where(allowed, dot(key, masked_query[h], 1, 1), -1e30) for h in range(heads)]
            for h in range(heads):
                lines = slice(h * head_dim, (h + 1) * head_dim)
                old = peak[h : h + 1, :]
                new = jnp.maximum(old, jnp.max(scores[h], axis=0, keepdims=True))
                probs = jnp.exp(scores[h] - new)
                keep = jnp.exp(old - new)
                peak[h : h + 1, :] = new
                total[h : h + 1, :] = total[h : h + 1, :] * keep + jnp.sum(probs, axis=0, keepdims=True)
                value = values_turned[lines, pl.ds(start, BLOCK)]
                acc[lines, :] = acc[lines, :] * keep + dot(value, probs.astype(BF), 1, 0)
            return carry

        low, high = meeting(block, blocks)
        lax.fori_loop(low, high, body, 0)
        parts = [acc[h * head_dim : (h + 1) * head_dim, :] / total[h : h + 1, :] for h in range(heads)]
        out = jnp.concatenate(parts, axis=0).T.astype(BF)
        o_ref[at, :] = out
        o_box[at, :] = out
        lse_ref[pl.ds(block, 1)] = (peak[...] + jnp.log(jnp.maximum(total[...], 1e-30)))[None]

        @pl.when(place < blocks - per)
        def _():
            result(place).start()

    @pl.when(step == final)
    def _():
        for s in range(per):
            result_here(s).start()
        for arrival, follow in at_step[final + 1]:
            go.arrived(arrival)
            go.launch(*follow)
        for copy in own_out + kept:
            copy.wait()
        for s in range(blocks - per):
            result(s).wait()
        for s in range(per):
            result_here(s).wait()
        go.finish()


def forward_call(tok, vec, tag, table, weights, head_dim, wide, narrow):
    qkv, out, up, down = weights
    group_rows, depth = tok.shape
    rows = group_rows * narrow
    width = depth // narrow
    heads = width // head_dim
    blocks = rows // BLOCK
    column = wide // 2
    size = qkv.shape[0]
    half = up.shape[1] // 2
    copies = (wide - 1) + (narrow - 1) + 12 + (2 * column - 1)
    copies += 2 + 3 * (column - 1) + column + 2 * (2 * (2 * column - 1) + 2 * column)
    whole = lambda a: pl.BlockSpec(a.shape, lambda i: (0,) * len(a.shape), pipeline_mode=pl.Buffered(1))
    anywhere = pl.BlockSpec(memory_space=pl.ANY)
    shaped = jax.ShapeDtypeStruct
    head_rows = shaped((rows, width), BF)
    inside = [
        head_rows, head_rows, head_rows, shaped((rows, 256), F32), shaped((rows, depth), BF), shaped((16, depth), F32),
        shaped((blocks, 1, BLOCK), F32), shaped((rows, 1), F32), head_rows, shaped((blocks, 8, BLOCK), F32),
    ]
    inside_specs = [whole(a) for a in inside]
    inside_specs[4] = pl.BlockSpec((BLOCK, depth), lambda i: (jnp.minimum(jnp.maximum(i - 1, 0), blocks - 1), 0))
    outside = [
        shaped((rows, depth), BF), shaped((depth, 3 * width), BF), shaped((group_rows, depth), BF),
        shaped((depth, depth), BF), shaped((depth, half), BF), shaped((depth, half), BF),
    ]
    small = [(size, 3 * width), (size, depth // 2), (size, half), (size, half)]
    return pl.pallas_call(
        functools.partial(forward_kernel, heads, head_dim, wide, narrow),
        grid=(2 * blocks + 1,),
        in_specs=[whole(a) for a in (tok, vec, tag, table)] + [anywhere] * 4,
        out_specs=inside_specs + [anywhere] * 6,
        out_shape=inside + outside,
        scratch_shapes=[
            pltpu.VMEM((wide,) + vec.shape, BF),
            pltpu.VMEM((narrow,) + tag.shape, jnp.int32),
            pltpu.VMEM((rows, depth), BF),
            pltpu.VMEM((depth, 3 * width), BF),
        ]
        + [pltpu.VMEM(shape, BF) for shape in small]
        + [pltpu.VMEM(shape, F32) for shape in small]
        + [
            pltpu.VMEM((width, rows), BF),
            pltpu.VMEM((width, BLOCK), F32),
            pltpu.VMEM((8, BLOCK), F32),
            pltpu.VMEM((8, BLOCK), F32),
            pltpu.VMEM((rows, width), BF),
            pltpu.SemaphoreType.DMA((copies,)),
            pltpu.SemaphoreType.DMA((copies,)),
            pltpu.SemaphoreType.DMA((blocks,)),
            pltpu.SemaphoreType.DMA((blocks,)),
            pltpu.SemaphoreType.DMA((6,)),
            pltpu.SemaphoreType.DMA((7 + blocks // narrow,)),
        ],
        compiler_params=pltpu.CompilerParams(
            collective_id=3, has_side_effects=True, vmem_limit_bytes=48 * 1024 * 1024
        ),
        cost_estimate=pl.CostEstimate(
            flops=heads * rows * rows * width * 4, bytes_accessed=rows * width * 8, transcendentals=heads * rows * rows
        ),
        name="attention_forward",
    )(tok, vec, tag, table, qkv, out, up, down)


class Scatter:
    def __init__(self, go, wide, narrow, split, part, near_in, own, far_out, far_in, box, local, *extra):
        w, self.n = lax.axis_index("wide"), lax.axis_index("narrow")
        self.go, self.column, self.split = go, wide // 2, split
        self.near_in, self.own, self.far_out, self.far_in, self.box = near_in, own, far_out, far_in, box
        z, y, x = w // 2, lax.rem(w, 2), self.n // 2
        near, mate, cross = w + 1 - 2 * y, self.n + 1 - 2 * lax.rem(self.n, 2), lax.rem(self.n + 2, narrow)
        size, cols = part.shape[0] // wide, box.shape[2]
        towards = [lax.rem(z + d, self.column) for d in range(1, self.column + 1)]
        theirs, ours = [to * 2 + 1 - y for to in towards], [to * 2 + y for to in towards]
        here = pl.ds(pl.multiple_of(x * cols, cols), cols) if split else pl.ds(0, cols)
        self.loads = [
            pltpu.make_async_copy(part.at[rows_at(i, size), here], own.at[k], local.at[k])
            for k, i in enumerate(ours + theirs if split else ours)
        ]
        self.zero = []
        if split:
            self.cross_in, self.out = extra
            there = pl.ds(pl.multiple_of((1 - x) * cols, cols), cols)
            order = list(enumerate(ours + theirs))
            order = order[self.column :] + order[: self.column]
            self.zero = {
                k: go.make(part.at[rows_at(i, size), there], self.cross_in.at[k], narrow=cross) for k, i in order
            }
        self.first = [
            go.make(self.out.at[k] if split else part.at[rows_at(i, size)], near_in.at[k], wide=near)
            for k, i in enumerate(theirs)
        ]
        self.second = [go.make(far_out.at[k], far_in.at[k], wide=i) for k, i in enumerate(ours[:-1])]
        self.over = go.make(box.at[self.n], box.at[self.n], narrow=cross)
        self.beside = go.make(box.at[self.n], box.at[self.n], narrow=mate)
        self.passed = go.make(box.at[cross], box.at[cross], narrow=mate)

    def load(self):
        for copy in self.loads:
            copy.start()
        if self.split:
            self.go.launch(*self.zero.values())

    def summed(self, k):
        self.loads[k].wait()
        value = self.own[k].astype(F32)
        if self.split:
            self.go.arrived(self.zero[k])
            value = value + self.cross_in[k].astype(F32)
        return value

    def send(self, k):
        if self.split:
            self.out[k] = self.summed(self.column + k).astype(BF)
        self.go.launch(self.first[k])

    def relay(self, k):
        self.go.arrived(self.first[k])
        if k < self.column - 1:
            self.far_out[k] = (self.summed(k) + self.near_in[k].astype(F32)).astype(BF)
            self.go.launch(self.second[k])

    def total(self):
        value = self.summed(self.column - 1) + self.near_in[self.column - 1].astype(F32)
        for k in range(self.column - 1):
            self.go.arrived(self.second[k])
            value = value + self.far_in[k].astype(F32)
        self.box[pl.ds(self.n, 1)] = value.astype(BF)[None]
        self.go.launch(self.over, self.beside)

    def share(self):
        self.go.arrived(self.over)
        self.go.launch(self.passed)

    @staticmethod
    def copies(wide, split):
        return 2 * (wide // 2) - 1 + 3 + (wide if split else 0)

    @staticmethod
    def scratch(wide, narrow, rows, cols, split):
        column, size = wide // 2, rows // wide
        cols = cols // 2 if split else cols
        many = wide if split else column
        sizes = [column, many, column - 1, column - 1, narrow]
        first = [pltpu.VMEM((count, size, cols), BF) for count in sizes] + [pltpu.SemaphoreType.DMA((many,))]
        return first + ([pltpu.VMEM((count, size, cols), BF) for count in (wide, column)] if split else [])


def backward_kernel(
    heads, head_dim, wide, narrow,
    q_ref, k_ref, v_ref, o_ref, g_ref, lse_ref, seg_ref, tag_ref, turn_ref, part_out, part_down, part_up,
    grads_out, shards_out, shards_down, shards_up,
    q_heads, g_heads, delta, grad_query, send, recv, *boxes,
):
    step = pl.program_id(0)
    rows, width = q_ref.shape
    blocks = rows // BLOCK
    last = blocks - 1
    scale = head_dim**-0.5
    half = head_dim // 2
    go = Copies(send, recv)
    column = wide // 2
    outs = Scatter(go, wide, narrow, False, part_out, *boxes[:6])
    ups = Scatter(go, wide, narrow, False, part_up, *boxes[6:12])
    downs = Scatter(go, wide, narrow, True, part_down, *boxes[12:])

    @pl.when(step == 0)
    def _():
        w, n = lax.axis_index("wide"), lax.axis_index("narrow")
        z, y = w // 2, lax.rem(w, 2)
        greet(
            [{"wide": w + 1 - 2 * y}]
            + [{"wide": lax.rem(z + d, column) * 2 + y} for d in range(1, column)]
            + [{"narrow": n + 1 - 2 * lax.rem(n, 2)}, {"narrow": lax.rem(n + 2, narrow)}]
        )
        downs.load()
        outs.load()
        ups.load()
        for k in range(column):
            outs.send(k)
        for k in range(column // 4):
            ups.send(k)

    quarter = lambda i: range(column * i // 4, column * (i + 1) // 4)
    plan = [
        [(outs.relay, range(column)), (ups.send, quarter(1))],
        [(ups.relay, quarter(0)), (downs.send, range(column // 2)), (ups.send, quarter(2))],
        [(ups.relay, quarter(1)), (downs.send, range(column // 2, column)), (ups.send, quarter(3))],
        [(ups.relay, quarter(2)), (outs.total, None)],
        [(ups.relay, quarter(3)), (downs.relay, range(column // 2)), (outs.share, None)],
        [(downs.relay, range(column // 2, column))],
        [(ups.total, None)],
    ]
    actions = [[] for _ in range(last)]
    for i, entries in enumerate(plan):
        for action, ks in entries:
            actions[min(i, last - 1)] += [action] if ks is None else [functools.partial(action, k) for k in ks]
    for i in range(last):
        if actions[i]:

            @pl.when(step == i + 1)
            def _():
                for action in actions[i]:
                    action()

    @pl.when(step == 0)
    def _():
        grad_query[...] = jnp.zeros_like(grad_query)
        row = lax.broadcasted_iota(jnp.int32, (8, width), 0)
        lane = lax.broadcasted_iota(jnp.int32, (8, width), 1)
        pick = jnp.where(lane // head_dim == row, 1.0, 0.0)

        def prepare(i, carry):
            at = pl.ds(pl.multiple_of(i * BLOCK, BLOCK), BLOCK)
            query = q_ref[at, :] * jnp.asarray(scale, BF)
            grad = g_ref[at, :]
            for h in range(heads):
                lanes = head_lanes(query.shape, h, head_dim)
                q_heads[h, at, :] = jnp.where(lanes, query, jnp.zeros_like(query))
                g_heads[h, at, :] = jnp.where(lanes, grad, jnp.zeros_like(grad))
            product = grad.astype(F32) * o_ref[at, :].astype(F32)
            delta[pl.ds(i, 1)] = lax.dot_general(
                pick,
                product,
                (((1,), (1,)), ((), ())),
                precision=lax.Precision.HIGHEST,
                preferred_element_type=F32,
            )[None]
            return carry

        lax.fori_loop(0, blocks, prepare, 0)

    key = k_ref[...]
    value = v_ref[...]
    tag = tag_ref[...]
    masked_key = [jnp.where(head_lanes(key.shape, h, head_dim), key, jnp.zeros_like(key)) for h in range(heads)]

    def body(i, carry):
        grad_key, grad_value = carry
        at = pl.ds(pl.multiple_of(i * BLOCK, BLOCK), BLOCK)
        allowed = tag == seg_ref[pl.ds(i, 1), :]
        lse = lse_ref[pl.ds(i, 1)][0]
        dlt = delta[pl.ds(i, 1)][0]
        total = None
        for h in range(heads):
            query = q_heads[h, at, :]
            grad = g_heads[h, at, :]
            scores = dot(key, query, 1, 1)
            probs = jnp.where(allowed, jnp.exp(scores - lse[h : h + 1, :]), 0.0)
            grad_probs = dot(value, grad, 1, 1)
            grad_scores = (probs * (grad_probs - dlt[h : h + 1, :])).astype(BF)
            grad_value = grad_value + dot(probs.astype(BF), grad, 1, 0)
            grad_key = grad_key + dot(grad_scores, query, 1, 0)
            term = dot(grad_scores, masked_key[h], 0, 0)
            total = term if total is None else total + term
        grad_query[at, :] += total
        return grad_key, grad_value

    zero = jnp.zeros((BLOCK, width), F32)
    low, high = meeting(step, blocks)
    grad_key, grad_value = lax.fori_loop(low, high, body, (zero, zero))
    here = pl.ds(pl.multiple_of(step * BLOCK, BLOCK), BLOCK)
    cosine, sine = turn_ref[here, :128], turn_ref[here, 128:]
    grads_out[here, width : 2 * width] = turn(grad_key, cosine, sine, half, -1).astype(BF)
    grads_out[here, 2 * width :] = grad_value.astype(BF)

    @pl.when(step == last)
    def _():
        ups.share()
        downs.total()

        def finish(i, carry):
            at = pl.ds(pl.multiple_of(i * BLOCK, BLOCK), BLOCK)
            grads = grad_query[at, :] * scale
            grads_out[at, :width] = turn(grads, turn_ref[at, :128], turn_ref[at, 128:], half, -1).astype(BF)
            return carry

        lax.fori_loop(0, blocks, finish, 0)
        downs.share()
        go.finish()
        shards_out[...] = outs.box[...]
        shards_down[...] = downs.box[...]
        shards_up[...] = ups.box[...]


def backward_call(q, k, v, o, g, lse, seg_rows, tag_col, turns, part_out, part_down, part_up, head_dim, wide, narrow):
    rows, width = q.shape
    heads = width // head_dim
    blocks = rows // BLOCK
    whole = lambda a: pl.BlockSpec(a.shape, lambda i: (0,) * len(a.shape), pipeline_mode=pl.Buffered(1))
    block = pl.BlockSpec((BLOCK, width), lambda i: (i, 0))
    anywhere = pl.BlockSpec(memory_space=pl.ANY)
    depth = part_up.shape[0]
    results = [
        jax.ShapeDtypeStruct((rows, 3 * width), BF),
        jax.ShapeDtypeStruct((narrow, depth // wide, part_out.shape[1]), BF),
        jax.ShapeDtypeStruct((narrow, depth // wide, part_down.shape[1] // 2), BF),
        jax.ShapeDtypeStruct((narrow, depth // wide, part_up.shape[1]), BF),
    ]
    copies = 2 * Scatter.copies(wide, False) + Scatter.copies(wide, True)
    return pl.pallas_call(
        functools.partial(backward_kernel, heads, head_dim, wide, narrow),
        grid=(blocks,),
        in_specs=[
            whole(q), block, block, whole(o), whole(g), whole(lse), whole(seg_rows),
            pl.BlockSpec((BLOCK, 1), lambda i: (i, 0)),
            whole(turns), anywhere, anywhere, anywhere,
        ],
        out_specs=[whole(a) for a in results],
        out_shape=results,
        scratch_shapes=[
            pltpu.VMEM((heads, rows, width), BF),
            pltpu.VMEM((heads, rows, width), BF),
            pltpu.VMEM((blocks, 8, BLOCK), F32),
            pltpu.VMEM((rows, width), F32),
            pltpu.SemaphoreType.DMA((copies,)),
            pltpu.SemaphoreType.DMA((copies,)),
        ]
        + Scatter.scratch(wide, narrow, depth, part_out.shape[1], False)
        + Scatter.scratch(wide, narrow, depth, part_up.shape[1], False)
        + Scatter.scratch(wide, narrow, depth, part_down.shape[1], True),
        compiler_params=pltpu.CompilerParams(
            collective_id=4, has_side_effects=True, vmem_limit_bytes=60 * 1024 * 1024
        ),
        cost_estimate=pl.CostEstimate(
            flops=heads * rows * rows * width * 7, bytes_accessed=rows * width * 20, transcendentals=heads * rows * rows
        ),
        name="attention_backward",
    )(q, k, v, o, g, lse, seg_rows, tag_col, turns, part_out, part_down, part_up)


def norm_parts(values):
    center = values - jnp.mean(values, axis=-1, keepdims=True)
    inverse = lax.rsqrt(jnp.mean(center * center, axis=-1, keepdims=True) + 1e-06)
    return center * inverse, inverse


def norm_back(grads, gain, unit, inverse):
    scaled = grads * gain
    return inverse * (
        scaled - jnp.mean(scaled, axis=-1, keepdims=True) - unit * jnp.mean(scaled * unit, axis=-1, keepdims=True)
    )


def adamw(param, grad, first, second, clip, rate, decay, fix_first, fix_second):
    clipped = grad * clip
    moment = 0.9 * first + 0.1 * clipped
    square = 0.999 * second + 0.001 * clipped * clipped
    direction = moment / fix_first / (jnp.sqrt(square / fix_second) + 1e-08)
    return (param - rate * (direction + decay * param), moment, square)


def on_device(
    tokens, cotangent, segment_ids, key_keep, patch_coords, step_count,
    weight_qkv, weight_out, weight_up, weight_down, vectors,
    first_qkv, first_out, first_up, first_down, first_vectors,
    second_qkv, second_out, second_up, second_down, second_vectors,
):
    rows, width = tokens.shape
    hidden = weight_up.shape[1]
    head_dim = width // HEADS
    narrow = lax.axis_size("narrow")
    wide = lax.axis_size("wide")
    shard_rows = width // wide
    me = lax.axis_index("narrow")
    side = me % 2
    mine = width // narrow
    half_hidden = hidden // 2
    group = rows * narrow

    def mate(value):
        return lax.ppermute(value, "narrow", [(i, i ^ 1) for i in range(narrow)])

    def across(value):
        return lax.ppermute(value, "narrow", [(i, i ^ 2) for i in range(narrow)])

    def take(value, start, size, axis=1):
        return lax.dynamic_slice_in_dim(value, start, size, axis)

    shard_cols = vectors.shape[1]
    vec_shard = jnp.pad(vectors.astype(BF), ((0, 16 - vectors.shape[0]), (0, -shard_cols % 128)))
    tag = jnp.concatenate([segment_ids[None], key_keep[None], patch_coords, patch_coords], axis=0)
    (
        query, keys, values, turns, normed1_all, vec, seg_rows, tag_col, mixed_mine, lse,
        tokens_all, qkv_w, mixed, out_w, up_w, down_w,
    ) = forward_call(
        tokens, vec_shard, tag, rotary_table(head_dim), (weight_qkv, weight_out, weight_up, weight_down),
        head_dim, wide, narrow,
    )
    vec = vec[: vectors.shape[0]]
    xin = tokens.astype(F32)
    unit1, inverse1 = norm_parts(xin)
    cot_pair = jnp.concatenate([cotangent, mate(cotangent)], axis=0)

    resid = xin + (dot(mixed, out_w, 1, 0) + vec[5])
    unit2, inverse2 = norm_parts(resid)
    normed2 = (unit2 * vec[6] + vec[7]).astype(BF)
    normed2_pair = jnp.concatenate([normed2, mate(normed2)], axis=0)
    up_bias = take(vec[9:].reshape(1, -1), side * half_hidden, half_hidden)
    up_pre = dot(normed2_pair, up_w, 1, 0) + up_bias
    erf_part = 0.5 * (1.0 + lax.erf(up_pre * (0.5**0.5)))
    act = (up_pre * erf_part).astype(BF)
    slope = erf_part + up_pre * (jnp.exp(-0.5 * up_pre * up_pre) * ((2.0 * jnp.pi) ** -0.5))
    down_part = dot(act, down_w, 1, 1)
    down = down_part[:rows] + mate(down_part[rows:])
    layer_out = (resid + (down + vec[8])).astype(BF)

    part_down = dot(cot_pair, act, 0, 0).astype(BF)
    grad_up_act = (dot(cot_pair, down_w, 1, 0) * slope).astype(BF)
    part_up = dot(normed2_pair, grad_up_act, 0, 0).astype(BF)
    grad_normed2_part = dot(grad_up_act, up_w, 1, 1)
    grad_normed2 = grad_normed2_part[:rows] + mate(grad_normed2_part[rows:])
    cot = cotangent.astype(F32)
    grad_resid = cot + norm_back(grad_normed2, vec[6], unit2, inverse2)
    grad_branch = grad_resid.astype(BF)
    grad_mixed = dot(grad_branch, out_w, 1, 1).astype(BF)
    part_out = dot(mixed, grad_branch, 0, 0)
    own_out = take(part_out, side * (width // 2), width // 2)
    other_out = take(part_out, (1 - side) * (width // 2), width // 2)
    part_out = (own_out + mate(other_out.astype(BF)).astype(F32)).astype(BF)

    grad_mixed_mine = lax.all_to_all(grad_mixed, "narrow", 1, 0, tiled=True)
    grad_proj, shards_out, shards_down, shards_up = backward_call(
        query, keys, values, mixed_mine, grad_mixed_mine, lse, seg_rows[:, 0], tag_col, turns, part_out, part_down, part_up, head_dim, wide, narrow,
    )
    part_qkv = dot(normed1_all, grad_proj, 0, 0).astype(BF)

    proj_sums = jnp.sum(grad_proj.astype(F32), axis=0).reshape(3, mine)
    proj_rows = lax.dynamic_update_slice(jnp.zeros((3, width), F32), proj_sums, (0, me * mine))
    up_sums = jnp.sum(grad_up_act.astype(F32), axis=0)
    up_rows = lax.dynamic_update_slice(jnp.zeros((hidden,), F32), up_sums, (side * half_hidden,))
    vector_part = jnp.concatenate(
        [
            jnp.zeros((2, width), F32),
            proj_rows,
            jnp.sum(grad_branch.astype(F32), axis=0)[None],
            jnp.sum(grad_normed2 * unit2, axis=0)[None],
            jnp.sum(grad_normed2, axis=0)[None],
            jnp.sum(cot, axis=0)[None],
            up_rows.reshape(hidden // width, width),
            jnp.zeros((16 - vectors.shape[0], width), F32),
        ],
        axis=0,
    )
    grad_normed1, quarters, vector_group = tail_call(
        part_qkv, grad_proj, qkv_w, tokens_all, vector_part, wide, narrow
    )
    grad_tokens = (grad_resid + norm_back(grad_normed1, vec[0], unit1, inverse1)).astype(BF)

    def join(shards):
        shards = shards.astype(F32)
        return jnp.concatenate([shards[0] + shards[2], shards[1] + shards[3]], axis=1)

    total_up = join(shards_up)
    total_down = jnp.concatenate([shards_down[i] for i in (0, 2, 1, 3)], axis=1).astype(F32)
    total_out = join(shards_out)
    total_qkv = jnp.concatenate(
        [quarters[i, :, j * mine : (j + 1) * mine] for j in range(3) for i in range(narrow)], axis=1
    ).astype(F32)

    squares = sum(jnp.sum(g * g) for g in (total_qkv, total_out, total_up, total_down))
    slices = jnp.moveaxis(vector_group.reshape(16, wide, shard_rows), 1, 0)
    slices = jnp.pad(slices, ((0, 0), (0, 0), (0, -shard_rows % 128)))
    place = (jnp.arange(16)[:, None] == 15) & (jnp.arange(slices.shape[2])[None, :] == 0)
    slices = jnp.where(place[None], squares, slices)
    vector_total, vector_squares = norm_call(slices, wide)
    grad_norm = jnp.sqrt(vector_total[15, 0] + jnp.sum(vector_squares))
    clip = 1.0 / jnp.maximum(grad_norm, 1.0)
    count = step_count[0].astype(F32)
    rate = 0.4 * count / (count + 4.0)
    decay = 0.04 + 0.018 * count
    fix_first = 1.0 - jnp.power(0.9, count)
    fix_second = 1.0 - jnp.power(0.999, count)
    grad_vectors = vector_total[: vectors.shape[0], :shard_rows]

    def update(param, grad, first, second, decay_here):
        return adamw(param, grad, first, second, clip, rate, decay_here, fix_first, fix_second)

    new_qkv = update(weight_qkv, total_qkv, first_qkv, second_qkv, decay)
    new_out = update(weight_out, total_out, first_out, second_out, decay)
    new_up = update(weight_up, total_up, first_up, second_up, decay)
    new_down = update(weight_down, total_down, first_down, second_down, decay)
    new_vectors = update(vectors, grad_vectors, first_vectors, second_vectors, 0.0)
    news = (new_qkv, new_out, new_up, new_down, new_vectors)
    return (layer_out, grad_tokens) + tuple(n[i] for i in range(3) for n in news) + (grad_norm, grad_vectors[8])


def solution(mesh):
    by_token = P(("wide", "narrow"), None)
    ids = P(("wide", "narrow"))
    by_row = P("wide", None)
    by_column = P(None, "wide")
    params = (by_row,) * 4 + (by_column,)
    return jax.shard_map(
        on_device,
        mesh=mesh,
        in_specs=(by_token, by_token, ids, ids, P(None, ("wide", "narrow")), P()) + params * 3,
        out_specs=(by_token, by_token) + params * 3 + (P(), P("wide")),
        check_vma=False,
    )
```

```python
import functools

import jax
import jax.numpy as jnp
from jax import lax
from jax.experimental import pallas as pl
from jax.experimental.pallas import tpu as pltpu
from jax.sharding import PartitionSpec as P

HEADS = 16
BLOCK = 256
BF = jnp.bfloat16
F32 = jnp.float32
MESH = pl.DeviceIdType.MESH


def dot(a, b, ca, cb):
    return lax.dot_general(a, b, (((ca,), (cb,)), ((), ())), preferred_element_type=F32)


def swap_halves(x, half):
    lane = lax.broadcasted_iota(jnp.int32, x.shape, 1)
    width = x.shape[1]
    return jnp.where(
        lane % (2 * half) < half, pltpu.roll(x, width - half, 1), pltpu.roll(x, half, 1)
    )


def turn(x, cosine, sine, half, sign):
    parts = []
    for start in range(0, x.shape[1], 128):
        part = x[:, start : start + 128]
        other = swap_halves(part, half) * sine
        parts.append(part * cosine + other if sign > 0 else part * cosine - other)
    return jnp.concatenate(parts, axis=1)


def rotary_table(head_dim):
    half = head_dim // 2
    lane = jnp.arange(128)
    pair = lane % half
    rates = jnp.power(10000.0, -(pair // 3).astype(F32) / ((half + 2) // 3))
    row = jnp.arange(128)
    axis = row // 14
    value = (row % 14).astype(F32)
    live = (axis[:, None] == (pair % 3)[None, :]) & (row[:, None] < 42)
    angle = value[:, None] * rates[None, :]
    signs = jnp.where(lane % head_dim < half, -1.0, 1.0)
    return jnp.concatenate(
        [
            jnp.where(live, jnp.cos(angle), 0.0),
            jnp.where(live, jnp.sin(angle) * signs[None, :], 0.0),
        ],
        axis=1,
    )


def greet(targets):
    barrier = pltpu.get_barrier_semaphore()
    for target in targets:
        pl.semaphore_signal(barrier, inc=1, device_id=target, device_id_type=MESH)
    pl.semaphore_wait(barrier, len(targets))


def others(name, index, size):
    return [{name: lax.rem(index + d, size)} for d in range(1, size)]


class Copies:
    def __init__(self, send, recv):
        self.send, self.recv, self.all = send, recv, []

    def make(self, src, dst, **target):
        i = len(self.all)
        copy = pltpu.make_async_remote_copy(
            src_ref=src, dst_ref=dst, send_sem=self.send.at[i], recv_sem=self.recv.at[i],
            device_id=target, device_id_type=MESH,
        )
        self.all.append([copy, False])
        return i

    def launch(self, *indices):
        for i in indices:
            self.all[i][0].start()

    def start(self, src, dst, **target):
        i = self.make(src, dst, **target)
        self.launch(i)
        return i

    def arrived(self, i):
        if not self.all[i][1]:
            self.all[i][0].wait_recv()
            self.all[i][1] = True

    def finish(self):
        for i in range(len(self.all)):
            self.arrived(i)
        for copy, _ in self.all:
            copy.wait_send()


def rows_at(index, size):
    return pl.ds(pl.multiple_of(index * size, size), size)


def tail_kernel(
    wide, narrow, part, grad_proj, weight, tok, vec_in, squares_in, normed_out, qkv_out, vec_out, square_out,
    partial, mate_in, cross_out, cross_in, near_in, far_out, far_in, shards, vec_box, sums,
    slices, slice_box, square_box, send, recv,
):
    w, n = lax.axis_index("wide"), lax.axis_index("narrow")
    column = wide // 2
    z, y = w // 2, lax.rem(w, 2)
    x, c = n // 2, lax.rem(n, 2)
    near, mate, cross = w + 1 - 2 * y, n + 1 - 2 * c, lax.rem(n + 2, narrow)
    wide_rows, group_rows = part.shape[0] // wide, normed_out.shape[0]
    towards = [lax.rem(z + d, column) for d in range(1, column + 1)]
    greet(others("wide", w, wide) + others("narrow", n, narrow))
    go = Copies(send, recv)
    first = [
        go.start(part.at[rows_at(towards[k] * 2 + 1 - y, wide_rows)], near_in.at[k], wide=near) for k in range(column)
    ]

    seconds, kept = [], []

    def relay(k):
        go.arrived(first[k])
        value = part[rows_at(towards[k] * 2 + y, wide_rows), :].astype(F32) + near_in[k].astype(F32)
        if k < column - 1:
            far_out[k] = value.astype(BF)
            seconds.append(go.start(far_out.at[k], far_in.at[k], wide=towards[k] * 2 + y))
        else:
            kept.append(value)

    sums[...] = jnp.zeros_like(sums)
    owners = [(1 - x) * 2 + 1 - c, (1 - x) * 2 + c, x * 2 + 1 - c, n]
    half = group_rows // 2
    mates, overs = [], []
    for slot, owner in enumerate(owners):

        def body(i, carry):
            at = pl.ds(pl.multiple_of(owner * group_rows + i * BLOCK, BLOCK), BLOCK)
            here = pl.ds(pl.multiple_of(i * BLOCK, BLOCK), BLOCK)
            grads = dot(grad_proj[at, :], weight[...], 1, 1)
            unit, _ = norm_parts(tok[at, :].astype(F32))
            sums[0:1, :] += jnp.sum(grads * unit, axis=0, keepdims=True)
            sums[1:2, :] += jnp.sum(grads, axis=0, keepdims=True)
            if slot < 3:
                partial[slot, here, :] = grads.astype(BF)
            else:
                normed_out[here, :] = grads
            return carry

        lax.fori_loop(0, group_rows // BLOCK, body, 0)
        if slot == 0:
            mates.append(go.start(partial.at[0], mate_in.at[0], narrow=mate))
        if slot == 2:
            mates.append(go.start(partial.at[2], mate_in.at[1], narrow=mate))
        if slot == 1:
            go.arrived(mates[0])
            for p in range(2):
                at = pl.ds(p * half, half)
                cross_out[at, :] = (partial[1, at, :].astype(F32) + mate_in[0, at, :].astype(F32)).astype(BF)
                overs.append(go.start(cross_out.at[at], cross_in.at[at], narrow=cross))
        for k in range(column * slot // 4, column * (slot + 1) // 4):
            if k < column - 1:
                relay(k)

    vec_box[pl.ds(n, 1)] = vec_in[...][None]
    vec_box[pl.ds(n, 1), 0:2, :] = sums[0:2, :][None]
    vecs = [go.start(vec_box.at[n], vec_box.at[n], narrow=lax.rem(n + d, narrow)) for d in range(1, narrow)]
    for i in vecs:
        go.arrived(i)
    group = vec_box[0]
    for i in range(1, narrow):
        group = group + vec_box[i]
    cols = group.shape[1] // wide
    slices[...] = jnp.zeros_like(slices)
    for i in range(wide):
        slices[i, :, :cols] = group[:, i * cols : (i + 1) * cols]
    peers = [lax.rem(w + d, wide) for d in range(1, wide)]
    pieces = [go.start(slices.at[peer], slice_box.at[w], wide=peer) for peer in peers]
    slice_box[pl.ds(w, 1)] = slices[pl.ds(w, 1)]
    relay(column - 1)
    total = kept[0]
    for k in range(column - 1):
        go.arrived(seconds[k])
        total = total + far_in[k].astype(F32)
    shards[pl.ds(n, 1)] = total.astype(BF)[None]
    over = go.start(shards.at[n], shards.at[n], narrow=cross)
    beside = go.start(shards.at[n], shards.at[n], narrow=mate)

    go.arrived(mates[1])
    for p in range(2):
        go.arrived(overs[p])
        at = pl.ds(p * half, half)
        normed_out[at, :] += mate_in[1, at, :].astype(F32) + cross_in[at, :].astype(F32)
    for i in pieces:
        go.arrived(i)
    vectors = slice_box[0]
    for i in range(1, wide):
        vectors = vectors + slice_box[i]
    vec_out[...] = vectors

    go.arrived(over)
    passed = go.start(shards.at[cross], shards.at[cross], narrow=mate)
    for i in (beside, passed):
        go.arrived(i)
    squares = square_sum(vectors)
    width = part.shape[1] // 3
    for i in range(narrow):
        shard = shards[i]
        squares += square_sum(shard.astype(F32))
        for j in range(3):
            qkv_out[:, (j * narrow + i) * width : (j * narrow + i + 1) * width] = shard[:, j * width : (j + 1) * width]
    square_box[pl.ds(w, 1)] = (squares_in[...] + squares)[None]
    for peer in peers:
        go.start(square_box.at[w], square_box.at[w], wide=peer)
    go.finish()
    total = square_box[0]
    for i in range(1, wide):
        total = total + square_box[i]
    square_out[...] = total


def tail_call(part, grad_proj, weight, tok, vec_in, squares_in, wide, narrow):
    depth, cols = part.shape
    rows = tok.shape[0] // narrow
    wide_rows = depth // wide
    column = wide // 2
    copies = 2 * column - 1 + 2 + (narrow - 1) + 2 + 3 + 2 * (wide - 1)
    vmem = pl.BlockSpec(memory_space=pltpu.VMEM)
    return pl.pallas_call(
        functools.partial(tail_kernel, wide, narrow),
        in_specs=[vmem] * 6,
        out_specs=[vmem] * 4,
        out_shape=[
            jax.ShapeDtypeStruct((rows, depth), F32),
            jax.ShapeDtypeStruct((wide_rows, narrow * cols), BF),
            jax.ShapeDtypeStruct((16, 128), F32),
            jax.ShapeDtypeStruct((8, 128), F32),
        ],
        scratch_shapes=[
            pltpu.VMEM((3, rows, depth), BF),
            pltpu.VMEM((2, rows, depth), BF),
            pltpu.VMEM((rows, depth), BF),
            pltpu.VMEM((rows, depth), BF),
            pltpu.VMEM((column, wide_rows, cols), BF),
            pltpu.VMEM((column - 1, wide_rows, cols), BF),
            pltpu.VMEM((column - 1, wide_rows, cols), BF),
            pltpu.VMEM((narrow, wide_rows, cols), BF),
            pltpu.VMEM((narrow,) + vec_in.shape, F32),
            pltpu.VMEM((8, depth), F32),
            pltpu.VMEM((wide, 16, 128), F32),
            pltpu.VMEM((wide, 16, 128), F32),
            pltpu.VMEM((wide, 8, 128), F32),
            pltpu.SemaphoreType.DMA((copies,)),
            pltpu.SemaphoreType.DMA((copies,)),
        ],
        compiler_params=pltpu.CompilerParams(
            collective_id=1, has_side_effects=True, vmem_limit_bytes=56 * 1024 * 1024
        ),
        name="tail",
    )(part, grad_proj, weight, tok, vec_in, squares_in)


CLIP = 784


def head_lanes(shape, head, head_dim):
    lane = lax.broadcasted_iota(jnp.int32, shape, 1)
    return lane // head_dim == head


def meeting(block, blocks):
    before, after = CLIP // BLOCK, -(-2 * CLIP // BLOCK)
    low = before * (block // after)
    high = blocks - (blocks - after) * (1 - jnp.minimum(block // before, 1))
    return low, high


def forward_kernel(
    heads, head_dim, wide, narrow,
    tok, vec, tag, table, qkv_f32, out_f32, up_f32, down_f32,
    q_ref, k_ref, v_ref, turn_ref, norm_ref, vec_ref, seg_ref, tag_ref, o_ref, lse_ref,
    tok_all, qkv_all, mixed_ref, out_all, up_all, down_all,
    vec_box, tag_box, tok_box, qkv_box, qkv_own, out_own, up_own, down_own, stage_qkv, stage_out, stage_up, stage_down,
    values_turned, acc, peak, total, o_box, send, recv, mix_send, mix_recv, local, leave,
):
    step = pl.program_id(0)
    rows, width = q_ref.shape
    depth = tok.shape[1]
    blocks = rows // BLOCK
    per = blocks // narrow
    final = 2 * blocks
    w, n = lax.axis_index("wide"), lax.axis_index("narrow")
    column = wide // 2
    z, y, side = w // 2, lax.rem(w, 2), lax.rem(n, 2)
    near, mate, cross = w + 1 - 2 * y, n + 1 - 2 * side, lax.rem(n + 2, narrow)
    source = lambda d: lax.rem(z - d + column, column) * 2 + y
    target = lambda d: lax.rem(z + d, column) * 2 + y
    beside = lambda d: lax.rem(z - d + column, column) * 2 + 1 - y
    wide_rows, out_half = out_own.shape
    half = up_own.shape[1]
    group_rows = tok.shape[0]

    loads = [
        pltpu.make_async_copy(
            qkv_f32.at[:, pl.ds(pl.multiple_of(i * depth + n * width, width), width)],
            stage_qkv.at[:, pl.ds(i * width, width)],
            local.at[i],
        )
        for i in range(3)
    ] + [
        pltpu.make_async_copy(
            whole.at[:, pl.ds(pl.multiple_of(side * size, size), size)], stage, local.at[3 + i]
        )
        for i, (whole, stage, size) in enumerate(
            [(out_f32, stage_out, out_half), (up_f32, stage_up, half), (down_f32, stage_down, half)]
        )
    ]

    go = Copies(send, recv)
    small = [go.make(vec, vec_box.at[w], wide=lax.rem(w + d, wide)) for d in range(1, wide)]
    small += [go.make(tag, tag_box.at[n], narrow=lax.rem(n + d, narrow)) for d in range(1, narrow)]
    pieces = 4
    piece = group_rows // pieces
    token_rows = lambda i, p: tok_box.at[rows_at(i * pieces + p, piece)]
    own_piece = lambda p: tok.at[pl.ds(p * piece, piece)]
    over = [go.make(own_piece(p), token_rows(n, p), narrow=cross) for p in range(pieces)]
    to_mate = [go.make(own_piece(p), token_rows(n, p), narrow=mate) for p in range(pieces)]
    passed = [go.make(token_rows(cross, p), token_rows(cross, p), narrow=mate) for p in range(pieces)]
    qkv_at = lambda i: qkv_box.at[rows_at(i, wide_rows)]
    qkv_far = [go.make(qkv_own, qkv_at(w), wide=target(d)) for d in range(1, column)]
    qkv_near = [go.make(qkv_own, qkv_at(w), wide=near)]
    qkv_near += [go.make(qkv_at(source(d)), qkv_at(source(d)), wide=near) for d in range(1, column)]

    at_step = [[] for _ in range(final + 2)]
    out_cols = pl.ds(pl.multiple_of(side * out_half, out_half), out_half)
    out_at = lambda i: out_all.at[rows_at(i, wide_rows), out_cols]
    out_near = [go.make(out_own, out_at(w), wide=near)]
    out_starts = [go.make(out_own, out_at(w), narrow=mate)]
    at_step[1].append((None, [out_near[0]]))
    for d in range(1, column):
        out_starts.append(go.make(out_own, out_at(w), wide=target(d)))
        ref = out_at(source(d))
        out_near.append(go.make(ref, ref, wide=near))
        at_step[5].append((out_starts[-1], [out_near[-1], go.make(ref, ref, narrow=mate)]))
    for d in range(column):
        ref = out_at(beside(d))
        at_step[blocks + 2].append((out_near[d], [go.make(ref, ref, narrow=mate)]))

    quarter = half // 4
    shared = pl.ds(pl.multiple_of(n // 2 * quarter, quarter), quarter)
    both = pl.ds(2 * quarter, 2 * quarter)
    own_out = [pltpu.make_async_copy(out_own, out_at(w), leave.at[0])]

    def spread(own, result, steps, slot):
        starts = []
        for cols in (shared, both):
            piece_at = lambda i: result.at[rows_at(i, wide_rows), cols]
            passes = lambda i: [go.make(piece_at(i), piece_at(i), narrow=cross)] if cols is shared else []
            nears = [go.make(own.at[:, cols], piece_at(w), wide=near)]
            at_step[1].append((None, [nears[0]]))
            if cols is shared:
                starts.append(go.make(own.at[:, cols], piece_at(w), narrow=cross))
            for d in range(1, column):
                starts.append(go.make(own.at[:, cols], piece_at(w), wide=target(d)))
                ref = piece_at(source(d))
                nears.append(go.make(ref, ref, wide=near))
                turn_at = steps[0] if cols is shared else steps[2] + (d - 1) * 2 // column
                at_step[min(turn_at, final + 1)].append((starts[-1], [nears[-1]] + passes(source(d))))
            if cols is shared:
                for d in range(column):
                    at_step[steps[1]].append((nears[d], passes(beside(d))))
            own_out.append(pltpu.make_async_copy(own.at[:, cols], piece_at(w), leave.at[slot + (cols is both)]))
        return starts

    up_starts = spread(up_own, up_all, (blocks + 1, blocks + 3, blocks + 4), 1)
    down_starts = spread(down_own, down_all, (final - 1, final + 1, final + 1), 3)

    mine = pl.ds(pl.multiple_of(n * width, width), width)

    def result(s):
        at = lax.rem((n + 1) * per + s, blocks)
        return pltpu.make_async_remote_copy(
            src_ref=o_box.at[rows_at(at, BLOCK)],
            dst_ref=mixed_ref.at[rows_at(lax.rem(s, per), BLOCK), mine],
            send_sem=mix_send.at[s],
            recv_sem=mix_recv.at[s],
            device_id={"narrow": lax.rem(n + 1 + s // per, narrow)},
            device_id_type=MESH,
        )

    def result_here(s):
        return pltpu.make_async_copy(
            o_box.at[rows_at(n * per + s, BLOCK)], mixed_ref.at[rows_at(s, BLOCK), mine], leave.at[7 + s]
        )

    kept = [
        pltpu.make_async_copy(tok_box, tok_all, leave.at[5]),
        pltpu.make_async_copy(qkv_box, qkv_all, leave.at[6]),
    ]

    @pl.when(step == 0)
    def _():
        for copy in loads:
            copy.start()
        greet(others("wide", w, wide) + others("narrow", n, narrow))
        go.launch(*small, *over)
        for copy in loads[:3]:
            copy.wait()
        qkv_own[...] = stage_qkv[...].astype(BF)
        go.launch(*qkv_far, qkv_near[0], *to_mate)
        for copy, stage, own, starts in zip(
            loads[3:],
            (stage_out, stage_up, stage_down),
            (out_own, up_own, down_own),
            (out_starts, up_starts, down_starts),
        ):
            copy.wait()
            own[...] = stage[...].astype(BF)
            go.launch(*starts)
        tok_box[rows_at(n, group_rows), :] = tok[...]
        qkv_box[rows_at(w, wide_rows), :] = qkv_own[...]
        vec_box[pl.ds(w, 1)] = vec[...][None]
        tag_box[pl.ds(n, 1)] = tag[...][None]
        for copy in own_out:
            copy.start()
        for i in small:
            go.arrived(i)
        cols = depth // wide
        for i in range(wide):
            vec_ref[:, i * cols : (i + 1) * cols] = vec_box[i].astype(F32)[:, :cols]
        for i in range(max(pieces, column - 1)):
            if i < column - 1:
                go.arrived(qkv_far[i])
                go.launch(qkv_near[i + 1])
            if i < pieces:
                go.arrived(over[i])
                go.launch(passed[i])
        for i in qkv_near + to_mate + passed:
            go.arrived(i)
        for copy in kept:
            copy.start()

    for i in range(1, final + 1):
        if at_step[i]:

            @pl.when(step == i)
            def _():
                for arrival, follow in at_step[i]:
                    if arrival is not None:
                        go.arrived(arrival)
                    go.launch(*follow)

    @pl.when((step > 0) & (step <= blocks))
    def _():
        block = step - 1
        at = rows_at(block, BLOCK)
        marks = tag_box[pl.ds(block // per, 1), :, pl.ds(pl.multiple_of(lax.rem(block, per) * BLOCK, BLOCK), BLOCK)]
        marks = marks[0].astype(F32)
        seg_ref[pl.ds(block, 1)] = marks[0:1][None]
        marks = marks.T
        tag_ref[at, :] = jnp.where(marks[:, 1:2] == 1.0, marks[:, 0:1], -1.0)
        slot = lax.broadcasted_iota(jnp.int32, (BLOCK, 128), 1).astype(F32)
        spot = (slot == marks[:, 2:3]) | (slot == 14 + marks[:, 3:4]) | (slot == 28 + marks[:, 4:5])
        angles = lax.dot_general(
            jnp.where(spot, 1.0, 0.0),
            table[...],
            (((1,), (0,)), ((), ())),
            precision=lax.Precision.HIGHEST,
            preferred_element_type=F32,
        )
        turn_ref[at, :] = angles
        cosine, sine = angles[:, :128], angles[:, 128:]
        unit, _ = norm_parts(tok_box[at, :].astype(F32))
        normed = (unit * vec_ref[0:1, :] + vec_ref[1:2, :]).astype(BF)
        norm_ref[...] = normed
        proj = dot(normed, qkv_box[...], 1, 0)
        parts = [proj[:, i * width : (i + 1) * width] + vec_ref[2 + i : 3 + i, mine] for i in range(3)]
        q_ref[at, :] = turn(parts[0], cosine, sine, head_dim // 2, 1).astype(BF)
        k_ref[at, :] = turn(parts[1], cosine, sine, head_dim // 2, 1).astype(BF)
        v_ref[at, :] = parts[2].astype(BF)
        values_turned[:, at] = parts[2].T.astype(BF)

    @pl.when(step > blocks)
    def _():
        place = step - blocks - 1
        block = lax.rem((n + 1) * per + place, blocks)
        at = rows_at(block, BLOCK)
        query = q_ref[at, :] * jnp.asarray(head_dim**-0.5, BF)
        seg = seg_ref[pl.ds(block, 1)][0]
        masked_query = [
            jnp.where(head_lanes(query.shape, h, head_dim), query, jnp.zeros_like(query)) for h in range(heads)
        ]
        acc[...] = jnp.zeros_like(acc)
        peak[...] = jnp.full_like(peak, -1e30)
        total[...] = jnp.zeros_like(total)

        def body(j, carry):
            start = pl.multiple_of(j * BLOCK, BLOCK)
            key = k_ref[pl.ds(start, BLOCK), :]
            allowed = tag_ref[pl.ds(start, BLOCK), :] == seg
            scores = [jnp.where(allowed, dot(key, masked_query[h], 1, 1), -1e30) for h in range(heads)]
            for h in range(heads):
                lines = slice(h * head_dim, (h + 1) * head_dim)
                old = peak[h : h + 1, :]
                new = jnp.maximum(old, jnp.max(scores[h], axis=0, keepdims=True))
                probs = jnp.exp(scores[h] - new)
                keep = jnp.exp(old - new)
                peak[h : h + 1, :] = new
                total[h : h + 1, :] = total[h : h + 1, :] * keep + jnp.sum(probs, axis=0, keepdims=True)
                value = values_turned[lines, pl.ds(start, BLOCK)]
                acc[lines, :] = acc[lines, :] * keep + dot(value, probs.astype(BF), 1, 0)
            return carry

        low, high = meeting(block, blocks)
        lax.fori_loop(low, high, body, 0)
        parts = [acc[h * head_dim : (h + 1) * head_dim, :] / total[h : h + 1, :] for h in range(heads)]
        out = jnp.concatenate(parts, axis=0).T.astype(BF)
        o_ref[at, :] = out
        o_box[at, :] = out
        lse_ref[pl.ds(block, 1)] = (peak[...] + jnp.log(jnp.maximum(total[...], 1e-30)))[None]

        @pl.when(place < blocks - per)
        def _():
            result(place).start()

    @pl.when(step == final)
    def _():
        for s in range(per):
            result_here(s).start()
        for arrival, follow in at_step[final + 1]:
            go.arrived(arrival)
            go.launch(*follow)
        for copy in own_out + kept:
            copy.wait()
        for s in range(blocks - per):
            result(s).wait()
        for s in range(per):
            result_here(s).wait()
        go.finish()


def forward_call(tok, vec, tag, table, weights, head_dim, wide, narrow):
    qkv, out, up, down = weights
    group_rows, depth = tok.shape
    rows = group_rows * narrow
    width = depth // narrow
    heads = width // head_dim
    blocks = rows // BLOCK
    column = wide // 2
    size = qkv.shape[0]
    half = up.shape[1] // 2
    copies = (wide - 1) + (narrow - 1) + 12 + (2 * column - 1)
    copies += 2 + 3 * (column - 1) + column + 2 * (2 * (2 * column - 1) + 2 * column)
    whole = lambda a: pl.BlockSpec(a.shape, lambda i: (0,) * len(a.shape), pipeline_mode=pl.Buffered(1))
    anywhere = pl.BlockSpec(memory_space=pl.ANY)
    shaped = jax.ShapeDtypeStruct
    head_rows = shaped((rows, width), BF)
    inside = [
        head_rows, head_rows, head_rows, shaped((rows, 256), F32), shaped((rows, depth), BF), shaped((16, depth), F32),
        shaped((blocks, 1, BLOCK), F32), shaped((rows, 1), F32), head_rows, shaped((blocks, 8, BLOCK), F32),
    ]
    inside_specs = [whole(a) for a in inside]
    inside_specs[4] = pl.BlockSpec((BLOCK, depth), lambda i: (jnp.minimum(jnp.maximum(i - 1, 0), blocks - 1), 0))
    outside = [
        shaped((rows, depth), BF), shaped((depth, 3 * width), BF), shaped((group_rows, depth), BF),
        shaped((depth, depth), BF), shaped((depth, half), BF), shaped((depth, half), BF),
    ]
    small = [(size, 3 * width), (size, depth // 2), (size, half), (size, half)]
    return pl.pallas_call(
        functools.partial(forward_kernel, heads, head_dim, wide, narrow),
        grid=(2 * blocks + 1,),
        in_specs=[whole(a) for a in (tok, vec, tag, table)] + [anywhere] * 4,
        out_specs=inside_specs + [anywhere] * 6,
        out_shape=inside + outside,
        scratch_shapes=[
            pltpu.VMEM((wide,) + vec.shape, BF),
            pltpu.VMEM((narrow,) + tag.shape, jnp.int32),
            pltpu.VMEM((rows, depth), BF),
            pltpu.VMEM((depth, 3 * width), BF),
        ]
        + [pltpu.VMEM(shape, BF) for shape in small]
        + [pltpu.VMEM(shape, F32) for shape in small]
        + [
            pltpu.VMEM((width, rows), BF),
            pltpu.VMEM((width, BLOCK), F32),
            pltpu.VMEM((8, BLOCK), F32),
            pltpu.VMEM((8, BLOCK), F32),
            pltpu.VMEM((rows, width), BF),
            pltpu.SemaphoreType.DMA((copies,)),
            pltpu.SemaphoreType.DMA((copies,)),
            pltpu.SemaphoreType.DMA((blocks,)),
            pltpu.SemaphoreType.DMA((blocks,)),
            pltpu.SemaphoreType.DMA((6,)),
            pltpu.SemaphoreType.DMA((7 + blocks // narrow,)),
        ],
        compiler_params=pltpu.CompilerParams(
            collective_id=3, has_side_effects=True, vmem_limit_bytes=48 * 1024 * 1024
        ),
        cost_estimate=pl.CostEstimate(
            flops=heads * rows * rows * width * 4, bytes_accessed=rows * width * 8, transcendentals=heads * rows * rows
        ),
        name="attention_forward",
    )(tok, vec, tag, table, qkv, out, up, down)


class Scatter:
    def __init__(self, go, wide, narrow, part, near_in, own, far_out, far_in, box, local):
        w, self.n = lax.axis_index("wide"), lax.axis_index("narrow")
        self.go, self.column = go, wide // 2
        self.near_in, self.own, self.far_out, self.far_in, self.box = near_in, own, far_out, far_in, box
        z, y = w // 2, lax.rem(w, 2)
        near, mate, cross = w + 1 - 2 * y, self.n + 1 - 2 * lax.rem(self.n, 2), lax.rem(self.n + 2, narrow)
        size = part.shape[0] // wide
        towards = [lax.rem(z + d, self.column) for d in range(1, self.column + 1)]
        self.first = [
            go.make(part.at[rows_at(to * 2 + 1 - y, size)], near_in.at[k], wide=near) for k, to in enumerate(towards)
        ]
        self.loads = [
            pltpu.make_async_copy(part.at[rows_at(to * 2 + y, size)], own.at[k], local.at[k])
            for k, to in enumerate(towards)
        ]
        self.second = [
            go.make(far_out.at[k], far_in.at[k], wide=to * 2 + y) for k, to in enumerate(towards[:-1])
        ]
        self.over = go.make(box.at[self.n], box.at[self.n], narrow=cross)
        self.beside = go.make(box.at[self.n], box.at[self.n], narrow=mate)
        self.passed = go.make(box.at[cross], box.at[cross], narrow=mate)

    def begin(self):
        self.go.launch(*self.first)
        for copy in self.loads:
            copy.start()

    def relay(self, k):
        self.go.arrived(self.first[k])
        self.loads[k].wait()
        if k < self.column - 1:
            self.far_out[k] = (self.own[k].astype(F32) + self.near_in[k].astype(F32)).astype(BF)
            self.go.launch(self.second[k])

    def total(self):
        value = self.own[self.column - 1].astype(F32) + self.near_in[self.column - 1].astype(F32)
        for k in range(self.column - 1):
            self.go.arrived(self.second[k])
            value = value + self.far_in[k].astype(F32)
        self.box[pl.ds(self.n, 1)] = value.astype(BF)[None]
        self.go.launch(self.over, self.beside)

    def share(self):
        self.go.arrived(self.over)
        self.go.launch(self.passed)

    @staticmethod
    def copies(wide):
        return 2 * (wide // 2) - 1 + 3

    @staticmethod
    def scratch(wide, narrow, rows, cols):
        column, size = wide // 2, rows // wide
        sizes = [column, column, column - 1, column - 1, narrow]
        return [pltpu.VMEM((count, size, cols), BF) for count in sizes] + [pltpu.SemaphoreType.DMA((column,))]


def square_sum(value):
    return jnp.sum(jnp.sum(value * value, axis=0, keepdims=True), axis=1, keepdims=True)


def backward_kernel(
    heads, head_dim, wide, narrow,
    q_ref, k_ref, v_ref, o_ref, g_ref, lse_ref, seg_ref, tag_ref, turn_ref, part_out, part_down, part_up,
    grads_out, shards_out, shards_down, shards_up, squares_out,
    q_heads, g_heads, delta, grad_query, send, recv, *boxes,
):
    step = pl.program_id(0)
    rows, width = q_ref.shape
    blocks = rows // BLOCK
    last = blocks - 1
    scale = head_dim**-0.5
    half = head_dim // 2
    go = Copies(send, recv)
    column = wide // 2
    outs = Scatter(go, wide, narrow, part_out, *boxes[:6])
    ups = Scatter(go, wide, narrow, part_up, *boxes[6:12])
    downs = Scatter(go, wide, narrow, part_down, *boxes[12:])

    @pl.when(step == 0)
    def _():
        w, n = lax.axis_index("wide"), lax.axis_index("narrow")
        z, y = w // 2, lax.rem(w, 2)
        greet(
            [{"wide": w + 1 - 2 * y}]
            + [{"wide": lax.rem(z + d, column) * 2 + y} for d in range(1, column)]
            + [{"narrow": n + 1 - 2 * lax.rem(n, 2)}, {"narrow": lax.rem(n + 2, narrow)}]
        )
        outs.begin()
        ups.begin()
        downs.begin()

    part = lambda i: range(column * i // 4, column * (i + 1) // 4)
    plan = [
        [],
        [(outs.relay, range(column))],
        [(ups.relay, part(0))],
        [(ups.relay, part(1)), (outs.total, None)],
        [(ups.relay, part(2)), (outs.share, None)],
        [(ups.relay, part(3))],
        [(downs.relay, part(0)), (ups.total, None)],
    ]
    actions = [[] for _ in range(last)]
    for i, entries in enumerate(plan):
        for action, ks in entries:
            actions[min(i, last - 1)] += [action] if ks is None else [functools.partial(action, k) for k in ks]
    for i in range(last):
        if actions[i]:

            @pl.when(step == i + 1)
            def _():
                for action in actions[i]:
                    action()

    @pl.when(step == 0)
    def _():
        grad_query[...] = jnp.zeros_like(grad_query)
        row = lax.broadcasted_iota(jnp.int32, (8, width), 0)
        lane = lax.broadcasted_iota(jnp.int32, (8, width), 1)
        pick = jnp.where(lane // head_dim == row, 1.0, 0.0)

        def prepare(i, carry):
            at = pl.ds(pl.multiple_of(i * BLOCK, BLOCK), BLOCK)
            query = q_ref[at, :] * jnp.asarray(scale, BF)
            grad = g_ref[at, :]
            for h in range(heads):
                lanes = head_lanes(query.shape, h, head_dim)
                q_heads[h, at, :] = jnp.where(lanes, query, jnp.zeros_like(query))
                g_heads[h, at, :] = jnp.where(lanes, grad, jnp.zeros_like(grad))
            product = grad.astype(F32) * o_ref[at, :].astype(F32)
            delta[pl.ds(i, 1)] = lax.dot_general(
                pick,
                product,
                (((1,), (1,)), ((), ())),
                precision=lax.Precision.HIGHEST,
                preferred_element_type=F32,
            )[None]
            return carry

        lax.fori_loop(0, blocks, prepare, 0)

    key = k_ref[...]
    value = v_ref[...]
    tag = tag_ref[...]
    masked_key = [jnp.where(head_lanes(key.shape, h, head_dim), key, jnp.zeros_like(key)) for h in range(heads)]

    def body(i, carry):
        grad_key, grad_value = carry
        at = pl.ds(pl.multiple_of(i * BLOCK, BLOCK), BLOCK)
        allowed = tag == seg_ref[pl.ds(i, 1), :]
        lse = lse_ref[pl.ds(i, 1)][0]
        dlt = delta[pl.ds(i, 1)][0]
        total = None
        for h in range(heads):
            query = q_heads[h, at, :]
            grad = g_heads[h, at, :]
            scores = dot(key, query, 1, 1)
            probs = jnp.where(allowed, jnp.exp(scores - lse[h : h + 1, :]), 0.0)
            grad_probs = dot(value, grad, 1, 1)
            grad_scores = (probs * (grad_probs - dlt[h : h + 1, :])).astype(BF)
            grad_value = grad_value + dot(probs.astype(BF), grad, 1, 0)
            grad_key = grad_key + dot(grad_scores, query, 1, 0)
            term = dot(grad_scores, masked_key[h], 0, 0)
            total = term if total is None else total + term
        grad_query[at, :] += total
        return grad_key, grad_value

    zero = jnp.zeros((BLOCK, width), F32)
    low, high = meeting(step, blocks)
    grad_key, grad_value = lax.fori_loop(low, high, body, (zero, zero))
    here = pl.ds(pl.multiple_of(step * BLOCK, BLOCK), BLOCK)
    cosine, sine = turn_ref[here, :128], turn_ref[here, 128:]
    grads_out[here, width : 2 * width] = turn(grad_key, cosine, sine, half, -1).astype(BF)
    grads_out[here, 2 * width :] = grad_value.astype(BF)

    @pl.when(step == last)
    def _():
        for k in range(column // 4, column):
            downs.relay(k)
        ups.share()

        def finish(i, carry):
            at = pl.ds(pl.multiple_of(i * BLOCK, BLOCK), BLOCK)
            grads = grad_query[at, :] * scale
            grads_out[at, :width] = turn(grads, turn_ref[at, :128], turn_ref[at, 128:], half, -1).astype(BF)
            return carry

        lax.fori_loop(0, blocks, finish, 0)
        downs.total()
        downs.share()
        go.finish()
        squares = jnp.zeros((1, 1), F32)
        for box in (outs.box, ups.box):
            for i in range(2):
                squares += square_sum(box[i].astype(F32) + box[i + 2].astype(F32))
        for i in range(narrow):
            squares += square_sum(downs.box[i].astype(F32))
        squares_out[...] = jnp.broadcast_to(squares, squares_out.shape)
        shards_out[...] = outs.box[...]
        shards_down[...] = downs.box[...]
        shards_up[...] = ups.box[...]


def backward_call(q, k, v, o, g, lse, seg_rows, tag_col, turns, part_out, part_down, part_up, head_dim, wide, narrow):
    rows, width = q.shape
    heads = width // head_dim
    blocks = rows // BLOCK
    whole = lambda a: pl.BlockSpec(a.shape, lambda i: (0,) * len(a.shape), pipeline_mode=pl.Buffered(1))
    block = pl.BlockSpec((BLOCK, width), lambda i: (i, 0))
    anywhere = pl.BlockSpec(memory_space=pl.ANY)
    depth = part_up.shape[0]
    results = [
        jax.ShapeDtypeStruct((rows, 3 * width), BF),
        jax.ShapeDtypeStruct((narrow, depth // wide, part_out.shape[1]), BF),
        jax.ShapeDtypeStruct((narrow, depth // wide, part_down.shape[1]), BF),
        jax.ShapeDtypeStruct((narrow, depth // wide, part_up.shape[1]), BF),
        jax.ShapeDtypeStruct((8, 128), F32),
    ]
    copies = 3 * Scatter.copies(wide)
    return pl.pallas_call(
        functools.partial(backward_kernel, heads, head_dim, wide, narrow),
        grid=(blocks,),
        in_specs=[
            whole(q), block, block, whole(o), whole(g), whole(lse), whole(seg_rows),
            pl.BlockSpec((BLOCK, 1), lambda i: (i, 0)),
            whole(turns), anywhere, anywhere, anywhere,
        ],
        out_specs=[whole(a) for a in results],
        out_shape=results,
        scratch_shapes=[
            pltpu.VMEM((heads, rows, width), BF),
            pltpu.VMEM((heads, rows, width), BF),
            pltpu.VMEM((blocks, 8, BLOCK), F32),
            pltpu.VMEM((rows, width), F32),
            pltpu.SemaphoreType.DMA((copies,)),
            pltpu.SemaphoreType.DMA((copies,)),
        ]
        + Scatter.scratch(wide, narrow, depth, part_out.shape[1])
        + Scatter.scratch(wide, narrow, depth, part_up.shape[1])
        + Scatter.scratch(wide, narrow, depth, part_down.shape[1]),
        compiler_params=pltpu.CompilerParams(
            collective_id=4, has_side_effects=True, vmem_limit_bytes=60 * 1024 * 1024
        ),
        cost_estimate=pl.CostEstimate(
            flops=heads * rows * rows * width * 7, bytes_accessed=rows * width * 20, transcendentals=heads * rows * rows
        ),
        name="attention_backward",
    )(q, k, v, o, g, lse, seg_rows, tag_col, turns, part_out, part_down, part_up)


def norm_parts(values):
    center = values - jnp.mean(values, axis=-1, keepdims=True)
    inverse = lax.rsqrt(jnp.mean(center * center, axis=-1, keepdims=True) + 1e-06)
    return center * inverse, inverse


def norm_back(grads, gain, unit, inverse):
    scaled = grads * gain
    return inverse * (
        scaled - jnp.mean(scaled, axis=-1, keepdims=True) - unit * jnp.mean(scaled * unit, axis=-1, keepdims=True)
    )


def adamw(param, grad, first, second, clip, rate, decay, fix_first, fix_second):
    clipped = grad * clip
    moment = 0.9 * first + 0.1 * clipped
    square = 0.999 * second + 0.001 * clipped * clipped
    direction = moment / fix_first / (jnp.sqrt(square / fix_second) + 1e-08)
    return (param - rate * (direction + decay * param), moment, square)


def on_device(
    tokens, cotangent, segment_ids, key_keep, patch_coords, step_count,
    weight_qkv, weight_out, weight_up, weight_down, vectors,
    first_qkv, first_out, first_up, first_down, first_vectors,
    second_qkv, second_out, second_up, second_down, second_vectors,
):
    rows, width = tokens.shape
    hidden = weight_up.shape[1]
    head_dim = width // HEADS
    narrow = lax.axis_size("narrow")
    wide = lax.axis_size("wide")
    shard_rows = width // wide
    me = lax.axis_index("narrow")
    side = me % 2
    mine = width // narrow
    half_hidden = hidden // 2
    group = rows * narrow

    def mate(value):
        return lax.ppermute(value, "narrow", [(i, i ^ 1) for i in range(narrow)])

    def across(value):
        return lax.ppermute(value, "narrow", [(i, i ^ 2) for i in range(narrow)])

    def take(value, start, size, axis=1):
        return lax.dynamic_slice_in_dim(value, start, size, axis)

    shard_cols = vectors.shape[1]
    vec_shard = jnp.pad(vectors.astype(BF), ((0, 16 - vectors.shape[0]), (0, -shard_cols % 128)))
    tag = jnp.concatenate([segment_ids[None], key_keep[None], patch_coords, patch_coords], axis=0)
    (
        query, keys, values, turns, normed1_all, vec, seg_rows, tag_col, mixed_mine, lse,
        tokens_all, qkv_w, mixed, out_w, up_w, down_w,
    ) = forward_call(
        tokens, vec_shard, tag, rotary_table(head_dim), (weight_qkv, weight_out, weight_up, weight_down),
        head_dim, wide, narrow,
    )
    vec = vec[: vectors.shape[0]]
    xin = tokens.astype(F32)
    unit1, inverse1 = norm_parts(xin)
    cot_pair = jnp.concatenate([cotangent, mate(cotangent)], axis=0)

    resid = xin + (dot(mixed, out_w, 1, 0) + vec[5])
    unit2, inverse2 = norm_parts(resid)
    normed2 = (unit2 * vec[6] + vec[7]).astype(BF)
    normed2_pair = jnp.concatenate([normed2, mate(normed2)], axis=0)
    up_bias = take(vec[9:].reshape(1, -1), side * half_hidden, half_hidden)
    up_pre = dot(normed2_pair, up_w, 1, 0) + up_bias
    erf_part = 0.5 * (1.0 + lax.erf(up_pre * (0.5**0.5)))
    act = (up_pre * erf_part).astype(BF)
    slope = erf_part + up_pre * (jnp.exp(-0.5 * up_pre * up_pre) * ((2.0 * jnp.pi) ** -0.5))
    part_down = dot(cot_pair, act, 0, 0).astype(BF)
    far_side = me // 2
    quarter_hidden = half_hidden // 2
    leaving = take(part_down, (1 - far_side) * quarter_hidden, quarter_hidden)
    act, leaving = lax.optimization_barrier((act, leaving))
    came = across(leaving)
    part_down = take(part_down, far_side * quarter_hidden, quarter_hidden)
    down_part = dot(act, down_w, 1, 1)
    down = down_part[:rows] + mate(down_part[rows:])
    layer_out = (resid + (down + vec[8])).astype(BF)

    grad_up_act = (dot(cot_pair, down_w, 1, 0) * slope).astype(BF)
    part_up = dot(normed2_pair, grad_up_act, 0, 0).astype(BF)
    grad_normed2_part = dot(grad_up_act, up_w, 1, 1)
    grad_normed2 = grad_normed2_part[:rows] + mate(grad_normed2_part[rows:])
    cot = cotangent.astype(F32)
    grad_resid = cot + norm_back(grad_normed2, vec[6], unit2, inverse2)
    grad_branch = grad_resid.astype(BF)
    grad_mixed = dot(grad_branch, out_w, 1, 1).astype(BF)
    part_out = dot(mixed, grad_branch, 0, 0)
    own_out = take(part_out, side * (width // 2), width // 2)
    other_out = take(part_out, (1 - side) * (width // 2), width // 2)
    part_out = (own_out + mate(other_out.astype(BF)).astype(F32)).astype(BF)

    part_down = (part_down.astype(F32) + came.astype(F32)).astype(BF)

    grad_mixed_mine = lax.all_to_all(grad_mixed, "narrow", 1, 0, tiled=True)
    grad_proj, shards_out, shards_down, shards_up, squares = backward_call(
        query, keys, values, mixed_mine, grad_mixed_mine, lse, seg_rows[:, 0], tag_col, turns, part_out, part_down, part_up, head_dim, wide, narrow,
    )
    part_qkv = dot(normed1_all, grad_proj, 0, 0).astype(BF)

    proj_sums = jnp.sum(grad_proj.astype(F32), axis=0).reshape(3, mine)
    proj_rows = lax.dynamic_update_slice(jnp.zeros((3, width), F32), proj_sums, (0, me * mine))
    up_sums = jnp.sum(grad_up_act.astype(F32), axis=0)
    up_rows = lax.dynamic_update_slice(jnp.zeros((hidden,), F32), up_sums, (side * half_hidden,))
    vector_part = jnp.concatenate(
        [
            jnp.zeros((2, width), F32),
            proj_rows,
            jnp.sum(grad_branch.astype(F32), axis=0)[None],
            jnp.sum(grad_normed2 * unit2, axis=0)[None],
            jnp.sum(grad_normed2, axis=0)[None],
            jnp.sum(cot, axis=0)[None],
            up_rows.reshape(hidden // width, width),
            jnp.zeros((16 - vectors.shape[0], width), F32),
        ],
        axis=0,
    )
    grad_normed1, total_qkv, vector_total, square_total = tail_call(
        part_qkv, grad_proj, qkv_w, tokens_all, vector_part, squares, wide, narrow
    )
    grad_tokens = (grad_resid + norm_back(grad_normed1, vec[0], unit1, inverse1)).astype(BF)

    def join(shards):
        shards = shards.astype(F32)
        return jnp.concatenate([shards[0] + shards[2], shards[1] + shards[3]], axis=1)

    total_up = join(shards_up)
    total_down = jnp.concatenate([shards_down[i] for i in (0, 2, 1, 3)], axis=1).astype(F32)
    total_out = join(shards_out)
    total_qkv = total_qkv.astype(F32)
    grad_norm = jnp.sqrt(square_total[0, 0])
    clip = 1.0 / jnp.maximum(grad_norm, 1.0)
    count = step_count[0].astype(F32)
    rate = 0.4 * count / (count + 4.0)
    decay = 0.04 + 0.018 * count
    fix_first = 1.0 - jnp.power(0.9, count)
    fix_second = 1.0 - jnp.power(0.999, count)
    grad_vectors = vector_total[: vectors.shape[0], :shard_rows]

    def update(param, grad, first, second, decay_here):
        return adamw(param, grad, first, second, clip, rate, decay_here, fix_first, fix_second)

    new_qkv = update(weight_qkv, total_qkv, first_qkv, second_qkv, decay)
    new_out = update(weight_out, total_out, first_out, second_out, decay)
    new_up = update(weight_up, total_up, first_up, second_up, decay)
    new_down = update(weight_down, total_down, first_down, second_down, decay)
    new_vectors = update(vectors, grad_vectors, first_vectors, second_vectors, 0.0)
    news = (new_qkv, new_out, new_up, new_down, new_vectors)
    return (layer_out, grad_tokens) + tuple(n[i] for i in range(3) for n in news) + (grad_norm, grad_vectors[8])


def solution(mesh):
    by_token = P(("wide", "narrow"), None)
    ids = P(("wide", "narrow"))
    by_row = P("wide", None)
    by_column = P(None, "wide")
    params = (by_row,) * 4 + (by_column,)
    return jax.shard_map(
        on_device,
        mesh=mesh,
        in_specs=(by_token, by_token, ids, ids, P(None, ("wide", "narrow")), P()) + params * 3,
        out_specs=(by_token, by_token) + params * 3 + (P(), P("wide")),
        check_vma=False,
    )
```

```python
import functools

import jax
import jax.numpy as jnp
from jax import lax
from jax.experimental import pallas as pl
from jax.experimental.pallas import tpu as pltpu
from jax.sharding import PartitionSpec as P

HEADS = 16
BLOCK = 256
BF = jnp.bfloat16
F32 = jnp.float32
MESH = pl.DeviceIdType.MESH


def dot(a, b, ca, cb):
    return lax.dot_general(a, b, (((ca,), (cb,)), ((), ())), preferred_element_type=F32)


def swap_halves(x, half):
    lane = lax.broadcasted_iota(jnp.int32, x.shape, 1)
    width = x.shape[1]
    return jnp.where(
        lane % (2 * half) < half, pltpu.roll(x, width - half, 1), pltpu.roll(x, half, 1)
    )


def turn(x, cosine, sine, half, sign):
    parts = []
    for start in range(0, x.shape[1], 128):
        part = x[:, start : start + 128]
        other = swap_halves(part, half) * sine
        parts.append(part * cosine + other if sign > 0 else part * cosine - other)
    return jnp.concatenate(parts, axis=1)


def rotary_table(head_dim):
    half = head_dim // 2
    lane = jnp.arange(128)
    pair = lane % half
    rates = jnp.power(10000.0, -(pair // 3).astype(F32) / ((half + 2) // 3))
    row = jnp.arange(128)
    axis = row // 14
    value = (row % 14).astype(F32)
    live = (axis[:, None] == (pair % 3)[None, :]) & (row[:, None] < 42)
    angle = value[:, None] * rates[None, :]
    signs = jnp.where(lane % head_dim < half, -1.0, 1.0)
    return jnp.concatenate(
        [
            jnp.where(live, jnp.cos(angle), 0.0),
            jnp.where(live, jnp.sin(angle) * signs[None, :], 0.0),
        ],
        axis=1,
    )


def greet(targets):
    barrier = pltpu.get_barrier_semaphore()
    for target in targets:
        pl.semaphore_signal(barrier, inc=1, device_id=target, device_id_type=MESH)
    pl.semaphore_wait(barrier, len(targets))


def others(name, index, size):
    return [{name: lax.rem(index + d, size)} for d in range(1, size)]


class Copies:
    def __init__(self, send, recv):
        self.send, self.recv, self.all = send, recv, []

    def make(self, src, dst, **target):
        i = len(self.all)
        copy = pltpu.make_async_remote_copy(
            src_ref=src, dst_ref=dst, send_sem=self.send.at[i], recv_sem=self.recv.at[i],
            device_id=target, device_id_type=MESH,
        )
        self.all.append([copy, False])
        return i

    def launch(self, *indices):
        for i in indices:
            self.all[i][0].start()

    def start(self, src, dst, **target):
        i = self.make(src, dst, **target)
        self.launch(i)
        return i

    def arrived(self, i):
        if not self.all[i][1]:
            self.all[i][0].wait_recv()
            self.all[i][1] = True

    def finish(self):
        for i in range(len(self.all)):
            self.arrived(i)
        for copy, _ in self.all:
            copy.wait_send()


def rows_at(index, size):
    return pl.ds(pl.multiple_of(index * size, size), size)


def tail_kernel(
    wide, narrow, part, grad_proj, weight, tok, vec_in, squares_in, normed_out, qkv_out, vec_out, square_out,
    partial, mate_in, cross_out, cross_in, near_in, far_out, far_in, shards, vec_box, sums,
    slices, slice_box, square_box, send, recv,
):
    w, n = lax.axis_index("wide"), lax.axis_index("narrow")
    column = wide // 2
    z, y = w // 2, lax.rem(w, 2)
    x, c = n // 2, lax.rem(n, 2)
    near, mate, cross = w + 1 - 2 * y, n + 1 - 2 * c, lax.rem(n + 2, narrow)
    wide_rows, group_rows = part.shape[0] // wide, normed_out.shape[0]
    towards = [lax.rem(z + d, column) for d in range(1, column + 1)]
    greet(others("wide", w, wide) + others("narrow", n, narrow))
    go = Copies(send, recv)
    first = [
        go.start(part.at[rows_at(towards[k] * 2 + 1 - y, wide_rows)], near_in.at[k], wide=near) for k in range(column)
    ]

    seconds, kept = [], []

    def relay(k):
        go.arrived(first[k])
        value = part[rows_at(towards[k] * 2 + y, wide_rows), :].astype(F32) + near_in[k].astype(F32)
        if k < column - 1:
            far_out[k] = value.astype(BF)
            seconds.append(go.start(far_out.at[k], far_in.at[k], wide=towards[k] * 2 + y))
        else:
            kept.append(value)

    sums[...] = jnp.zeros_like(sums)
    owners = [(1 - x) * 2 + 1 - c, (1 - x) * 2 + c, x * 2 + 1 - c, n]
    half = group_rows // 2
    mates, overs = [], []
    for slot, owner in enumerate(owners):

        def body(i, carry):
            at = pl.ds(pl.multiple_of(owner * group_rows + i * BLOCK, BLOCK), BLOCK)
            here = pl.ds(pl.multiple_of(i * BLOCK, BLOCK), BLOCK)
            grads = dot(grad_proj[at, :], weight[...], 1, 1)
            unit, _ = norm_parts(tok[at, :].astype(F32))
            sums[0:1, :] += jnp.sum(grads * unit, axis=0, keepdims=True)
            sums[1:2, :] += jnp.sum(grads, axis=0, keepdims=True)
            if slot < 3:
                partial[slot, here, :] = grads.astype(BF)
            else:
                normed_out[here, :] = grads
            return carry

        lax.fori_loop(0, group_rows // BLOCK, body, 0)
        if slot == 0:
            mates.append(go.start(partial.at[0], mate_in.at[0], narrow=mate))
        if slot == 2:
            mates.append(go.start(partial.at[2], mate_in.at[1], narrow=mate))
        if slot == 1:
            go.arrived(mates[0])
            for p in range(2):
                at = pl.ds(p * half, half)
                cross_out[at, :] = (partial[1, at, :].astype(F32) + mate_in[0, at, :].astype(F32)).astype(BF)
                overs.append(go.start(cross_out.at[at], cross_in.at[at], narrow=cross))
        for k in range(column * slot // 4, column * (slot + 1) // 4):
            if k < column - 1:
                relay(k)

    vec_box[pl.ds(n, 1)] = vec_in[...][None]
    vec_box[pl.ds(n, 1), 0:2, :] = sums[0:2, :][None]
    vecs = [go.start(vec_box.at[n], vec_box.at[n], narrow=lax.rem(n + d, narrow)) for d in range(1, narrow)]
    for i in vecs:
        go.arrived(i)
    group = vec_box[0]
    for i in range(1, narrow):
        group = group + vec_box[i]
    cols = group.shape[1] // wide
    slices[...] = jnp.zeros_like(slices)
    for i in range(wide):
        slices[i, :, :cols] = group[:, i * cols : (i + 1) * cols]
    peers = [lax.rem(w + d, wide) for d in range(1, wide)]
    pieces = [go.start(slices.at[peer], slice_box.at[w], wide=peer) for peer in peers]
    slice_box[pl.ds(w, 1)] = slices[pl.ds(w, 1)]
    relay(column - 1)
    total = kept[0]
    for k in range(column - 1):
        go.arrived(seconds[k])
        total = total + far_in[k].astype(F32)
    shards[pl.ds(n, 1)] = total.astype(BF)[None]
    over = go.start(shards.at[n], shards.at[n], narrow=cross)
    beside = go.start(shards.at[n], shards.at[n], narrow=mate)

    go.arrived(mates[1])
    for p in range(2):
        go.arrived(overs[p])
        at = pl.ds(p * half, half)
        normed_out[at, :] += mate_in[1, at, :].astype(F32) + cross_in[at, :].astype(F32)
    for i in pieces:
        go.arrived(i)
    vectors = slice_box[0]
    for i in range(1, wide):
        vectors = vectors + slice_box[i]
    vec_out[...] = vectors

    go.arrived(over)
    passed = go.start(shards.at[cross], shards.at[cross], narrow=mate)
    for i in (beside, passed):
        go.arrived(i)
    squares = square_sum(vectors)
    width = part.shape[1] // 3
    for i in range(narrow):
        shard = shards[i]
        squares += square_sum(shard.astype(F32))
        for j in range(3):
            qkv_out[:, (j * narrow + i) * width : (j * narrow + i + 1) * width] = shard[:, j * width : (j + 1) * width]
    square_box[pl.ds(w, 1)] = (squares_in[...] + squares)[None]
    for peer in peers:
        go.start(square_box.at[w], square_box.at[w], wide=peer)
    go.finish()
    total = square_box[0]
    for i in range(1, wide):
        total = total + square_box[i]
    square_out[...] = total


def tail_call(part, grad_proj, weight, tok, vec_in, squares_in, wide, narrow):
    depth, cols = part.shape
    rows = tok.shape[0] // narrow
    wide_rows = depth // wide
    column = wide // 2
    copies = 2 * column - 1 + 2 + (narrow - 1) + 2 + 3 + 2 * (wide - 1)
    vmem = pl.BlockSpec(memory_space=pltpu.VMEM)
    return pl.pallas_call(
        functools.partial(tail_kernel, wide, narrow),
        in_specs=[vmem] * 6,
        out_specs=[vmem] * 4,
        out_shape=[
            jax.ShapeDtypeStruct((rows, depth), F32),
            jax.ShapeDtypeStruct((wide_rows, narrow * cols), BF),
            jax.ShapeDtypeStruct((16, 128), F32),
            jax.ShapeDtypeStruct((8, 128), F32),
        ],
        scratch_shapes=[
            pltpu.VMEM((3, rows, depth), BF),
            pltpu.VMEM((2, rows, depth), BF),
            pltpu.VMEM((rows, depth), BF),
            pltpu.VMEM((rows, depth), BF),
            pltpu.VMEM((column, wide_rows, cols), BF),
            pltpu.VMEM((column - 1, wide_rows, cols), BF),
            pltpu.VMEM((column - 1, wide_rows, cols), BF),
            pltpu.VMEM((narrow, wide_rows, cols), BF),
            pltpu.VMEM((narrow,) + vec_in.shape, F32),
            pltpu.VMEM((8, depth), F32),
            pltpu.VMEM((wide, 16, 128), F32),
            pltpu.VMEM((wide, 16, 128), F32),
            pltpu.VMEM((wide, 8, 128), F32),
            pltpu.SemaphoreType.DMA((copies,)),
            pltpu.SemaphoreType.DMA((copies,)),
        ],
        compiler_params=pltpu.CompilerParams(
            collective_id=1, has_side_effects=True, vmem_limit_bytes=56 * 1024 * 1024
        ),
        name="tail",
    )(part, grad_proj, weight, tok, vec_in, squares_in)


CLIP = 784


def head_lanes(shape, head, head_dim):
    lane = lax.broadcasted_iota(jnp.int32, shape, 1)
    return lane // head_dim == head


def meeting(block, blocks):
    before, after = CLIP // BLOCK, -(-2 * CLIP // BLOCK)
    low = before * (block // after)
    high = blocks - (blocks - after) * (1 - jnp.minimum(block // before, 1))
    return low, high


def forward_kernel(
    heads, head_dim, wide, narrow,
    tok, vec, tag, table, qkv_f32, out_f32, up_f32, down_f32,
    q_ref, k_ref, v_ref, turn_ref, norm_ref, vec_ref, seg_ref, tag_ref, o_ref, lse_ref,
    tok_all, qkv_all, mixed_ref, out_all, up_all, down_all,
    vec_box, tag_box, tok_box, qkv_box, qkv_own, out_own, up_own, down_own, stage_qkv, stage_out, stage_up, stage_down,
    values_turned, acc, peak, total, o_box, send, recv, mix_send, mix_recv, local, leave,
):
    step = pl.program_id(0)
    rows, width = q_ref.shape
    depth = tok.shape[1]
    blocks = rows // BLOCK
    per = blocks // narrow
    final = 2 * blocks
    w, n = lax.axis_index("wide"), lax.axis_index("narrow")
    column = wide // 2
    z, y, side = w // 2, lax.rem(w, 2), lax.rem(n, 2)
    near, mate, cross = w + 1 - 2 * y, n + 1 - 2 * side, lax.rem(n + 2, narrow)
    source = lambda d: lax.rem(z - d + column, column) * 2 + y
    target = lambda d: lax.rem(z + d, column) * 2 + y
    beside = lambda d: lax.rem(z - d + column, column) * 2 + 1 - y
    wide_rows, out_half = out_own.shape
    half = up_own.shape[1]
    group_rows = tok.shape[0]

    loads = [
        pltpu.make_async_copy(
            qkv_f32.at[:, pl.ds(pl.multiple_of(i * depth + n * width, width), width)],
            stage_qkv.at[:, pl.ds(i * width, width)],
            local.at[i],
        )
        for i in range(3)
    ] + [
        pltpu.make_async_copy(
            whole.at[:, pl.ds(pl.multiple_of(side * size, size), size)], stage, local.at[3 + i]
        )
        for i, (whole, stage, size) in enumerate(
            [(out_f32, stage_out, out_half), (up_f32, stage_up, half), (down_f32, stage_down, half)]
        )
    ]

    go = Copies(send, recv)
    small = [go.make(vec, vec_box.at[w], wide=lax.rem(w + d, wide)) for d in range(1, wide)]
    small += [go.make(tag, tag_box.at[n], narrow=lax.rem(n + d, narrow)) for d in range(1, narrow)]
    pieces = 4
    piece = group_rows // pieces
    token_rows = lambda i, p: tok_box.at[rows_at(i * pieces + p, piece)]
    own_piece = lambda p: tok.at[pl.ds(p * piece, piece)]
    over = [go.make(own_piece(p), token_rows(n, p), narrow=cross) for p in range(pieces)]
    to_mate = [go.make(own_piece(p), token_rows(n, p), narrow=mate) for p in range(pieces)]
    passed = [go.make(token_rows(cross, p), token_rows(cross, p), narrow=mate) for p in range(pieces)]
    qkv_at = lambda i: qkv_box.at[rows_at(i, wide_rows)]
    qkv_far = [go.make(qkv_own, qkv_at(w), wide=target(d)) for d in range(1, column)]
    qkv_near = [go.make(qkv_own, qkv_at(w), wide=near)]
    qkv_near += [go.make(qkv_at(source(d)), qkv_at(source(d)), wide=near) for d in range(1, column)]

    at_step = [[] for _ in range(final + 2)]
    soon = []
    out_cols = pl.ds(pl.multiple_of(side * out_half, out_half), out_half)
    out_at = lambda i: out_all.at[rows_at(i, wide_rows), out_cols]
    out_near = [go.make(out_own, out_at(w), wide=near)]
    out_starts = [go.make(out_own, out_at(w), narrow=mate)]
    at_step[blocks + 6].append((None, [out_near[0]]))
    out_late = []
    for d in range(1, column):
        out_starts.append(go.make(out_own, out_at(w), wide=target(d)))
        ref = out_at(source(d))
        out_near.append(go.make(ref, ref, wide=near))
        out_late.append((out_starts[-1], [out_near[-1], go.make(ref, ref, narrow=mate)]))
    for d in range(column):
        ref = out_at(beside(d))
        out_late.append((out_near[d], [go.make(ref, ref, narrow=mate)]))

    quarter = half // 4
    shared = pl.ds(pl.multiple_of(n // 2 * quarter, quarter), quarter)
    both = pl.ds(2 * quarter, 2 * quarter)
    own_out = [pltpu.make_async_copy(out_own, out_at(w), leave.at[0])]

    def spread(own, result, cols, steps, slot):
        piece_at = lambda i: result.at[rows_at(i, wide_rows), cols]
        over_x = cols is shared
        passes = lambda i: [go.make(piece_at(i), piece_at(i), narrow=cross)] if over_x else []
        nears = [go.make(own.at[:, cols], piece_at(w), wide=near)]
        (soon if over_x else at_step[steps[0]]).append((None, nears[:1]))
        starts = [go.make(own.at[:, cols], piece_at(w), narrow=cross)] if over_x else []
        for d in range(1, column):
            starts.append(go.make(own.at[:, cols], piece_at(w), wide=target(d)))
            ref = piece_at(source(d))
            nears.append(go.make(ref, ref, wide=near))
            at_step[steps[1][(d - 1) * 3 // (column - 1)]].append((starts[-1], [nears[-1]] + passes(source(d))))
        if over_x:
            for d in range(column):
                at_step[steps[2]].append((nears[d], passes(beside(d))))
        own_out.append(pltpu.make_async_copy(own.at[:, cols], piece_at(w), leave.at[slot]))
        return starts

    b = blocks
    weight_starts = (
        spread(up_own, up_all, shared, (0, (4, 4, 4), b + 2), 1)
        + spread(down_own, down_all, shared, (0, (b + 2, b + 2, b + 2), b + 4), 2)
        + spread(up_own, up_all, both, (1, (b + 3, b + 5, b + 6)), 3)
        + spread(down_own, down_all, both, (b + 2, (b + 7, b + 8, b + 9)), 4)
        + out_starts
    )
    at_step[final + 1] += out_late

    mine = pl.ds(pl.multiple_of(n * width, width), width)

    def result(s):
        at = lax.rem((n + 1) * per + s, blocks)
        return pltpu.make_async_remote_copy(
            src_ref=o_box.at[rows_at(at, BLOCK)],
            dst_ref=mixed_ref.at[rows_at(lax.rem(s, per), BLOCK), mine],
            send_sem=mix_send.at[s],
            recv_sem=mix_recv.at[s],
            device_id={"narrow": lax.rem(n + 1 + s // per, narrow)},
            device_id_type=MESH,
        )

    def result_here(s):
        return pltpu.make_async_copy(
            o_box.at[rows_at(n * per + s, BLOCK)], mixed_ref.at[rows_at(s, BLOCK), mine], leave.at[7 + s]
        )

    kept = [
        pltpu.make_async_copy(tok_box, tok_all, leave.at[5]),
        pltpu.make_async_copy(qkv_box, qkv_all, leave.at[6]),
    ]

    @pl.when(step == 0)
    def _():
        for copy in loads:
            copy.start()
        greet(others("wide", w, wide) + others("narrow", n, narrow))
        go.launch(*small, *over)
        for copy in loads[:3]:
            copy.wait()
        qkv_own[...] = stage_qkv[...].astype(BF)
        go.launch(*qkv_far, qkv_near[0], *to_mate)
        for copy, stage, own in zip(
            loads[3:], (stage_out, stage_up, stage_down), (out_own, up_own, down_own)
        ):
            copy.wait()
            own[...] = stage[...].astype(BF)
        go.launch(*weight_starts)
        tok_box[rows_at(n, group_rows), :] = tok[...]
        qkv_box[rows_at(w, wide_rows), :] = qkv_own[...]
        vec_box[pl.ds(w, 1)] = vec[...][None]
        tag_box[pl.ds(n, 1)] = tag[...][None]
        for copy in own_out:
            copy.start()
        for i in small:
            go.arrived(i)
        cols = depth // wide
        for i in range(wide):
            vec_ref[:, i * cols : (i + 1) * cols] = vec_box[i].astype(F32)[:, :cols]
        for i in range(max(pieces, column - 1)):
            if i < column - 1:
                go.arrived(qkv_far[i])
                go.launch(qkv_near[i + 1])
            if i == 0:
                for _, follow in soon:
                    go.launch(*follow)
            if i < pieces:
                go.arrived(over[i])
                go.launch(passed[i])
        for i in qkv_near + to_mate + passed:
            go.arrived(i)
        for copy in kept:
            copy.start()

    for i in range(1, final + 1):
        if at_step[i]:

            @pl.when(step == i)
            def _():
                for arrival, follow in at_step[i]:
                    if arrival is not None:
                        go.arrived(arrival)
                    go.launch(*follow)

    @pl.when((step > 0) & (step <= blocks))
    def _():
        block = step - 1
        at = rows_at(block, BLOCK)
        marks = tag_box[pl.ds(block // per, 1), :, pl.ds(pl.multiple_of(lax.rem(block, per) * BLOCK, BLOCK), BLOCK)]
        marks = marks[0].astype(F32)
        seg_ref[pl.ds(block, 1)] = marks[0:1][None]
        marks = marks.T
        tag_ref[at, :] = jnp.where(marks[:, 1:2] == 1.0, marks[:, 0:1], -1.0)
        slot = lax.broadcasted_iota(jnp.int32, (BLOCK, 128), 1).astype(F32)
        spot = (slot == marks[:, 2:3]) | (slot == 14 + marks[:, 3:4]) | (slot == 28 + marks[:, 4:5])
        angles = lax.dot_general(
            jnp.where(spot, 1.0, 0.0),
            table[...],
            (((1,), (0,)), ((), ())),
            precision=lax.Precision.HIGHEST,
            preferred_element_type=F32,
        )
        turn_ref[at, :] = angles
        cosine, sine = angles[:, :128], angles[:, 128:]
        unit, _ = norm_parts(tok_box[at, :].astype(F32))
        normed = (unit * vec_ref[0:1, :] + vec_ref[1:2, :]).astype(BF)
        norm_ref[...] = normed
        proj = dot(normed, qkv_box[...], 1, 0)
        parts = [proj[:, i * width : (i + 1) * width] + vec_ref[2 + i : 3 + i, mine] for i in range(3)]
        q_ref[at, :] = turn(parts[0], cosine, sine, head_dim // 2, 1).astype(BF)
        k_ref[at, :] = turn(parts[1], cosine, sine, head_dim // 2, 1).astype(BF)
        v_ref[at, :] = parts[2].astype(BF)
        values_turned[:, at] = parts[2].T.astype(BF)

    @pl.when(step > blocks)
    def _():
        place = step - blocks - 1
        block = lax.rem((n + 1) * per + place, blocks)
        at = rows_at(block, BLOCK)
        query = q_ref[at, :] * jnp.asarray(head_dim**-0.5, BF)
        seg = seg_ref[pl.ds(block, 1)][0]
        masked_query = [
            jnp.where(head_lanes(query.shape, h, head_dim), query, jnp.zeros_like(query)) for h in range(heads)
        ]
        acc[...] = jnp.zeros_like(acc)
        peak[...] = jnp.full_like(peak, -1e30)
        total[...] = jnp.zeros_like(total)

        def body(j, carry):
            start = pl.multiple_of(j * BLOCK, BLOCK)
            key = k_ref[pl.ds(start, BLOCK), :]
            allowed = tag_ref[pl.ds(start, BLOCK), :] == seg
            scores = [jnp.where(allowed, dot(key, masked_query[h], 1, 1), -1e30) for h in range(heads)]
            for h in range(heads):
                lines = slice(h * head_dim, (h + 1) * head_dim)
                old = peak[h : h + 1, :]
                new = jnp.maximum(old, jnp.max(scores[h], axis=0, keepdims=True))
                probs = jnp.exp(scores[h] - new)
                keep = jnp.exp(old - new)
                peak[h : h + 1, :] = new
                total[h : h + 1, :] = total[h : h + 1, :] * keep + jnp.sum(probs, axis=0, keepdims=True)
                value = values_turned[lines, pl.ds(start, BLOCK)]
                acc[lines, :] = acc[lines, :] * keep + dot(value, probs.astype(BF), 1, 0)
            return carry

        low, high = meeting(block, blocks)
        lax.fori_loop(low, high, body, 0)
        parts = [acc[h * head_dim : (h + 1) * head_dim, :] / total[h : h + 1, :] for h in range(heads)]
        out = jnp.concatenate(parts, axis=0).T.astype(BF)
        o_ref[at, :] = out
        o_box[at, :] = out
        lse_ref[pl.ds(block, 1)] = (peak[...] + jnp.log(jnp.maximum(total[...], 1e-30)))[None]

        @pl.when(place < blocks - per)
        def _():
            result(place).start()

    @pl.when(step == final)
    def _():
        for s in range(per):
            result_here(s).start()
        for arrival, follow in at_step[final + 1]:
            go.arrived(arrival)
            go.launch(*follow)
        for copy in own_out + kept:
            copy.wait()
        for s in range(blocks - per):
            result(s).wait()
        for s in range(per):
            result_here(s).wait()
        go.finish()


def forward_call(tok, vec, tag, table, weights, head_dim, wide, narrow):
    qkv, out, up, down = weights
    group_rows, depth = tok.shape
    rows = group_rows * narrow
    width = depth // narrow
    heads = width // head_dim
    blocks = rows // BLOCK
    column = wide // 2
    size = qkv.shape[0]
    half = up.shape[1] // 2
    copies = (wide - 1) + (narrow - 1) + 12 + (2 * column - 1)
    copies += 2 + 3 * (column - 1) + column + 2 * (2 * (2 * column - 1) + 2 * column)
    whole = lambda a: pl.BlockSpec(a.shape, lambda i: (0,) * len(a.shape), pipeline_mode=pl.Buffered(1))
    anywhere = pl.BlockSpec(memory_space=pl.ANY)
    shaped = jax.ShapeDtypeStruct
    head_rows = shaped((rows, width), BF)
    inside = [
        head_rows, head_rows, head_rows, shaped((rows, 256), F32), shaped((rows, depth), BF), shaped((16, depth), F32),
        shaped((blocks, 1, BLOCK), F32), shaped((rows, 1), F32), head_rows, shaped((blocks, 8, BLOCK), F32),
    ]
    inside_specs = [whole(a) for a in inside]
    inside_specs[4] = pl.BlockSpec((BLOCK, depth), lambda i: (jnp.minimum(jnp.maximum(i - 1, 0), blocks - 1), 0))
    outside = [
        shaped((rows, depth), BF), shaped((depth, 3 * width), BF), shaped((group_rows, depth), BF),
        shaped((depth, depth), BF), shaped((depth, half), BF), shaped((depth, half), BF),
    ]
    small = [(size, 3 * width), (size, depth // 2), (size, half), (size, half)]
    return pl.pallas_call(
        functools.partial(forward_kernel, heads, head_dim, wide, narrow),
        grid=(2 * blocks + 1,),
        in_specs=[whole(a) for a in (tok, vec, tag, table)] + [anywhere] * 4,
        out_specs=inside_specs + [anywhere] * 6,
        out_shape=inside + outside,
        scratch_shapes=[
            pltpu.VMEM((wide,) + vec.shape, BF),
            pltpu.VMEM((narrow,) + tag.shape, jnp.int32),
            pltpu.VMEM((rows, depth), BF),
            pltpu.VMEM((depth, 3 * width), BF),
        ]
        + [pltpu.VMEM(shape, BF) for shape in small]
        + [pltpu.VMEM(shape, F32) for shape in small]
        + [
            pltpu.VMEM((width, rows), BF),
            pltpu.VMEM((width, BLOCK), F32),
            pltpu.VMEM((8, BLOCK), F32),
            pltpu.VMEM((8, BLOCK), F32),
            pltpu.VMEM((rows, width), BF),
            pltpu.SemaphoreType.DMA((copies,)),
            pltpu.SemaphoreType.DMA((copies,)),
            pltpu.SemaphoreType.DMA((blocks,)),
            pltpu.SemaphoreType.DMA((blocks,)),
            pltpu.SemaphoreType.DMA((6,)),
            pltpu.SemaphoreType.DMA((7 + blocks // narrow,)),
        ],
        compiler_params=pltpu.CompilerParams(
            collective_id=3, has_side_effects=True, vmem_limit_bytes=48 * 1024 * 1024
        ),
        cost_estimate=pl.CostEstimate(
            flops=heads * rows * rows * width * 4, bytes_accessed=rows * width * 8, transcendentals=heads * rows * rows
        ),
        name="attention_forward",
    )(tok, vec, tag, table, qkv, out, up, down)


class Scatter:
    def __init__(self, go, wide, narrow, split, part, near_in, own, far_out, far_in, box, local, *extra):
        w, self.n = lax.axis_index("wide"), lax.axis_index("narrow")
        self.go, self.column, self.split = go, wide // 2, split
        self.near_in, self.own, self.far_out, self.far_in, self.box = near_in, own, far_out, far_in, box
        z, y, x = w // 2, lax.rem(w, 2), self.n // 2
        near, mate, cross = w + 1 - 2 * y, self.n + 1 - 2 * lax.rem(self.n, 2), lax.rem(self.n + 2, narrow)
        size, cols = part.shape[0] // wide, box.shape[2]
        towards = [lax.rem(z + d, self.column) for d in range(1, self.column + 1)]
        theirs, ours = [to * 2 + 1 - y for to in towards], [to * 2 + y for to in towards]
        here = pl.ds(pl.multiple_of(x * cols, cols), cols) if split else pl.ds(0, cols)
        self.loads = [
            pltpu.make_async_copy(part.at[rows_at(i, size), here], own.at[k], local.at[k])
            for k, i in enumerate(ours + theirs if split else ours)
        ]
        self.zero = []
        if split:
            self.cross_in, self.out = extra
            there = pl.ds(pl.multiple_of((1 - x) * cols, cols), cols)
            order = list(enumerate(ours + theirs))
            order = order[self.column :] + order[: self.column]
            self.zero = {
                k: go.make(part.at[rows_at(i, size), there], self.cross_in.at[k], narrow=cross) for k, i in order
            }
        self.first = [
            go.make(self.out.at[k] if split else part.at[rows_at(i, size)], near_in.at[k], wide=near)
            for k, i in enumerate(theirs)
        ]
        self.second = [go.make(far_out.at[k], far_in.at[k], wide=i) for k, i in enumerate(ours[:-1])]
        self.over = go.make(box.at[self.n], box.at[self.n], narrow=cross)
        self.beside = go.make(box.at[self.n], box.at[self.n], narrow=mate)
        self.passed = go.make(box.at[cross], box.at[cross], narrow=mate)

    def load(self):
        for copy in self.loads:
            copy.start()
        if self.split:
            self.go.launch(*self.zero.values())

    def summed(self, k):
        self.loads[k].wait()
        value = self.own[k].astype(F32)
        if self.split:
            self.go.arrived(self.zero[k])
            value = value + self.cross_in[k].astype(F32)
        return value

    def send(self, k):
        if self.split:
            self.out[k] = self.summed(self.column + k).astype(BF)
        self.go.launch(self.first[k])

    def relay(self, k):
        self.go.arrived(self.first[k])
        if k < self.column - 1:
            self.far_out[k] = (self.summed(k) + self.near_in[k].astype(F32)).astype(BF)
            self.go.launch(self.second[k])

    def total(self):
        value = self.summed(self.column - 1) + self.near_in[self.column - 1].astype(F32)
        for k in range(self.column - 1):
            self.go.arrived(self.second[k])
            value = value + self.far_in[k].astype(F32)
        self.box[pl.ds(self.n, 1)] = value.astype(BF)[None]
        self.go.launch(self.over, self.beside)

    def share(self):
        self.go.arrived(self.over)
        self.go.launch(self.passed)

    @staticmethod
    def copies(wide, split):
        return 2 * (wide // 2) - 1 + 3 + (wide if split else 0)

    @staticmethod
    def scratch(wide, narrow, rows, cols, split):
        column, size = wide // 2, rows // wide
        cols = cols // 2 if split else cols
        many = wide if split else column
        sizes = [column, many, column - 1, column - 1, narrow]
        first = [pltpu.VMEM((count, size, cols), BF) for count in sizes] + [pltpu.SemaphoreType.DMA((many,))]
        return first + ([pltpu.VMEM((count, size, cols), BF) for count in (wide, column)] if split else [])


def square_sum(value):
    return jnp.sum(jnp.sum(value * value, axis=0, keepdims=True), axis=1, keepdims=True)


def backward_kernel(
    heads, head_dim, wide, narrow,
    q_ref, k_ref, v_ref, o_ref, g_ref, lse_ref, seg_ref, tag_ref, turn_ref, part_out, part_down, part_up,
    grads_out, shards_out, shards_down, shards_up, squares_out,
    q_heads, g_heads, delta, grad_query, send, recv, *boxes,
):
    step = pl.program_id(0)
    rows, width = q_ref.shape
    blocks = rows // BLOCK
    last = blocks - 1
    scale = head_dim**-0.5
    half = head_dim // 2
    go = Copies(send, recv)
    column = wide // 2
    outs = Scatter(go, wide, narrow, False, part_out, *boxes[:6])
    ups = Scatter(go, wide, narrow, False, part_up, *boxes[6:12])
    downs = Scatter(go, wide, narrow, True, part_down, *boxes[12:])

    @pl.when(step == 0)
    def _():
        w, n = lax.axis_index("wide"), lax.axis_index("narrow")
        z, y = w // 2, lax.rem(w, 2)
        greet(
            [{"wide": w + 1 - 2 * y}]
            + [{"wide": lax.rem(z + d, column) * 2 + y} for d in range(1, column)]
            + [{"narrow": n + 1 - 2 * lax.rem(n, 2)}, {"narrow": lax.rem(n + 2, narrow)}]
        )
        for k in range(column):
            ups.send(k)
        for scatter in (downs, ups, outs):
            scatter.load()

    part = lambda i: range(column * i // 4, column * (i + 1) // 4)
    plan = {
        2: [(ups.relay, part(0))],
        4: [(ups.relay, part(1))],
        5: [(downs.send, range(column // 2))],
        6: [(ups.relay, part(2))],
        7: [(downs.send, range(column // 2, column))],
        8: [(ups.relay, part(3)), (outs.send, range(column))],
        10: [(downs.relay, part(0))],
        11: [(downs.relay, part(1)), (ups.total, None)],
        12: [(downs.relay, part(2))],
        13: [(downs.relay, part(3)), (ups.share, None)],
        14: [(outs.relay, range(column // 2))],
        15: [(outs.relay, range(column // 2, column)), (downs.total, None)],
    }

    def act(i):
        for action, ks in plan[i]:
            for k in [None] if ks is None else ks:
                action() if k is None else action(k)

    for i in range(0, 2 * blocks, 2):
        if i in plan:

            @pl.when(step == i // 2)
            def _():
                act(i)

    @pl.when(step == 0)
    def _():
        grad_query[...] = jnp.zeros_like(grad_query)
        row = lax.broadcasted_iota(jnp.int32, (8, width), 0)
        lane = lax.broadcasted_iota(jnp.int32, (8, width), 1)
        pick = jnp.where(lane // head_dim == row, 1.0, 0.0)

        def prepare(i, carry):
            at = pl.ds(pl.multiple_of(i * BLOCK, BLOCK), BLOCK)
            query = q_ref[at, :] * jnp.asarray(scale, BF)
            grad = g_ref[at, :]
            for h in range(heads):
                lanes = head_lanes(query.shape, h, head_dim)
                q_heads[h, at, :] = jnp.where(lanes, query, jnp.zeros_like(query))
                g_heads[h, at, :] = jnp.where(lanes, grad, jnp.zeros_like(grad))
            product = grad.astype(F32) * o_ref[at, :].astype(F32)
            delta[pl.ds(i, 1)] = lax.dot_general(
                pick,
                product,
                (((1,), (1,)), ((), ())),
                precision=lax.Precision.HIGHEST,
                preferred_element_type=F32,
            )[None]
            return carry

        lax.fori_loop(0, blocks, prepare, 0)

    key = k_ref[...]
    value = v_ref[...]
    tag = tag_ref[...]
    masked_key = [jnp.where(head_lanes(key.shape, h, head_dim), key, jnp.zeros_like(key)) for h in range(heads)]

    def body(i, carry):
        for half_step in range(1, 2 * blocks, 2):
            if half_step in plan:

                @pl.when((step == half_step // 2) & (i == blocks // 2))
                def _():
                    act(half_step)

        grad_key, grad_value = carry
        at = pl.ds(pl.multiple_of(i * BLOCK, BLOCK), BLOCK)
        allowed = tag == seg_ref[pl.ds(i, 1), :]
        lse = lse_ref[pl.ds(i, 1)][0]
        dlt = delta[pl.ds(i, 1)][0]
        total = None
        for h in range(heads):
            query = q_heads[h, at, :]
            grad = g_heads[h, at, :]
            scores = dot(key, query, 1, 1)
            probs = jnp.where(allowed, jnp.exp(scores - lse[h : h + 1, :]), 0.0)
            grad_probs = dot(value, grad, 1, 1)
            grad_scores = (probs * (grad_probs - dlt[h : h + 1, :])).astype(BF)
            grad_value = grad_value + dot(probs.astype(BF), grad, 1, 0)
            grad_key = grad_key + dot(grad_scores, query, 1, 0)
            term = dot(grad_scores, masked_key[h], 0, 0)
            total = term if total is None else total + term
        grad_query[at, :] += total
        return grad_key, grad_value

    zero = jnp.zeros((BLOCK, width), F32)
    low, high = meeting(step, blocks)
    grad_key, grad_value = lax.fori_loop(low, high, body, (zero, zero))
    here = pl.ds(pl.multiple_of(step * BLOCK, BLOCK), BLOCK)
    cosine, sine = turn_ref[here, :128], turn_ref[here, 128:]
    grads_out[here, width : 2 * width] = turn(grad_key, cosine, sine, half, -1).astype(BF)
    grads_out[here, 2 * width :] = grad_value.astype(BF)

    @pl.when(step == last)
    def _():
        downs.share()
        outs.total()

        def finish(i, carry):
            at = pl.ds(pl.multiple_of(i * BLOCK, BLOCK), BLOCK)
            grads = grad_query[at, :] * scale
            grads_out[at, :width] = turn(grads, turn_ref[at, :128], turn_ref[at, 128:], half, -1).astype(BF)
            return carry

        lax.fori_loop(0, blocks, finish, 0)
        outs.share()
        go.finish()
        squares = jnp.zeros((1, 1), F32)
        for box in (outs.box, ups.box):
            for i in range(2):
                squares += square_sum(box[i].astype(F32) + box[i + 2].astype(F32))
        for i in range(narrow):
            squares += square_sum(downs.box[i].astype(F32))
        squares_out[...] = jnp.broadcast_to(squares, squares_out.shape)
        shards_out[...] = outs.box[...]
        shards_down[...] = downs.box[...]
        shards_up[...] = ups.box[...]


def backward_call(q, k, v, o, g, lse, seg_rows, tag_col, turns, part_out, part_down, part_up, head_dim, wide, narrow):
    rows, width = q.shape
    heads = width // head_dim
    blocks = rows // BLOCK
    whole = lambda a: pl.BlockSpec(a.shape, lambda i: (0,) * len(a.shape), pipeline_mode=pl.Buffered(1))
    block = pl.BlockSpec((BLOCK, width), lambda i: (i, 0))
    anywhere = pl.BlockSpec(memory_space=pl.ANY)
    depth = part_up.shape[0]
    results = [
        jax.ShapeDtypeStruct((rows, 3 * width), BF),
        jax.ShapeDtypeStruct((narrow, depth // wide, part_out.shape[1]), BF),
        jax.ShapeDtypeStruct((narrow, depth // wide, part_down.shape[1] // 2), BF),
        jax.ShapeDtypeStruct((narrow, depth // wide, part_up.shape[1]), BF),
        jax.ShapeDtypeStruct((8, 128), F32),
    ]
    copies = 2 * Scatter.copies(wide, False) + Scatter.copies(wide, True)
    return pl.pallas_call(
        functools.partial(backward_kernel, heads, head_dim, wide, narrow),
        grid=(blocks,),
        in_specs=[
            whole(q), block, block, whole(o), whole(g), whole(lse), whole(seg_rows),
            pl.BlockSpec((BLOCK, 1), lambda i: (i, 0)),
            whole(turns), anywhere, anywhere, anywhere,
        ],
        out_specs=[whole(a) for a in results],
        out_shape=results,
        scratch_shapes=[
            pltpu.VMEM((heads, rows, width), BF),
            pltpu.VMEM((heads, rows, width), BF),
            pltpu.VMEM((blocks, 8, BLOCK), F32),
            pltpu.VMEM((rows, width), F32),
            pltpu.SemaphoreType.DMA((copies,)),
            pltpu.SemaphoreType.DMA((copies,)),
        ]
        + Scatter.scratch(wide, narrow, depth, part_out.shape[1], False)
        + Scatter.scratch(wide, narrow, depth, part_up.shape[1], False)
        + Scatter.scratch(wide, narrow, depth, part_down.shape[1], True),
        compiler_params=pltpu.CompilerParams(
            collective_id=4, has_side_effects=True, vmem_limit_bytes=60 * 1024 * 1024
        ),
        cost_estimate=pl.CostEstimate(
            flops=heads * rows * rows * width * 7, bytes_accessed=rows * width * 20, transcendentals=heads * rows * rows
        ),
        name="attention_backward",
    )(q, k, v, o, g, lse, seg_rows, tag_col, turns, part_out, part_down, part_up)


def norm_parts(values):
    center = values - jnp.mean(values, axis=-1, keepdims=True)
    inverse = lax.rsqrt(jnp.mean(center * center, axis=-1, keepdims=True) + 1e-06)
    return center * inverse, inverse


def norm_back(grads, gain, unit, inverse):
    scaled = grads * gain
    return inverse * (
        scaled - jnp.mean(scaled, axis=-1, keepdims=True) - unit * jnp.mean(scaled * unit, axis=-1, keepdims=True)
    )


def adamw(param, grad, first, second, clip, rate, decay, fix_first, fix_second):
    clipped = grad * clip
    moment = 0.9 * first + 0.1 * clipped
    square = 0.999 * second + 0.001 * clipped * clipped
    direction = moment / fix_first / (jnp.sqrt(square / fix_second) + 1e-08)
    return (param - rate * (direction + decay * param), moment, square)


def on_device(
    tokens, cotangent, segment_ids, key_keep, patch_coords, step_count,
    weight_qkv, weight_out, weight_up, weight_down, vectors,
    first_qkv, first_out, first_up, first_down, first_vectors,
    second_qkv, second_out, second_up, second_down, second_vectors,
):
    rows, width = tokens.shape
    hidden = weight_up.shape[1]
    head_dim = width // HEADS
    narrow = lax.axis_size("narrow")
    wide = lax.axis_size("wide")
    shard_rows = width // wide
    me = lax.axis_index("narrow")
    side = me % 2
    mine = width // narrow
    half_hidden = hidden // 2
    group = rows * narrow

    def mate(value):
        return lax.ppermute(value, "narrow", [(i, i ^ 1) for i in range(narrow)])

    def across(value):
        return lax.ppermute(value, "narrow", [(i, i ^ 2) for i in range(narrow)])

    def take(value, start, size, axis=1):
        return lax.dynamic_slice_in_dim(value, start, size, axis)

    shard_cols = vectors.shape[1]
    vec_shard = jnp.pad(vectors.astype(BF), ((0, 16 - vectors.shape[0]), (0, -shard_cols % 128)))
    tag = jnp.concatenate([segment_ids[None], key_keep[None], patch_coords, patch_coords], axis=0)
    (
        query, keys, values, turns, normed1_all, vec, seg_rows, tag_col, mixed_mine, lse,
        tokens_all, qkv_w, mixed, out_w, up_w, down_w,
    ) = forward_call(
        tokens, vec_shard, tag, rotary_table(head_dim), (weight_qkv, weight_out, weight_up, weight_down),
        head_dim, wide, narrow,
    )
    vec = vec[: vectors.shape[0]]
    xin = tokens.astype(F32)
    unit1, inverse1 = norm_parts(xin)
    cot_pair = jnp.concatenate([cotangent, mate(cotangent)], axis=0)

    resid = xin + (dot(mixed, out_w, 1, 0) + vec[5])
    unit2, inverse2 = norm_parts(resid)
    normed2 = (unit2 * vec[6] + vec[7]).astype(BF)
    normed2_pair = jnp.concatenate([normed2, mate(normed2)], axis=0)
    up_bias = take(vec[9:].reshape(1, -1), side * half_hidden, half_hidden)
    up_pre = dot(normed2_pair, up_w, 1, 0) + up_bias
    erf_part = 0.5 * (1.0 + lax.erf(up_pre * (0.5**0.5)))
    act = (up_pre * erf_part).astype(BF)
    slope = erf_part + up_pre * (jnp.exp(-0.5 * up_pre * up_pre) * ((2.0 * jnp.pi) ** -0.5))
    part_down = dot(cot_pair, act, 0, 0).astype(BF)
    down_part = dot(act, down_w, 1, 1)
    down = down_part[:rows] + mate(down_part[rows:])
    layer_out = (resid + (down + vec[8])).astype(BF)

    grad_up_act = (dot(cot_pair, down_w, 1, 0) * slope).astype(BF)
    part_up = dot(normed2_pair, grad_up_act, 0, 0).astype(BF)
    grad_normed2_part = dot(grad_up_act, up_w, 1, 1)
    grad_normed2 = grad_normed2_part[:rows] + mate(grad_normed2_part[rows:])
    cot = cotangent.astype(F32)
    grad_resid = cot + norm_back(grad_normed2, vec[6], unit2, inverse2)
    grad_branch = grad_resid.astype(BF)
    grad_mixed = dot(grad_branch, out_w, 1, 1).astype(BF)
    part_out = dot(mixed, grad_branch, 0, 0)
    own_out = take(part_out, side * (width // 2), width // 2)
    other_out = take(part_out, (1 - side) * (width // 2), width // 2)
    part_out = (own_out + mate(other_out.astype(BF)).astype(F32)).astype(BF)

    grad_mixed_mine = lax.all_to_all(grad_mixed, "narrow", 1, 0, tiled=True)
    grad_proj, shards_out, shards_down, shards_up, squares = backward_call(
        query, keys, values, mixed_mine, grad_mixed_mine, lse, seg_rows[:, 0], tag_col, turns, part_out, part_down, part_up, head_dim, wide, narrow,
    )
    part_qkv = dot(normed1_all, grad_proj, 0, 0).astype(BF)

    proj_sums = jnp.sum(grad_proj.astype(F32), axis=0).reshape(3, mine)
    proj_rows = lax.dynamic_update_slice(jnp.zeros((3, width), F32), proj_sums, (0, me * mine))
    up_sums = jnp.sum(grad_up_act.astype(F32), axis=0)
    up_rows = lax.dynamic_update_slice(jnp.zeros((hidden,), F32), up_sums, (side * half_hidden,))
    vector_part = jnp.concatenate(
        [
            jnp.zeros((2, width), F32),
            proj_rows,
            jnp.sum(grad_branch.astype(F32), axis=0)[None],
            jnp.sum(grad_normed2 * unit2, axis=0)[None],
            jnp.sum(grad_normed2, axis=0)[None],
            jnp.sum(cot, axis=0)[None],
            up_rows.reshape(hidden // width, width),
            jnp.zeros((16 - vectors.shape[0], width), F32),
        ],
        axis=0,
    )
    grad_normed1, total_qkv, vector_total, square_total = tail_call(
        part_qkv, grad_proj, qkv_w, tokens_all, vector_part, squares, wide, narrow
    )
    grad_tokens = (grad_resid + norm_back(grad_normed1, vec[0], unit1, inverse1)).astype(BF)

    def join(shards):
        shards = shards.astype(F32)
        return jnp.concatenate([shards[0] + shards[2], shards[1] + shards[3]], axis=1)

    total_up = join(shards_up)
    total_down = jnp.concatenate([shards_down[i] for i in (0, 2, 1, 3)], axis=1).astype(F32)
    total_out = join(shards_out)
    total_qkv = total_qkv.astype(F32)
    grad_norm = jnp.sqrt(square_total[0, 0])
    clip = 1.0 / jnp.maximum(grad_norm, 1.0)
    count = step_count[0].astype(F32)
    rate = 0.4 * count / (count + 4.0)
    decay = 0.04 + 0.018 * count
    fix_first = 1.0 - jnp.power(0.9, count)
    fix_second = 1.0 - jnp.power(0.999, count)
    grad_vectors = vector_total[: vectors.shape[0], :shard_rows]

    def update(param, grad, first, second, decay_here):
        return adamw(param, grad, first, second, clip, rate, decay_here, fix_first, fix_second)

    new_qkv = update(weight_qkv, total_qkv, first_qkv, second_qkv, decay)
    new_out = update(weight_out, total_out, first_out, second_out, decay)
    new_up = update(weight_up, total_up, first_up, second_up, decay)
    new_down = update(weight_down, total_down, first_down, second_down, decay)
    new_vectors = update(vectors, grad_vectors, first_vectors, second_vectors, 0.0)
    news = (new_qkv, new_out, new_up, new_down, new_vectors)
    return (layer_out, grad_tokens) + tuple(n[i] for i in range(3) for n in news) + (grad_norm, grad_vectors[8])


def solution(mesh):
    by_token = P(("wide", "narrow"), None)
    ids = P(("wide", "narrow"))
    by_row = P("wide", None)
    by_column = P(None, "wide")
    params = (by_row,) * 4 + (by_column,)
    return jax.shard_map(
        on_device,
        mesh=mesh,
        in_specs=(by_token, by_token, ids, ids, P(None, ("wide", "narrow")), P()) + params * 3,
        out_specs=(by_token, by_token) + params * 3 + (P(), P("wide")),
        check_vma=False,
    )
```

```python
import functools

import jax
import jax.numpy as jnp
from jax import lax
from jax.experimental import pallas as pl
from jax.experimental.pallas import tpu as pltpu
from jax.sharding import PartitionSpec as P

HEADS = 16
BLOCK = 256
BF = jnp.bfloat16
F32 = jnp.float32
MESH = pl.DeviceIdType.MESH


def dot(a, b, ca, cb):
    return lax.dot_general(a, b, (((ca,), (cb,)), ((), ())), preferred_element_type=F32)


def swap_halves(x, half):
    lane = lax.broadcasted_iota(jnp.int32, x.shape, 1)
    width = x.shape[1]
    return jnp.where(
        lane % (2 * half) < half, pltpu.roll(x, width - half, 1), pltpu.roll(x, half, 1)
    )


def turn(x, cosine, sine, half, sign):
    parts = []
    for start in range(0, x.shape[1], 128):
        part = x[:, start : start + 128]
        other = swap_halves(part, half) * sine
        parts.append(part * cosine + other if sign > 0 else part * cosine - other)
    return jnp.concatenate(parts, axis=1)


def rotary_table(head_dim):
    half = head_dim // 2
    lane = jnp.arange(128)
    pair = lane % half
    rates = jnp.power(10000.0, -(pair // 3).astype(F32) / ((half + 2) // 3))
    row = jnp.arange(128)
    axis = row // 14
    value = (row % 14).astype(F32)
    live = (axis[:, None] == (pair % 3)[None, :]) & (row[:, None] < 42)
    angle = value[:, None] * rates[None, :]
    signs = jnp.where(lane % head_dim < half, -1.0, 1.0)
    return jnp.concatenate(
        [
            jnp.where(live, jnp.cos(angle), 0.0),
            jnp.where(live, jnp.sin(angle) * signs[None, :], 0.0),
        ],
        axis=1,
    )


def greet(targets):
    barrier = pltpu.get_barrier_semaphore()
    for target in targets:
        pl.semaphore_signal(barrier, inc=1, device_id=target, device_id_type=MESH)
    pl.semaphore_wait(barrier, len(targets))


def others(name, index, size):
    return [{name: lax.rem(index + d, size)} for d in range(1, size)]


class Copies:
    def __init__(self, send, recv):
        self.send, self.recv, self.all = send, recv, []

    def make(self, src, dst, **target):
        i = len(self.all)
        copy = pltpu.make_async_remote_copy(
            src_ref=src, dst_ref=dst, send_sem=self.send.at[i], recv_sem=self.recv.at[i],
            device_id=target, device_id_type=MESH,
        )
        self.all.append([copy, False])
        return i

    def launch(self, *indices):
        for i in indices:
            self.all[i][0].start()

    def start(self, src, dst, **target):
        i = self.make(src, dst, **target)
        self.launch(i)
        return i

    def arrived(self, i):
        if not self.all[i][1]:
            self.all[i][0].wait_recv()
            self.all[i][1] = True

    def finish(self):
        for i in range(len(self.all)):
            self.arrived(i)
        for copy, _ in self.all:
            copy.wait_send()


def rows_at(index, size):
    return pl.ds(pl.multiple_of(index * size, size), size)


def tail_kernel(
    wide, narrow, normed, grad_proj, weight_in, tok_in, vec_in, squares_in, normed_out, qkv_out, vec_out, square_out,
    partial, mate_in, cross_out, cross_in, near_in, far_out, far_in, shards, vec_box, sums,
    slices, slice_box, square_box, part, weight, tok, send, recv, local,
):
    w, n = lax.axis_index("wide"), lax.axis_index("narrow")
    column = wide // 2
    z, y = w // 2, lax.rem(w, 2)
    x, c = n // 2, lax.rem(n, 2)
    near, mate, cross = w + 1 - 2 * y, n + 1 - 2 * c, lax.rem(n + 2, narrow)
    wide_rows, group_rows = part.shape[0] // wide, normed_out.shape[0]
    towards = [lax.rem(z + d, column) for d in range(1, column + 1)]
    loads = [
        pltpu.make_async_copy(weight_in, weight, local.at[0]),
        pltpu.make_async_copy(tok_in, tok, local.at[1]),
    ]
    for copy in loads:
        copy.start()
    greet(others("wide", w, wide) + others("narrow", n, narrow))
    go = Copies(send, recv)
    depth, chunk = part.shape[0], 128
    sent = lambda k: go.make(part.at[rows_at(towards[k] * 2 + 1 - y, wide_rows)], near_in.at[k], wide=near)
    first = [sent(k) for k in range(column)]
    one_each = wide_rows == chunk

    def rows_of(index):
        at = rows_at(index, chunk)
        part[at, :] = dot(normed[:, at], grad_proj[...], 0, 0).astype(BF)

    if one_each:
        for k in range(column):
            rows_of(towards[k] * 2 + 1 - y)
            go.launch(first[k])

        def ours(k, carry):
            rows_of(lax.rem(z + 1 + k, column) * 2 + y)
            return carry

        lax.fori_loop(0, column, ours, 0)
    else:

        def each(index, carry):
            rows_of(index)
            return carry

        lax.fori_loop(0, depth // chunk, each, 0)
        go.launch(*first)
    for copy in loads:
        copy.wait()

    seconds, kept = [], []

    def relay(k):
        go.arrived(first[k])
        value = part[rows_at(towards[k] * 2 + y, wide_rows), :].astype(F32) + near_in[k].astype(F32)
        if k < column - 1:
            far_out[k] = value.astype(BF)
            seconds.append(go.start(far_out.at[k], far_in.at[k], wide=towards[k] * 2 + y))
        else:
            kept.append(value)

    sums[...] = jnp.zeros_like(sums)
    owners = [(1 - x) * 2 + 1 - c, (1 - x) * 2 + c, x * 2 + 1 - c, n]
    half = group_rows // 2
    mates, overs = [], []
    for slot, owner in enumerate(owners):

        def body(i, carry):
            at = pl.ds(pl.multiple_of(owner * group_rows + i * BLOCK, BLOCK), BLOCK)
            here = pl.ds(pl.multiple_of(i * BLOCK, BLOCK), BLOCK)
            grads = dot(grad_proj[at, :], weight[...], 1, 1)
            unit, _ = norm_parts(tok[at, :].astype(F32))
            sums[0:1, :] += jnp.sum(grads * unit, axis=0, keepdims=True)
            sums[1:2, :] += jnp.sum(grads, axis=0, keepdims=True)
            if slot < 3:
                partial[slot, here, :] = grads.astype(BF)
            else:
                normed_out[here, :] = grads
            return carry

        lax.fori_loop(0, group_rows // BLOCK, body, 0)
        if slot == 0:
            mates.append(go.start(partial.at[0], mate_in.at[0], narrow=mate))
        if slot == 2:
            mates.append(go.start(partial.at[2], mate_in.at[1], narrow=mate))
        if slot == 1:
            go.arrived(mates[0])
            for p in range(2):
                at = pl.ds(p * half, half)
                cross_out[at, :] = (partial[1, at, :].astype(F32) + mate_in[0, at, :].astype(F32)).astype(BF)
                overs.append(go.start(cross_out.at[at], cross_in.at[at], narrow=cross))
        for k in range(column * slot // 4, column * (slot + 1) // 4):
            if k < column - 1:
                relay(k)

    vec_box[pl.ds(n, 1)] = vec_in[...][None]
    vec_box[pl.ds(n, 1), 0:2, :] = sums[0:2, :][None]
    vecs = [go.start(vec_box.at[n], vec_box.at[n], narrow=lax.rem(n + d, narrow)) for d in range(1, narrow)]
    for i in vecs:
        go.arrived(i)
    group = vec_box[0]
    for i in range(1, narrow):
        group = group + vec_box[i]
    cols = group.shape[1] // wide
    slices[...] = jnp.zeros_like(slices)
    for i in range(wide):
        slices[i, :, :cols] = group[:, i * cols : (i + 1) * cols]
    peers = [lax.rem(w + d, wide) for d in range(1, wide)]
    pieces = [go.start(slices.at[peer], slice_box.at[w], wide=peer) for peer in peers]
    slice_box[pl.ds(w, 1)] = slices[pl.ds(w, 1)]
    relay(column - 1)
    total = kept[0]
    for k in range(column - 1):
        go.arrived(seconds[k])
        total = total + far_in[k].astype(F32)
    shards[pl.ds(n, 1)] = total.astype(BF)[None]
    over = go.start(shards.at[n], shards.at[n], narrow=cross)
    beside = go.start(shards.at[n], shards.at[n], narrow=mate)

    go.arrived(mates[1])
    for p in range(2):
        go.arrived(overs[p])
        at = pl.ds(p * half, half)
        normed_out[at, :] += mate_in[1, at, :].astype(F32) + cross_in[at, :].astype(F32)
    for i in pieces:
        go.arrived(i)
    vectors = slice_box[0]
    for i in range(1, wide):
        vectors = vectors + slice_box[i]
    vec_out[...] = vectors

    go.arrived(over)
    passed = go.start(shards.at[cross], shards.at[cross], narrow=mate)
    for i in (beside, passed):
        go.arrived(i)
    squares = square_sum(vectors)
    width = part.shape[1] // 3
    for i in range(narrow):
        shard = shards[i]
        squares += square_sum(shard.astype(F32))
        for j in range(3):
            qkv_out[:, (j * narrow + i) * width : (j * narrow + i + 1) * width] = shard[:, j * width : (j + 1) * width]
    square_box[pl.ds(w, 1)] = (squares_in[...] + squares)[None]
    for peer in peers:
        go.start(square_box.at[w], square_box.at[w], wide=peer)
    go.finish()
    total = square_box[0]
    for i in range(1, wide):
        total = total + square_box[i]
    square_out[...] = total


def tail_call(normed, grad_proj, weight, tok, vec_in, squares_in, wide, narrow):
    depth, cols = weight.shape
    rows = tok.shape[0] // narrow
    wide_rows = depth // wide
    column = wide // 2
    copies = 2 * column - 1 + 2 + (narrow - 1) + 2 + 3 + 2 * (wide - 1)
    vmem = pl.BlockSpec(memory_space=pltpu.VMEM)
    anywhere = pl.BlockSpec(memory_space=pl.ANY)
    return pl.pallas_call(
        functools.partial(tail_kernel, wide, narrow),
        in_specs=[vmem, vmem, anywhere, anywhere, vmem, vmem],
        out_specs=[vmem] * 4,
        out_shape=[
            jax.ShapeDtypeStruct((rows, depth), F32),
            jax.ShapeDtypeStruct((wide_rows, narrow * cols), BF),
            jax.ShapeDtypeStruct((16, 128), F32),
            jax.ShapeDtypeStruct((8, 128), F32),
        ],
        scratch_shapes=[
            pltpu.VMEM((3, rows, depth), BF),
            pltpu.VMEM((2, rows, depth), BF),
            pltpu.VMEM((rows, depth), BF),
            pltpu.VMEM((rows, depth), BF),
            pltpu.VMEM((column, wide_rows, cols), BF),
            pltpu.VMEM((column - 1, wide_rows, cols), BF),
            pltpu.VMEM((column - 1, wide_rows, cols), BF),
            pltpu.VMEM((narrow, wide_rows, cols), BF),
            pltpu.VMEM((narrow,) + vec_in.shape, F32),
            pltpu.VMEM((8, depth), F32),
            pltpu.VMEM((wide, 16, 128), F32),
            pltpu.VMEM((wide, 16, 128), F32),
            pltpu.VMEM((wide, 8, 128), F32),
            pltpu.VMEM((depth, cols), BF),
            pltpu.VMEM((depth, cols), BF),
            pltpu.VMEM(tok.shape, BF),
            pltpu.SemaphoreType.DMA((copies,)),
            pltpu.SemaphoreType.DMA((copies,)),
            pltpu.SemaphoreType.DMA((2,)),
        ],
        compiler_params=pltpu.CompilerParams(
            collective_id=1, has_side_effects=True, vmem_limit_bytes=56 * 1024 * 1024
        ),
        name="tail",
    )(normed, grad_proj, weight, tok, vec_in, squares_in)


CLIP = 784


def head_lanes(shape, head, head_dim):
    lane = lax.broadcasted_iota(jnp.int32, shape, 1)
    return lane // head_dim == head


def meeting(block, blocks):
    before, after = CLIP // BLOCK, -(-2 * CLIP // BLOCK)
    low = before * (block // after)
    high = blocks - (blocks - after) * (1 - jnp.minimum(block // before, 1))
    return low, high


def forward_kernel(
    heads, head_dim, wide, narrow,
    tok, vec, tag, table, qkv_f32, out_f32, up_f32, down_f32,
    q_ref, k_ref, v_ref, turn_ref, norm_ref, vec_ref, seg_ref, tag_ref, o_ref, lse_ref,
    tok_all, qkv_all, mixed_ref, out_all, up_all, down_all,
    vec_box, tag_box, tok_box, qkv_box, qkv_own, out_own, up_own, down_own, stage_qkv, stage_out, stage_up, stage_down,
    values_turned, acc, peak, total, o_box, send, recv, mix_send, mix_recv, local, leave,
):
    step = pl.program_id(0)
    rows, width = q_ref.shape
    depth = tok.shape[1]
    blocks = rows // BLOCK
    per = blocks // narrow
    final = 2 * blocks
    w, n = lax.axis_index("wide"), lax.axis_index("narrow")
    column = wide // 2
    z, y, side = w // 2, lax.rem(w, 2), lax.rem(n, 2)
    near, mate, cross = w + 1 - 2 * y, n + 1 - 2 * side, lax.rem(n + 2, narrow)
    source = lambda d: lax.rem(z - d + column, column) * 2 + y
    target = lambda d: lax.rem(z + d, column) * 2 + y
    beside = lambda d: lax.rem(z - d + column, column) * 2 + 1 - y
    wide_rows, out_half = out_own.shape
    half = up_own.shape[1]
    group_rows = tok.shape[0]

    loads = [
        pltpu.make_async_copy(
            qkv_f32.at[:, pl.ds(pl.multiple_of(i * depth + n * width, width), width)],
            stage_qkv.at[:, pl.ds(i * width, width)],
            local.at[i],
        )
        for i in range(3)
    ] + [
        pltpu.make_async_copy(
            whole.at[:, pl.ds(pl.multiple_of(side * size, size), size)], stage, local.at[3 + i]
        )
        for i, (whole, stage, size) in enumerate(
            [(out_f32, stage_out, out_half), (up_f32, stage_up, half), (down_f32, stage_down, half)]
        )
    ]

    go = Copies(send, recv)
    small = [go.make(vec, vec_box.at[w], wide=lax.rem(w + d, wide)) for d in range(1, wide)]
    small += [go.make(tag, tag_box.at[n], narrow=lax.rem(n + d, narrow)) for d in range(1, narrow)]
    pieces = 4
    piece = group_rows // pieces
    token_rows = lambda i, p: tok_box.at[rows_at(i * pieces + p, piece)]
    own_piece = lambda p: tok.at[pl.ds(p * piece, piece)]
    over = [go.make(own_piece(p), token_rows(n, p), narrow=cross) for p in range(pieces)]
    to_mate = [go.make(own_piece(p), token_rows(n, p), narrow=mate) for p in range(pieces)]
    passed = [go.make(token_rows(cross, p), token_rows(cross, p), narrow=mate) for p in range(pieces)]
    qkv_at = lambda i: qkv_box.at[rows_at(i, wide_rows)]
    qkv_far = [go.make(qkv_own, qkv_at(w), wide=target(d)) for d in range(1, column)]
    qkv_near = [go.make(qkv_own, qkv_at(w), wide=near)]
    qkv_near += [go.make(qkv_at(source(d)), qkv_at(source(d)), wide=near) for d in range(1, column)]

    at_step = [[] for _ in range(final + 2)]
    soon = []
    out_cols = pl.ds(pl.multiple_of(side * out_half, out_half), out_half)
    out_at = lambda i: out_all.at[rows_at(i, wide_rows), out_cols]
    out_near = [go.make(out_own, out_at(w), wide=near)]
    out_starts = [go.make(out_own, out_at(w), narrow=mate)]
    at_step[blocks + 6].append((None, [out_near[0]]))
    out_late = []
    for d in range(1, column):
        out_starts.append(go.make(out_own, out_at(w), wide=target(d)))
        ref = out_at(source(d))
        out_near.append(go.make(ref, ref, wide=near))
        out_late.append((out_starts[-1], [out_near[-1], go.make(ref, ref, narrow=mate)]))
    for d in range(column):
        ref = out_at(beside(d))
        out_late.append((out_near[d], [go.make(ref, ref, narrow=mate)]))

    quarter = half // 4
    shared = pl.ds(pl.multiple_of(n // 2 * quarter, quarter), quarter)
    both = pl.ds(2 * quarter, 2 * quarter)
    own_out = [pltpu.make_async_copy(out_own, out_at(w), leave.at[0])]

    def spread(own, result, cols, steps, slot):
        piece_at = lambda i: result.at[rows_at(i, wide_rows), cols]
        over_x = cols is shared
        passes = lambda i: [go.make(piece_at(i), piece_at(i), narrow=cross)] if over_x else []
        nears = [go.make(own.at[:, cols], piece_at(w), wide=near)]
        (soon if over_x else at_step[steps[0]]).append((None, nears[:1]))
        starts = [go.make(own.at[:, cols], piece_at(w), narrow=cross)] if over_x else []
        for d in range(1, column):
            starts.append(go.make(own.at[:, cols], piece_at(w), wide=target(d)))
            ref = piece_at(source(d))
            nears.append(go.make(ref, ref, wide=near))
            at_step[steps[1][(d - 1) * 3 // (column - 1)]].append((starts[-1], [nears[-1]] + passes(source(d))))
        if over_x:
            for d in range(column):
                at_step[steps[2]].append((nears[d], passes(beside(d))))
        own_out.append(pltpu.make_async_copy(own.at[:, cols], piece_at(w), leave.at[slot]))
        return starts

    b = blocks
    weight_starts = spread(up_own, up_all, shared, (0, (4, 4, 4), b + 2), 1)
    weight_starts += spread(down_own, down_all, shared, (0, (b + 2, b + 2, b + 2), b + 4), 2)
    at_step[6].append((None, spread(up_own, up_all, both, (1, (b + 3, b + 5, b + 6)), 3)))
    at_step[b + 3].append((None, spread(down_own, down_all, both, (b + 2, (b + 7, b + 8, b + 9)), 4)))
    at_step[b + 6].append((None, out_starts))
    at_step[final + 1] += out_late

    mine = pl.ds(pl.multiple_of(n * width, width), width)

    def result(s):
        at = lax.rem((n + 1) * per + s, blocks)
        return pltpu.make_async_remote_copy(
            src_ref=o_box.at[rows_at(at, BLOCK)],
            dst_ref=mixed_ref.at[rows_at(lax.rem(s, per), BLOCK), mine],
            send_sem=mix_send.at[s],
            recv_sem=mix_recv.at[s],
            device_id={"narrow": lax.rem(n + 1 + s // per, narrow)},
            device_id_type=MESH,
        )

    def result_here(s):
        return pltpu.make_async_copy(
            o_box.at[rows_at(n * per + s, BLOCK)], mixed_ref.at[rows_at(s, BLOCK), mine], leave.at[7 + s]
        )

    kept = [
        pltpu.make_async_copy(tok_box, tok_all, leave.at[5]),
        pltpu.make_async_copy(qkv_box, qkv_all, leave.at[6]),
    ]

    @pl.when(step == 0)
    def _():
        for copy in loads:
            copy.start()
        greet(others("wide", w, wide) + others("narrow", n, narrow))
        go.launch(*small, *over)
        for copy in loads[:3]:
            copy.wait()
        qkv_own[...] = stage_qkv[...].astype(BF)
        go.launch(*qkv_far, qkv_near[0], *to_mate)
        for copy, stage, own in zip(
            loads[3:], (stage_out, stage_up, stage_down), (out_own, up_own, down_own)
        ):
            copy.wait()
            own[...] = stage[...].astype(BF)
        go.launch(*weight_starts)
        tok_box[rows_at(n, group_rows), :] = tok[...]
        qkv_box[rows_at(w, wide_rows), :] = qkv_own[...]
        vec_box[pl.ds(w, 1)] = vec[...][None]
        tag_box[pl.ds(n, 1)] = tag[...][None]
        for copy in own_out:
            copy.start()
        for i in small:
            go.arrived(i)
        cols = depth // wide
        for i in range(wide):
            vec_ref[:, i * cols : (i + 1) * cols] = vec_box[i].astype(F32)[:, :cols]
        for i in range(max(pieces, column - 1)):
            if i < column - 1:
                go.arrived(qkv_far[i])
                go.launch(qkv_near[i + 1])
            if i == 0:
                for _, follow in soon:
                    go.launch(*follow)
            if i < pieces:
                go.arrived(over[i])
                go.launch(passed[i])
        for i in qkv_near + to_mate + passed:
            go.arrived(i)
        for copy in kept:
            copy.start()

    for i in range(1, final + 1):
        if at_step[i]:

            @pl.when(step == i)
            def _():
                for arrival, follow in at_step[i]:
                    if arrival is not None:
                        go.arrived(arrival)
                    go.launch(*follow)

    @pl.when((step > 0) & (step <= blocks))
    def _():
        block = step - 1
        at = rows_at(block, BLOCK)
        marks = tag_box[pl.ds(block // per, 1), :, pl.ds(pl.multiple_of(lax.rem(block, per) * BLOCK, BLOCK), BLOCK)]
        marks = marks[0].astype(F32)
        seg_ref[pl.ds(block, 1)] = marks[0:1][None]
        marks = marks.T
        tag_ref[at, :] = jnp.where(marks[:, 1:2] == 1.0, marks[:, 0:1], -1.0)
        slot = lax.broadcasted_iota(jnp.int32, (BLOCK, 128), 1).astype(F32)
        spot = (slot == marks[:, 2:3]) | (slot == 14 + marks[:, 3:4]) | (slot == 28 + marks[:, 4:5])
        angles = lax.dot_general(
            jnp.where(spot, 1.0, 0.0),
            table[...],
            (((1,), (0,)), ((), ())),
            precision=lax.Precision.HIGHEST,
            preferred_element_type=F32,
        )
        turn_ref[at, :] = angles
        cosine, sine = angles[:, :128], angles[:, 128:]
        unit, _ = norm_parts(tok_box[at, :].astype(F32))
        normed = (unit * vec_ref[0:1, :] + vec_ref[1:2, :]).astype(BF)
        norm_ref[...] = normed
        proj = dot(normed, qkv_box[...], 1, 0)
        parts = [proj[:, i * width : (i + 1) * width] + vec_ref[2 + i : 3 + i, mine] for i in range(3)]
        q_ref[at, :] = turn(parts[0], cosine, sine, head_dim // 2, 1).astype(BF)
        k_ref[at, :] = turn(parts[1], cosine, sine, head_dim // 2, 1).astype(BF)
        v_ref[at, :] = parts[2].astype(BF)
        values_turned[:, at] = parts[2].T.astype(BF)

    @pl.when(step > blocks)
    def _():
        place = step - blocks - 1
        block = lax.rem((n + 1) * per + place, blocks)
        at = rows_at(block, BLOCK)
        query = q_ref[at, :] * jnp.asarray(head_dim**-0.5, BF)
        seg = seg_ref[pl.ds(block, 1)][0]
        masked_query = [
            jnp.where(head_lanes(query.shape, h, head_dim), query, jnp.zeros_like(query)) for h in range(heads)
        ]
        acc[...] = jnp.zeros_like(acc)
        peak[...] = jnp.full_like(peak, -1e30)
        total[...] = jnp.zeros_like(total)

        def body(j, carry):
            start = pl.multiple_of(j * BLOCK, BLOCK)
            key = k_ref[pl.ds(start, BLOCK), :]
            allowed = tag_ref[pl.ds(start, BLOCK), :] == seg
            scores = [jnp.where(allowed, dot(key, masked_query[h], 1, 1), -1e30) for h in range(heads)]
            for h in range(heads):
                lines = slice(h * head_dim, (h + 1) * head_dim)
                old = peak[h : h + 1, :]
                new = jnp.maximum(old, jnp.max(scores[h], axis=0, keepdims=True))
                probs = jnp.exp(scores[h] - new)
                keep = jnp.exp(old - new)
                peak[h : h + 1, :] = new
                total[h : h + 1, :] = total[h : h + 1, :] * keep + jnp.sum(probs, axis=0, keepdims=True)
                value = values_turned[lines, pl.ds(start, BLOCK)]
                acc[lines, :] = acc[lines, :] * keep + dot(value, probs.astype(BF), 1, 0)
            return carry

        low, high = meeting(block, blocks)
        lax.fori_loop(low, high, body, 0)
        parts = [acc[h * head_dim : (h + 1) * head_dim, :] / total[h : h + 1, :] for h in range(heads)]
        out = jnp.concatenate(parts, axis=0).T.astype(BF)
        o_ref[at, :] = out
        o_box[at, :] = out
        lse_ref[pl.ds(block, 1)] = (peak[...] + jnp.log(jnp.maximum(total[...], 1e-30)))[None]

        @pl.when(place < blocks - per)
        def _():
            result(place).start()

    @pl.when(step == final)
    def _():
        for s in range(per):
            result_here(s).start()
        for arrival, follow in at_step[final + 1]:
            go.arrived(arrival)
            go.launch(*follow)
        for copy in own_out + kept:
            copy.wait()
        for s in range(blocks - per):
            result(s).wait()
        for s in range(per):
            result_here(s).wait()
        go.finish()


def forward_call(tok, vec, tag, table, weights, head_dim, wide, narrow):
    qkv, out, up, down = weights
    group_rows, depth = tok.shape
    rows = group_rows * narrow
    width = depth // narrow
    heads = width // head_dim
    blocks = rows // BLOCK
    column = wide // 2
    size = qkv.shape[0]
    half = up.shape[1] // 2
    copies = (wide - 1) + (narrow - 1) + 12 + (2 * column - 1)
    copies += 2 + 3 * (column - 1) + column + 2 * (2 * (2 * column - 1) + 2 * column)
    whole = lambda a: pl.BlockSpec(a.shape, lambda i: (0,) * len(a.shape), pipeline_mode=pl.Buffered(1))
    anywhere = pl.BlockSpec(memory_space=pl.ANY)
    shaped = jax.ShapeDtypeStruct
    head_rows = shaped((rows, width), BF)
    inside = [
        head_rows, head_rows, head_rows, shaped((rows, 256), F32), shaped((rows, depth), BF), shaped((16, depth), F32),
        shaped((blocks, 1, BLOCK), F32), shaped((rows, 1), F32), head_rows, shaped((blocks, 8, BLOCK), F32),
    ]
    inside_specs = [whole(a) for a in inside]
    inside_specs[4] = pl.BlockSpec((BLOCK, depth), lambda i: (jnp.minimum(jnp.maximum(i - 1, 0), blocks - 1), 0))
    outside = [
        shaped((rows, depth), BF), shaped((depth, 3 * width), BF), shaped((group_rows, depth), BF),
        shaped((depth, depth), BF), shaped((depth, half), BF), shaped((depth, half), BF),
    ]
    small = [(size, 3 * width), (size, depth // 2), (size, half), (size, half)]
    return pl.pallas_call(
        functools.partial(forward_kernel, heads, head_dim, wide, narrow),
        grid=(2 * blocks + 1,),
        in_specs=[whole(a) for a in (tok, vec, tag, table)] + [anywhere] * 4,
        out_specs=inside_specs + [anywhere] * 6,
        out_shape=inside + outside,
        scratch_shapes=[
            pltpu.VMEM((wide,) + vec.shape, BF),
            pltpu.VMEM((narrow,) + tag.shape, jnp.int32),
            pltpu.VMEM((rows, depth), BF),
            pltpu.VMEM((depth, 3 * width), BF),
        ]
        + [pltpu.VMEM(shape, BF) for shape in small]
        + [pltpu.VMEM(shape, F32) for shape in small]
        + [
            pltpu.VMEM((width, rows), BF),
            pltpu.VMEM((width, BLOCK), F32),
            pltpu.VMEM((8, BLOCK), F32),
            pltpu.VMEM((8, BLOCK), F32),
            pltpu.VMEM((rows, width), BF),
            pltpu.SemaphoreType.DMA((copies,)),
            pltpu.SemaphoreType.DMA((copies,)),
            pltpu.SemaphoreType.DMA((blocks,)),
            pltpu.SemaphoreType.DMA((blocks,)),
            pltpu.SemaphoreType.DMA((6,)),
            pltpu.SemaphoreType.DMA((7 + blocks // narrow,)),
        ],
        compiler_params=pltpu.CompilerParams(
            collective_id=3, has_side_effects=True, vmem_limit_bytes=48 * 1024 * 1024
        ),
        cost_estimate=pl.CostEstimate(
            flops=heads * rows * rows * width * 4, bytes_accessed=rows * width * 8, transcendentals=heads * rows * rows
        ),
        name="attention_forward",
    )(tok, vec, tag, table, qkv, out, up, down)


class Scatter:
    def __init__(self, go, wide, narrow, split, part, near_in, own, far_out, far_in, box, local, *extra):
        w, self.n = lax.axis_index("wide"), lax.axis_index("narrow")
        self.go, self.column, self.split = go, wide // 2, split
        self.near_in, self.own, self.far_out, self.far_in, self.box = near_in, own, far_out, far_in, box
        z, y, x = w // 2, lax.rem(w, 2), self.n // 2
        near, mate, cross = w + 1 - 2 * y, self.n + 1 - 2 * lax.rem(self.n, 2), lax.rem(self.n + 2, narrow)
        size, cols = part.shape[0] // wide, box.shape[2]
        towards = [lax.rem(z + d, self.column) for d in range(1, self.column + 1)]
        theirs, ours = [to * 2 + 1 - y for to in towards], [to * 2 + y for to in towards]
        here = pl.ds(pl.multiple_of(x * cols, cols), cols) if split else pl.ds(0, cols)
        self.loads = [
            pltpu.make_async_copy(part.at[rows_at(i, size), here], own.at[k], local.at[k])
            for k, i in enumerate(ours + theirs if split else ours)
        ]
        self.zero = []
        if split:
            self.cross_in, self.out = extra
            there = pl.ds(pl.multiple_of((1 - x) * cols, cols), cols)
            order = list(enumerate(ours + theirs))
            order = order[self.column :] + order[: self.column]
            self.zero = {
                k: go.make(part.at[rows_at(i, size), there], self.cross_in.at[k], narrow=cross) for k, i in order
            }
        self.first = [
            go.make(self.out.at[k] if split else part.at[rows_at(i, size)], near_in.at[k], wide=near)
            for k, i in enumerate(theirs)
        ]
        self.second = [go.make(far_out.at[k], far_in.at[k], wide=i) for k, i in enumerate(ours[:-1])]
        self.over = go.make(box.at[self.n], box.at[self.n], narrow=cross)
        self.beside = go.make(box.at[self.n], box.at[self.n], narrow=mate)
        self.passed = go.make(box.at[cross], box.at[cross], narrow=mate)

    def load(self):
        for copy in self.loads:
            copy.start()
        if self.split:
            self.go.launch(*self.zero.values())

    def summed(self, k):
        self.loads[k].wait()
        value = self.own[k].astype(F32)
        if self.split:
            self.go.arrived(self.zero[k])
            value = value + self.cross_in[k].astype(F32)
        return value

    def send(self, k):
        if self.split:
            self.out[k] = self.summed(self.column + k).astype(BF)
        self.go.launch(self.first[k])

    def relay(self, k):
        self.go.arrived(self.first[k])
        if k < self.column - 1:
            self.far_out[k] = (self.summed(k) + self.near_in[k].astype(F32)).astype(BF)
            self.go.launch(self.second[k])

    def total(self):
        value = self.summed(self.column - 1) + self.near_in[self.column - 1].astype(F32)
        for k in range(self.column - 1):
            self.go.arrived(self.second[k])
            value = value + self.far_in[k].astype(F32)
        self.box[pl.ds(self.n, 1)] = value.astype(BF)[None]
        self.go.launch(self.over, self.beside)

    def share(self):
        self.go.arrived(self.over)
        self.go.launch(self.passed)

    @staticmethod
    def copies(wide, split):
        return 2 * (wide // 2) - 1 + 3 + (wide if split else 0)

    @staticmethod
    def scratch(wide, narrow, rows, cols, split):
        column, size = wide // 2, rows // wide
        cols = cols // 2 if split else cols
        many = wide if split else column
        sizes = [column, many, column - 1, column - 1, narrow]
        first = [pltpu.VMEM((count, size, cols), BF) for count in sizes] + [pltpu.SemaphoreType.DMA((many,))]
        return first + ([pltpu.VMEM((count, size, cols), BF) for count in (wide, column)] if split else [])


def square_sum(value):
    return jnp.sum(jnp.sum(value * value, axis=0, keepdims=True), axis=1, keepdims=True)


def backward_kernel(
    heads, head_dim, wide, narrow,
    q_ref, k_ref, v_ref, o_ref, g_ref, lse_ref, seg_ref, tag_ref, turn_ref, part_out, part_down, part_up,
    grads_out, shards_out, shards_down, shards_up, squares_out,
    q_heads, g_heads, delta, grad_query, send, recv, *boxes,
):
    step = pl.program_id(0)
    rows, width = q_ref.shape
    blocks = rows // BLOCK
    last = blocks - 1
    scale = head_dim**-0.5
    half = head_dim // 2
    go = Copies(send, recv)
    column = wide // 2
    outs = Scatter(go, wide, narrow, False, part_out, *boxes[:6])
    ups = Scatter(go, wide, narrow, False, part_up, *boxes[6:12])
    downs = Scatter(go, wide, narrow, True, part_down, *boxes[12:])

    @pl.when(step == 0)
    def _():
        w, n = lax.axis_index("wide"), lax.axis_index("narrow")
        z, y = w // 2, lax.rem(w, 2)
        greet(
            [{"wide": w + 1 - 2 * y}]
            + [{"wide": lax.rem(z + d, column) * 2 + y} for d in range(1, column)]
            + [{"narrow": n + 1 - 2 * lax.rem(n, 2)}, {"narrow": lax.rem(n + 2, narrow)}]
        )
        for k in range(column):
            ups.send(k)
        for scatter in (downs, ups, outs):
            scatter.load()

    part = lambda i: range(column * i // 4, column * (i + 1) // 4)
    plan = {
        2: [(ups.relay, part(0))],
        4: [(ups.relay, part(1))],
        5: [(downs.send, range(column // 2))],
        6: [(ups.relay, part(2))],
        7: [(downs.send, range(column // 2, column))],
        8: [(ups.relay, part(3)), (outs.send, range(column))],
        10: [(downs.relay, part(0))],
        11: [(downs.relay, part(1)), (ups.total, None)],
        12: [(downs.relay, part(2))],
        13: [(downs.relay, part(3)), (ups.share, None)],
        14: [(outs.relay, range(column // 2))],
        15: [(outs.relay, range(column // 2, column)), (downs.total, None)],
    }

    def act(i):
        for action, ks in plan[i]:
            for k in [None] if ks is None else ks:
                action() if k is None else action(k)

    for i in range(0, 2 * blocks, 2):
        if i in plan:

            @pl.when(step == i // 2)
            def _():
                act(i)

    @pl.when(step == 0)
    def _():
        grad_query[...] = jnp.zeros_like(grad_query)
        row = lax.broadcasted_iota(jnp.int32, (8, width), 0)
        lane = lax.broadcasted_iota(jnp.int32, (8, width), 1)
        pick = jnp.where(lane // head_dim == row, 1.0, 0.0)

        def prepare(i, carry):
            at = pl.ds(pl.multiple_of(i * BLOCK, BLOCK), BLOCK)
            query = q_ref[at, :] * jnp.asarray(scale, BF)
            grad = g_ref[at, :]
            for h in range(heads):
                lanes = head_lanes(query.shape, h, head_dim)
                q_heads[h, at, :] = jnp.where(lanes, query, jnp.zeros_like(query))
                g_heads[h, at, :] = jnp.where(lanes, grad, jnp.zeros_like(grad))
            product = grad.astype(F32) * o_ref[at, :].astype(F32)
            delta[pl.ds(i, 1)] = lax.dot_general(
                pick,
                product,
                (((1,), (1,)), ((), ())),
                precision=lax.Precision.HIGHEST,
                preferred_element_type=F32,
            )[None]
            return carry

        lax.fori_loop(0, blocks, prepare, 0)

    key = k_ref[...]
    value = v_ref[...]
    tag = tag_ref[...]
    masked_key = [jnp.where(head_lanes(key.shape, h, head_dim), key, jnp.zeros_like(key)) for h in range(heads)]

    def body(i, carry):
        for half_step in range(1, 2 * blocks, 2):
            if half_step in plan:

                @pl.when((step == half_step // 2) & (i == blocks // 2))
                def _():
                    act(half_step)

        grad_key, grad_value = carry
        at = pl.ds(pl.multiple_of(i * BLOCK, BLOCK), BLOCK)
        allowed = tag == seg_ref[pl.ds(i, 1), :]
        lse = lse_ref[pl.ds(i, 1)][0]
        dlt = delta[pl.ds(i, 1)][0]
        total = None
        for h in range(heads):
            query = q_heads[h, at, :]
            grad = g_heads[h, at, :]
            scores = dot(key, query, 1, 1)
            probs = jnp.where(allowed, jnp.exp(scores - lse[h : h + 1, :]), 0.0)
            grad_probs = dot(value, grad, 1, 1)
            grad_scores = (probs * (grad_probs - dlt[h : h + 1, :])).astype(BF)
            grad_value = grad_value + dot(probs.astype(BF), grad, 1, 0)
            grad_key = grad_key + dot(grad_scores, query, 1, 0)
            term = dot(grad_scores, masked_key[h], 0, 0)
            total = term if total is None else total + term
        grad_query[at, :] += total
        return grad_key, grad_value

    zero = jnp.zeros((BLOCK, width), F32)
    low, high = meeting(step, blocks)
    grad_key, grad_value = lax.fori_loop(low, high, body, (zero, zero))
    here = pl.ds(pl.multiple_of(step * BLOCK, BLOCK), BLOCK)
    cosine, sine = turn_ref[here, :128], turn_ref[here, 128:]
    grads_out[here, width : 2 * width] = turn(grad_key, cosine, sine, half, -1).astype(BF)
    grads_out[here, 2 * width :] = grad_value.astype(BF)

    @pl.when(step == last)
    def _():
        downs.share()
        outs.total()

        def finish(i, carry):
            at = pl.ds(pl.multiple_of(i * BLOCK, BLOCK), BLOCK)
            grads = grad_query[at, :] * scale
            grads_out[at, :width] = turn(grads, turn_ref[at, :128], turn_ref[at, 128:], half, -1).astype(BF)
            return carry

        lax.fori_loop(0, blocks, finish, 0)
        outs.share()
        go.finish()
        squares = jnp.zeros((1, 1), F32)
        for box in (outs.box, ups.box):
            for i in range(2):
                squares += square_sum(box[i].astype(F32) + box[i + 2].astype(F32))
        for i in range(narrow):
            squares += square_sum(downs.box[i].astype(F32))
        squares_out[...] = jnp.broadcast_to(squares, squares_out.shape)
        shards_out[...] = outs.box[...]
        shards_down[...] = downs.box[...]
        shards_up[...] = ups.box[...]


def backward_call(q, k, v, o, g, lse, seg_rows, tag_col, turns, part_out, part_down, part_up, head_dim, wide, narrow):
    rows, width = q.shape
    heads = width // head_dim
    blocks = rows // BLOCK
    whole = lambda a: pl.BlockSpec(a.shape, lambda i: (0,) * len(a.shape), pipeline_mode=pl.Buffered(1))
    block = pl.BlockSpec((BLOCK, width), lambda i: (i, 0))
    anywhere = pl.BlockSpec(memory_space=pl.ANY)
    depth = part_up.shape[0]
    results = [
        jax.ShapeDtypeStruct((rows, 3 * width), BF),
        jax.ShapeDtypeStruct((narrow, depth // wide, part_out.shape[1]), BF),
        jax.ShapeDtypeStruct((narrow, depth // wide, part_down.shape[1] // 2), BF),
        jax.ShapeDtypeStruct((narrow, depth // wide, part_up.shape[1]), BF),
        jax.ShapeDtypeStruct((8, 128), F32),
    ]
    copies = 2 * Scatter.copies(wide, False) + Scatter.copies(wide, True)
    return pl.pallas_call(
        functools.partial(backward_kernel, heads, head_dim, wide, narrow),
        grid=(blocks,),
        in_specs=[
            whole(q), block, block, whole(o), whole(g), whole(lse), whole(seg_rows),
            pl.BlockSpec((BLOCK, 1), lambda i: (i, 0)),
            whole(turns), anywhere, anywhere, anywhere,
        ],
        out_specs=[whole(a) for a in results],
        out_shape=results,
        scratch_shapes=[
            pltpu.VMEM((heads, rows, width), BF),
            pltpu.VMEM((heads, rows, width), BF),
            pltpu.VMEM((blocks, 8, BLOCK), F32),
            pltpu.VMEM((rows, width), F32),
            pltpu.SemaphoreType.DMA((copies,)),
            pltpu.SemaphoreType.DMA((copies,)),
        ]
        + Scatter.scratch(wide, narrow, depth, part_out.shape[1], False)
        + Scatter.scratch(wide, narrow, depth, part_up.shape[1], False)
        + Scatter.scratch(wide, narrow, depth, part_down.shape[1], True),
        compiler_params=pltpu.CompilerParams(
            collective_id=4, has_side_effects=True, vmem_limit_bytes=60 * 1024 * 1024
        ),
        cost_estimate=pl.CostEstimate(
            flops=heads * rows * rows * width * 7, bytes_accessed=rows * width * 20, transcendentals=heads * rows * rows
        ),
        name="attention_backward",
    )(q, k, v, o, g, lse, seg_rows, tag_col, turns, part_out, part_down, part_up)


def norm_parts(values):
    center = values - jnp.mean(values, axis=-1, keepdims=True)
    inverse = lax.rsqrt(jnp.mean(center * center, axis=-1, keepdims=True) + 1e-06)
    return center * inverse, inverse


def norm_back(grads, gain, unit, inverse):
    scaled = grads * gain
    return inverse * (
        scaled - jnp.mean(scaled, axis=-1, keepdims=True) - unit * jnp.mean(scaled * unit, axis=-1, keepdims=True)
    )


def adamw(param, grad, first, second, clip, rate, decay, fix_first, fix_second):
    clipped = grad * clip
    moment = 0.9 * first + 0.1 * clipped
    square = 0.999 * second + 0.001 * clipped * clipped
    direction = moment / fix_first / (jnp.sqrt(square / fix_second) + 1e-08)
    return (param - rate * (direction + decay * param), moment, square)


def on_device(
    tokens, cotangent, segment_ids, key_keep, patch_coords, step_count,
    weight_qkv, weight_out, weight_up, weight_down, vectors,
    first_qkv, first_out, first_up, first_down, first_vectors,
    second_qkv, second_out, second_up, second_down, second_vectors,
):
    rows, width = tokens.shape
    hidden = weight_up.shape[1]
    head_dim = width // HEADS
    narrow = lax.axis_size("narrow")
    wide = lax.axis_size("wide")
    shard_rows = width // wide
    me = lax.axis_index("narrow")
    side = me % 2
    mine = width // narrow
    half_hidden = hidden // 2
    group = rows * narrow

    def mate(value):
        return lax.ppermute(value, "narrow", [(i, i ^ 1) for i in range(narrow)])

    def across(value):
        return lax.ppermute(value, "narrow", [(i, i ^ 2) for i in range(narrow)])

    def take(value, start, size, axis=1):
        return lax.dynamic_slice_in_dim(value, start, size, axis)

    shard_cols = vectors.shape[1]
    vec_shard = jnp.pad(vectors.astype(BF), ((0, 16 - vectors.shape[0]), (0, -shard_cols % 128)))
    tag = jnp.concatenate([segment_ids[None], key_keep[None], patch_coords, patch_coords], axis=0)
    (
        query, keys, values, turns, normed1_all, vec, seg_rows, tag_col, mixed_mine, lse,
        tokens_all, qkv_w, mixed, out_w, up_w, down_w,
    ) = forward_call(
        tokens, vec_shard, tag, rotary_table(head_dim), (weight_qkv, weight_out, weight_up, weight_down),
        head_dim, wide, narrow,
    )
    vec = vec[: vectors.shape[0]]
    xin = tokens.astype(F32)
    unit1, inverse1 = norm_parts(xin)
    cot_pair = jnp.concatenate([cotangent, mate(cotangent)], axis=0)

    resid = xin + (dot(mixed, out_w, 1, 0) + vec[5])
    unit2, inverse2 = norm_parts(resid)
    normed2 = (unit2 * vec[6] + vec[7]).astype(BF)
    normed2_pair = jnp.concatenate([normed2, mate(normed2)], axis=0)
    up_bias = take(vec[9:].reshape(1, -1), side * half_hidden, half_hidden)
    up_pre = dot(normed2_pair, up_w, 1, 0) + up_bias
    erf_part = 0.5 * (1.0 + lax.erf(up_pre * (0.5**0.5)))
    act = (up_pre * erf_part).astype(BF)
    slope = erf_part + up_pre * (jnp.exp(-0.5 * up_pre * up_pre) * ((2.0 * jnp.pi) ** -0.5))
    part_down = dot(cot_pair, act, 0, 0).astype(BF)
    down_part = dot(act, down_w, 1, 1)
    down = down_part[:rows] + mate(down_part[rows:])
    layer_out = (resid + (down + vec[8])).astype(BF)

    grad_up_act = (dot(cot_pair, down_w, 1, 0) * slope).astype(BF)
    part_up = dot(normed2_pair, grad_up_act, 0, 0).astype(BF)
    grad_normed2_part = dot(grad_up_act, up_w, 1, 1)
    grad_normed2 = grad_normed2_part[:rows] + mate(grad_normed2_part[rows:])
    cot = cotangent.astype(F32)
    grad_resid = cot + norm_back(grad_normed2, vec[6], unit2, inverse2)
    grad_branch = grad_resid.astype(BF)
    grad_mixed = dot(grad_branch, out_w, 1, 1).astype(BF)
    part_out = dot(mixed, grad_branch, 0, 0)
    own_out = take(part_out, side * (width // 2), width // 2)
    other_out = take(part_out, (1 - side) * (width // 2), width // 2)
    part_out = (own_out + mate(other_out.astype(BF)).astype(F32)).astype(BF)

    grad_mixed_mine = lax.all_to_all(grad_mixed, "narrow", 1, 0, tiled=True)
    grad_proj, shards_out, shards_down, shards_up, squares = backward_call(
        query, keys, values, mixed_mine, grad_mixed_mine, lse, seg_rows[:, 0], tag_col, turns, part_out, part_down, part_up, head_dim, wide, narrow,
    )
    proj_sums = jnp.sum(grad_proj.astype(F32), axis=0).reshape(3, mine)
    proj_rows = lax.dynamic_update_slice(jnp.zeros((3, width), F32), proj_sums, (0, me * mine))
    up_sums = jnp.sum(grad_up_act.astype(F32), axis=0)
    up_rows = lax.dynamic_update_slice(jnp.zeros((hidden,), F32), up_sums, (side * half_hidden,))
    vector_part = jnp.concatenate(
        [
            jnp.zeros((2, width), F32),
            proj_rows,
            jnp.sum(grad_branch.astype(F32), axis=0)[None],
            jnp.sum(grad_normed2 * unit2, axis=0)[None],
            jnp.sum(grad_normed2, axis=0)[None],
            jnp.sum(cot, axis=0)[None],
            up_rows.reshape(hidden // width, width),
            jnp.zeros((16 - vectors.shape[0], width), F32),
        ],
        axis=0,
    )
    grad_normed1, total_qkv, vector_total, square_total = tail_call(
        normed1_all, grad_proj, qkv_w, tokens_all, vector_part, squares, wide, narrow
    )
    grad_tokens = (grad_resid + norm_back(grad_normed1, vec[0], unit1, inverse1)).astype(BF)

    def join(shards):
        shards = shards.astype(F32)
        return jnp.concatenate([shards[0] + shards[2], shards[1] + shards[3]], axis=1)

    total_up = join(shards_up)
    total_down = jnp.concatenate([shards_down[i] for i in (0, 2, 1, 3)], axis=1).astype(F32)
    total_out = join(shards_out)
    total_qkv = total_qkv.astype(F32)
    grad_norm = jnp.sqrt(square_total[0, 0])
    clip = 1.0 / jnp.maximum(grad_norm, 1.0)
    count = step_count[0].astype(F32)
    rate = 0.4 * count / (count + 4.0)
    decay = 0.04 + 0.018 * count
    fix_first = 1.0 - jnp.power(0.9, count)
    fix_second = 1.0 - jnp.power(0.999, count)
    grad_vectors = vector_total[: vectors.shape[0], :shard_rows]

    def update(param, grad, first, second, decay_here):
        return adamw(param, grad, first, second, clip, rate, decay_here, fix_first, fix_second)

    new_qkv = update(weight_qkv, total_qkv, first_qkv, second_qkv, decay)
    new_out = update(weight_out, total_out, first_out, second_out, decay)
    new_up = update(weight_up, total_up, first_up, second_up, decay)
    new_down = update(weight_down, total_down, first_down, second_down, decay)
    new_vectors = update(vectors, grad_vectors, first_vectors, second_vectors, 0.0)
    news = (new_qkv, new_out, new_up, new_down, new_vectors)
    return (layer_out, grad_tokens) + tuple(n[i] for i in range(3) for n in news) + (grad_norm, grad_vectors[8])


def solution(mesh):
    by_token = P(("wide", "narrow"), None)
    ids = P(("wide", "narrow"))
    by_row = P("wide", None)
    by_column = P(None, "wide")
    params = (by_row,) * 4 + (by_column,)
    return jax.shard_map(
        on_device,
        mesh=mesh,
        in_specs=(by_token, by_token, ids, ids, P(None, ("wide", "narrow")), P()) + params * 3,
        out_specs=(by_token, by_token) + params * 3 + (P(), P("wide")),
        check_vma=False,
    )
```

```python
import functools

import jax
import jax.numpy as jnp
from jax import lax
from jax.experimental import pallas as pl
from jax.experimental.pallas import tpu as pltpu
from jax.sharding import PartitionSpec as P

HEADS = 16
BLOCK = 256
BF = jnp.bfloat16
F32 = jnp.float32
MESH = pl.DeviceIdType.MESH


def dot(a, b, ca, cb):
    return lax.dot_general(a, b, (((ca,), (cb,)), ((), ())), preferred_element_type=F32)


def swap_halves(x, half):
    lane = lax.broadcasted_iota(jnp.int32, x.shape, 1)
    width = x.shape[1]
    return jnp.where(
        lane % (2 * half) < half, pltpu.roll(x, width - half, 1), pltpu.roll(x, half, 1)
    )


def turn(x, cosine, sine, half, sign):
    parts = []
    for start in range(0, x.shape[1], 128):
        part = x[:, start : start + 128]
        other = swap_halves(part, half) * sine
        parts.append(part * cosine + other if sign > 0 else part * cosine - other)
    return jnp.concatenate(parts, axis=1)


def rotary_table(head_dim):
    half = head_dim // 2
    lane = jnp.arange(128)
    pair = lane % half
    rates = jnp.power(10000.0, -(pair // 3).astype(F32) / ((half + 2) // 3))
    row = jnp.arange(128)
    axis = row // 14
    value = (row % 14).astype(F32)
    live = (axis[:, None] == (pair % 3)[None, :]) & (row[:, None] < 42)
    angle = value[:, None] * rates[None, :]
    signs = jnp.where(lane % head_dim < half, -1.0, 1.0)
    return jnp.concatenate(
        [
            jnp.where(live, jnp.cos(angle), 0.0),
            jnp.where(live, jnp.sin(angle) * signs[None, :], 0.0),
        ],
        axis=1,
    )


def greet(targets):
    barrier = pltpu.get_barrier_semaphore()
    for target in targets:
        pl.semaphore_signal(barrier, inc=1, device_id=target, device_id_type=MESH)
    pl.semaphore_wait(barrier, len(targets))


def others(name, index, size):
    return [{name: lax.rem(index + d, size)} for d in range(1, size)]


class Copies:
    def __init__(self, send, recv):
        self.send, self.recv, self.all = send, recv, []

    def make(self, src, dst, **target):
        i = len(self.all)
        copy = pltpu.make_async_remote_copy(
            src_ref=src, dst_ref=dst, send_sem=self.send.at[i], recv_sem=self.recv.at[i],
            device_id=target, device_id_type=MESH,
        )
        self.all.append([copy, False])
        return i

    def launch(self, *indices):
        for i in indices:
            self.all[i][0].start()

    def start(self, src, dst, **target):
        i = self.make(src, dst, **target)
        self.launch(i)
        return i

    def arrived(self, i):
        if not self.all[i][1]:
            self.all[i][0].wait_recv()
            self.all[i][1] = True

    def finish(self):
        for i in range(len(self.all)):
            self.arrived(i)
        for copy, _ in self.all:
            copy.wait_send()


def across_column(z, d):
    bits = [1 << b for b in range(d.bit_length()) if d >> b & 1]
    return z + sum(bit * (1 - 2 * lax.rem(z // bit, 2)) for bit in bits)


def rows_at(index, size):
    return pl.ds(pl.multiple_of(index * size, size), size)


def tail_kernel(
    wide, narrow, normed, grad_proj, weight_in, tok_in, vec_in, squares_in, normed_out, qkv_out, vec_out, square_out,
    partial, mate_in, cross_out, cross_in, near_in, far_out, far_in, shards, vec_box, sums,
    slices, slice_box, square_box, part, weight, tok, send, recv, local,
):
    w, n = lax.axis_index("wide"), lax.axis_index("narrow")
    column = wide // 2
    z, y = w // 2, lax.rem(w, 2)
    x, c = n // 2, lax.rem(n, 2)
    near, mate, cross = w + 1 - 2 * y, n + 1 - 2 * c, lax.rem(n + 2, narrow)
    wide_rows, group_rows = part.shape[0] // wide, normed_out.shape[0]
    towards = [across_column(z, d) for d in range(column - 1, -1, -1)]
    loads = [
        pltpu.make_async_copy(weight_in, weight, local.at[0]),
        pltpu.make_async_copy(tok_in, tok, local.at[1]),
    ]
    for copy in loads:
        copy.start()
    greet(others("wide", w, wide) + others("narrow", n, narrow))
    go = Copies(send, recv)
    depth, chunk = part.shape[0], 128
    sent = lambda k: go.make(part.at[rows_at(towards[k] * 2 + 1 - y, wide_rows)], near_in.at[k], wide=near)
    first = [sent(k) for k in range(column)]
    one_each = wide_rows == chunk

    def rows_of(index):
        at = rows_at(index, chunk)
        part[at, :] = dot(normed[:, at], grad_proj[...], 0, 0).astype(BF)

    if one_each:
        for k in range(column):
            rows_of(towards[k] * 2 + 1 - y)
            go.launch(first[k])

        def ours(k, carry):
            rows_of(lax.rem(z + 1 + k, column) * 2 + y)
            return carry

        lax.fori_loop(0, column, ours, 0)
    else:

        def each(index, carry):
            rows_of(index)
            return carry

        lax.fori_loop(0, depth // chunk, each, 0)
        go.launch(*first)
    for copy in loads:
        copy.wait()

    seconds, kept = [], []

    def relay(k):
        go.arrived(first[k])
        value = part[rows_at(towards[k] * 2 + y, wide_rows), :].astype(F32) + near_in[k].astype(F32)
        if k < column - 1:
            far_out[k] = value.astype(BF)
            seconds.append(go.start(far_out.at[k], far_in.at[k], wide=towards[k] * 2 + y))
        else:
            kept.append(value)

    sums[...] = jnp.zeros_like(sums)
    owners = [(1 - x) * 2 + 1 - c, (1 - x) * 2 + c, x * 2 + 1 - c, n]
    half = group_rows // 2
    mates, overs = [], []
    for slot, owner in enumerate(owners):

        def body(i, carry):
            at = pl.ds(pl.multiple_of(owner * group_rows + i * BLOCK, BLOCK), BLOCK)
            here = pl.ds(pl.multiple_of(i * BLOCK, BLOCK), BLOCK)
            grads = dot(grad_proj[at, :], weight[...], 1, 1)
            unit, _ = norm_parts(tok[at, :].astype(F32))
            sums[0:1, :] += jnp.sum(grads * unit, axis=0, keepdims=True)
            sums[1:2, :] += jnp.sum(grads, axis=0, keepdims=True)
            if slot < 3:
                partial[slot, here, :] = grads.astype(BF)
            else:
                normed_out[here, :] = grads
            return carry

        lax.fori_loop(0, group_rows // BLOCK, body, 0)
        if slot == 0:
            mates.append(go.start(partial.at[0], mate_in.at[0], narrow=mate))
        if slot == 2:
            mates.append(go.start(partial.at[2], mate_in.at[1], narrow=mate))
        if slot == 1:
            go.arrived(mates[0])
            for p in range(2):
                at = pl.ds(p * half, half)
                cross_out[at, :] = (partial[1, at, :].astype(F32) + mate_in[0, at, :].astype(F32)).astype(BF)
                overs.append(go.start(cross_out.at[at], cross_in.at[at], narrow=cross))
        for k in range(column * slot // 4, column * (slot + 1) // 4):
            if k < column - 1:
                relay(k)

    vec_box[pl.ds(n, 1)] = vec_in[...][None]
    vec_box[pl.ds(n, 1), 0:2, :] = sums[0:2, :][None]
    vecs = [go.start(vec_box.at[n], vec_box.at[n], narrow=lax.rem(n + d, narrow)) for d in range(1, narrow)]
    for i in vecs:
        go.arrived(i)
    group = vec_box[0]
    for i in range(1, narrow):
        group = group + vec_box[i]
    cols = group.shape[1] // wide
    slices[...] = jnp.zeros_like(slices)
    for i in range(wide):
        slices[i, :, :cols] = group[:, i * cols : (i + 1) * cols]
    peers = [lax.rem(w + d, wide) for d in range(1, wide)]
    pieces = [go.start(slices.at[peer], slice_box.at[w], wide=peer) for peer in peers]
    slice_box[pl.ds(w, 1)] = slices[pl.ds(w, 1)]
    relay(column - 1)
    total = kept[0]
    for k in range(column - 1):
        go.arrived(seconds[k])
        total = total + far_in[k].astype(F32)
    shards[pl.ds(n, 1)] = total.astype(BF)[None]
    over = go.start(shards.at[n], shards.at[n], narrow=cross)
    beside = go.start(shards.at[n], shards.at[n], narrow=mate)

    go.arrived(mates[1])
    for p in range(2):
        go.arrived(overs[p])
        at = pl.ds(p * half, half)
        normed_out[at, :] += mate_in[1, at, :].astype(F32) + cross_in[at, :].astype(F32)
    for i in pieces:
        go.arrived(i)
    vectors = slice_box[0]
    for i in range(1, wide):
        vectors = vectors + slice_box[i]
    vec_out[...] = vectors

    go.arrived(over)
    passed = go.start(shards.at[cross], shards.at[cross], narrow=mate)
    for i in (beside, passed):
        go.arrived(i)
    squares = square_sum(vectors)
    width = part.shape[1] // 3
    for i in range(narrow):
        shard = shards[i]
        squares += square_sum(shard.astype(F32))
        for j in range(3):
            qkv_out[:, (j * narrow + i) * width : (j * narrow + i + 1) * width] = shard[:, j * width : (j + 1) * width]
    square_box[pl.ds(w, 1)] = (squares_in[...] + squares)[None]
    for peer in peers:
        go.start(square_box.at[w], square_box.at[w], wide=peer)
    go.finish()
    total = square_box[0]
    for i in range(1, wide):
        total = total + square_box[i]
    square_out[...] = total


def tail_call(normed, grad_proj, weight, tok, vec_in, squares_in, wide, narrow):
    depth, cols = weight.shape
    rows = tok.shape[0] // narrow
    wide_rows = depth // wide
    column = wide // 2
    copies = 2 * column - 1 + 2 + (narrow - 1) + 2 + 3 + 2 * (wide - 1)
    vmem = pl.BlockSpec(memory_space=pltpu.VMEM)
    anywhere = pl.BlockSpec(memory_space=pl.ANY)
    return pl.pallas_call(
        functools.partial(tail_kernel, wide, narrow),
        in_specs=[vmem, vmem, anywhere, anywhere, vmem, vmem],
        out_specs=[vmem] * 4,
        out_shape=[
            jax.ShapeDtypeStruct((rows, depth), F32),
            jax.ShapeDtypeStruct((wide_rows, narrow * cols), BF),
            jax.ShapeDtypeStruct((16, 128), F32),
            jax.ShapeDtypeStruct((8, 128), F32),
        ],
        scratch_shapes=[
            pltpu.VMEM((3, rows, depth), BF),
            pltpu.VMEM((2, rows, depth), BF),
            pltpu.VMEM((rows, depth), BF),
            pltpu.VMEM((rows, depth), BF),
            pltpu.VMEM((column, wide_rows, cols), BF),
            pltpu.VMEM((column - 1, wide_rows, cols), BF),
            pltpu.VMEM((column - 1, wide_rows, cols), BF),
            pltpu.VMEM((narrow, wide_rows, cols), BF),
            pltpu.VMEM((narrow,) + vec_in.shape, F32),
            pltpu.VMEM((8, depth), F32),
            pltpu.VMEM((wide, 16, 128), F32),
            pltpu.VMEM((wide, 16, 128), F32),
            pltpu.VMEM((wide, 8, 128), F32),
            pltpu.VMEM((depth, cols), BF),
            pltpu.VMEM((depth, cols), BF),
            pltpu.VMEM(tok.shape, BF),
            pltpu.SemaphoreType.DMA((copies,)),
            pltpu.SemaphoreType.DMA((copies,)),
            pltpu.SemaphoreType.DMA((2,)),
        ],
        compiler_params=pltpu.CompilerParams(
            collective_id=1, has_side_effects=True, vmem_limit_bytes=56 * 1024 * 1024
        ),
        name="tail",
    )(normed, grad_proj, weight, tok, vec_in, squares_in)


CLIP = 784


def head_lanes(shape, head, head_dim):
    lane = lax.broadcasted_iota(jnp.int32, shape, 1)
    return lane // head_dim == head


def meeting(block, blocks):
    before, after = CLIP // BLOCK, -(-2 * CLIP // BLOCK)
    low = before * (block // after)
    high = blocks - (blocks - after) * (1 - jnp.minimum(block // before, 1))
    return low, high


def forward_kernel(
    heads, head_dim, wide, narrow,
    tok, vec, tag, table, qkv_f32, out_f32, up_f32, down_f32,
    q_ref, k_ref, v_ref, turn_ref, norm_ref, vec_ref, seg_ref, tag_ref, o_ref, lse_ref,
    tok_all, qkv_all, mixed_ref, out_all, up_all, down_all,
    vec_box, tag_box, tok_box, qkv_box, qkv_own, out_own, up_own, down_own, stage_qkv, stage_out, stage_up, stage_down,
    values_turned, acc, peak, total, o_box, send, recv, mix_send, mix_recv, local, leave,
):
    step = pl.program_id(0)
    rows, width = q_ref.shape
    depth = tok.shape[1]
    blocks = rows // BLOCK
    per = blocks // narrow
    final = 2 * blocks
    w, n = lax.axis_index("wide"), lax.axis_index("narrow")
    column = wide // 2
    z, y, side = w // 2, lax.rem(w, 2), lax.rem(n, 2)
    near, mate, cross = w + 1 - 2 * y, n + 1 - 2 * side, lax.rem(n + 2, narrow)
    source = target = lambda d: across_column(z, d) * 2 + y
    beside = lambda d: across_column(z, d) * 2 + 1 - y
    wide_rows, out_half = out_own.shape
    half = up_own.shape[1]
    group_rows = tok.shape[0]

    loads = [
        pltpu.make_async_copy(
            qkv_f32.at[:, pl.ds(pl.multiple_of(i * depth + n * width, width), width)],
            stage_qkv.at[:, pl.ds(i * width, width)],
            local.at[i],
        )
        for i in range(3)
    ] + [
        pltpu.make_async_copy(
            whole.at[:, pl.ds(pl.multiple_of(side * size, size), size)], stage, local.at[3 + i]
        )
        for i, (whole, stage, size) in enumerate(
            [(out_f32, stage_out, out_half), (up_f32, stage_up, half), (down_f32, stage_down, half)]
        )
    ]

    go = Copies(send, recv)
    small = [go.make(vec, vec_box.at[w], wide=lax.rem(w + d, wide)) for d in range(1, wide)]
    small += [go.make(tag, tag_box.at[n], narrow=lax.rem(n + d, narrow)) for d in range(1, narrow)]
    pieces = 4
    piece = group_rows // pieces
    token_rows = lambda i, p: tok_box.at[rows_at(i * pieces + p, piece)]
    own_piece = lambda p: tok.at[pl.ds(p * piece, piece)]
    over = [go.make(own_piece(p), token_rows(n, p), narrow=cross) for p in range(pieces)]
    to_mate = [go.make(own_piece(p), token_rows(n, p), narrow=mate) for p in range(pieces)]
    passed = [go.make(token_rows(cross, p), token_rows(cross, p), narrow=mate) for p in range(pieces)]
    qkv_at = lambda i: qkv_box.at[rows_at(i, wide_rows)]
    qkv_far = [go.make(qkv_own, qkv_at(w), wide=target(d)) for d in range(1, column)]
    qkv_near = [go.make(qkv_own, qkv_at(w), wide=near)]
    qkv_near += [go.make(qkv_at(source(d)), qkv_at(source(d)), wide=near) for d in range(1, column)]

    at_step = [[] for _ in range(final + 2)]
    soon = []
    out_cols = pl.ds(pl.multiple_of(side * out_half, out_half), out_half)
    out_at = lambda i: out_all.at[rows_at(i, wide_rows), out_cols]
    out_near = [go.make(out_own, out_at(w), wide=near)]
    out_starts = [go.make(out_own, out_at(w), narrow=mate)]
    at_step[blocks + 6].append((None, [out_near[0]]))
    out_late = []
    for d in range(1, column):
        out_starts.append(go.make(out_own, out_at(w), wide=target(d)))
        ref = out_at(source(d))
        out_near.append(go.make(ref, ref, wide=near))
        out_late.append((out_starts[-1], [out_near[-1], go.make(ref, ref, narrow=mate)]))
    for d in range(column):
        ref = out_at(beside(d))
        out_late.append((out_near[d], [go.make(ref, ref, narrow=mate)]))

    quarter = half // 4
    shared = pl.ds(pl.multiple_of(n // 2 * quarter, quarter), quarter)
    both = pl.ds(2 * quarter, 2 * quarter)
    own_out = [pltpu.make_async_copy(out_own, out_at(w), leave.at[0])]

    def spread(own, result, cols, steps, slot):
        piece_at = lambda i: result.at[rows_at(i, wide_rows), cols]
        over_x = cols is shared
        passes = lambda i: [go.make(piece_at(i), piece_at(i), narrow=cross)] if over_x else []
        nears = [go.make(own.at[:, cols], piece_at(w), wide=near)]
        (soon if over_x else at_step[steps[0]]).append((None, nears[:1]))
        starts = [go.make(own.at[:, cols], piece_at(w), narrow=cross)] if over_x else []
        for d in range(1, column):
            starts.append(go.make(own.at[:, cols], piece_at(w), wide=target(d)))
            ref = piece_at(source(d))
            nears.append(go.make(ref, ref, wide=near))
            at_step[steps[1][(d - 1) * 3 // (column - 1)]].append((starts[-1], [nears[-1]] + passes(source(d))))
        if over_x:
            for d in range(column):
                at_step[steps[2]].append((nears[d], passes(beside(d))))
        own_out.append(pltpu.make_async_copy(own.at[:, cols], piece_at(w), leave.at[slot]))
        return starts

    b = blocks
    weight_starts = spread(up_own, up_all, shared, (0, (4, 4, 4), b + 2), 1)
    weight_starts += spread(down_own, down_all, shared, (0, (b + 2, b + 2, b + 2), b + 4), 2)
    at_step[6].append((None, spread(up_own, up_all, both, (1, (b + 3, b + 5, b + 6)), 3)))
    at_step[b + 3].append((None, spread(down_own, down_all, both, (b + 2, (b + 7, b + 8, b + 9)), 4)))
    at_step[b + 6].append((None, out_starts))
    at_step[final + 1] += out_late

    mine = pl.ds(pl.multiple_of(n * width, width), width)

    def result(s):
        at = lax.rem((n + 1) * per + s, blocks)
        return pltpu.make_async_remote_copy(
            src_ref=o_box.at[rows_at(at, BLOCK)],
            dst_ref=mixed_ref.at[rows_at(lax.rem(s, per), BLOCK), mine],
            send_sem=mix_send.at[s],
            recv_sem=mix_recv.at[s],
            device_id={"narrow": lax.rem(n + 1 + s // per, narrow)},
            device_id_type=MESH,
        )

    def result_here(s):
        return pltpu.make_async_copy(
            o_box.at[rows_at(n * per + s, BLOCK)], mixed_ref.at[rows_at(s, BLOCK), mine], leave.at[7 + s]
        )

    kept = [
        pltpu.make_async_copy(tok_box, tok_all, leave.at[5]),
        pltpu.make_async_copy(qkv_box, qkv_all, leave.at[6]),
    ]

    @pl.when(step == 0)
    def _():
        for copy in loads:
            copy.start()
        greet(others("wide", w, wide) + others("narrow", n, narrow))
        go.launch(*small, *over)
        for copy in loads[:3]:
            copy.wait()
        qkv_own[...] = stage_qkv[...].astype(BF)
        go.launch(*qkv_far, qkv_near[0], *to_mate)
        for copy, stage, own in zip(
            loads[3:], (stage_out, stage_up, stage_down), (out_own, up_own, down_own)
        ):
            copy.wait()
            own[...] = stage[...].astype(BF)
        go.launch(*weight_starts)
        tok_box[rows_at(n, group_rows), :] = tok[...]
        qkv_box[rows_at(w, wide_rows), :] = qkv_own[...]
        vec_box[pl.ds(w, 1)] = vec[...][None]
        tag_box[pl.ds(n, 1)] = tag[...][None]
        for copy in own_out:
            copy.start()
        for i in small:
            go.arrived(i)
        cols = depth // wide
        for i in range(wide):
            vec_ref[:, i * cols : (i + 1) * cols] = vec_box[i].astype(F32)[:, :cols]
        for i in range(max(pieces, column - 1)):
            if i < column - 1:
                go.arrived(qkv_far[i])
                go.launch(qkv_near[i + 1])
            if i == 0:
                for _, follow in soon:
                    go.launch(*follow)
            if i < pieces:
                go.arrived(over[i])
                go.launch(passed[i])
        for i in qkv_near + to_mate + passed:
            go.arrived(i)
        for copy in kept:
            copy.start()

    for i in range(1, final + 1):
        if at_step[i]:

            @pl.when(step == i)
            def _():
                for arrival, follow in at_step[i]:
                    if arrival is not None:
                        go.arrived(arrival)
                    go.launch(*follow)

    @pl.when((step > 0) & (step <= blocks))
    def _():
        block = step - 1
        at = rows_at(block, BLOCK)
        marks = tag_box[pl.ds(block // per, 1), :, pl.ds(pl.multiple_of(lax.rem(block, per) * BLOCK, BLOCK), BLOCK)]
        marks = marks[0].astype(F32)
        seg_ref[pl.ds(block, 1)] = marks[0:1][None]
        marks = marks.T
        tag_ref[at, :] = jnp.where(marks[:, 1:2] == 1.0, marks[:, 0:1], -1.0)
        slot = lax.broadcasted_iota(jnp.int32, (BLOCK, 128), 1).astype(F32)
        spot = (slot == marks[:, 2:3]) | (slot == 14 + marks[:, 3:4]) | (slot == 28 + marks[:, 4:5])
        angles = lax.dot_general(
            jnp.where(spot, 1.0, 0.0),
            table[...],
            (((1,), (0,)), ((), ())),
            precision=lax.Precision.HIGHEST,
            preferred_element_type=F32,
        )
        turn_ref[at, :] = angles
        cosine, sine = angles[:, :128], angles[:, 128:]
        unit, _ = norm_parts(tok_box[at, :].astype(F32))
        normed = (unit * vec_ref[0:1, :] + vec_ref[1:2, :]).astype(BF)
        norm_ref[...] = normed
        proj = dot(normed, qkv_box[...], 1, 0)
        parts = [proj[:, i * width : (i + 1) * width] + vec_ref[2 + i : 3 + i, mine] for i in range(3)]
        q_ref[at, :] = turn(parts[0], cosine, sine, head_dim // 2, 1).astype(BF)
        k_ref[at, :] = turn(parts[1], cosine, sine, head_dim // 2, 1).astype(BF)
        v_ref[at, :] = parts[2].astype(BF)
        values_turned[:, at] = parts[2].T.astype(BF)

    @pl.when(step > blocks)
    def _():
        place = step - blocks - 1
        block = lax.rem((n + 1) * per + place, blocks)
        at = rows_at(block, BLOCK)
        query = q_ref[at, :] * jnp.asarray(head_dim**-0.5, BF)
        seg = seg_ref[pl.ds(block, 1)][0]
        masked_query = [
            jnp.where(head_lanes(query.shape, h, head_dim), query, jnp.zeros_like(query)) for h in range(heads)
        ]
        acc[...] = jnp.zeros_like(acc)
        peak[...] = jnp.full_like(peak, -1e30)
        total[...] = jnp.zeros_like(total)

        def body(j, carry):
            start = pl.multiple_of(j * BLOCK, BLOCK)
            key = k_ref[pl.ds(start, BLOCK), :]
            allowed = tag_ref[pl.ds(start, BLOCK), :] == seg
            scores = [jnp.where(allowed, dot(key, masked_query[h], 1, 1), -1e30) for h in range(heads)]
            for h in range(heads):
                lines = slice(h * head_dim, (h + 1) * head_dim)
                old = peak[h : h + 1, :]
                new = jnp.maximum(old, jnp.max(scores[h], axis=0, keepdims=True))
                probs = jnp.exp(scores[h] - new)
                keep = jnp.exp(old - new)
                peak[h : h + 1, :] = new
                total[h : h + 1, :] = total[h : h + 1, :] * keep + jnp.sum(probs, axis=0, keepdims=True)
                value = values_turned[lines, pl.ds(start, BLOCK)]
                acc[lines, :] = acc[lines, :] * keep + dot(value, probs.astype(BF), 1, 0)
            return carry

        low, high = meeting(block, blocks)
        lax.fori_loop(low, high, body, 0)
        parts = [acc[h * head_dim : (h + 1) * head_dim, :] / total[h : h + 1, :] for h in range(heads)]
        out = jnp.concatenate(parts, axis=0).T.astype(BF)
        o_ref[at, :] = out
        o_box[at, :] = out
        lse_ref[pl.ds(block, 1)] = (peak[...] + jnp.log(jnp.maximum(total[...], 1e-30)))[None]

        @pl.when(place < blocks - per)
        def _():
            result(place).start()

    @pl.when(step == final)
    def _():
        for s in range(per):
            result_here(s).start()
        for arrival, follow in at_step[final + 1]:
            go.arrived(arrival)
            go.launch(*follow)
        for copy in own_out + kept:
            copy.wait()
        for s in range(blocks - per):
            result(s).wait()
        for s in range(per):
            result_here(s).wait()
        go.finish()


def forward_call(tok, vec, tag, table, weights, head_dim, wide, narrow):
    qkv, out, up, down = weights
    group_rows, depth = tok.shape
    rows = group_rows * narrow
    width = depth // narrow
    heads = width // head_dim
    blocks = rows // BLOCK
    column = wide // 2
    size = qkv.shape[0]
    half = up.shape[1] // 2
    copies = (wide - 1) + (narrow - 1) + 12 + (2 * column - 1)
    copies += 2 + 3 * (column - 1) + column + 2 * (2 * (2 * column - 1) + 2 * column)
    whole = lambda a: pl.BlockSpec(a.shape, lambda i: (0,) * len(a.shape), pipeline_mode=pl.Buffered(1))
    anywhere = pl.BlockSpec(memory_space=pl.ANY)
    shaped = jax.ShapeDtypeStruct
    head_rows = shaped((rows, width), BF)
    inside = [
        head_rows, head_rows, head_rows, shaped((rows, 256), F32), shaped((rows, depth), BF), shaped((16, depth), F32),
        shaped((blocks, 1, BLOCK), F32), shaped((rows, 1), F32), head_rows, shaped((blocks, 8, BLOCK), F32),
    ]
    inside_specs = [whole(a) for a in inside]
    inside_specs[4] = pl.BlockSpec((BLOCK, depth), lambda i: (jnp.minimum(jnp.maximum(i - 1, 0), blocks - 1), 0))
    outside = [
        shaped((rows, depth), BF), shaped((depth, 3 * width), BF), shaped((group_rows, depth), BF),
        shaped((depth, depth), BF), shaped((depth, half), BF), shaped((depth, half), BF),
    ]
    small = [(size, 3 * width), (size, depth // 2), (size, half), (size, half)]
    return pl.pallas_call(
        functools.partial(forward_kernel, heads, head_dim, wide, narrow),
        grid=(2 * blocks + 1,),
        in_specs=[whole(a) for a in (tok, vec, tag, table)] + [anywhere] * 4,
        out_specs=inside_specs + [anywhere] * 6,
        out_shape=inside + outside,
        scratch_shapes=[
            pltpu.VMEM((wide,) + vec.shape, BF),
            pltpu.VMEM((narrow,) + tag.shape, jnp.int32),
            pltpu.VMEM((rows, depth), BF),
            pltpu.VMEM((depth, 3 * width), BF),
        ]
        + [pltpu.VMEM(shape, BF) for shape in small]
        + [pltpu.VMEM(shape, F32) for shape in small]
        + [
            pltpu.VMEM((width, rows), BF),
            pltpu.VMEM((width, BLOCK), F32),
            pltpu.VMEM((8, BLOCK), F32),
            pltpu.VMEM((8, BLOCK), F32),
            pltpu.VMEM((rows, width), BF),
            pltpu.SemaphoreType.DMA((copies,)),
            pltpu.SemaphoreType.DMA((copies,)),
            pltpu.SemaphoreType.DMA((blocks,)),
            pltpu.SemaphoreType.DMA((blocks,)),
            pltpu.SemaphoreType.DMA((6,)),
            pltpu.SemaphoreType.DMA((7 + blocks // narrow,)),
        ],
        compiler_params=pltpu.CompilerParams(
            collective_id=3, has_side_effects=True, vmem_limit_bytes=48 * 1024 * 1024
        ),
        cost_estimate=pl.CostEstimate(
            flops=heads * rows * rows * width * 4, bytes_accessed=rows * width * 8, transcendentals=heads * rows * rows
        ),
        name="attention_forward",
    )(tok, vec, tag, table, qkv, out, up, down)


class Scatter:
    def __init__(self, go, wide, narrow, split, part, near_in, own, far_out, far_in, box, local, *extra):
        w, self.n = lax.axis_index("wide"), lax.axis_index("narrow")
        self.go, self.column, self.split = go, wide // 2, split
        self.near_in, self.own, self.far_out, self.far_in, self.box = near_in, own, far_out, far_in, box
        z, y, x = w // 2, lax.rem(w, 2), self.n // 2
        near, mate, cross = w + 1 - 2 * y, self.n + 1 - 2 * lax.rem(self.n, 2), lax.rem(self.n + 2, narrow)
        size, cols = part.shape[0] // wide, box.shape[2]
        towards = [across_column(z, d) for d in range(self.column - 1, -1, -1)]
        theirs, ours = [to * 2 + 1 - y for to in towards], [to * 2 + y for to in towards]
        here = pl.ds(pl.multiple_of(x * cols, cols), cols) if split else pl.ds(0, cols)
        self.loads = [
            pltpu.make_async_copy(part.at[rows_at(i, size), here], own.at[k], local.at[k])
            for k, i in enumerate(ours + theirs if split else ours)
        ]
        self.zero = []
        if split:
            self.cross_in, self.out = extra
            there = pl.ds(pl.multiple_of((1 - x) * cols, cols), cols)
            order = list(enumerate(ours + theirs))
            order = order[self.column :] + order[: self.column]
            self.zero = {
                k: go.make(part.at[rows_at(i, size), there], self.cross_in.at[k], narrow=cross) for k, i in order
            }
        self.first = [
            go.make(self.out.at[k] if split else part.at[rows_at(i, size)], near_in.at[k], wide=near)
            for k, i in enumerate(theirs)
        ]
        self.second = [go.make(far_out.at[k], far_in.at[k], wide=i) for k, i in enumerate(ours[:-1])]
        self.over = go.make(box.at[self.n], box.at[self.n], narrow=cross)
        self.beside = go.make(box.at[self.n], box.at[self.n], narrow=mate)
        self.passed = go.make(box.at[cross], box.at[cross], narrow=mate)

    def load(self):
        for copy in self.loads:
            copy.start()
        if self.split:
            self.go.launch(*self.zero.values())

    def summed(self, k):
        self.loads[k].wait()
        value = self.own[k].astype(F32)
        if self.split:
            self.go.arrived(self.zero[k])
            value = value + self.cross_in[k].astype(F32)
        return value

    def send(self, k):
        if self.split:
            self.out[k] = self.summed(self.column + k).astype(BF)
        self.go.launch(self.first[k])

    def relay(self, k):
        self.go.arrived(self.first[k])
        if k < self.column - 1:
            self.far_out[k] = (self.summed(k) + self.near_in[k].astype(F32)).astype(BF)
            self.go.launch(self.second[k])

    def total(self):
        value = self.summed(self.column - 1) + self.near_in[self.column - 1].astype(F32)
        for k in range(self.column - 1):
            self.go.arrived(self.second[k])
            value = value + self.far_in[k].astype(F32)
        self.box[pl.ds(self.n, 1)] = value.astype(BF)[None]
        self.go.launch(self.over, self.beside)

    def share(self):
        self.go.arrived(self.over)
        self.go.launch(self.passed)

    @staticmethod
    def copies(wide, split):
        return 2 * (wide // 2) - 1 + 3 + (wide if split else 0)

    @staticmethod
    def scratch(wide, narrow, rows, cols, split):
        column, size = wide // 2, rows // wide
        cols = cols // 2 if split else cols
        many = wide if split else column
        sizes = [column, many, column - 1, column - 1, narrow]
        first = [pltpu.VMEM((count, size, cols), BF) for count in sizes] + [pltpu.SemaphoreType.DMA((many,))]
        return first + ([pltpu.VMEM((count, size, cols), BF) for count in (wide, column)] if split else [])


def square_sum(value):
    return jnp.sum(jnp.sum(value * value, axis=0, keepdims=True), axis=1, keepdims=True)


def backward_kernel(
    heads, head_dim, wide, narrow,
    q_ref, k_ref, v_ref, o_ref, g_ref, lse_ref, seg_ref, tag_ref, turn_ref, part_out, part_down, part_up,
    grads_out, shards_out, shards_down, shards_up, squares_out,
    q_heads, g_heads, delta, grad_query, send, recv, *boxes,
):
    step = pl.program_id(0)
    rows, width = q_ref.shape
    blocks = rows // BLOCK
    last = blocks - 1
    scale = head_dim**-0.5
    half = head_dim // 2
    go = Copies(send, recv)
    column = wide // 2
    outs = Scatter(go, wide, narrow, False, part_out, *boxes[:6])
    ups = Scatter(go, wide, narrow, False, part_up, *boxes[6:12])
    downs = Scatter(go, wide, narrow, True, part_down, *boxes[12:])

    @pl.when(step == 0)
    def _():
        w, n = lax.axis_index("wide"), lax.axis_index("narrow")
        z, y = w // 2, lax.rem(w, 2)
        greet(
            [{"wide": w + 1 - 2 * y}]
            + [{"wide": across_column(z, d) * 2 + y} for d in range(1, column)]
            + [{"narrow": n + 1 - 2 * lax.rem(n, 2)}, {"narrow": lax.rem(n + 2, narrow)}]
        )
        for k in range(column):
            ups.send(k)
        for scatter in (downs, ups, outs):
            scatter.load()

    part = lambda i: range(column * i // 4, column * (i + 1) // 4)
    plan = {
        2: [(ups.relay, part(0))],
        4: [(ups.relay, part(1))],
        5: [(downs.send, range(column // 2))],
        6: [(ups.relay, part(2))],
        7: [(downs.send, range(column // 2, column))],
        8: [(ups.relay, part(3)), (outs.send, range(column))],
        10: [(downs.relay, part(0))],
        11: [(downs.relay, part(1)), (ups.total, None)],
        12: [(downs.relay, part(2))],
        13: [(downs.relay, part(3)), (ups.share, None)],
        14: [(outs.relay, range(column // 2))],
        15: [(outs.relay, range(column // 2, column)), (downs.total, None)],
    }

    def act(i):
        for action, ks in plan[i]:
            for k in [None] if ks is None else ks:
                action() if k is None else action(k)

    for i in range(0, 2 * blocks, 2):
        if i in plan:

            @pl.when(step == i // 2)
            def _():
                act(i)

    @pl.when(step == 0)
    def _():
        grad_query[...] = jnp.zeros_like(grad_query)
        row = lax.broadcasted_iota(jnp.int32, (8, width), 0)
        lane = lax.broadcasted_iota(jnp.int32, (8, width), 1)
        pick = jnp.where(lane // head_dim == row, 1.0, 0.0)

        def prepare(i, carry):
            at = pl.ds(pl.multiple_of(i * BLOCK, BLOCK), BLOCK)
            query = q_ref[at, :] * jnp.asarray(scale, BF)
            grad = g_ref[at, :]
            for h in range(heads):
                lanes = head_lanes(query.shape, h, head_dim)
                q_heads[h, at, :] = jnp.where(lanes, query, jnp.zeros_like(query))
                g_heads[h, at, :] = jnp.where(lanes, grad, jnp.zeros_like(grad))
            product = grad.astype(F32) * o_ref[at, :].astype(F32)
            delta[pl.ds(i, 1)] = lax.dot_general(
                pick,
                product,
                (((1,), (1,)), ((), ())),
                precision=lax.Precision.HIGHEST,
                preferred_element_type=F32,
            )[None]
            return carry

        lax.fori_loop(0, blocks, prepare, 0)

    key = k_ref[...]
    value = v_ref[...]
    tag = tag_ref[...]
    masked_key = [jnp.where(head_lanes(key.shape, h, head_dim), key, jnp.zeros_like(key)) for h in range(heads)]

    def body(i, carry):
        for half_step in range(1, 2 * blocks, 2):
            if half_step in plan:

                @pl.when((step == half_step // 2) & (i == blocks // 2))
                def _():
                    act(half_step)

        grad_key, grad_value = carry
        at = pl.ds(pl.multiple_of(i * BLOCK, BLOCK), BLOCK)
        allowed = tag == seg_ref[pl.ds(i, 1), :]
        lse = lse_ref[pl.ds(i, 1)][0]
        dlt = delta[pl.ds(i, 1)][0]
        total = None
        for h in range(heads):
            query = q_heads[h, at, :]
            grad = g_heads[h, at, :]
            scores = dot(key, query, 1, 1)
            probs = jnp.where(allowed, jnp.exp(scores - lse[h : h + 1, :]), 0.0)
            grad_probs = dot(value, grad, 1, 1)
            grad_scores = (probs * (grad_probs - dlt[h : h + 1, :])).astype(BF)
            grad_value = grad_value + dot(probs.astype(BF), grad, 1, 0)
            grad_key = grad_key + dot(grad_scores, query, 1, 0)
            term = dot(grad_scores, masked_key[h], 0, 0)
            total = term if total is None else total + term
        grad_query[at, :] += total
        return grad_key, grad_value

    zero = jnp.zeros((BLOCK, width), F32)
    low, high = meeting(step, blocks)
    grad_key, grad_value = lax.fori_loop(low, high, body, (zero, zero))
    here = pl.ds(pl.multiple_of(step * BLOCK, BLOCK), BLOCK)
    cosine, sine = turn_ref[here, :128], turn_ref[here, 128:]
    grads_out[here, width : 2 * width] = turn(grad_key, cosine, sine, half, -1).astype(BF)
    grads_out[here, 2 * width :] = grad_value.astype(BF)

    @pl.when(step == last)
    def _():
        downs.share()
        outs.total()

        def finish(i, carry):
            at = pl.ds(pl.multiple_of(i * BLOCK, BLOCK), BLOCK)
            grads = grad_query[at, :] * scale
            grads_out[at, :width] = turn(grads, turn_ref[at, :128], turn_ref[at, 128:], half, -1).astype(BF)
            return carry

        lax.fori_loop(0, blocks, finish, 0)
        outs.share()
        go.finish()
        squares = jnp.zeros((1, 1), F32)
        for box in (outs.box, ups.box):
            for i in range(2):
                squares += square_sum(box[i].astype(F32) + box[i + 2].astype(F32))
        for i in range(narrow):
            squares += square_sum(downs.box[i].astype(F32))
        squares_out[...] = jnp.broadcast_to(squares, squares_out.shape)
        shards_out[...] = outs.box[...]
        shards_down[...] = downs.box[...]
        shards_up[...] = ups.box[...]


def backward_call(q, k, v, o, g, lse, seg_rows, tag_col, turns, part_out, part_down, part_up, head_dim, wide, narrow):
    rows, width = q.shape
    heads = width // head_dim
    blocks = rows // BLOCK
    whole = lambda a: pl.BlockSpec(a.shape, lambda i: (0,) * len(a.shape), pipeline_mode=pl.Buffered(1))
    block = pl.BlockSpec((BLOCK, width), lambda i: (i, 0))
    anywhere = pl.BlockSpec(memory_space=pl.ANY)
    depth = part_up.shape[0]
    results = [
        jax.ShapeDtypeStruct((rows, 3 * width), BF),
        jax.ShapeDtypeStruct((narrow, depth // wide, part_out.shape[1]), BF),
        jax.ShapeDtypeStruct((narrow, depth // wide, part_down.shape[1] // 2), BF),
        jax.ShapeDtypeStruct((narrow, depth // wide, part_up.shape[1]), BF),
        jax.ShapeDtypeStruct((8, 128), F32),
    ]
    copies = 2 * Scatter.copies(wide, False) + Scatter.copies(wide, True)
    return pl.pallas_call(
        functools.partial(backward_kernel, heads, head_dim, wide, narrow),
        grid=(blocks,),
        in_specs=[
            whole(q), block, block, whole(o), whole(g), whole(lse), whole(seg_rows),
            pl.BlockSpec((BLOCK, 1), lambda i: (i, 0)),
            whole(turns), anywhere, anywhere, anywhere,
        ],
        out_specs=[whole(a) for a in results],
        out_shape=results,
        scratch_shapes=[
            pltpu.VMEM((heads, rows, width), BF),
            pltpu.VMEM((heads, rows, width), BF),
            pltpu.VMEM((blocks, 8, BLOCK), F32),
            pltpu.VMEM((rows, width), F32),
            pltpu.SemaphoreType.DMA((copies,)),
            pltpu.SemaphoreType.DMA((copies,)),
        ]
        + Scatter.scratch(wide, narrow, depth, part_out.shape[1], False)
        + Scatter.scratch(wide, narrow, depth, part_up.shape[1], False)
        + Scatter.scratch(wide, narrow, depth, part_down.shape[1], True),
        compiler_params=pltpu.CompilerParams(
            collective_id=4, has_side_effects=True, vmem_limit_bytes=60 * 1024 * 1024
        ),
        cost_estimate=pl.CostEstimate(
            flops=heads * rows * rows * width * 7, bytes_accessed=rows * width * 20, transcendentals=heads * rows * rows
        ),
        name="attention_backward",
    )(q, k, v, o, g, lse, seg_rows, tag_col, turns, part_out, part_down, part_up)


def norm_parts(values):
    center = values - jnp.mean(values, axis=-1, keepdims=True)
    inverse = lax.rsqrt(jnp.mean(center * center, axis=-1, keepdims=True) + 1e-06)
    return center * inverse, inverse


def norm_back(grads, gain, unit, inverse):
    scaled = grads * gain
    return inverse * (
        scaled - jnp.mean(scaled, axis=-1, keepdims=True) - unit * jnp.mean(scaled * unit, axis=-1, keepdims=True)
    )


def adamw(param, grad, first, second, clip, rate, decay, fix_first, fix_second):
    clipped = grad * clip
    moment = 0.9 * first + 0.1 * clipped
    square = 0.999 * second + 0.001 * clipped * clipped
    direction = moment / fix_first / (jnp.sqrt(square / fix_second) + 1e-08)
    return (param - rate * (direction + decay * param), moment, square)


def on_device(
    tokens, cotangent, segment_ids, key_keep, patch_coords, step_count,
    weight_qkv, weight_out, weight_up, weight_down, vectors,
    first_qkv, first_out, first_up, first_down, first_vectors,
    second_qkv, second_out, second_up, second_down, second_vectors,
):
    rows, width = tokens.shape
    hidden = weight_up.shape[1]
    head_dim = width // HEADS
    narrow = lax.axis_size("narrow")
    wide = lax.axis_size("wide")
    shard_rows = width // wide
    me = lax.axis_index("narrow")
    side = me % 2
    mine = width // narrow
    half_hidden = hidden // 2
    group = rows * narrow

    def mate(value):
        return lax.ppermute(value, "narrow", [(i, i ^ 1) for i in range(narrow)])

    def across(value):
        return lax.ppermute(value, "narrow", [(i, i ^ 2) for i in range(narrow)])

    def take(value, start, size, axis=1):
        return lax.dynamic_slice_in_dim(value, start, size, axis)

    shard_cols = vectors.shape[1]
    vec_shard = jnp.pad(vectors.astype(BF), ((0, 16 - vectors.shape[0]), (0, -shard_cols % 128)))
    tag = jnp.concatenate([segment_ids[None], key_keep[None], patch_coords, patch_coords], axis=0)
    (
        query, keys, values, turns, normed1_all, vec, seg_rows, tag_col, mixed_mine, lse,
        tokens_all, qkv_w, mixed, out_w, up_w, down_w,
    ) = forward_call(
        tokens, vec_shard, tag, rotary_table(head_dim), (weight_qkv, weight_out, weight_up, weight_down),
        head_dim, wide, narrow,
    )
    vec = vec[: vectors.shape[0]]
    xin = tokens.astype(F32)
    unit1, inverse1 = norm_parts(xin)
    cot_pair = jnp.concatenate([cotangent, mate(cotangent)], axis=0)

    resid = xin + (dot(mixed, out_w, 1, 0) + vec[5])
    unit2, inverse2 = norm_parts(resid)
    normed2 = (unit2 * vec[6] + vec[7]).astype(BF)
    normed2_pair = jnp.concatenate([normed2, mate(normed2)], axis=0)
    up_bias = take(vec[9:].reshape(1, -1), side * half_hidden, half_hidden)
    up_pre = dot(normed2_pair, up_w, 1, 0) + up_bias
    erf_part = 0.5 * (1.0 + lax.erf(up_pre * (0.5**0.5)))
    act = (up_pre * erf_part).astype(BF)
    slope = erf_part + up_pre * (jnp.exp(-0.5 * up_pre * up_pre) * ((2.0 * jnp.pi) ** -0.5))
    part_down = dot(cot_pair, act, 0, 0).astype(BF)
    down_part = dot(act, down_w, 1, 1)
    down = down_part[:rows] + mate(down_part[rows:])
    layer_out = (resid + (down + vec[8])).astype(BF)

    grad_up_act = (dot(cot_pair, down_w, 1, 0) * slope).astype(BF)
    part_up = dot(normed2_pair, grad_up_act, 0, 0).astype(BF)
    grad_normed2_part = dot(grad_up_act, up_w, 1, 1)
    grad_normed2 = grad_normed2_part[:rows] + mate(grad_normed2_part[rows:])
    cot = cotangent.astype(F32)
    grad_resid = cot + norm_back(grad_normed2, vec[6], unit2, inverse2)
    grad_branch = grad_resid.astype(BF)
    grad_mixed = dot(grad_branch, out_w, 1, 1).astype(BF)
    part_out = dot(mixed, grad_branch, 0, 0)
    own_out = take(part_out, side * (width // 2), width // 2)
    other_out = take(part_out, (1 - side) * (width // 2), width // 2)
    part_out = (own_out + mate(other_out.astype(BF)).astype(F32)).astype(BF)

    grad_mixed_mine = lax.all_to_all(grad_mixed, "narrow", 1, 0, tiled=True)
    grad_proj, shards_out, shards_down, shards_up, squares = backward_call(
        query, keys, values, mixed_mine, grad_mixed_mine, lse, seg_rows[:, 0], tag_col, turns, part_out, part_down, part_up, head_dim, wide, narrow,
    )
    proj_sums = jnp.sum(grad_proj.astype(F32), axis=0).reshape(3, mine)
    proj_rows = lax.dynamic_update_slice(jnp.zeros((3, width), F32), proj_sums, (0, me * mine))
    up_sums = jnp.sum(grad_up_act.astype(F32), axis=0)
    up_rows = lax.dynamic_update_slice(jnp.zeros((hidden,), F32), up_sums, (side * half_hidden,))
    vector_part = jnp.concatenate(
        [
            jnp.zeros((2, width), F32),
            proj_rows,
            jnp.sum(grad_branch.astype(F32), axis=0)[None],
            jnp.sum(grad_normed2 * unit2, axis=0)[None],
            jnp.sum(grad_normed2, axis=0)[None],
            jnp.sum(cot, axis=0)[None],
            up_rows.reshape(hidden // width, width),
            jnp.zeros((16 - vectors.shape[0], width), F32),
        ],
        axis=0,
    )
    grad_normed1, total_qkv, vector_total, square_total = tail_call(
        normed1_all, grad_proj, qkv_w, tokens_all, vector_part, squares, wide, narrow
    )
    grad_tokens = (grad_resid + norm_back(grad_normed1, vec[0], unit1, inverse1)).astype(BF)

    def join(shards):
        shards = shards.astype(F32)
        return jnp.concatenate([shards[0] + shards[2], shards[1] + shards[3]], axis=1)

    total_up = join(shards_up)
    total_down = jnp.concatenate([shards_down[i] for i in (0, 2, 1, 3)], axis=1).astype(F32)
    total_out = join(shards_out)
    total_qkv = total_qkv.astype(F32)
    grad_norm = jnp.sqrt(square_total[0, 0])
    clip = 1.0 / jnp.maximum(grad_norm, 1.0)
    count = step_count[0].astype(F32)
    rate = 0.4 * count / (count + 4.0)
    decay = 0.04 + 0.018 * count
    fix_first = 1.0 - jnp.power(0.9, count)
    fix_second = 1.0 - jnp.power(0.999, count)
    grad_vectors = vector_total[: vectors.shape[0], :shard_rows]

    def update(param, grad, first, second, decay_here):
        return adamw(param, grad, first, second, clip, rate, decay_here, fix_first, fix_second)

    new_qkv = update(weight_qkv, total_qkv, first_qkv, second_qkv, decay)
    new_out = update(weight_out, total_out, first_out, second_out, decay)
    new_up = update(weight_up, total_up, first_up, second_up, decay)
    new_down = update(weight_down, total_down, first_down, second_down, decay)
    new_vectors = update(vectors, grad_vectors, first_vectors, second_vectors, 0.0)
    news = (new_qkv, new_out, new_up, new_down, new_vectors)
    return (layer_out, grad_tokens) + tuple(n[i] for i in range(3) for n in news) + (grad_norm, grad_vectors[8])


def solution(mesh):
    by_token = P(("wide", "narrow"), None)
    ids = P(("wide", "narrow"))
    by_row = P("wide", None)
    by_column = P(None, "wide")
    params = (by_row,) * 4 + (by_column,)
    return jax.shard_map(
        on_device,
        mesh=mesh,
        in_specs=(by_token, by_token, ids, ids, P(None, ("wide", "narrow")), P()) + params * 3,
        out_specs=(by_token, by_token) + params * 3 + (P(), P("wide")),
        check_vma=False,
    )
```

```python
import functools

import jax
import jax.numpy as jnp
from jax import lax
from jax.experimental import pallas as pl
from jax.experimental.pallas import tpu as pltpu
from jax.sharding import PartitionSpec as P

HEADS = 16
BLOCK = 256
BF = jnp.bfloat16
F32 = jnp.float32
MESH = pl.DeviceIdType.MESH


def dot(a, b, ca, cb):
    return lax.dot_general(a, b, (((ca,), (cb,)), ((), ())), preferred_element_type=F32)


def swap_halves(x, half):
    lane = lax.broadcasted_iota(jnp.int32, x.shape, 1)
    width = x.shape[1]
    return jnp.where(
        lane % (2 * half) < half, pltpu.roll(x, width - half, 1), pltpu.roll(x, half, 1)
    )


def turn(x, cosine, sine, half, sign):
    parts = []
    for start in range(0, x.shape[1], 128):
        part = x[:, start : start + 128]
        other = swap_halves(part, half) * sine
        parts.append(part * cosine + other if sign > 0 else part * cosine - other)
    return jnp.concatenate(parts, axis=1)


def rotary_table(head_dim):
    half = head_dim // 2
    lane = jnp.arange(128)
    pair = lane % half
    rates = jnp.power(10000.0, -(pair // 3).astype(F32) / ((half + 2) // 3))
    row = jnp.arange(128)
    axis = row // 14
    value = (row % 14).astype(F32)
    live = (axis[:, None] == (pair % 3)[None, :]) & (row[:, None] < 42)
    angle = value[:, None] * rates[None, :]
    signs = jnp.where(lane % head_dim < half, -1.0, 1.0)
    return jnp.concatenate(
        [
            jnp.where(live, jnp.cos(angle), 0.0),
            jnp.where(live, jnp.sin(angle) * signs[None, :], 0.0),
        ],
        axis=1,
    )


def greet(targets):
    barrier = pltpu.get_barrier_semaphore()
    for target in targets:
        pl.semaphore_signal(barrier, inc=1, device_id=target, device_id_type=MESH)
    pl.semaphore_wait(barrier, len(targets))


def others(name, index, size):
    return [{name: lax.rem(index + d, size)} for d in range(1, size)]


class Copies:
    def __init__(self, send, recv):
        self.send, self.recv, self.all = send, recv, []

    def make(self, src, dst, **target):
        i = len(self.all)
        copy = pltpu.make_async_remote_copy(
            src_ref=src, dst_ref=dst, send_sem=self.send.at[i], recv_sem=self.recv.at[i],
            device_id=target, device_id_type=MESH,
        )
        self.all.append([copy, False])
        return i

    def launch(self, *indices):
        for i in indices:
            self.all[i][0].start()

    def start(self, src, dst, **target):
        i = self.make(src, dst, **target)
        self.launch(i)
        return i

    def arrived(self, i):
        if not self.all[i][1]:
            self.all[i][0].wait_recv()
            self.all[i][1] = True

    def finish(self):
        for i in range(len(self.all)):
            self.arrived(i)
        for copy, _ in self.all:
            copy.wait_send()


def across_column(z, d):
    bits = [1 << b for b in range(d.bit_length()) if d >> b & 1]
    return z + sum(bit * (1 - 2 * lax.rem(z // bit, 2)) for bit in bits)


def rows_at(index, size):
    return pl.ds(pl.multiple_of(index * size, size), size)


def tail_kernel(
    wide, narrow, normed, grad_proj, weight_in, tok_in, vec_in, squares_in, normed_out, qkv_out, vec_out, square_out,
    partial, mate_in, cross_out, cross_in, near_in, far_out, far_in, shards, vec_box, sums,
    slices, slice_box, square_box, part, weight, tok, send, recv, local,
):
    w, n = lax.axis_index("wide"), lax.axis_index("narrow")
    column = wide // 2
    z, y = w // 2, lax.rem(w, 2)
    x, c = n // 2, lax.rem(n, 2)
    near, mate, cross = w + 1 - 2 * y, n + 1 - 2 * c, lax.rem(n + 2, narrow)
    wide_rows, group_rows = part.shape[0] // wide, normed_out.shape[0]
    towards = [across_column(z, d) for d in range(column - 1, -1, -1)]
    loads = [
        pltpu.make_async_copy(weight_in, weight, local.at[0]),
        pltpu.make_async_copy(tok_in, tok, local.at[1]),
    ]
    for copy in loads:
        copy.start()
    greet(others("wide", w, wide) + others("narrow", n, narrow))
    go = Copies(send, recv)
    depth, chunk = part.shape[0], 128
    sent = lambda k: go.make(part.at[rows_at(towards[k] * 2 + 1 - y, wide_rows)], near_in.at[k], wide=near)
    first = [sent(k) for k in range(column)]
    one_each = wide_rows == chunk

    def rows_of(index):
        at = rows_at(index, chunk)
        part[at, :] = dot(normed[:, at], grad_proj[...], 0, 0).astype(BF)

    if one_each:
        for k in range(column):
            rows_of(towards[k] * 2 + 1 - y)
            go.launch(first[k])

        def ours(k, carry):
            rows_of(lax.rem(z + 1 + k, column) * 2 + y)
            return carry

        lax.fori_loop(0, column, ours, 0)
    else:

        def each(index, carry):
            rows_of(index)
            return carry

        lax.fori_loop(0, depth // chunk, each, 0)
        go.launch(*first)
    for copy in loads:
        copy.wait()

    seconds, kept = [], []

    def relay(k):
        go.arrived(first[k])
        value = part[rows_at(towards[k] * 2 + y, wide_rows), :].astype(F32) + near_in[k].astype(F32)
        if k < column - 1:
            far_out[k] = value.astype(BF)
            seconds.append(go.start(far_out.at[k], far_in.at[k], wide=towards[k] * 2 + y))
        else:
            kept.append(value)

    sums[...] = jnp.zeros_like(sums)
    owners = [(1 - x) * 2 + 1 - c, (1 - x) * 2 + c, x * 2 + 1 - c, n]
    half = group_rows // 2
    mates, overs = [], []
    for slot, owner in enumerate(owners):

        def body(i, carry):
            at = pl.ds(pl.multiple_of(owner * group_rows + i * BLOCK, BLOCK), BLOCK)
            here = pl.ds(pl.multiple_of(i * BLOCK, BLOCK), BLOCK)
            grads = dot(grad_proj[at, :], weight[...], 1, 1)
            unit, _ = norm_parts(tok[at, :].astype(F32))
            sums[0:1, :] += jnp.sum(grads * unit, axis=0, keepdims=True)
            sums[1:2, :] += jnp.sum(grads, axis=0, keepdims=True)
            if slot < 3:
                partial[slot, here, :] = grads.astype(BF)
            else:
                normed_out[here, :] = grads
            return carry

        lax.fori_loop(0, group_rows // BLOCK, body, 0)
        if slot == 0:
            mates.append(go.start(partial.at[0], mate_in.at[0], narrow=mate))
        if slot == 2:
            mates.append(go.start(partial.at[2], mate_in.at[1], narrow=mate))
        if slot == 1:
            go.arrived(mates[0])
            for p in range(2):
                at = pl.ds(p * half, half)
                cross_out[at, :] = (partial[1, at, :].astype(F32) + mate_in[0, at, :].astype(F32)).astype(BF)
                overs.append(go.start(cross_out.at[at], cross_in.at[at], narrow=cross))
        for k in range(column * slot // 4, column * (slot + 1) // 4):
            if k < column - 1:
                relay(k)

    vec_box[pl.ds(n, 1)] = vec_in[...][None]
    vec_box[pl.ds(n, 1), 0:2, :] = sums[0:2, :][None]
    vecs = [go.start(vec_box.at[n], vec_box.at[n], narrow=lax.rem(n + d, narrow)) for d in range(1, narrow)]
    for i in vecs:
        go.arrived(i)
    group = vec_box[0]
    for i in range(1, narrow):
        group = group + vec_box[i]
    cols = group.shape[1] // wide
    slices[...] = jnp.zeros_like(slices)
    for i in range(wide):
        slices[i, :, :cols] = group[:, i * cols : (i + 1) * cols]
    peers = [lax.rem(w + d, wide) for d in range(1, wide)]
    pieces = [go.start(slices.at[peer], slice_box.at[w], wide=peer) for peer in peers]
    slice_box[pl.ds(w, 1)] = slices[pl.ds(w, 1)]
    relay(column - 1)
    total = kept[0]
    for k in range(column - 1):
        go.arrived(seconds[k])
        total = total + far_in[k].astype(F32)
    shards[pl.ds(n, 1)] = total.astype(BF)[None]
    over = go.start(shards.at[n], shards.at[n], narrow=cross)
    beside = go.start(shards.at[n], shards.at[n], narrow=mate)

    go.arrived(mates[1])
    for p in range(2):
        go.arrived(overs[p])
        at = pl.ds(p * half, half)
        normed_out[at, :] += mate_in[1, at, :].astype(F32) + cross_in[at, :].astype(F32)
    for i in pieces:
        go.arrived(i)
    vectors = slice_box[0]
    for i in range(1, wide):
        vectors = vectors + slice_box[i]
    vec_out[...] = vectors

    go.arrived(over)
    passed = go.start(shards.at[cross], shards.at[cross], narrow=mate)
    for i in (beside, passed):
        go.arrived(i)
    squares = square_sum(vectors)
    width = part.shape[1] // 3
    for i in range(narrow):
        shard = shards[i]
        squares += square_sum(shard.astype(F32))
        for j in range(3):
            qkv_out[:, (j * narrow + i) * width : (j * narrow + i + 1) * width] = shard[:, j * width : (j + 1) * width]
    square_box[pl.ds(w, 1)] = (squares_in[...] + squares)[None]
    for peer in peers:
        go.start(square_box.at[w], square_box.at[w], wide=peer)
    go.finish()
    total = square_box[0]
    for i in range(1, wide):
        total = total + square_box[i]
    square_out[...] = total


def tail_call(normed, grad_proj, weight, tok, vec_in, squares_in, wide, narrow):
    depth, cols = weight.shape
    rows = tok.shape[0] // narrow
    wide_rows = depth // wide
    column = wide // 2
    copies = 2 * column - 1 + 2 + (narrow - 1) + 2 + 3 + 2 * (wide - 1)
    vmem = pl.BlockSpec(memory_space=pltpu.VMEM)
    anywhere = pl.BlockSpec(memory_space=pl.ANY)
    return pl.pallas_call(
        functools.partial(tail_kernel, wide, narrow),
        in_specs=[vmem, vmem, anywhere, anywhere, vmem, vmem],
        out_specs=[vmem] * 4,
        out_shape=[
            jax.ShapeDtypeStruct((rows, depth), F32),
            jax.ShapeDtypeStruct((wide_rows, narrow * cols), BF),
            jax.ShapeDtypeStruct((16, 128), F32),
            jax.ShapeDtypeStruct((8, 128), F32),
        ],
        scratch_shapes=[
            pltpu.VMEM((3, rows, depth), BF),
            pltpu.VMEM((2, rows, depth), BF),
            pltpu.VMEM((rows, depth), BF),
            pltpu.VMEM((rows, depth), BF),
            pltpu.VMEM((column, wide_rows, cols), BF),
            pltpu.VMEM((column - 1, wide_rows, cols), BF),
            pltpu.VMEM((column - 1, wide_rows, cols), BF),
            pltpu.VMEM((narrow, wide_rows, cols), BF),
            pltpu.VMEM((narrow,) + vec_in.shape, F32),
            pltpu.VMEM((8, depth), F32),
            pltpu.VMEM((wide, 16, 128), F32),
            pltpu.VMEM((wide, 16, 128), F32),
            pltpu.VMEM((wide, 8, 128), F32),
            pltpu.VMEM((depth, cols), BF),
            pltpu.VMEM((depth, cols), BF),
            pltpu.VMEM(tok.shape, BF),
            pltpu.SemaphoreType.DMA((copies,)),
            pltpu.SemaphoreType.DMA((copies,)),
            pltpu.SemaphoreType.DMA((2,)),
        ],
        compiler_params=pltpu.CompilerParams(
            collective_id=1, has_side_effects=True, vmem_limit_bytes=56 * 1024 * 1024
        ),
        name="tail",
    )(normed, grad_proj, weight, tok, vec_in, squares_in)


CLIP = 784


def head_lanes(shape, head, head_dim):
    lane = lax.broadcasted_iota(jnp.int32, shape, 1)
    return lane // head_dim == head


def meeting(block, blocks):
    before, after = CLIP // BLOCK, -(-2 * CLIP // BLOCK)
    low = before * (block // after)
    high = blocks - (blocks - after) * (1 - jnp.minimum(block // before, 1))
    return low, high


def forward_kernel(
    heads, head_dim, wide, narrow,
    tok, vec, tag, table, qkv_f32, out_f32, up_f32, down_f32,
    q_ref, k_ref, v_ref, turn_ref, norm_ref, vec_ref, seg_ref, tag_ref, o_ref, lse_ref,
    tok_all, qkv_all, mixed_ref, out_all, up_all, down_all,
    vec_box, tag_box, tok_box, qkv_box, qkv_own, out_own, up_own, down_own, stage_qkv, stage_out, stage_up, stage_down,
    values_turned, acc, peak, total, o_box, send, recv, mix_send, mix_recv, local, leave,
):
    step = pl.program_id(0)
    rows, width = q_ref.shape
    depth = tok.shape[1]
    blocks = rows // BLOCK
    per = blocks // narrow
    final = 2 * blocks
    w, n = lax.axis_index("wide"), lax.axis_index("narrow")
    column = wide // 2
    z, y, side = w // 2, lax.rem(w, 2), lax.rem(n, 2)
    near, mate, cross = w + 1 - 2 * y, n + 1 - 2 * side, lax.rem(n + 2, narrow)
    source = target = lambda d: across_column(z, d) * 2 + y
    beside = lambda d: across_column(z, d) * 2 + 1 - y
    wide_rows, out_half = out_own.shape
    half = up_own.shape[1]
    group_rows = tok.shape[0]

    loads = [
        pltpu.make_async_copy(
            qkv_f32.at[:, pl.ds(pl.multiple_of(i * depth + n * width, width), width)],
            stage_qkv.at[:, pl.ds(i * width, width)],
            local.at[i],
        )
        for i in range(3)
    ] + [
        pltpu.make_async_copy(
            whole.at[:, pl.ds(pl.multiple_of(side * size, size), size)], stage, local.at[3 + i]
        )
        for i, (whole, stage, size) in enumerate(
            [(out_f32, stage_out, out_half), (up_f32, stage_up, half), (down_f32, stage_down, half)]
        )
    ]

    go = Copies(send, recv)
    small = [go.make(vec, vec_box.at[w], wide=lax.rem(w + d, wide)) for d in range(1, wide)]
    small += [go.make(tag, tag_box.at[n], narrow=lax.rem(n + d, narrow)) for d in range(1, narrow)]
    pieces = 4
    piece = group_rows // pieces
    token_rows = lambda i, p: tok_box.at[rows_at(i * pieces + p, piece)]
    own_piece = lambda p: tok.at[pl.ds(p * piece, piece)]
    over = [go.make(own_piece(p), token_rows(n, p), narrow=cross) for p in range(pieces)]
    to_mate = [go.make(own_piece(p), token_rows(n, p), narrow=mate) for p in range(pieces)]
    passed = [go.make(token_rows(cross, p), token_rows(cross, p), narrow=mate) for p in range(pieces)]
    qkv_at = lambda i: qkv_box.at[rows_at(i, wide_rows)]
    qkv_far = [go.make(qkv_own, qkv_at(w), wide=target(d)) for d in range(1, column)]
    qkv_near = [go.make(qkv_own, qkv_at(w), wide=near)]
    qkv_near += [go.make(qkv_at(source(d)), qkv_at(source(d)), wide=near) for d in range(1, column)]

    at_step = [[] for _ in range(final + 2)]
    soon = []
    out_cols = pl.ds(pl.multiple_of(side * out_half, out_half), out_half)
    out_at = lambda i: out_all.at[rows_at(i, wide_rows), out_cols]
    out_near = [go.make(out_own, out_at(w), wide=near)]
    out_starts = [go.make(out_own, out_at(w), narrow=mate)]
    at_step[blocks + 6].append((None, [out_near[0]]))
    out_late = []
    for d in range(1, column):
        out_starts.append(go.make(out_own, out_at(w), wide=target(d)))
        ref = out_at(source(d))
        out_near.append(go.make(ref, ref, wide=near))
        out_late.append((out_starts[-1], [out_near[-1], go.make(ref, ref, narrow=mate)]))
    for d in range(column):
        ref = out_at(beside(d))
        out_late.append((out_near[d], [go.make(ref, ref, narrow=mate)]))

    quarter = half // 4
    shared = pl.ds(pl.multiple_of(n // 2 * quarter, quarter), quarter)
    both = pl.ds(2 * quarter, 2 * quarter)
    own_out = [pltpu.make_async_copy(out_own, out_at(w), leave.at[0])]

    def spread(own, result, cols, steps, slot):
        piece_at = lambda i: result.at[rows_at(i, wide_rows), cols]
        over_x = cols is shared
        passes = lambda i: [go.make(piece_at(i), piece_at(i), narrow=cross)] if over_x else []
        nears = [go.make(own.at[:, cols], piece_at(w), wide=near)]
        (soon if over_x else at_step[steps[0]]).append((None, nears[:1]))
        starts = [go.make(own.at[:, cols], piece_at(w), narrow=cross)] if over_x else []
        for d in range(1, column):
            starts.append(go.make(own.at[:, cols], piece_at(w), wide=target(d)))
            ref = piece_at(source(d))
            nears.append(go.make(ref, ref, wide=near))
            at_step[steps[1][(d - 1) * 3 // (column - 1)]].append((starts[-1], [nears[-1]] + passes(source(d))))
        if over_x:
            for d in range(column):
                at_step[steps[2]].append((nears[d], passes(beside(d))))
        own_out.append(pltpu.make_async_copy(own.at[:, cols], piece_at(w), leave.at[slot]))
        return starts

    b = blocks
    weight_starts = spread(up_own, up_all, shared, (0, (4, 4, 4), b + 2), 1)
    weight_starts += spread(down_own, down_all, shared, (0, (b + 2, b + 2, b + 2), b + 4), 2)
    at_step[6].append((None, spread(up_own, up_all, both, (1, (b + 3, b + 5, b + 6)), 3)))
    at_step[b + 3].append((None, spread(down_own, down_all, both, (b + 2, (b + 7, b + 8, b + 9)), 4)))
    at_step[b + 6].append((None, out_starts))
    at_step[final + 1] += out_late

    mine = pl.ds(pl.multiple_of(n * width, width), width)

    def result(s):
        at = lax.rem((n + 1) * per + s, blocks)
        return pltpu.make_async_remote_copy(
            src_ref=o_box.at[rows_at(at, BLOCK)],
            dst_ref=mixed_ref.at[rows_at(lax.rem(s, per), BLOCK), mine],
            send_sem=mix_send.at[s],
            recv_sem=mix_recv.at[s],
            device_id={"narrow": lax.rem(n + 1 + s // per, narrow)},
            device_id_type=MESH,
        )

    def result_here(s):
        return pltpu.make_async_copy(
            o_box.at[rows_at(n * per + s, BLOCK)], mixed_ref.at[rows_at(s, BLOCK), mine], leave.at[7 + s]
        )

    kept = [
        pltpu.make_async_copy(tok_box, tok_all, leave.at[5]),
        pltpu.make_async_copy(qkv_box, qkv_all, leave.at[6]),
    ]

    @pl.when(step == 0)
    def _():
        for copy in loads:
            copy.start()
        greet(others("wide", w, wide) + others("narrow", n, narrow))
        go.launch(*small, *over)
        for copy in loads[:3]:
            copy.wait()
        qkv_own[...] = stage_qkv[...].astype(BF)
        go.launch(*qkv_far, qkv_near[0], *to_mate)
        for copy, stage, own in zip(
            loads[3:], (stage_out, stage_up, stage_down), (out_own, up_own, down_own)
        ):
            copy.wait()
            own[...] = stage[...].astype(BF)
        go.launch(*weight_starts)
        tok_box[rows_at(n, group_rows), :] = tok[...]
        qkv_box[rows_at(w, wide_rows), :] = qkv_own[...]
        vec_box[pl.ds(w, 1)] = vec[...][None]
        tag_box[pl.ds(n, 1)] = tag[...][None]
        for copy in own_out:
            copy.start()
        for i in small:
            go.arrived(i)
        cols = depth // wide
        for i in range(wide):
            vec_ref[:, i * cols : (i + 1) * cols] = vec_box[i].astype(F32)[:, :cols]
        for i in range(max(pieces, column - 1)):
            if i < column - 1:
                go.arrived(qkv_far[i])
                go.launch(qkv_near[i + 1])
            if i == 0:
                for _, follow in soon:
                    go.launch(*follow)
            if i < pieces:
                go.arrived(over[i])
                go.launch(passed[i])
        for i in qkv_near + to_mate + passed:
            go.arrived(i)
        for copy in kept:
            copy.start()

    for i in range(1, final + 1):
        if at_step[i]:

            @pl.when(step == i)
            def _():
                for arrival, follow in at_step[i]:
                    if arrival is not None:
                        go.arrived(arrival)
                    go.launch(*follow)

    @pl.when((step > 0) & (step <= blocks))
    def _():
        block = step - 1
        at = rows_at(block, BLOCK)
        marks = tag_box[pl.ds(block // per, 1), :, pl.ds(pl.multiple_of(lax.rem(block, per) * BLOCK, BLOCK), BLOCK)]
        marks = marks[0].astype(F32)
        seg_ref[pl.ds(block, 1)] = marks[0:1][None]
        marks = marks.T
        tag_ref[at, :] = jnp.where(marks[:, 1:2] == 1.0, marks[:, 0:1], -1.0)
        slot = lax.broadcasted_iota(jnp.int32, (BLOCK, 128), 1).astype(F32)
        spot = (slot == marks[:, 2:3]) | (slot == 14 + marks[:, 3:4]) | (slot == 28 + marks[:, 4:5])
        angles = lax.dot_general(
            jnp.where(spot, 1.0, 0.0),
            table[...],
            (((1,), (0,)), ((), ())),
            precision=lax.Precision.HIGHEST,
            preferred_element_type=F32,
        )
        turn_ref[at, :] = angles
        cosine, sine = angles[:, :128], angles[:, 128:]
        unit, _ = norm_parts(tok_box[at, :].astype(F32))
        normed = (unit * vec_ref[0:1, :] + vec_ref[1:2, :]).astype(BF)
        norm_ref[...] = normed
        proj = dot(normed, qkv_box[...], 1, 0)
        parts = [proj[:, i * width : (i + 1) * width] + vec_ref[2 + i : 3 + i, mine] for i in range(3)]
        q_ref[at, :] = turn(parts[0], cosine, sine, head_dim // 2, 1).astype(BF)
        k_ref[at, :] = turn(parts[1], cosine, sine, head_dim // 2, 1).astype(BF)
        v_ref[at, :] = parts[2].astype(BF)
        values_turned[:, at] = parts[2].T.astype(BF)

    @pl.when(step > blocks)
    def _():
        place = step - blocks - 1
        block = lax.rem((n + 1) * per + place, blocks)
        at = rows_at(block, BLOCK)
        query = q_ref[at, :] * jnp.asarray(head_dim**-0.5, BF)
        seg = seg_ref[pl.ds(block, 1)][0]
        masked_query = [
            jnp.where(head_lanes(query.shape, h, head_dim), query, jnp.zeros_like(query)) for h in range(heads)
        ]
        acc[...] = jnp.zeros_like(acc)
        peak[...] = jnp.full_like(peak, -1e30)
        total[...] = jnp.zeros_like(total)

        def body(j, carry):
            start = pl.multiple_of(j * BLOCK, BLOCK)
            key = k_ref[pl.ds(start, BLOCK), :]
            allowed = tag_ref[pl.ds(start, BLOCK), :] == seg
            scores = [jnp.where(allowed, dot(key, masked_query[h], 1, 1), -1e30) for h in range(heads)]
            for h in range(heads):
                lines = slice(h * head_dim, (h + 1) * head_dim)
                old = peak[h : h + 1, :]
                new = jnp.maximum(old, jnp.max(scores[h], axis=0, keepdims=True))
                probs = jnp.exp(scores[h] - new)
                keep = jnp.exp(old - new)
                peak[h : h + 1, :] = new
                total[h : h + 1, :] = total[h : h + 1, :] * keep + jnp.sum(probs, axis=0, keepdims=True)
                value = values_turned[lines, pl.ds(start, BLOCK)]
                acc[lines, :] = acc[lines, :] * keep + dot(value, probs.astype(BF), 1, 0)
            return carry

        low, high = meeting(block, blocks)
        lax.fori_loop(low, high, body, 0)
        parts = [acc[h * head_dim : (h + 1) * head_dim, :] / total[h : h + 1, :] for h in range(heads)]
        out = jnp.concatenate(parts, axis=0).T.astype(BF)
        o_ref[at, :] = out
        o_box[at, :] = out
        lse_ref[pl.ds(block, 1)] = (peak[...] + jnp.log(jnp.maximum(total[...], 1e-30)))[None]

        @pl.when(place < blocks - per)
        def _():
            result(place).start()

    @pl.when(step == final)
    def _():
        for s in range(per):
            result_here(s).start()
        for arrival, follow in at_step[final + 1]:
            go.arrived(arrival)
            go.launch(*follow)
        for copy in own_out + kept:
            copy.wait()
        for s in range(blocks - per):
            result(s).wait()
        for s in range(per):
            result_here(s).wait()
        go.finish()


def forward_call(tok, vec, tag, table, weights, head_dim, wide, narrow):
    qkv, out, up, down = weights
    group_rows, depth = tok.shape
    rows = group_rows * narrow
    width = depth // narrow
    heads = width // head_dim
    blocks = rows // BLOCK
    column = wide // 2
    size = qkv.shape[0]
    half = up.shape[1] // 2
    copies = (wide - 1) + (narrow - 1) + 12 + (2 * column - 1)
    copies += 2 + 3 * (column - 1) + column + 2 * (2 * (2 * column - 1) + 2 * column)
    whole = lambda a: pl.BlockSpec(a.shape, lambda i: (0,) * len(a.shape), pipeline_mode=pl.Buffered(1))
    anywhere = pl.BlockSpec(memory_space=pl.ANY)
    shaped = jax.ShapeDtypeStruct
    head_rows = shaped((rows, width), BF)
    inside = [
        head_rows, head_rows, head_rows, shaped((rows, 256), F32), shaped((rows, depth), BF), shaped((16, depth), F32),
        shaped((blocks, 1, BLOCK), F32), shaped((rows, 1), F32), head_rows, shaped((blocks, 8, BLOCK), F32),
    ]
    inside_specs = [whole(a) for a in inside]
    inside_specs[4] = pl.BlockSpec((BLOCK, depth), lambda i: (jnp.minimum(jnp.maximum(i - 1, 0), blocks - 1), 0))
    outside = [
        shaped((rows, depth), BF), shaped((depth, 3 * width), BF), shaped((group_rows, depth), BF),
        shaped((depth, depth), BF), shaped((depth, half), BF), shaped((depth, half), BF),
    ]
    small = [(size, 3 * width), (size, depth // 2), (size, half), (size, half)]
    return pl.pallas_call(
        functools.partial(forward_kernel, heads, head_dim, wide, narrow),
        grid=(2 * blocks + 1,),
        in_specs=[whole(a) for a in (tok, vec, tag, table)] + [anywhere] * 4,
        out_specs=inside_specs + [anywhere] * 6,
        out_shape=inside + outside,
        scratch_shapes=[
            pltpu.VMEM((wide,) + vec.shape, BF),
            pltpu.VMEM((narrow,) + tag.shape, jnp.int32),
            pltpu.VMEM((rows, depth), BF),
            pltpu.VMEM((depth, 3 * width), BF),
        ]
        + [pltpu.VMEM(shape, BF) for shape in small]
        + [pltpu.VMEM(shape, F32) for shape in small]
        + [
            pltpu.VMEM((width, rows), BF),
            pltpu.VMEM((width, BLOCK), F32),
            pltpu.VMEM((8, BLOCK), F32),
            pltpu.VMEM((8, BLOCK), F32),
            pltpu.VMEM((rows, width), BF),
            pltpu.SemaphoreType.DMA((copies,)),
            pltpu.SemaphoreType.DMA((copies,)),
            pltpu.SemaphoreType.DMA((blocks,)),
            pltpu.SemaphoreType.DMA((blocks,)),
            pltpu.SemaphoreType.DMA((6,)),
            pltpu.SemaphoreType.DMA((7 + blocks // narrow,)),
        ],
        compiler_params=pltpu.CompilerParams(
            collective_id=3, has_side_effects=True, vmem_limit_bytes=48 * 1024 * 1024
        ),
        cost_estimate=pl.CostEstimate(
            flops=heads * rows * rows * width * 4, bytes_accessed=rows * width * 8, transcendentals=heads * rows * rows
        ),
        name="attention_forward",
    )(tok, vec, tag, table, qkv, out, up, down)


class Scatter:
    def __init__(self, go, wide, narrow, split, part, near_in, own, far_out, far_in, box, local, *extra):
        w, self.n = lax.axis_index("wide"), lax.axis_index("narrow")
        self.go, self.column, self.split = go, wide // 2, split
        self.near_in, self.own, self.far_out, self.far_in, self.box = near_in, own, far_out, far_in, box
        z, y, x = w // 2, lax.rem(w, 2), self.n // 2
        near, mate, cross = w + 1 - 2 * y, self.n + 1 - 2 * lax.rem(self.n, 2), lax.rem(self.n + 2, narrow)
        size, cols = part.shape[0] // wide, box.shape[2]
        towards = [across_column(z, d) for d in range(self.column - 1, -1, -1)]
        theirs, ours = [to * 2 + 1 - y for to in towards], [to * 2 + y for to in towards]
        here = pl.ds(pl.multiple_of(x * cols, cols), cols) if split else pl.ds(0, cols)
        self.loads = [
            pltpu.make_async_copy(part.at[rows_at(i, size), here], own.at[k], local.at[k])
            for k, i in enumerate(ours + theirs if split else ours)
        ]
        self.zero = []
        if split:
            self.cross_in, self.out = extra
            there = pl.ds(pl.multiple_of((1 - x) * cols, cols), cols)
            order = list(enumerate(ours + theirs))
            order = order[self.column :] + order[: self.column]
            self.zero = {
                k: go.make(part.at[rows_at(i, size), there], self.cross_in.at[k], narrow=cross) for k, i in order
            }
        self.first = [
            go.make(self.out.at[k] if split else part.at[rows_at(i, size)], near_in.at[k], wide=near)
            for k, i in enumerate(theirs)
        ]
        self.second = [go.make(far_out.at[k], far_in.at[k], wide=i) for k, i in enumerate(ours[:-1])]
        self.over = go.make(box.at[self.n], box.at[self.n], narrow=cross)
        self.beside = go.make(box.at[self.n], box.at[self.n], narrow=mate)
        self.passed = go.make(box.at[cross], box.at[cross], narrow=mate)

    def load(self):
        for copy in self.loads:
            copy.start()
        if self.split:
            self.go.launch(*self.zero.values())

    def summed(self, k):
        self.loads[k].wait()
        value = self.own[k].astype(F32)
        if self.split:
            self.go.arrived(self.zero[k])
            value = value + self.cross_in[k].astype(F32)
        return value

    def send(self, k):
        if self.split:
            self.out[k] = self.summed(self.column + k).astype(BF)
        self.go.launch(self.first[k])

    def relay(self, k):
        self.go.arrived(self.first[k])
        if k < self.column - 1:
            self.far_out[k] = (self.summed(k) + self.near_in[k].astype(F32)).astype(BF)
            self.go.launch(self.second[k])

    def total(self):
        value = self.summed(self.column - 1) + self.near_in[self.column - 1].astype(F32)
        for k in range(self.column - 1):
            self.go.arrived(self.second[k])
            value = value + self.far_in[k].astype(F32)
        self.box[pl.ds(self.n, 1)] = value.astype(BF)[None]
        self.go.launch(self.over, self.beside)

    def share(self):
        self.go.arrived(self.over)
        self.go.launch(self.passed)

    @staticmethod
    def copies(wide, split):
        return 2 * (wide // 2) - 1 + 3 + (wide if split else 0)

    @staticmethod
    def scratch(wide, narrow, rows, cols, split):
        column, size = wide // 2, rows // wide
        cols = cols // 2 if split else cols
        many = wide if split else column
        sizes = [column, many, column - 1, column - 1, narrow]
        first = [pltpu.VMEM((count, size, cols), BF) for count in sizes] + [pltpu.SemaphoreType.DMA((many,))]
        return first + ([pltpu.VMEM((count, size, cols), BF) for count in (wide, column)] if split else [])


def square_sum(value):
    return jnp.sum(jnp.sum(value * value, axis=0, keepdims=True), axis=1, keepdims=True)


def backward_kernel(
    heads, head_dim, wide, narrow,
    q_ref, k_ref, v_ref, o_ref, g_ref, lse_ref, seg_ref, tag_ref, turn_ref, part_out, part_down, part_up,
    grads_out, shards_out, shards_down, shards_up, squares_out,
    q_heads, g_heads, delta, grad_query, send, recv, *boxes,
):
    step = pl.program_id(0)
    rows, width = q_ref.shape
    blocks = rows // BLOCK
    last = blocks - 1
    scale = head_dim**-0.5
    half = head_dim // 2
    go = Copies(send, recv)
    column = wide // 2
    outs = Scatter(go, wide, narrow, False, part_out, *boxes[:6])
    ups = Scatter(go, wide, narrow, False, part_up, *boxes[6:12])
    downs = Scatter(go, wide, narrow, True, part_down, *boxes[12:])

    @pl.when(step == 0)
    def _():
        w, n = lax.axis_index("wide"), lax.axis_index("narrow")
        z, y = w // 2, lax.rem(w, 2)
        greet(
            [{"wide": w + 1 - 2 * y}]
            + [{"wide": across_column(z, d) * 2 + y} for d in range(1, column)]
            + [{"narrow": n + 1 - 2 * lax.rem(n, 2)}, {"narrow": lax.rem(n + 2, narrow)}]
        )
        for k in range(column):
            ups.send(k)
        for scatter in (downs, ups, outs):
            scatter.load()

    part = lambda i: range(column * i // 4, column * (i + 1) // 4)
    plan = {
        2: [(ups.relay, part(0))],
        4: [(ups.relay, part(1))],
        5: [(downs.send, range(column // 2))],
        6: [(ups.relay, part(2))],
        7: [(downs.send, range(column // 2, column))],
        8: [(ups.relay, part(3)), (outs.send, range(column))],
        10: [(downs.relay, part(0))],
        11: [(downs.relay, part(1)), (ups.total, None)],
        12: [(downs.relay, part(2))],
        13: [(downs.relay, part(3)), (ups.share, None)],
        14: [(outs.relay, range(column // 2))],
        15: [(outs.relay, range(column // 2, column)), (downs.total, None)],
    }

    def act(i):
        for action, ks in plan[i]:
            for k in [None] if ks is None else ks:
                action() if k is None else action(k)

    for i in range(0, 2 * blocks, 2):
        if i in plan:

            @pl.when(step == i // 2)
            def _():
                act(i)

    @pl.when(step == 0)
    def _():
        grad_query[...] = jnp.zeros_like(grad_query)
        row = lax.broadcasted_iota(jnp.int32, (8, width), 0)
        lane = lax.broadcasted_iota(jnp.int32, (8, width), 1)
        pick = jnp.where(lane // head_dim == row, 1.0, 0.0)

        def prepare(i, carry):
            at = pl.ds(pl.multiple_of(i * BLOCK, BLOCK), BLOCK)
            query = q_ref[at, :] * jnp.asarray(scale, BF)
            grad = g_ref[at, :]
            for h in range(heads):
                lanes = head_lanes(query.shape, h, head_dim)
                q_heads[h, at, :] = jnp.where(lanes, query, jnp.zeros_like(query))
                g_heads[h, at, :] = jnp.where(lanes, grad, jnp.zeros_like(grad))
            product = grad.astype(F32) * o_ref[at, :].astype(F32)
            delta[pl.ds(i, 1)] = lax.dot_general(
                pick,
                product,
                (((1,), (1,)), ((), ())),
                precision=lax.Precision.HIGHEST,
                preferred_element_type=F32,
            )[None]
            return carry

        lax.fori_loop(0, blocks, prepare, 0)

    key = k_ref[...]
    value = v_ref[...]
    tag = tag_ref[...]
    masked_key = [jnp.where(head_lanes(key.shape, h, head_dim), key, jnp.zeros_like(key)) for h in range(heads)]

    def body(i, carry):
        for half_step in range(1, 2 * blocks, 2):
            if half_step in plan:

                @pl.when((step == half_step // 2) & (i == blocks // 2))
                def _():
                    act(half_step)

        grad_key, grad_value = carry
        at = pl.ds(pl.multiple_of(i * BLOCK, BLOCK), BLOCK)
        allowed = tag == seg_ref[pl.ds(i, 1), :]
        lse = lse_ref[pl.ds(i, 1)][0]
        dlt = delta[pl.ds(i, 1)][0]
        total = None
        for h in range(heads):
            query = q_heads[h, at, :]
            grad = g_heads[h, at, :]
            scores = dot(key, query, 1, 1)
            probs = jnp.where(allowed, jnp.exp(scores - lse[h : h + 1, :]), 0.0)
            grad_probs = dot(value, grad, 1, 1)
            grad_scores = (probs * (grad_probs - dlt[h : h + 1, :])).astype(BF)
            grad_value = grad_value + dot(probs.astype(BF), grad, 1, 0)
            grad_key = grad_key + dot(grad_scores, query, 1, 0)
            term = dot(grad_scores, masked_key[h], 0, 0)
            total = term if total is None else total + term
        grad_query[at, :] += total
        return grad_key, grad_value

    zero = jnp.zeros((BLOCK, width), F32)
    low, high = meeting(step, blocks)
    grad_key, grad_value = lax.fori_loop(low, high, body, (zero, zero))
    here = pl.ds(pl.multiple_of(step * BLOCK, BLOCK), BLOCK)
    cosine, sine = turn_ref[here, :128], turn_ref[here, 128:]
    grads_out[here, width : 2 * width] = turn(grad_key, cosine, sine, half, -1).astype(BF)
    grads_out[here, 2 * width :] = grad_value.astype(BF)

    @pl.when(step == last)
    def _():
        downs.share()
        outs.total()

        def finish(i, carry):
            at = pl.ds(pl.multiple_of(i * BLOCK, BLOCK), BLOCK)
            grads = grad_query[at, :] * scale
            grads_out[at, :width] = turn(grads, turn_ref[at, :128], turn_ref[at, 128:], half, -1).astype(BF)
            return carry

        lax.fori_loop(0, blocks, finish, 0)
        outs.share()
        go.finish()
        squares = jnp.zeros((1, 1), F32)
        for box in (outs.box, ups.box):
            for i in range(2):
                squares += square_sum(box[i].astype(F32) + box[i + 2].astype(F32))
        for i in range(narrow):
            squares += square_sum(downs.box[i].astype(F32))
        squares_out[...] = jnp.broadcast_to(squares, squares_out.shape)
        shards_out[...] = outs.box[...]
        shards_down[...] = downs.box[...]
        shards_up[...] = ups.box[...]


def backward_call(q, k, v, o, g, lse, seg_rows, tag_col, turns, part_out, part_down, part_up, head_dim, wide, narrow):
    rows, width = q.shape
    heads = width // head_dim
    blocks = rows // BLOCK
    whole = lambda a: pl.BlockSpec(a.shape, lambda i: (0,) * len(a.shape), pipeline_mode=pl.Buffered(1))
    block = pl.BlockSpec((BLOCK, width), lambda i: (i, 0))
    anywhere = pl.BlockSpec(memory_space=pl.ANY)
    depth = part_up.shape[0]
    results = [
        jax.ShapeDtypeStruct((rows, 3 * width), BF),
        jax.ShapeDtypeStruct((narrow, depth // wide, part_out.shape[1]), BF),
        jax.ShapeDtypeStruct((narrow, depth // wide, part_down.shape[1] // 2), BF),
        jax.ShapeDtypeStruct((narrow, depth // wide, part_up.shape[1]), BF),
        jax.ShapeDtypeStruct((8, 128), F32),
    ]
    copies = 2 * Scatter.copies(wide, False) + Scatter.copies(wide, True)
    return pl.pallas_call(
        functools.partial(backward_kernel, heads, head_dim, wide, narrow),
        grid=(blocks,),
        in_specs=[
            whole(q), block, block, whole(o), whole(g), whole(lse), whole(seg_rows),
            pl.BlockSpec((BLOCK, 1), lambda i: (i, 0)),
            whole(turns), anywhere, anywhere, anywhere,
        ],
        out_specs=[whole(a) for a in results],
        out_shape=results,
        scratch_shapes=[
            pltpu.VMEM((heads, rows, width), BF),
            pltpu.VMEM((heads, rows, width), BF),
            pltpu.VMEM((blocks, 8, BLOCK), F32),
            pltpu.VMEM((rows, width), F32),
            pltpu.SemaphoreType.DMA((copies,)),
            pltpu.SemaphoreType.DMA((copies,)),
        ]
        + Scatter.scratch(wide, narrow, depth, part_out.shape[1], False)
        + Scatter.scratch(wide, narrow, depth, part_up.shape[1], False)
        + Scatter.scratch(wide, narrow, depth, part_down.shape[1], True),
        compiler_params=pltpu.CompilerParams(
            collective_id=4, has_side_effects=True, vmem_limit_bytes=60 * 1024 * 1024
        ),
        cost_estimate=pl.CostEstimate(
            flops=heads * rows * rows * width * 7, bytes_accessed=rows * width * 20, transcendentals=heads * rows * rows
        ),
        name="attention_backward",
    )(q, k, v, o, g, lse, seg_rows, tag_col, turns, part_out, part_down, part_up)


def norm_parts(values):
    center = values - jnp.mean(values, axis=-1, keepdims=True)
    inverse = lax.rsqrt(jnp.mean(center * center, axis=-1, keepdims=True) + 1e-06)
    return center * inverse, inverse


def norm_back(grads, gain, unit, inverse):
    scaled = grads * gain
    return inverse * (
        scaled - jnp.mean(scaled, axis=-1, keepdims=True) - unit * jnp.mean(scaled * unit, axis=-1, keepdims=True)
    )


def adamw(param, grad, first, second, clip, rate, decay, fix_first, fix_second):
    clipped = grad * clip
    moment = 0.9 * first + 0.1 * clipped
    square = 0.999 * second + 0.001 * clipped * clipped
    direction = moment / fix_first / (jnp.sqrt(square / fix_second) + 1e-08)
    return (param - rate * (direction + decay * param), moment, square)


def on_device(
    tokens, cotangent, segment_ids, key_keep, patch_coords, step_count,
    weight_qkv, weight_out, weight_up, weight_down, vectors,
    first_qkv, first_out, first_up, first_down, first_vectors,
    second_qkv, second_out, second_up, second_down, second_vectors,
):
    rows, width = tokens.shape
    hidden = weight_up.shape[1]
    head_dim = width // HEADS
    narrow = lax.axis_size("narrow")
    wide = lax.axis_size("wide")
    shard_rows = width // wide
    me = lax.axis_index("narrow")
    side = me % 2
    mine = width // narrow
    half_hidden = hidden // 2
    group = rows * narrow

    def mate(value):
        return lax.ppermute(value, "narrow", [(i, i ^ 1) for i in range(narrow)])

    def across(value):
        return lax.ppermute(value, "narrow", [(i, i ^ 2) for i in range(narrow)])

    def take(value, start, size, axis=1):
        return lax.dynamic_slice_in_dim(value, start, size, axis)

    shard_cols = vectors.shape[1]
    vec_shard = jnp.pad(vectors.astype(BF), ((0, 16 - vectors.shape[0]), (0, -shard_cols % 128)))
    tag = jnp.concatenate([segment_ids[None], key_keep[None], patch_coords, patch_coords], axis=0)
    (
        query, keys, values, turns, normed1_all, vec, seg_rows, tag_col, mixed_mine, lse,
        tokens_all, qkv_w, mixed, out_w, up_w, down_w,
    ) = forward_call(
        tokens, vec_shard, tag, rotary_table(head_dim), (weight_qkv, weight_out, weight_up, weight_down),
        head_dim, wide, narrow,
    )
    vec = vec[: vectors.shape[0]]
    xin = tokens.astype(F32)
    unit1, inverse1 = norm_parts(xin)
    cot_pair = jnp.concatenate([cotangent, mate(cotangent)], axis=0)

    resid = xin + (dot(mixed, out_w, 1, 0) + vec[5])
    unit2, inverse2 = norm_parts(resid)
    normed2 = (unit2 * vec[6] + vec[7]).astype(BF)
    normed2_pair = jnp.concatenate([normed2, mate(normed2)], axis=0)
    up_bias = take(vec[9:].reshape(1, -1), side * half_hidden, half_hidden)
    up_pre = dot(normed2_pair, up_w, 1, 0) + up_bias
    erf_part = 0.5 * (1.0 + lax.erf(up_pre * (0.5**0.5)))
    act = (up_pre * erf_part).astype(BF)
    slope = erf_part + up_pre * (jnp.exp(-0.5 * up_pre * up_pre) * ((2.0 * jnp.pi) ** -0.5))
    part_down = dot(cot_pair, act, 0, 0).astype(BF)
    down_theirs = mate(dot(act[rows:], down_w, 1, 1))
    down = dot(act[:rows], down_w, 1, 1) + down_theirs
    layer_out = (resid + (down + vec[8])).astype(BF)

    grad_up_act = (dot(cot_pair, down_w, 1, 0) * slope).astype(BF)
    part_up = dot(normed2_pair, grad_up_act, 0, 0).astype(BF)
    grad_theirs = mate(dot(grad_up_act[rows:], up_w, 1, 1))
    grad_normed2 = dot(grad_up_act[:rows], up_w, 1, 1) + grad_theirs
    cot = cotangent.astype(F32)
    grad_resid = cot + norm_back(grad_normed2, vec[6], unit2, inverse2)
    grad_branch = grad_resid.astype(BF)
    grad_mixed = dot(grad_branch, out_w, 1, 1).astype(BF)
    part_out = dot(mixed, grad_branch, 0, 0)
    own_out = take(part_out, side * (width // 2), width // 2)
    other_out = take(part_out, (1 - side) * (width // 2), width // 2)
    part_out = (own_out + mate(other_out.astype(BF)).astype(F32)).astype(BF)

    grad_mixed_mine = lax.all_to_all(grad_mixed, "narrow", 1, 0, tiled=True)
    grad_proj, shards_out, shards_down, shards_up, squares = backward_call(
        query, keys, values, mixed_mine, grad_mixed_mine, lse, seg_rows[:, 0], tag_col, turns, part_out, part_down, part_up, head_dim, wide, narrow,
    )
    proj_sums = jnp.sum(grad_proj.astype(F32), axis=0).reshape(3, mine)
    proj_rows = lax.dynamic_update_slice(jnp.zeros((3, width), F32), proj_sums, (0, me * mine))
    up_sums = jnp.sum(grad_up_act.astype(F32), axis=0)
    up_rows = lax.dynamic_update_slice(jnp.zeros((hidden,), F32), up_sums, (side * half_hidden,))
    vector_part = jnp.concatenate(
        [
            jnp.zeros((2, width), F32),
            proj_rows,
            jnp.sum(grad_branch.astype(F32), axis=0)[None],
            jnp.sum(grad_normed2 * unit2, axis=0)[None],
            jnp.sum(grad_normed2, axis=0)[None],
            jnp.sum(cot, axis=0)[None],
            up_rows.reshape(hidden // width, width),
            jnp.zeros((16 - vectors.shape[0], width), F32),
        ],
        axis=0,
    )
    grad_normed1, total_qkv, vector_total, square_total = tail_call(
        normed1_all, grad_proj, qkv_w, tokens_all, vector_part, squares, wide, narrow
    )
    grad_tokens = (grad_resid + norm_back(grad_normed1, vec[0], unit1, inverse1)).astype(BF)

    def join(shards):
        shards = shards.astype(F32)
        return jnp.concatenate([shards[0] + shards[2], shards[1] + shards[3]], axis=1)

    total_up = join(shards_up)
    total_down = jnp.concatenate([shards_down[i] for i in (0, 2, 1, 3)], axis=1).astype(F32)
    total_out = join(shards_out)
    total_qkv = total_qkv.astype(F32)
    grad_norm = jnp.sqrt(square_total[0, 0])
    clip = 1.0 / jnp.maximum(grad_norm, 1.0)
    count = step_count[0].astype(F32)
    rate = 0.4 * count / (count + 4.0)
    decay = 0.04 + 0.018 * count
    fix_first = 1.0 - jnp.power(0.9, count)
    fix_second = 1.0 - jnp.power(0.999, count)
    grad_vectors = vector_total[: vectors.shape[0], :shard_rows]

    def update(param, grad, first, second, decay_here):
        return adamw(param, grad, first, second, clip, rate, decay_here, fix_first, fix_second)

    new_qkv = update(weight_qkv, total_qkv, first_qkv, second_qkv, decay)
    new_out = update(weight_out, total_out, first_out, second_out, decay)
    new_up = update(weight_up, total_up, first_up, second_up, decay)
    new_down = update(weight_down, total_down, first_down, second_down, decay)
    new_vectors = update(vectors, grad_vectors, first_vectors, second_vectors, 0.0)
    news = (new_qkv, new_out, new_up, new_down, new_vectors)
    return (layer_out, grad_tokens) + tuple(n[i] for i in range(3) for n in news) + (grad_norm, grad_vectors[8])


def solution(mesh):
    by_token = P(("wide", "narrow"), None)
    ids = P(("wide", "narrow"))
    by_row = P("wide", None)
    by_column = P(None, "wide")
    params = (by_row,) * 4 + (by_column,)
    return jax.shard_map(
        on_device,
        mesh=mesh,
        in_specs=(by_token, by_token, ids, ids, P(None, ("wide", "narrow")), P()) + params * 3,
        out_specs=(by_token, by_token) + params * 3 + (P(), P("wide")),
        check_vma=False,
    )
```
